32 devices in a mesh: expert: 4 (over y, x), shard: 8 (over z, core).
Axes of the slice: x: 2, y: 2, z: 4, core: 2. Of those that a mesh axis runs over, the one named last changes fastest.
Arguments:
- tokens: bfloat16 [4096, 2304], P(('expert', 'shard')), may hold values from -6 to 6
- seq_lengths: int32 [32, 2], P(('expert', 'shard')), may hold values from 32 to 96, as said below
- routes: int32 [4096, 2], P(('expert', 'shard')), may hold values from 0 to 3, all different within a row; in each aligned block of 128 rows (0 to 127, 128 to 255, ...) at most 80 rows name the same one
- norm_attn: bfloat16 [2304], P('shard'), may hold values from 0.5 to 1.5
- w_query: bfloat16 [2304, 2304], P('shard'), may hold values from -0.125 to 0.125
- w_key: bfloat16 [2304, 2304], P('shard'), may hold values from -0.125 to 0.125
- w_value: bfloat16 [2304, 2304], P('shard'), may hold values from -0.125 to 0.125
- w_output: bfloat16 [2304, 2304], P('shard'), may hold values from -4 to 4
- norm_ffn: bfloat16 [2304], P('shard'), may hold values from 0.5 to 1.5
- w_router: bfloat16 [2304, 4], P('shard'), may hold values from -0.125 to 0.125
- w_in: bfloat16 [2304, 4, 11520], P('shard', 'expert'), may hold values from -0.125 to 0.125
- w_down: bfloat16 [5760, 4, 2304], P('shard', 'expert'), may hold values from -0.3125 to 0.3125
- cotangent: bfloat16 [4096, 2304], P(('expert', 'shard')), may hold values from -6 to 6
Outputs:
- activations: bfloat16 [4096, 2304], P(('expert', 'shard'))
- grad_tokens: float32 [4096, 2304], P(('expert', 'shard'))
- grad_norm_attn: float32 [2304], P('shard')
- grad_w_query: float32 [2304, 2304], P('shard')
- grad_w_key: float32 [2304, 2304], P('shard')
- grad_w_value: float32 [2304, 2304], P('shard')
- grad_w_output: float32 [2304, 2304], P('shard')
- grad_norm_ffn: float32 [2304], P('shard')
- grad_w_router: float32 [2304, 4], P('shard')
- grad_w_in: float32 [2304, 4, 11520], P('shard', 'expert')
- grad_w_down: float32 [5760, 4, 2304], P('shard', 'expert')
The draws below stay inside these ranges and needn't reach their ends.
Inputs may be any that keep to these rules, and one draw needn't show every extreme that they name: `routes`: within the 128 rows of one device no expert is named by more than 80 rows; each row names two different experts. `seq_lengths`: the two lengths of a device add up to 128; its first sequence takes its first rows.
All inputs are finite; a program needn't handle non-finite values.
Results may differ from the reference program's by a relative error of at most 0.014.
The reference program's roundings to bfloat16 on the way count: a program that leaves them out, or rounds other values in their place, can miss the bound.
Values may be sent and summed in bfloat16 or wider, within the bound.
A program may use at most 704 MiB of HBM per device.

```python
import math
import jax
import jax.numpy as jnp
import numpy as np
from jax import lax

D = 2304
HEADS = 36
FF = 5760
TOK_DEV = 128
EXPERTS = 4
CAP = 80
GROUPS = 32
TOKENS = 4096
N_EXPERT = 4
N_SHARD = 8


def draw_seq_lengths(key, part):
    lowest = TOK_DEV // 4
    highest = TOK_DEV - lowest
    leading = jax.random.randint(jax.random.fold_in(key, 31), (GROUPS,), lowest, highest + 1).astype(jnp.int32)
    picked = jax.random.randint(jax.random.fold_in(key, 32), (), 0, GROUPS)
    leading = leading.at[picked].set(highest)
    return jnp.stack([leading, TOK_DEV - leading], axis=1).astype(jnp.int32)


def shard_levels(own_key, dims, split, least, top_value):
    loudness = 1.0
    for position, blocks in split:
        heights = jax.random.uniform(jax.random.fold_in(jax.random.fold_in(own_key, 6), position), (blocks,), jnp.float32, least / len(split), top_value / len(split))
        loudness = loudness * jnp.repeat(jnp.exp(heights), dims[position] // blocks).reshape((-1,) + (1,) * (len(dims) - 1 - position))
    return loudness


def shared_out(own_key, own, number, rows, amount, top, reach, skew):
    order = jax.random.permutation(own_key, amount)
    crowded, common = load_shares(amount, rows * top, reach, skew, True), load_shares(amount, rows * top, reach, skew, False)
    places = jnp.arange(amount)

    def named(sizes, rotation):
        used = int((sizes > 0).sum())
        fixed = max(1, used // 4)
        shifted = fixed + (places - fixed + rotation * (used - fixed)) % max(1, amount - fixed)
        return jnp.zeros((amount,), jnp.int32).at[order[jnp.where(places < fixed, places, shifted)]].set(jnp.asarray(sizes, jnp.int32))

    sizes = jnp.where(number % 4 == 0, named(crowded, number // 4), named(common, number - number // 4 - 1))
    mixed = jax.random.permutation(jax.random.fold_in(own, 3), amount)
    donor, receiver = mixed[0:amount // 2 * 2:2], mixed[1:amount // 2 * 2:2]
    room = jnp.minimum(sizes[donor] - 1, reach - sizes[receiver]) // 2
    room = jnp.where((donor == order[0]) | (receiver == order[0]) | (sizes[receiver] == 0), 0, jnp.maximum(room, 0))
    shifted = jax.random.randint(jax.random.fold_in(own, 4), (amount // 2,), 0, 1 << 20) % (room + 1)
    sizes = sizes.at[donor].add(-shifted).at[receiver].add(shifted)
    items = jnp.searchsorted(jnp.cumsum(sizes), jnp.arange(rows * top), side="right").astype(jnp.int32)
    grid = items.reshape(top, rows).T
    grid = grid[jax.random.permutation(jax.random.fold_in(own, 1), rows)]
    rotation = jax.random.randint(jax.random.fold_in(own, 2), (rows, 1), 0, top)
    return jnp.take_along_axis(grid, (jnp.arange(top)[None, :] + rotation) % top, axis=1)


def load_shares(count, total, limit, skew, full):
    weights = [(1 << 20) // math.isqrt(rank ** skew) + 1 for rank in range(1, count + 1)]
    largest = limit if full else min(limit, max(-(-total // count), total * weights[0] // sum(weights)))
    least = 1 if total - largest >= count - 1 else 0
    holding, surplus = [largest] + [least] * (count - 1), total - largest - least * (count - 1)
    while surplus > 0:
        free = [i for i in range(1, count) if holding[i] < largest] or [i for i in range(1, count) if holding[i] < limit]
        pool, left = sum([weights[i] for i in free]), surplus
        for i in free:
            addition = min(limit - holding[i], max(1, left * weights[i] // pool), surplus)
            holding[i] = holding[i] + addition
            surplus = surplus - addition
    return np.array(holding)


def noise(own_key, shape, deviation, reach, cuts=(), dtype=jnp.bfloat16):
    result = jax.random.normal(own_key, shape, jnp.float32) * deviation
    if len(cuts) > 0:
        result = shard_levels(own_key, shape, cuts, -0.22, 0.18) * result
    return jnp.clip(result, min=-reach, max=reach).astype(dtype)


def setup_inputs(seed: int = 0) -> dict:
    arg_keys = jax.random.split(jax.random.key(seed), 14)
    tokens = noise(arg_keys[0], (TOKENS, D), 1.0, 6.0, ((0, 32),))
    seq_lengths = draw_seq_lengths(jax.random.fold_in(arg_keys[13], 71), 0)
    routes_keys = jax.random.split(jax.random.fold_in(arg_keys[2], 1), TOKENS // TOK_DEV)
    routes_turns = jax.random.permutation(jax.random.fold_in(arg_keys[2], 3), TOKENS // TOK_DEV)
    routes = jax.vmap(lambda own, number: shared_out(jax.random.fold_in(arg_keys[2], 2), own, number, TOK_DEV, EXPERTS, 2, CAP, 1))(routes_keys, routes_turns).reshape((TOKENS, 2))
    norm_attn = jnp.clip(1.0 + 0.1 * jax.random.normal(arg_keys[3], (D,), jnp.float32), 0.5, 1.5).astype(jnp.bfloat16)
    w_query = noise(arg_keys[4], (D, D), D ** -0.5, 0.125, ((0, 8),))
    w_key = noise(arg_keys[5], (D, D), D ** -0.5, 0.125, ((0, 8),))
    w_value = noise(arg_keys[6], (D, D), D ** -0.5, 0.125, ((0, 8),))
    w_output = noise(arg_keys[7], (D, D), (max(D // 1024, 1)) ** -0.5, 4.0, ((0, 8),))
    norm_ffn = jnp.clip(1.0 + 0.1 * jax.random.normal(arg_keys[8], (D,), jnp.float32), 0.5, 1.5).astype(jnp.bfloat16)
    w_router = noise(arg_keys[9], (D, EXPERTS), D ** -0.5, 0.125, ((0, 8),))
    w_in = noise(arg_keys[10], (D, EXPERTS, 2 * FF), D ** -0.5, 0.125, ((0, 8), (1, 4)))
    w_down = noise(arg_keys[11], (FF, EXPERTS, D), (FF // 16) ** -0.5, 0.3125, ((0, 8), (1, 4)))
    cotangent = noise(arg_keys[12], (TOKENS, D), 1.0, 6.0, ((0, 32),))
    return dict(tokens=tokens, seq_lengths=seq_lengths, routes=routes, norm_attn=norm_attn, w_query=w_query, w_key=w_key, w_value=w_value, w_output=w_output, norm_ffn=norm_ffn, w_router=w_router, w_in=w_in, w_down=w_down, cotangent=cotangent)


eps_norm = 1e-05
branch_scale = 1.4 / math.sqrt(40.0)
rope_base = 10000.0
masked_score = -1e+30

def rope_tables(positions, head_width):
    half_width = head_width // 2
    exponents = jnp.arange(half_width).astype(jnp.float32) * 2.0 / head_width
    frequency = rope_base ** (-exponents)
    angles = positions.astype(jnp.float32)[:, None] * frequency[None, :]
    return (jnp.cos(angles), jnp.sin(angles))

def rotate(values, cosine, sine_table):
    half_width = values.shape[-1] // 2
    leading = values[..., :half_width]
    trailing = values[..., half_width:]
    cos_rows = cosine[:, None, :]
    sin_rows = sine_table[:, None, :]
    return jnp.concatenate([leading * cos_rows - trailing * sin_rows, trailing * cos_rows + leading * sin_rows], axis=-1)

def rms_forward(values, norm_gain):
    inverse = lax.rsqrt(lax.optimization_barrier(jnp.mean(values * values, axis=-1, keepdims=True)) + eps_norm)
    return (values * inverse * norm_gain, inverse)

def rms_backward(values, inverse, norm_gain, upstream):
    weighted = upstream * norm_gain
    gain_grad = lax.optimization_barrier(jnp.sum(upstream * values * inverse, axis=0))
    inner_mean = lax.optimization_barrier(jnp.mean(weighted * values, axis=-1, keepdims=True))
    return (inverse * weighted - values * inverse * inverse * inverse * inner_mean, gain_grad)

def masked_scores(queries, keys_rot, allowed):
    head_width = queries.shape[-1]
    scores = jnp.einsum('qhd,khd->hqk', queries.astype(jnp.float32), keys_rot.astype(jnp.float32)) * (1.0 / math.sqrt(head_width))
    return jnp.where(allowed[None], scores, masked_score)

def reference(tokens, seq_lengths, routes, norm_attn, w_query, w_key, w_value, w_output, norm_ffn, w_router, w_in, w_down, cotangent):
    head_width = D // HEADS
    head_shape = (TOK_DEV, HEADS, head_width)
    gain_attn = norm_attn.astype(jnp.float32)
    gain_ffn = norm_ffn.astype(jnp.float32)
    router_float = w_router.astype(jnp.float32)
    highest = lax.Precision.HIGHEST

    def layer_front(token_block, lengths):
        row_index = jnp.arange(TOK_DEV).astype(jnp.int32)
        first_length = lengths[0]
        segment = (row_index >= first_length).astype(jnp.int32)
        positions = row_index - first_length * segment
        allowed = (segment[:, None] == segment[None, :]) & (row_index[None, :] <= row_index[:, None])
        cosine, sine_table = rope_tables(positions, head_width)
        residual_in = token_block.astype(jnp.float32)
        normed_in, inverse_in = rms_forward(residual_in, gain_attn)
        normed_half = normed_in.astype(jnp.bfloat16)
        queries = rotate(jnp.dot(normed_half, w_query, preferred_element_type=jnp.float32).reshape(head_shape), cosine, sine_table).astype(jnp.bfloat16)
        keys_rot = rotate(jnp.dot(normed_half, w_key, preferred_element_type=jnp.float32).reshape(head_shape), cosine, sine_table).astype(jnp.bfloat16)
        values = jnp.dot(normed_half, w_value, preferred_element_type=jnp.float32).astype(jnp.bfloat16).reshape(head_shape)
        scores = masked_scores(queries, keys_rot, allowed)
        row_peak = lax.optimization_barrier(jnp.max(scores, axis=-1, keepdims=True))
        log_total = row_peak + jnp.log(lax.optimization_barrier(jnp.sum(jnp.exp(scores - row_peak), axis=-1, keepdims=True)))
        probs_half = jnp.exp(scores - log_total).astype(jnp.bfloat16)
        context = jnp.einsum('hqk,khd->qhd', probs_half.astype(jnp.float32), values.astype(jnp.float32)).astype(jnp.bfloat16)
        context_flat = context.reshape(TOK_DEV, D)
        residual_mid = residual_in + branch_scale * jnp.dot(context_flat, w_output, preferred_element_type=jnp.float32)
        normed_mid, inverse_mid = rms_forward(residual_mid, gain_ffn)
        normed_mid_half = normed_mid.astype(jnp.bfloat16)
        return (allowed, cosine, sine_table, residual_in, inverse_in, normed_half, queries, keys_rot, values, log_total, context, residual_mid, inverse_mid, normed_mid_half)
    token_blocks = tokens.reshape(GROUPS, TOK_DEV, D)
    route_blocks = routes.reshape(GROUPS, TOK_DEV, 2)
    cot_blocks = cotangent.reshape(GROUPS, TOK_DEV, D)

    def front_block(block_args):
        token_block, lengths, route_block = block_args
        front = layer_front(token_block, lengths)
        normed_mid_half = front[13]
        logits = jnp.dot(normed_mid_half, w_router, preferred_element_type=jnp.float32)
        chosen = jnp.take_along_axis(logits, route_block, axis=1)
        return (normed_mid_half, jax.nn.softmax(chosen, axis=-1))
    normed_blocks, gate_blocks = lax.map(front_block, (token_blocks, seq_lengths, route_blocks))
    normed_all = normed_blocks.reshape(TOKENS, D)
    gate_all = gate_blocks.reshape(TOKENS, 2)
    flat_routes = routes.reshape(GROUPS, 2 * TOK_DEV)
    route_hits = (flat_routes[:, :, None] == jnp.arange(EXPERTS).astype(jnp.int32)[None, None, :]).astype(jnp.int32)
    earlier = jnp.cumsum(route_hits, axis=1) - route_hits
    slot_index = lax.optimization_barrier(jnp.sum(earlier * route_hits, axis=2)).astype(jnp.int32)
    group_ids = jnp.broadcast_to(jnp.arange(GROUPS).astype(jnp.int32)[:, None], flat_routes.shape)
    assign_ids = jnp.broadcast_to(jnp.arange(2 * TOK_DEV).astype(jnp.int32)[None, :], flat_routes.shape)
    slot_table = jnp.full((GROUPS, EXPERTS, CAP), 2 * TOK_DEV, jnp.int32).at[group_ids, flat_routes, slot_index].set(assign_ids)
    span_rows = N_SHARD * CAP

    def expert_loop(outer_carry, expert_id):
        gate_up_weight = lax.dynamic_index_in_dim(w_in, expert_id, 1, keepdims=False)
        down_weight = lax.dynamic_index_in_dim(w_down, expert_id, 1, keepdims=False)

        def span_step(running, block_id):
            mixture, mid_grad_acc, gate_grad_acc, grad_gate_up, grad_down_acc = running
            table_rows = lax.dynamic_slice(slot_table, (block_id * N_SHARD, expert_id, jnp.int32(0)), (N_SHARD, 1, CAP)).reshape(span_rows)
            valid = table_rows < 2 * TOK_DEV
            safe_rows = jnp.where(valid, table_rows, 0)
            group_of_row = block_id * N_SHARD + jnp.arange(span_rows).astype(jnp.int32) // CAP
            token_index = group_of_row * TOK_DEV + safe_rows // 2
            pick_index = safe_rows % 2
            expert_input = jnp.where(valid[:, None], normed_all[token_index], jnp.zeros((), jnp.bfloat16))
            gate_up = jnp.dot(expert_input, gate_up_weight, preferred_element_type=jnp.float32)
            gate_part = gate_up[:, :FF]
            up_part = gate_up[:, FF:]
            activated = (jax.nn.silu(gate_part) * up_part).astype(jnp.bfloat16)
            expert_out = jnp.dot(activated, down_weight, preferred_element_type=jnp.float32).astype(jnp.bfloat16)
            out_float = expert_out.astype(jnp.float32)
            weight_rows = jnp.where(valid, gate_all[token_index, pick_index], 0.0)
            mixture = mixture.at[token_index].add(weight_rows[:, None] * out_float)
            mixture_rows = branch_scale * cotangent[token_index].astype(jnp.float32)
            gate_grad_acc = gate_grad_acc.at[token_index, pick_index].add(jnp.where(valid, lax.optimization_barrier(jnp.sum(mixture_rows * out_float, axis=-1)), 0.0))
            out_grad = (weight_rows[:, None] * mixture_rows).astype(jnp.bfloat16)
            act_grad = jnp.dot(out_grad, jnp.transpose(down_weight), preferred_element_type=jnp.float32)
            sigmoid_gate = jax.nn.sigmoid(gate_part)
            pre_grad = jnp.concatenate([act_grad * up_part * sigmoid_gate * (1.0 + gate_part * (1.0 - sigmoid_gate)), act_grad * jax.nn.silu(gate_part)], axis=-1).astype(jnp.bfloat16)
            grad_down_acc = grad_down_acc + jnp.dot(jnp.transpose(activated), out_grad, preferred_element_type=jnp.float32)
            grad_gate_up = grad_gate_up + jnp.dot(jnp.transpose(expert_input), pre_grad, preferred_element_type=jnp.float32)
            input_grad = jnp.dot(pre_grad, jnp.transpose(gate_up_weight), preferred_element_type=jnp.float32).astype(jnp.bfloat16)
            mid_grad_acc = mid_grad_acc.at[token_index].add(jnp.where(valid[:, None], input_grad.astype(jnp.float32), 0.0))
            return ((mixture, mid_grad_acc, gate_grad_acc, grad_gate_up, grad_down_acc), None)
        mixture, mid_grad_acc, gate_grad_acc = outer_carry
        start = (mixture, mid_grad_acc, gate_grad_acc, jnp.zeros((D, 2 * FF), jnp.float32), jnp.zeros((FF, D), jnp.float32))
        finished, _ = lax.scan(span_step, start, jnp.arange(N_EXPERT).astype(jnp.int32))
        return ((finished[0], finished[1], finished[2]), (finished[3], finished[4]))
    expert_start = (jnp.zeros((TOKENS, D), jnp.float32), jnp.zeros((TOKENS, D), jnp.float32), jnp.zeros((TOKENS, 2), jnp.float32))
    (mixture_all, mid_grad_all, gate_grad_all), (grads_in_all, grads_down_all) = lax.scan(expert_loop, expert_start, jnp.arange(EXPERTS).astype(jnp.int32))
    grad_w_in = jnp.transpose(grads_in_all, (1, 0, 2))
    grad_w_down = jnp.transpose(grads_down_all, (1, 0, 2))

    def back_block(running, block_args):
        token_block, lengths, route_block, mixture_block, mid_grad_block, gate_block, gate_grad_block, cot_block = block_args
        allowed, cosine, sine_table, residual_in, inverse_in, normed_half, queries, keys_rot, values, log_total, context, residual_mid, inverse_mid, normed_mid_half = layer_front(token_block, lengths)
        context_flat = context.reshape(TOK_DEV, D)
        activations = (residual_mid + branch_scale * mixture_block).astype(jnp.bfloat16)
        upstream = cot_block.astype(jnp.float32)
        chosen_grad = gate_block * (gate_grad_block - lax.optimization_barrier(jnp.sum(gate_block * gate_grad_block, axis=-1, keepdims=True)))
        route_mask = (route_block[:, :, None] == jnp.arange(EXPERTS).astype(jnp.int32)[None, None, :]).astype(jnp.float32)
        logit_grad = lax.optimization_barrier(jnp.sum(chosen_grad[:, :, None] * route_mask, axis=1))
        normed_mid_grad = mid_grad_block + jnp.dot(logit_grad, jnp.transpose(router_float), precision=highest)
        router_grad = jnp.dot(jnp.transpose(normed_mid_half.astype(jnp.float32)), logit_grad, precision=highest)
        mid_norm_grad, gain_ffn_grad = rms_backward(residual_mid, inverse_mid, gain_ffn, normed_mid_grad)
        residual_grad = upstream + mid_norm_grad
        branch_grad = (branch_scale * residual_grad).astype(jnp.bfloat16)
        output_grad = jnp.dot(jnp.transpose(context_flat), branch_grad, preferred_element_type=jnp.float32)
        context_grad = jnp.dot(branch_grad, jnp.transpose(w_output), preferred_element_type=jnp.float32).reshape(head_shape)
        scale_factor = 1.0 / math.sqrt(head_width)
        attn_probs = jnp.exp(masked_scores(queries, keys_rot, allowed) - log_total)
        probs_half = attn_probs.astype(jnp.bfloat16)
        row_delta = lax.optimization_barrier(jnp.sum(context_grad * context.astype(jnp.float32), axis=-1))
        context_half = context_grad.astype(jnp.bfloat16)
        probs_grad = jnp.einsum('qhd,khd->hqk', context_half.astype(jnp.float32), values.astype(jnp.float32))
        scores_grad = (attn_probs * (probs_grad - jnp.transpose(row_delta)[:, :, None]) * scale_factor).astype(jnp.bfloat16)
        queries_grad_rot = jnp.einsum('hqk,khd->qhd', scores_grad.astype(jnp.float32), keys_rot.astype(jnp.float32))
        keys_grad_rot = jnp.einsum('hqk,qhd->khd', scores_grad.astype(jnp.float32), queries.astype(jnp.float32))
        values_grad = jnp.einsum('hqk,qhd->khd', probs_half.astype(jnp.float32), context_half.astype(jnp.float32))
        queries_grad = rotate(queries_grad_rot, cosine, -sine_table).reshape(TOK_DEV, D).astype(jnp.bfloat16)
        keys_grad = rotate(keys_grad_rot, cosine, -sine_table).reshape(TOK_DEV, D).astype(jnp.bfloat16)
        values_grad_half = values_grad.reshape(TOK_DEV, D).astype(jnp.bfloat16)
        query_weight_grad = jnp.dot(jnp.transpose(normed_half), queries_grad, preferred_element_type=jnp.float32)
        key_weight_grad = jnp.dot(jnp.transpose(normed_half), keys_grad, preferred_element_type=jnp.float32)
        value_weight_grad = jnp.dot(jnp.transpose(normed_half), values_grad_half, preferred_element_type=jnp.float32)
        normed_in_grad = jnp.dot(queries_grad, jnp.transpose(w_query), preferred_element_type=jnp.float32)
        normed_in_grad = normed_in_grad + jnp.dot(keys_grad, jnp.transpose(w_key), preferred_element_type=jnp.float32)
        normed_in_grad = normed_in_grad + jnp.dot(values_grad_half, jnp.transpose(w_value), preferred_element_type=jnp.float32)
        in_norm_grad, gain_attn_grad = rms_backward(residual_in, inverse_in, gain_attn, normed_in_grad)
        grad_tokens_block = residual_grad + in_norm_grad
        updates = (query_weight_grad, key_weight_grad, value_weight_grad, output_grad, router_grad, gain_attn_grad, gain_ffn_grad)
        running = tuple((total + update for total, update in zip(running, updates)))
        return (running, (activations, grad_tokens_block))
    grad_start = (jnp.zeros((D, D), jnp.float32), jnp.zeros((D, D), jnp.float32), jnp.zeros((D, D), jnp.float32), jnp.zeros((D, D), jnp.float32), jnp.zeros((D, EXPERTS), jnp.float32), jnp.zeros((D,), jnp.float32), jnp.zeros((D,), jnp.float32))
    block_inputs = (token_blocks, seq_lengths, route_blocks, mixture_all.reshape(GROUPS, TOK_DEV, D), mid_grad_all.reshape(GROUPS, TOK_DEV, D), gate_blocks, gate_grad_all.reshape(GROUPS, TOK_DEV, 2), cot_blocks)
    grad_totals, (activation_blocks, grad_token_blocks) = lax.scan(back_block, grad_start, block_inputs)
    activations = activation_blocks.reshape(TOKENS, D)
    grad_tokens = grad_token_blocks.reshape(TOKENS, D)
    grad_w_query, grad_w_key, grad_w_value, grad_w_output, grad_w_router, grad_norm_attn, grad_norm_ffn = grad_totals
    return (activations, grad_tokens, grad_norm_attn, grad_w_query, grad_w_key, grad_w_value, grad_w_output, grad_norm_ffn, grad_w_router, grad_w_in, grad_w_down)
```

```python
import math

import jax
import jax.numpy as jnp
from jax import lax
from jax.sharding import Mesh, PartitionSpec as P

HEADS = 36

eps_norm = 1e-05
branch_scale = 1.4 / math.sqrt(40.0)
rope_base = 10000.0
masked_score = -1e30
bf16 = jnp.bfloat16
f32 = jnp.float32
SHARD = ("z", "core")
GRID = ("z", "expert")


def rope_tables(positions, head_width):
    half_width = head_width // 2
    exponents = jnp.arange(half_width).astype(f32) * 2.0 / head_width
    frequency = rope_base ** (-exponents)
    angles = positions.astype(f32)[..., None] * frequency
    return (jnp.cos(angles), jnp.sin(angles))


def rotate(values, cosine, sine_table):
    half_width = values.shape[-1] // 2
    leading = values[..., :half_width]
    trailing = values[..., half_width:]
    cos_rows = cosine[:, :, None, :]
    sin_rows = sine_table[:, :, None, :]
    return jnp.concatenate(
        [leading * cos_rows - trailing * sin_rows, trailing * cos_rows + leading * sin_rows],
        axis=-1,
    )


def rms_forward(values, norm_gain):
    inverse = lax.rsqrt(jnp.mean(values * values, axis=-1, keepdims=True) + eps_norm)
    return (values * inverse * norm_gain, inverse)


def rms_backward(values, inverse, norm_gain, upstream):
    weighted = upstream * norm_gain
    gain_grad = jnp.sum(upstream * values * inverse, axis=0)
    inner_mean = jnp.mean(weighted * values, axis=-1, keepdims=True)
    return (inverse * weighted - values * inverse * inverse * inverse * inner_mean, gain_grad)


def dot32(a, b):
    return jnp.dot(a, b, preferred_element_type=f32)


def dot_dims(a, b, da, db):
    return lax.dot_general(a, b, (((da,), (db,)), ((), ())), preferred_element_type=f32)


def ein32(spec, a, b):
    return jnp.einsum(spec, a, b, preferred_element_type=f32)


def swap_core(x, split, concat):
    return lax.all_to_all(x, "core", split_axis=split, concat_axis=concat, tiled=True)


def on_device(
    tokens,
    seq_lengths,
    routes,
    norm_attn,
    w_query,
    w_key,
    w_value,
    w_output,
    norm_ffn,
    w_router,
    w_in,
    w_down,
    cotangent,
):
    T, D = tokens.shape
    R = w_query.shape[0]
    H = D // 2
    head_width = D // HEADS
    heads = HEADS // 2
    n_exp = lax.axis_size("expert")
    n_shard = lax.axis_size("z") * lax.axis_size("core")
    experts = w_router.shape[1]
    local_experts = w_in.shape[1]
    F = w_down.shape[0]
    FF = F * n_shard
    capacity = 10 * T // (4 * experts)
    slots = experts * capacity
    highest = lax.Precision.HIGHEST
    e_index = lax.axis_index("expert")
    core = lax.axis_index("core")

    quarter = 2 * R // n_exp
    per_core = n_exp // 2
    first = (e_index % per_core) * quarter

    def column_half(weights):
        piece = [lax.dynamic_slice_in_dim(w, first, quarter, 0) for w in weights]
        mine = jnp.concatenate([lax.dynamic_slice_in_dim(p, core * H, H, 1) for p in piece], axis=1)
        other = jnp.concatenate(
            [lax.dynamic_slice_in_dim(p, (1 - core) * H, H, 1) for p in piece], axis=1
        )
        landed = lax.ppermute(other, "core", [(0, 1), (1, 0)])
        return jnp.where(core == e_index // per_core, mine, landed)

    full_qkv = lax.all_gather(
        column_half((w_query, w_key, w_value)), GRID, axis=0, tiled=True
    )
    full_output = lax.all_gather(column_half((w_output,)), GRID, axis=0, tiled=True)
    small = jnp.concatenate([w_router, norm_attn[:, None], norm_ffn[:, None]], axis=1)
    full_small = lax.all_gather(small, SHARD, axis=0, tiled=True)
    full_router = full_small[:, :experts]
    gain_attn = full_small[:, experts].astype(f32)
    gain_ffn = full_small[:, experts + 1].astype(f32)

    w_gate_cols = []
    for part in range(2):
        piece = w_in[:, :, part * FF : (part + 1) * FF].reshape(R, local_experts, n_shard, F)
        piece = piece.transpose(2, 1, 0, 3)
        w_gate_cols.append(piece)

    def reshard(piece):
        moved = lax.all_to_all(piece, SHARD, split_axis=0, concat_axis=0, tiled=True)
        return moved.transpose(1, 0, 2, 3).reshape(local_experts, n_shard * R, F)

    w_gate, w_up = reshard(w_gate_cols[0]), reshard(w_gate_cols[1])

    both = (2, T)
    residual_in = tokens.astype(f32)
    normed_in, inverse_in = rms_forward(residual_in, gain_attn)
    normed_own = normed_in.astype(bf16)
    normed_half = lax.all_gather(normed_own, "core", axis=0, tiled=True)
    lengths = lax.all_gather(seq_lengths[:, 0], "core", axis=0, tiled=True)
    row_index = jnp.arange(T)
    segment = (row_index[None, :] >= lengths[:, None]).astype(jnp.int32)
    positions = row_index[None, :] - lengths[:, None] * segment
    allowed = (segment[:, :, None] == segment[:, None, :]) & (
        row_index[None, None, :] <= row_index[None, :, None]
    )
    cosine, sine_table = rope_tables(positions, head_width)
    head_shape = both + (heads, head_width)
    qkv = dot32(normed_half, full_qkv)
    queries = rotate(qkv[:, :H].reshape(head_shape), cosine, sine_table).astype(bf16)
    keys_rot = rotate(qkv[:, H : 2 * H].reshape(head_shape), cosine, sine_table).astype(bf16)
    values = qkv[:, 2 * H :].astype(bf16).reshape(head_shape)
    score_scale = 1.0 / math.sqrt(head_width)
    scores = ein32("bqhd,bkhd->bhqk", queries, keys_rot) * score_scale
    scores = jnp.where(allowed[:, None], scores, masked_score)
    row_peak = jnp.max(scores, axis=-1, keepdims=True)
    log_total = row_peak + jnp.log(jnp.sum(jnp.exp(scores - row_peak), axis=-1, keepdims=True))
    attn_probs = jnp.exp(scores - log_total)
    probs_half = attn_probs.astype(bf16)
    context = ein32("bhqk,bkhd->bqhd", probs_half, values).astype(bf16)
    context_half = context.reshape(2 * T, H)
    context_full = lax.all_gather(context_half, "core", axis=1, tiled=True)
    mid_half = dot32(context_full, full_output)
    mid_own = swap_core(mid_half, 0, 1)
    residual_mid = residual_in + branch_scale * mid_own
    normed_mid, inverse_mid = rms_forward(residual_mid, gain_ffn)
    normed_mid_half = normed_mid.astype(bf16)

    logits = dot32(normed_mid_half, full_router)
    expert_ids = jnp.arange(experts)
    route_mask = (routes[:, :, None] == expert_ids[None, None, :]).astype(f32)
    chosen = jnp.sum(logits[:, None, :] * route_mask, axis=-1)
    gate_probs = jax.nn.softmax(chosen, axis=-1)
    flat_routes = routes.reshape(2 * T)
    hits = (flat_routes[:, None] == expert_ids[None, :]).astype(bf16)
    order = jnp.arange(2 * T)
    before = (order[:, None] > order[None, :]).astype(bf16)
    earlier = dot32(before, hits)
    slot_index = jnp.sum(earlier * hits.astype(f32), axis=1).astype(jnp.int32)
    target = (flat_routes * capacity + slot_index).reshape(T, 2)
    slot_ids = jnp.arange(slots)
    pick = [(target[:, k][:, None] == slot_ids[None, :]).astype(bf16) for k in range(2)]

    def send_rows(rows0, rows1):
        out = dot_dims(pick[0], rows0, 0, 0) + dot_dims(pick[1], rows1, 0, 0)
        out = out.astype(bf16)
        moved = lax.all_to_all(out, "expert", split_axis=0, concat_axis=0, tiled=True)
        return moved

    def spread(moved):
        rows = lax.all_gather(moved, SHARD, axis=0, tiled=True)
        if local_experts == 1:
            return rows[None]
        rows = rows.reshape(n_shard * n_exp, local_experts, capacity, D)
        return rows.transpose(1, 0, 2, 3).reshape(local_experts, -1, D)

    def bring_back(partial_rows):
        part = partial_rows.astype(bf16)
        if local_experts > 1:
            part = part.reshape(local_experts, n_shard * n_exp, capacity, D).transpose(1, 0, 2, 3)
        part = part.reshape(n_shard * slots, D)
        mine = lax.psum_scatter(part, SHARD, scatter_dimension=0, tiled=True)
        back = lax.all_to_all(mine, "expert", split_axis=0, concat_axis=0, tiled=True)
        return [dot32(pick[k], back) for k in range(2)]

    def per_expert(fn, *arrays):
        return jnp.stack([fn(*[a[i] for a in arrays]) for i in range(local_experts)])

    arrived = spread(send_rows(normed_mid_half, normed_mid_half))
    upstream = cotangent.astype(f32)
    mixture_grad = branch_scale * upstream
    row_grads = (gate_probs[:, :, None] * mixture_grad[:, None, :]).astype(bf16)
    grad_arrived = spread(send_rows(row_grads[:, 0], row_grads[:, 1]))
    down = w_down.transpose(1, 0, 2)
    gate_part = per_expert(dot32, arrived, w_gate)
    up_part = per_expert(dot32, arrived, w_up)
    sigmoid_gate = jax.nn.sigmoid(gate_part)
    silu_gate = gate_part * sigmoid_gate
    activated = (silu_gate * up_part).astype(bf16)
    expert_rows = bring_back(per_expert(dot32, activated, down))
    mixture = gate_probs[:, 0:1] * expert_rows[0] + gate_probs[:, 1:2] * expert_rows[1]
    activations = (residual_mid + branch_scale * mixture).astype(bf16)

    act_grad = per_expert(lambda a, b: dot_dims(a, b, 1, 1), grad_arrived, down)
    gate_grads = (
        act_grad * up_part * sigmoid_gate * (1.0 + gate_part * (1.0 - sigmoid_gate))
    ).astype(bf16)
    up_grads = (act_grad * silu_gate).astype(bf16)
    input_rows = bring_back(
        per_expert(
            lambda a, b, c, d: dot_dims(a, b, 1, 1) + dot_dims(c, d, 1, 1),
            gate_grads,
            w_gate,
            up_grads,
            w_up,
        )
    )
    grad_w_down = per_expert(lambda a, b: dot_dims(a, b, 0, 0), activated, grad_arrived)
    grad_w_down = grad_w_down.transpose(1, 0, 2)

    def reshard_grad(grads):
        term = per_expert(lambda a, b: dot_dims(a, b, 0, 0), arrived, grads).astype(bf16)
        term = term.reshape(local_experts, n_shard, R, F).transpose(1, 0, 2, 3)
        moved = lax.all_to_all(term, SHARD, split_axis=0, concat_axis=0, tiled=True)
        return moved.transpose(2, 1, 0, 3).reshape(R, local_experts, FF).astype(f32)

    grad_w_in = jnp.concatenate([reshard_grad(gate_grads), reshard_grad(up_grads)], axis=2)

    gate_grad = jnp.stack(
        [jnp.sum(mixture_grad * expert_rows[k], axis=-1) for k in range(2)], axis=1
    )
    chosen_grad = gate_probs * (gate_grad - jnp.sum(gate_probs * gate_grad, axis=-1, keepdims=True))
    logit_grad = jnp.sum(chosen_grad[:, :, None] * route_mask, axis=1)
    normed_mid_grad = input_rows[0] + input_rows[1]
    normed_mid_grad = normed_mid_grad + jnp.dot(
        logit_grad, jnp.transpose(full_router.astype(f32)), precision=highest
    )
    router_grad = jnp.dot(
        jnp.transpose(normed_mid_half.astype(f32)), logit_grad, precision=highest
    )
    mid_norm_grad, gain_ffn_grad = rms_backward(
        residual_mid, inverse_mid, gain_ffn, normed_mid_grad
    )
    residual_grad = upstream + mid_norm_grad
    branch_own = (branch_scale * residual_grad).astype(bf16)

    branch_half = swap_core(branch_own, 1, 0)
    output_grad = dot_dims(context_full, branch_half, 0, 0)
    context_grad = dot_dims(branch_half, full_output, 1, 1)
    context_grad = lax.psum_scatter(
        context_grad.reshape(2 * T, 2, H).transpose(1, 0, 2).reshape(4 * T, H),
        "core",
        scatter_dimension=0,
        tiled=True,
    ).reshape(head_shape)
    row_delta = jnp.sum(context_grad * context.astype(f32), axis=-1)
    context_grad_half = context_grad.astype(bf16)
    probs_grad = ein32("bqhd,bkhd->bhqk", context_grad_half, values)
    scores_grad = (
        attn_probs * (probs_grad - jnp.transpose(row_delta, (0, 2, 1))[..., None]) * score_scale
    ).astype(bf16)
    queries_grad = ein32("bhqk,bkhd->bqhd", scores_grad, keys_rot)
    keys_grad = ein32("bhqk,bqhd->bkhd", scores_grad, queries)
    values_grad = ein32("bhqk,bqhd->bkhd", probs_half, context_grad_half)
    qkv_grad = jnp.concatenate(
        [
            rotate(queries_grad, cosine, -sine_table).reshape(2 * T, H).astype(bf16),
            rotate(keys_grad, cosine, -sine_table).reshape(2 * T, H).astype(bf16),
            values_grad.reshape(2 * T, H).astype(bf16),
        ],
        axis=1,
    )
    qkv_weight_grad = dot_dims(normed_half, qkv_grad, 0, 0)
    normed_in_grad = lax.psum_scatter(
        dot_dims(qkv_grad, full_qkv, 1, 1), "core", scatter_dimension=0, tiled=True
    )
    in_norm_grad, gain_attn_grad = rms_backward(residual_in, inverse_in, gain_attn, normed_in_grad)
    grad_tokens = residual_grad + in_norm_grad

    def total(term):
        mine = lax.psum_scatter(term.astype(bf16), GRID, scatter_dimension=0, tiled=True)
        return lax.all_gather(mine, "expert", axis=0, tiled=True)

    out_sum = swap_core(total(output_grad), 0, 1).astype(f32)
    qkv_sum = total(qkv_weight_grad)
    qkv_sum = [
        swap_core(qkv_sum[:, i * H : (i + 1) * H], 0, 1).astype(f32) for i in range(3)
    ]
    small_grad = jnp.concatenate(
        [router_grad, gain_attn_grad[:, None], gain_ffn_grad[:, None]], axis=1
    )
    small_sum = lax.psum(
        lax.psum_scatter(small_grad, SHARD, scatter_dimension=0, tiled=True), "expert"
    )
    return (
        activations,
        grad_tokens,
        small_sum[:, experts],
        qkv_sum[0],
        qkv_sum[1],
        qkv_sum[2],
        out_sum,
        small_sum[:, experts + 1],
        small_sum[:, :experts],
        grad_w_in,
        grad_w_down,
    )


def solution(mesh):
    n_expert, n_shard = mesh.devices.shape
    chips = Mesh(mesh.devices.reshape(n_expert, n_shard // 2, 2), ("expert", "z", "core"))
    rows = P(("expert", "z", "core"), None)
    shard = P(SHARD)
    shard2 = P(SHARD, None)
    shard3 = P(SHARD, "expert", None)
    in_specs = (
        rows,
        rows,
        rows,
        shard,
        shard2,
        shard2,
        shard2,
        shard2,
        shard,
        shard2,
        shard3,
        shard3,
        rows,
    )
    out_specs = (
        rows,
        rows,
        shard,
        shard2,
        shard2,
        shard2,
        shard2,
        shard,
        shard2,
        shard3,
        shard3,
    )
    return jax.shard_map(
        on_device, mesh=chips, in_specs=in_specs, out_specs=out_specs, check_vma=False
    )
```

```python
import functools
import math

import jax
import jax.numpy as jnp
from jax import lax
from jax.experimental import pallas as pl
from jax.experimental.pallas import tpu as pltpu
from jax.sharding import Mesh, PartitionSpec as P

HEADS = 36

eps_norm = 1e-05
branch_scale = 1.4 / math.sqrt(40.0)
rope_base = 10000.0
masked_score = -1e30
bf16 = jnp.bfloat16
f32 = jnp.float32
SHARD = ("z", "core")
GRID = ("z", "expert")
ANY = pl.BlockSpec(memory_space=pl.ANY)


def place():
    e, z, c = lax.axis_index("expert"), lax.axis_index("z"), lax.axis_index("core")
    across_x = e + 1 - 2 * (e % 2)
    across_y = (e + 2) % 4
    return e, z, c, across_x, across_y


def remote(src, dst, send, recv, e, z, c):
    return pltpu.make_async_remote_copy(
        src_ref=src,
        dst_ref=dst,
        send_sem=send,
        recv_sem=recv,
        device_id=(e, z, c),
        device_id_type=pl.DeviceIdType.MESH,
    )


def greet(nz, both_cores):
    e, z, c, ex, ey = place()
    barrier = pltpu.get_barrier_semaphore()

    def hail(te, tz, tc):
        pl.semaphore_signal(
            barrier, inc=1, device_id=(te, tz, tc), device_id_type=pl.DeviceIdType.MESH
        )

    cores = (c, 1 - c) if both_cores[0] else (c,)
    plane = (c, 1 - c) if both_cores[1] else (c,)
    hail(e, z, 1 - c)
    for t in plane:
        hail(ex, z, t)
        hail(ey, z, t)
    for step in (-1, 1):

        @pl.when((z + step >= 0) & (z + step < nz))
        def _():
            for t in cores:
                hail(e, z + step, t)

    ends = jnp.where(z > 0, 1, 0) + jnp.where(z < nz - 1, 1, 0)
    pl.semaphore_wait(barrier, 1 + 2 * len(plane) + len(cores) * ends)


def cut(k, Q):
    big = (Q // 2 + 15) // 16 * 16
    return big if k % 2 == 0 else Q - big


def gather_kernel(
    nz, Q, H,
    q_ref, k_ref, v_ref, o_ref, s_ref, t_ref, l_ref,
    qkv_out, o_out, s_out, t_out, l_out,
    zrecv, zhop, zsend, near_recv, near_send, far_recv, far_send, own, sib_send, sib_recv,
):
    e, z, c, ex, ey = place()
    holder, turn = e // 2, e % 2
    sources = (q_ref, k_ref, v_ref, o_ref, s_ref)
    K = len(sources)

    def src(k, half, j, count=1):
        rows = pl.ds(pl.multiple_of(j * Q, 16), count * Q)
        if k == 4:
            return sources[k].at[rows, :]
        return sources[k].at[rows, pl.ds(pl.multiple_of(half * H, 128), H)]

    def dst(k, zz, quarter, r0=0, n=Q):
        rows = pl.ds(pl.multiple_of((zz * 4 + quarter) * Q + r0, 16), n)
        if k < 3:
            return qkv_out.at[rows, pl.ds(k * H, H)]
        return (o_out if k == 3 else s_out).at[rows, :]

    greet(nz, (True, False))

    pairs = ((t_ref, t_out), (l_ref, l_out))
    extra = []
    for n, (a, b) in enumerate(pairs):
        mine = pltpu.make_async_copy(a, b.at[c], own.at[K + n])
        mine.start()
        theirs = remote(a, b.at[c], sib_send.at[K + n], sib_recv.at[K + n], e, z, 1 - c)
        theirs.start()
        extra += [mine, theirs]

    def first_hop(k, step, half):
        side = 0 if step > 0 else 1
        return remote(
            src(k, half, turn), dst(k, z, e), zhop.at[k, side, half], zrecv.at[k, side, 0],
            e, z + step, half,
        )

    for k in range(K):
        for step in (1, -1):

            @pl.when((c == holder) & (z + step >= 0) & (z + step < nz))
            def _():
                first_hop(k, step, 0).start()
                first_hop(k, step, 1).start()

    for k in range(K):
        rows = src(k, c, 0, 2), dst(k, z, 2 * c, 0, 2 * Q)
        mine = pltpu.make_async_copy(rows[0], rows[1], own.at[k])
        mine.start()
        theirs = remote(
            src(k, 1 - c, 0, 2), rows[1], sib_send.at[k], sib_recv.at[k], e, z, 1 - c
        )
        theirs.start()
        extra += [mine, theirs]

    def where(side, i):
        return z - 1 - i if side == 0 else z + 1 + i

    def onward(k, side, i):
        slab = dst(k, where(side, i), e)
        step = 1 if side == 0 else -1
        return remote(
            slab, slab, zsend.at[k, side, i], zrecv.at[k, side, i + 1], e, z + step, c
        )

    def near(k, side, i, axis):
        slab = dst(k, where(side, i), e)
        return remote(
            slab, slab, near_send.at[k, side, i, axis], near_recv.at[k, side, i, axis],
            ex if axis == 0 else ey, z, c,
        )

    def near_wait(k, side, i, axis):
        slab = dst(k, where(side, i), ex if axis == 0 else ey)
        remote(
            slab, slab, near_send.at[k, side, i, axis], near_recv.at[k, side, i, axis], ex, z, c
        ).wait_recv()

    def far(k, side, i, axis):
        a = cut(k, Q)
        if axis == 0:
            slab = dst(k, where(side, i), ex, 0, a)
        else:
            slab = dst(k, where(side, i), ey, a, Q - a)
        return remote(
            slab, slab, far_send.at[k, side, i, axis], far_recv.at[k, side, i, axis],
            ey if axis == 0 else ex, z, c,
        )

    def exists(side, i):
        zz = where(side, i)
        return (zz >= 0) & (zz < nz)

    def inside(side):
        return z < nz - 1 if side == 0 else z > 0

    def arrive(k, side, i):
        @pl.when(exists(side, i))
        def _():
            slab = dst(k, where(side, i), e)
            remote(
                slab, slab, zsend.at[k, side, i], zrecv.at[k, side, i], e, z, c
            ).wait_recv()
            if i < nz - 2:

                @pl.when(inside(side))
                def _():
                    onward(k, side, i).start()

            near(k, side, i, 0).start()
            near(k, side, i, 1).start()

    def relay(k, side, i):
        @pl.when(exists(side, i))
        def _():
            for axis in range(2):
                near_wait(k, side, i, axis)
                far(k, side, i, axis).start()

    steps = [(k, side, i) for i in range(nz - 1) for k in range(K) for side in range(2)]
    lag = 2 * K
    for n, step in enumerate(steps):
        arrive(*step)
        if n >= lag:
            relay(*steps[n - lag])
    for step in steps[len(steps) - lag :]:
        relay(*step)

    for k, side, i in steps:

        @pl.when(exists(side, i))
        def _():
            if i < nz - 2:

                @pl.when(inside(side))
                def _():
                    onward(k, side, i).wait_send()

            a = cut(k, Q)
            zz, diagonal = where(side, i), (ex + 2) % 4
            for axis in range(2):
                near(k, side, i, axis).wait_send()
                far(k, side, i, axis).wait_send()
                slab = dst(k, zz, diagonal, 0, a) if axis == 0 else dst(k, zz, diagonal, a, Q - a)
                remote(
                    slab, slab, far_send.at[k, side, i, axis], far_recv.at[k, side, i, axis],
                    ex, z, c,
                ).wait_recv()

    for k in range(K):
        for step in (1, -1):

            @pl.when((c == holder) & (z + step >= 0) & (z + step < nz))
            def _():
                first_hop(k, step, 0).wait_send()
                first_hop(k, step, 1).wait_send()

    for copy in extra:
        copy.wait()


def gather_attention(nz, weights, small, tokens, lengths):
    R, D = weights[0].shape
    Q, H = R // 2, D // 2
    K = len(weights) + 1
    dma = pltpu.SemaphoreType.DMA
    any_ = ANY
    W = small.shape[1]
    sd = jax.ShapeDtypeStruct
    outs = pl.pallas_call(
        functools.partial(gather_kernel, nz, Q, H),
        out_shape=(
            sd((nz * 4 * Q, 3 * H), bf16),
            sd((nz * 4 * Q, H), bf16),
            sd((nz * 4 * Q, W), bf16),
            sd((2,) + tokens.shape, bf16),
            sd((2,) + lengths.shape, lengths.dtype),
        ),
        in_specs=[any_] * 7,
        out_specs=(any_,) * 5,
        scratch_shapes=[
            dma((K, 2, nz - 1)),
            dma((K, 2, 2)),
            dma((K, 2, nz - 1)),
            dma((K, 2, nz - 1, 2)),
            dma((K, 2, nz - 1, 2)),
            dma((K, 2, nz - 1, 2)),
            dma((K, 2, nz - 1, 2)),
            dma((K + 2,)),
            dma((K + 2,)),
            dma((K + 2,)),
        ],
        compiler_params=pltpu.CompilerParams(collective_id=0, has_side_effects=True),
        cost_estimate=pl.CostEstimate(
            flops=10**11, bytes_accessed=8 * D * H * 2, transcendentals=0
        ),
        name="gather_attention",
    )(*weights, small, tokens, lengths)
    return outs


def reduce_kernel(
    nz, Q, widths,
    *refs,
):
    K = len(widths)
    parts, refs = refs[:K], refs[K:]
    outs, refs = refs[:K], refs[K:]
    (
        mine, mine_x, mine_y, from_x, from_y, via_x, via_y, from_z, result,
        load, via_send, via_recv, plain_send, plain_recv, sum_send, sum_recv,
        zsend, zrecv, fin_send, fin_recv, far_send, far_recv, own,
    ) = refs
    e, z, c, ex, ey = place()
    diagonal = (ex + 2) % 4
    holder, turn = e // 2, e % 2
    offs = [sum(widths[:k]) for k in range(K)]

    def order(i):
        code = 0
        for zz in range(nz):
            far_first = sorted(range(nz), key=lambda t: (-abs(t - zz), t))
            code += far_first[i] * nz**zz
        power = 1
        for zz in range(nz):
            power = power + (nz**zz - 1) * jnp.where(z == zz, 1, 0)
        return (code // power) % nz

    dest = [order(i) for i in range(nz)]

    def cols(k):
        return pl.ds(offs[k], widths[k])

    greet(nz, (False, True))

    def loads(k, i):
        a = cut(k, Q)
        zz = dest[i]
        out = [
            (parts[k].at[zz, e], mine.at[i, :, cols(k)]),
            (parts[k].at[zz, ex, pl.ds(a, Q - a), :], mine_x.at[i, pl.ds(0, Q - a), cols(k)]),
            (parts[k].at[zz, ey, pl.ds(0, a), :], mine_y.at[i, pl.ds(0, a), cols(k)]),
        ]
        return [pltpu.make_async_copy(s, d, load.at[k, i, n]) for n, (s, d) in enumerate(out)]

    def via(k, i, axis):
        a = cut(k, Q)
        zz = dest[i]
        if axis == 0:
            return remote(
                parts[k].at[zz, diagonal, pl.ds(0, a), :], via_x.at[i, pl.ds(0, a), cols(k)],
                via_send.at[k, i, 0], via_recv.at[k, i, 0], ex, z, c,
            )
        return remote(
            parts[k].at[zz, diagonal, pl.ds(a, Q - a), :], via_y.at[i, pl.ds(0, Q - a), cols(k)],
            via_send.at[k, i, 1], via_recv.at[k, i, 1], ey, z, c,
        )

    def plain(k, i, axis):
        a = cut(k, Q)
        zz = dest[i]
        if axis == 0:
            return remote(
                parts[k].at[zz, ex, pl.ds(0, a), :], from_x.at[i, pl.ds(0, a), cols(k)],
                plain_send.at[k, i, 0], plain_recv.at[k, i, 0], ex, z, c,
            )
        return remote(
            parts[k].at[zz, ey, pl.ds(a, Q - a), :], from_y.at[i, pl.ds(a, Q - a), cols(k)],
            plain_send.at[k, i, 1], plain_recv.at[k, i, 1], ey, z, c,
        )

    def summed(k, i, axis):
        a = cut(k, Q)
        if axis == 0:
            return remote(
                mine_x.at[i, pl.ds(0, Q - a), cols(k)], from_x.at[i, pl.ds(a, Q - a), cols(k)],
                sum_send.at[k, i, 0], sum_recv.at[k, i, 0], ex, z, c,
            )
        return remote(
            mine_y.at[i, pl.ds(0, a), cols(k)], from_y.at[i, pl.ds(0, a), cols(k)],
            sum_send.at[k, i, 1], sum_recv.at[k, i, 1], ey, z, c,
        )

    def add(target, others, n, k):
        @pl.loop(0, n // 16)
        def _(b):
            rows = pl.ds(pl.multiple_of(b * 16, 16), 16)
            acc = target[rows, cols(k)].astype(f32)
            for o in others:
                acc = acc + o[rows, cols(k)].astype(f32)
            target[rows, cols(k)] = acc.astype(bf16)

    pairs = [(k, i) for i in range(nz) for k in range(K)]
    for k, i in pairs:
        via(k, i, 0).start()
        via(k, i, 1).start()
        for copy in loads(k, i):
            copy.start()
        plain(k, i, 0).start()
        plain(k, i, 1).start()

    def combine(k, i):
        a = cut(k, Q)
        group = loads(k, i)
        group[1].wait()
        group[2].wait()
        via(k, i, 0).wait_recv()
        add(mine_y.at[i], [via_x.at[i]], a, k)
        summed(k, i, 1).start()
        via(k, i, 1).wait_recv()
        add(mine_x.at[i], [via_y.at[i]], Q - a, k)
        summed(k, i, 0).start()

    def zcopy(k, i):
        step = jnp.where(dest[i] > z, 1, -1)
        side = jnp.where(dest[i] > z, 0, 1)
        return remote(
            mine.at[i, :, cols(k)], from_z.at[side, dest[i], :, cols(k)],
            zsend.at[k, i], zrecv.at[k, side, dest[i]], e, z + step, c,
        )

    def zwait(k, side, zz):
        slab = from_z.at[side, zz, :, cols(k)]
        remote(slab, slab, zsend.at[k, 0], zrecv.at[k, side, zz], e, z, c).wait_recv()

    def finish(k, i):
        loads(k, i)[0].wait()
        for axis in range(2):
            plain(k, i, axis).wait_recv()
            summed(k, i, axis).wait_recv()
        add(mine.at[i], [from_x.at[i], from_y.at[i]], Q, k)
        zz = dest[i]
        if i < nz - 1:
            for side in range(2):
                going = zz > z if side == 0 else zz < z
                behind = z > 0 if side == 0 else z < nz - 1

                @pl.when(going & behind)
                def _():
                    zwait(k, side, zz)
                    add(mine.at[i], [from_z.at[side, zz]], Q, k)

            zcopy(k, i).start()

    def fin(k, axis):
        if widths[k] == widths[-1] and k == K - 1:
            land = outs[k].at[turn, c]
        else:
            land = outs[k].at[turn, :, pl.ds(pl.multiple_of(c * widths[k], 128), widths[k])]
        te = (ex, ey, e)[axis]
        return remote(
            result.at[:, cols(k)], land, fin_send.at[k, axis], fin_recv.at[k, axis, c],
            te, z, holder,
        )

    def total(k):
        last = nz - 1
        for side in range(2):
            behind = z > 0 if side == 0 else z < nz - 1

            @pl.when(behind)
            def _():
                zwait(k, side, z)
                add(mine.at[last], [from_z.at[side, z]], Q, k)

        @pl.loop(0, Q // 16)
        def _(b):
            rows = pl.ds(pl.multiple_of(b * 16, 16), 16)
            result[rows, cols(k)] = mine[last, rows, cols(k)]

        fin(k, 0).start()
        fin(k, 1).start()

        @pl.when(c == holder)
        def _():
            pltpu.make_async_copy(result.at[:, cols(k)], fin_own(k), own.at[k]).start()

        @pl.when(c != holder)
        def _():
            fin(k, 2).start()

    def fin_own(k):
        if k == K - 1:
            return outs[k].at[turn, c]
        return outs[k].at[turn, :, pl.ds(pl.multiple_of(c * widths[k], 128), widths[k])]

    lag = K
    for n, (k, i) in enumerate(pairs):
        combine(k, i)
        if n >= lag:
            k2, i2 = pairs[n - lag]
            finish(k2, i2)
    for k2, i2 in pairs[len(pairs) - lag :]:
        finish(k2, i2)
    for k in range(K):
        total(k)

    def slot(k, j, half, r0=0, n=Q):
        if k == K - 1:
            return outs[k].at[j, half, pl.ds(r0, n), :]
        return outs[k].at[j, pl.ds(r0, n), pl.ds(half * widths[k], widths[k])]

    def got(k, axis, half):
        j = (ex if axis == 0 else ey) % 2
        view = slot(k, j, half)
        return remote(
            view, view, fin_send.at[k, axis], fin_recv.at[k, axis, half], e, z, c
        )

    def passed(k, axis, half, quarter):
        a = cut(k, Q)
        j = quarter % 2
        view = slot(k, j, half, 0, a) if axis == 0 else slot(k, j, half, a, Q - a)
        return remote(
            view, view, far_send.at[k, half], far_recv.at[k, axis, half],
            ey if axis == 0 else ex, z, c,
        )

    for k in range(K):
        for axis in range(2):

            @pl.when((c == holder) if axis == 0 else (c != holder))
            def _():
                for half in range(2):
                    got(k, axis, half).wait_recv()
                    passed(k, axis, half, ex if axis == 0 else ey).start()

    for k in range(K):
        for axis in range(2):

            @pl.when((c == holder) if axis == 0 else (c != holder))
            def _():
                for half in range(2):
                    passed(k, axis, half, ex if axis == 0 else ey).wait_send()

        @pl.when(c != holder)
        def _():
            for half in range(2):
                passed(k, 0, half, diagonal).wait_recv()
                passed(k, 1, half, diagonal).wait_recv()
            fin(k, 2).wait_send()

        @pl.when(c == holder)
        def _():
            pltpu.make_async_copy(result.at[:, cols(k)], fin_own(k), own.at[k]).wait()
            other = slot_of(outs, k, K, turn, 1 - c, widths)
            remote(
                other, other, fin_send.at[k, 2], fin_recv.at[k, 2, 1 - c], e, z, c
            ).wait_recv()

        fin(k, 0).wait_send()
        fin(k, 1).wait_send()
        for i in range(nz):
            for axis in range(2):
                via(k, i, axis).wait_send()
                plain(k, i, axis).wait_send()
                summed(k, i, axis).wait_send()
            if i < nz - 1:
                zcopy(k, i).wait_send()


def slot_of(outs, k, K, j, half, widths):
    if k == K - 1:
        return outs[k].at[j, half]
    return outs[k].at[j, :, pl.ds(pl.multiple_of(half * widths[k], 128), widths[k])]


def reduce_attention(nz, parts):
    Q = parts[0].shape[2]
    widths = tuple(p.shape[3] for p in parts)
    W, K = sum(widths), len(parts)
    big = max(cut(0, Q), cut(1, Q))
    dma = pltpu.SemaphoreType.DMA
    sd = jax.ShapeDtypeStruct
    vm = pltpu.VMEM
    out_shape = tuple(sd((2, Q, 2 * w), bf16) for w in widths[:-1]) + (
        sd((2, 2, Q, widths[-1]), bf16),
    )
    return pl.pallas_call(
        functools.partial(reduce_kernel, nz, Q, widths),
        out_shape=out_shape,
        in_specs=[ANY] * K,
        out_specs=(ANY,) * K,
        scratch_shapes=[
            vm((nz, Q, W), bf16),
            vm((nz, big, W), bf16),
            vm((nz, big, W), bf16),
            vm((nz, Q, W), bf16),
            vm((nz, Q, W), bf16),
            vm((nz, big, W), bf16),
            vm((nz, big, W), bf16),
            vm((2, nz, Q, W), bf16),
            vm((Q, W), bf16),
            dma((K, nz, 3)),
            dma((K, nz, 2)),
            dma((K, nz, 2)),
            dma((K, nz, 2)),
            dma((K, nz, 2)),
            dma((K, nz, 2)),
            dma((K, nz, 2)),
            dma((K, nz)),
            dma((K, 2, nz)),
            dma((K, 3)),
            dma((K, 3, 2)),
            dma((K, 2)),
            dma((K, 2, 2)),
            dma((K,)),
        ],
        compiler_params=pltpu.CompilerParams(
            collective_id=1, has_side_effects=True, vmem_limit_bytes=60 << 20
        ),
        cost_estimate=pl.CostEstimate(
            flops=10**11, bytes_accessed=nz * 4 * Q * W * 2, transcendentals=0
        ),
        name="reduce_attention",
    )(*parts)


def gather_plain(nz, weights, small, tokens, lengths):
    core, H = lax.axis_index("core"), weights[0].shape[1] // 2
    full = [
        lax.all_gather(swap_core(w, 1, 0), "z", axis=0, tiled=True) for w in weights
    ]
    return (
        jnp.concatenate(full[:3], axis=1),
        full[3],
        lax.all_gather(small, SHARD, axis=0, tiled=True),
        lax.all_gather(tokens, "core", axis=0),
        lax.all_gather(lengths, "core", axis=0),
    )


def reduce_plain(nz, parts):
    n_exp = lax.axis_size("expert")
    out = []
    for k, part in enumerate(parts):
        Q, w = part.shape[2:]
        mine = lax.psum_scatter(part.reshape(nz * 4 * Q, w), "z", scatter_dimension=0, tiled=True)
        mine = lax.psum(mine, "expert")
        if k < len(parts) - 1:
            out.append(swap_core(mine, 0, 1).reshape(2, Q, 2 * w))
        else:
            both = lax.all_to_all(
                mine.reshape(2, 2 * Q, w), "core", split_axis=0, concat_axis=0, tiled=True
            )
            out.append(both.reshape(2, 2, Q, w).transpose(1, 0, 2, 3))
    return out


def rope_tables(positions, head_width):
    half_width = head_width // 2
    exponents = jnp.arange(half_width).astype(f32) * 2.0 / head_width
    frequency = rope_base ** (-exponents)
    angles = positions.astype(f32)[..., None] * frequency
    return (jnp.cos(angles), jnp.sin(angles))


def rotate(values, cosine, sine_table):
    half_width = values.shape[-1] // 2
    leading = values[..., :half_width]
    trailing = values[..., half_width:]
    cos_rows = cosine[:, :, None, :]
    sin_rows = sine_table[:, :, None, :]
    return jnp.concatenate(
        [leading * cos_rows - trailing * sin_rows, trailing * cos_rows + leading * sin_rows],
        axis=-1,
    )


def rms_forward(values, norm_gain):
    inverse = lax.rsqrt(jnp.mean(values * values, axis=-1, keepdims=True) + eps_norm)
    return (values * inverse * norm_gain, inverse)


def rms_backward(values, inverse, norm_gain, upstream):
    weighted = upstream * norm_gain
    gain_grad = jnp.sum(upstream * values * inverse, axis=0)
    inner_mean = jnp.mean(weighted * values, axis=-1, keepdims=True)
    return (inverse * weighted - values * inverse * inverse * inverse * inner_mean, gain_grad)


def dot32(a, b):
    return jnp.dot(a, b, preferred_element_type=f32)


def dot_dims(a, b, da, db):
    return lax.dot_general(a, b, (((da,), (db,)), ((), ())), preferred_element_type=f32)


def ein32(spec, a, b):
    return jnp.einsum(spec, a, b, preferred_element_type=f32)


def swap_core(x, split, concat):
    return lax.all_to_all(x, "core", split_axis=split, concat_axis=concat, tiled=True)


def on_device(
    tokens,
    seq_lengths,
    routes,
    norm_attn,
    w_query,
    w_key,
    w_value,
    w_output,
    norm_ffn,
    w_router,
    w_in,
    w_down,
    cotangent,
):
    T, D = tokens.shape
    R = w_query.shape[0]
    H = D // 2
    head_width = D // HEADS
    heads = HEADS // 2
    n_exp = lax.axis_size("expert")
    n_shard = lax.axis_size("z") * lax.axis_size("core")
    experts = w_router.shape[1]
    local_experts = w_in.shape[1]
    F = w_down.shape[0]
    FF = F * n_shard
    capacity = 10 * T // (4 * experts)
    slots = experts * capacity
    highest = lax.Precision.HIGHEST
    e_index = lax.axis_index("expert")
    core = lax.axis_index("core")

    nz = lax.axis_size("z")
    small = jnp.concatenate([w_router, norm_attn[:, None], norm_ffn[:, None]], axis=1)
    small = jnp.pad(small, ((0, 0), (0, 128 - small.shape[1])))
    length_rows = jnp.broadcast_to(seq_lengths[:, :1], (8, 128))
    gather = gather_attention if n_exp == 4 else gather_plain
    full_qkv, full_output, full_small, chip_tokens, chip_lengths = gather(
        nz, (w_query, w_key, w_value, w_output), small, tokens, length_rows
    )
    full_router = full_small[:, :experts]
    gain_attn = full_small[:, experts].astype(f32)
    gain_ffn = full_small[:, experts + 1].astype(f32)

    w_gate_cols = []
    for part in range(2):
        piece = w_in[:, :, part * FF : (part + 1) * FF].reshape(R, local_experts, n_shard, F)
        piece = piece.transpose(2, 1, 0, 3)
        w_gate_cols.append(piece)

    def reshard(piece):
        moved = lax.all_to_all(piece, SHARD, split_axis=0, concat_axis=0, tiled=True)
        return moved.transpose(1, 0, 2, 3).reshape(local_experts, n_shard * R, F)

    w_gate, w_up = reshard(w_gate_cols[0]), reshard(w_gate_cols[1])

    both = (2, T)
    residual_in = tokens.astype(f32)
    inverse_in = rms_forward(residual_in, gain_attn)[1]
    normed_half = rms_forward(chip_tokens.reshape(2 * T, D).astype(f32), gain_attn)[0].astype(bf16)
    lengths = chip_lengths[:, 0, 0]
    row_index = jnp.arange(T)
    segment = (row_index[None, :] >= lengths[:, None]).astype(jnp.int32)
    positions = row_index[None, :] - lengths[:, None] * segment
    allowed = (segment[:, :, None] == segment[:, None, :]) & (
        row_index[None, None, :] <= row_index[None, :, None]
    )
    cosine, sine_table = rope_tables(positions, head_width)
    head_shape = both + (heads, head_width)
    qkv = dot32(normed_half, full_qkv)
    queries = rotate(qkv[:, :H].reshape(head_shape), cosine, sine_table).astype(bf16)
    keys_rot = rotate(qkv[:, H : 2 * H].reshape(head_shape), cosine, sine_table).astype(bf16)
    values = qkv[:, 2 * H :].astype(bf16).reshape(head_shape)
    score_scale = 1.0 / math.sqrt(head_width)
    scores = ein32("bqhd,bkhd->bhqk", queries, keys_rot) * score_scale
    scores = jnp.where(allowed[:, None], scores, masked_score)
    row_peak = jnp.max(scores, axis=-1, keepdims=True)
    log_total = row_peak + jnp.log(jnp.sum(jnp.exp(scores - row_peak), axis=-1, keepdims=True))
    attn_probs = jnp.exp(scores - log_total)
    probs_half = attn_probs.astype(bf16)
    context = ein32("bhqk,bkhd->bqhd", probs_half, values).astype(bf16)
    context_half = context.reshape(2 * T, H)
    context_full = lax.all_gather(context_half, "core", axis=1, tiled=True)
    mid_half = dot32(context_full, full_output)
    mid_own = swap_core(mid_half, 0, 1)
    residual_mid = residual_in + branch_scale * mid_own
    normed_mid, inverse_mid = rms_forward(residual_mid, gain_ffn)
    normed_mid_half = normed_mid.astype(bf16)

    logits = dot32(normed_mid_half, full_router)
    expert_ids = jnp.arange(experts)
    route_mask = (routes[:, :, None] == expert_ids[None, None, :]).astype(f32)
    chosen = jnp.sum(logits[:, None, :] * route_mask, axis=-1)
    gate_probs = jax.nn.softmax(chosen, axis=-1)
    flat_routes = routes.reshape(2 * T)
    hits = (flat_routes[:, None] == expert_ids[None, :]).astype(bf16)
    order = jnp.arange(2 * T)
    before = (order[:, None] > order[None, :]).astype(bf16)
    earlier = dot32(before, hits)
    slot_index = jnp.sum(earlier * hits.astype(f32), axis=1).astype(jnp.int32)
    target = (flat_routes * capacity + slot_index).reshape(T, 2)
    slot_ids = jnp.arange(slots)
    pick = [(target[:, k][:, None] == slot_ids[None, :]).astype(bf16) for k in range(2)]

    def send_rows(rows0, rows1):
        out = dot_dims(pick[0], rows0, 0, 0) + dot_dims(pick[1], rows1, 0, 0)
        out = out.astype(bf16)
        moved = lax.all_to_all(out, "expert", split_axis=0, concat_axis=0, tiled=True)
        return moved

    def spread(moved):
        rows = lax.all_gather(moved, SHARD, axis=0, tiled=True)
        if local_experts == 1:
            return rows[None]
        rows = rows.reshape(n_shard * n_exp, local_experts, capacity, D)
        return rows.transpose(1, 0, 2, 3).reshape(local_experts, -1, D)

    def bring_back(partial_rows):
        part = partial_rows.astype(bf16)
        if local_experts > 1:
            part = part.reshape(local_experts, n_shard * n_exp, capacity, D).transpose(1, 0, 2, 3)
        part = part.reshape(n_shard * slots, D)
        mine = lax.psum_scatter(part, SHARD, scatter_dimension=0, tiled=True)
        back = lax.all_to_all(mine, "expert", split_axis=0, concat_axis=0, tiled=True)
        return [dot32(pick[k], back) for k in range(2)]

    def per_expert(fn, *arrays):
        return jnp.stack([fn(*[a[i] for a in arrays]) for i in range(local_experts)])

    arrived = spread(send_rows(normed_mid_half, normed_mid_half))
    upstream = cotangent.astype(f32)
    mixture_grad = branch_scale * upstream
    row_grads = (gate_probs[:, :, None] * mixture_grad[:, None, :]).astype(bf16)
    grad_arrived = spread(send_rows(row_grads[:, 0], row_grads[:, 1]))
    down = w_down.transpose(1, 0, 2)
    gate_part = per_expert(dot32, arrived, w_gate)
    up_part = per_expert(dot32, arrived, w_up)
    sigmoid_gate = jax.nn.sigmoid(gate_part)
    silu_gate = gate_part * sigmoid_gate
    activated = (silu_gate * up_part).astype(bf16)
    expert_rows = bring_back(per_expert(dot32, activated, down))
    mixture = gate_probs[:, 0:1] * expert_rows[0] + gate_probs[:, 1:2] * expert_rows[1]
    activations = (residual_mid + branch_scale * mixture).astype(bf16)

    act_grad = per_expert(lambda a, b: dot_dims(a, b, 1, 1), grad_arrived, down)
    gate_grads = (
        act_grad * up_part * sigmoid_gate * (1.0 + gate_part * (1.0 - sigmoid_gate))
    ).astype(bf16)
    up_grads = (act_grad * silu_gate).astype(bf16)
    input_rows = bring_back(
        per_expert(
            lambda a, b, c, d: dot_dims(a, b, 1, 1) + dot_dims(c, d, 1, 1),
            gate_grads,
            w_gate,
            up_grads,
            w_up,
        )
    )
    grad_w_down = per_expert(lambda a, b: dot_dims(a, b, 0, 0), activated, grad_arrived)
    grad_w_down = grad_w_down.transpose(1, 0, 2)

    def reshard_grad(grads):
        term = per_expert(lambda a, b: dot_dims(a, b, 0, 0), arrived, grads).astype(bf16)
        term = term.reshape(local_experts, n_shard, R, F).transpose(1, 0, 2, 3)
        moved = lax.all_to_all(term, SHARD, split_axis=0, concat_axis=0, tiled=True)
        return moved.transpose(2, 1, 0, 3).reshape(R, local_experts, FF).astype(f32)

    grad_w_in = jnp.concatenate([reshard_grad(gate_grads), reshard_grad(up_grads)], axis=2)

    gate_grad = jnp.stack(
        [jnp.sum(mixture_grad * expert_rows[k], axis=-1) for k in range(2)], axis=1
    )
    chosen_grad = gate_probs * (gate_grad - jnp.sum(gate_probs * gate_grad, axis=-1, keepdims=True))
    logit_grad = jnp.sum(chosen_grad[:, :, None] * route_mask, axis=1)
    normed_mid_grad = input_rows[0] + input_rows[1]
    normed_mid_grad = normed_mid_grad + jnp.dot(
        logit_grad, jnp.transpose(full_router.astype(f32)), precision=highest
    )
    router_grad = jnp.dot(
        jnp.transpose(normed_mid_half.astype(f32)), logit_grad, precision=highest
    )
    mid_norm_grad, gain_ffn_grad = rms_backward(
        residual_mid, inverse_mid, gain_ffn, normed_mid_grad
    )
    residual_grad = upstream + mid_norm_grad
    branch_own = (branch_scale * residual_grad).astype(bf16)

    branch_half = swap_core(branch_own, 1, 0)
    context_grad = dot_dims(branch_half, full_output, 1, 1)
    context_grad = lax.psum_scatter(
        context_grad.reshape(2 * T, 2, H).transpose(1, 0, 2).reshape(4 * T, H),
        "core",
        scatter_dimension=0,
        tiled=True,
    ).reshape(head_shape)
    row_delta = jnp.sum(context_grad * context.astype(f32), axis=-1)
    context_grad_half = context_grad.astype(bf16)
    probs_grad = ein32("bqhd,bkhd->bhqk", context_grad_half, values)
    scores_grad = (
        attn_probs * (probs_grad - jnp.transpose(row_delta, (0, 2, 1))[..., None]) * score_scale
    ).astype(bf16)
    queries_grad = ein32("bhqk,bkhd->bqhd", scores_grad, keys_rot)
    keys_grad = ein32("bhqk,bqhd->bkhd", scores_grad, queries)
    values_grad = ein32("bhqk,bqhd->bkhd", probs_half, context_grad_half)
    parts = [
        rotate(queries_grad, cosine, -sine_table).reshape(2 * T, H).astype(bf16),
        rotate(keys_grad, cosine, -sine_table).reshape(2 * T, H).astype(bf16),
        values_grad.reshape(2 * T, H).astype(bf16),
    ]
    weight_grads = [dot_dims(normed_half, p, 0, 0) for p in parts]
    weight_grads.append(dot_dims(context_full, branch_half, 0, 0))
    qkv_grad = jnp.concatenate(parts, axis=1)
    normed_in_grad = lax.psum_scatter(
        dot_dims(qkv_grad, full_qkv, 1, 1), "core", scatter_dimension=0, tiled=True
    )
    in_norm_grad, gain_attn_grad = rms_backward(residual_in, inverse_in, gain_attn, normed_in_grad)
    grad_tokens = residual_grad + in_norm_grad

    small_grad = jnp.concatenate(
        [router_grad, gain_attn_grad[:, None], gain_ffn_grad[:, None]], axis=1
    )
    weight_grads.append(jnp.pad(small_grad, ((0, 0), (0, 128 - small_grad.shape[1]))))
    reduce = reduce_attention if n_exp == 4 else reduce_plain
    sums = reduce(nz, [g.astype(bf16).reshape(nz, 4, -1, g.shape[1]) for g in weight_grads])
    small_sum = jnp.sum(sums[4].astype(f32), axis=1).reshape(R, 128)
    sums = [s.reshape(R, D).astype(f32) for s in sums[:4]]
    return (
        activations,
        grad_tokens,
        small_sum[:, experts],
        sums[0],
        sums[1],
        sums[2],
        sums[3],
        small_sum[:, experts + 1],
        small_sum[:, :experts],
        grad_w_in,
        grad_w_down,
    )


def solution(mesh):
    n_expert, n_shard = mesh.devices.shape
    chips = Mesh(mesh.devices.reshape(n_expert, n_shard // 2, 2), ("expert", "z", "core"))
    rows = P(("expert", "z", "core"), None)
    shard = P(SHARD)
    shard2 = P(SHARD, None)
    shard3 = P(SHARD, "expert", None)
    in_specs = (
        rows,
        rows,
        rows,
        shard,
        shard2,
        shard2,
        shard2,
        shard2,
        shard,
        shard2,
        shard3,
        shard3,
        rows,
    )
    out_specs = (
        rows,
        rows,
        shard,
        shard2,
        shard2,
        shard2,
        shard2,
        shard,
        shard2,
        shard3,
        shard3,
    )
    return jax.shard_map(
        on_device, mesh=chips, in_specs=in_specs, out_specs=out_specs, check_vma=False
    )
```

```python
import functools
import math

import jax
import jax.numpy as jnp
from jax import lax
from jax.experimental import pallas as pl
from jax.experimental.pallas import tpu as pltpu
from jax.sharding import Mesh, PartitionSpec as P

HEADS = 36

eps_norm = 1e-05
branch_scale = 1.4 / math.sqrt(40.0)
rope_base = 10000.0
masked_score = -1e30
bf16 = jnp.bfloat16
f32 = jnp.float32
SHARD = ("z", "core")
GRID = ("z", "expert")
AHEAD = 2
ANY = pl.BlockSpec(memory_space=pl.ANY)


def place():
    e, z, c = lax.axis_index("expert"), lax.axis_index("z"), lax.axis_index("core")
    across_x = e + 1 - 2 * (e % 2)
    across_y = (e + 2) % 4
    return e, z, c, across_x, across_y


def remote(src, dst, send, recv, e, z, c):
    return pltpu.make_async_remote_copy(
        src_ref=src,
        dst_ref=dst,
        send_sem=send,
        recv_sem=recv,
        device_id=(e, z, c),
        device_id_type=pl.DeviceIdType.MESH,
    )


def greet(nz, both_cores):
    e, z, c, ex, ey = place()
    barrier = pltpu.get_barrier_semaphore()

    def hail(te, tz, tc):
        pl.semaphore_signal(
            barrier, inc=1, device_id=(te, tz, tc), device_id_type=pl.DeviceIdType.MESH
        )

    cores = (c, 1 - c) if both_cores[0] else (c,)
    plane = (c, 1 - c) if both_cores[1] else (c,)
    hail(e, z, 1 - c)
    for t in plane:
        hail(ex, z, t)
        hail(ey, z, t)
    for step in (-1, 1):

        @pl.when((z + step >= 0) & (z + step < nz))
        def _():
            for t in cores:
                hail(e, z + step, t)

    ends = jnp.where(z > 0, 1, 0) + jnp.where(z < nz - 1, 1, 0)
    pl.semaphore_wait(barrier, 1 + 2 * len(plane) + len(cores) * ends)


def cut(k, Q):
    big = (Q // 2 + 15) // 16 * 16
    return big if k % 2 == 0 else Q - big


def gather_kernel(
    nz, Q, H,
    q_ref, k_ref, v_ref, o_ref, s_ref, t_ref, l_ref, p_ref,
    qkv_out, o_out, s_out, t_out, l_out, p_out,
    zrecv, zhop, zsend, near_recv, near_send, far_recv, far_send, own, sib_send, sib_recv,
    *payload,
):
    e, z, c, ex, ey = place()
    holder, turn = e // 2, e % 2
    sources = (q_ref, k_ref, v_ref, o_ref, s_ref)
    K = len(sources)

    def src(k, half, j, count=1):
        rows = pl.ds(pl.multiple_of(j * Q, 16), count * Q)
        if k == 4:
            return sources[k].at[rows, :]
        return sources[k].at[rows, pl.ds(pl.multiple_of(half * H, 128), H)]

    def dst(k, zz, quarter, r0=0, n=Q):
        rows = pl.ds(pl.multiple_of((zz * 4 + quarter) * Q + r0, 16), n)
        if k < 3:
            return qkv_out.at[rows, pl.ds(k * H, H)]
        return (o_out if k == 3 else s_out).at[rows, :]

    greet(nz, (True, False))

    pairs = ((t_ref, t_out), (l_ref, l_out))
    extra = []
    for n, (a, b) in enumerate(pairs):
        mine = pltpu.make_async_copy(a, b.at[c], own.at[K + n])
        mine.start()
        theirs = remote(a, b.at[c], sib_send.at[K + n], sib_recv.at[K + n], e, z, 1 - c)
        theirs.start()
        extra += [mine, theirs]

    def first_hop(k, step, half):
        side = 0 if step > 0 else 1
        return remote(
            src(k, half, turn), dst(k, z, e), zhop.at[k, side, half], zrecv.at[k, side, 0],
            e, z + step, half,
        )

    for k in range(K):
        for step in (1, -1):

            @pl.when((c == holder) & (z + step >= 0) & (z + step < nz))
            def _():
                first_hop(k, step, 0).start()
                first_hop(k, step, 1).start()

    stream = payload_stream(nz, p_ref, p_out, payload, p_ref.shape[0] // 2)
    stream[0]()
    for k in range(K):
        rows = src(k, c, 0, 2), dst(k, z, 2 * c, 0, 2 * Q)
        mine = pltpu.make_async_copy(rows[0], rows[1], own.at[k])
        mine.start()
        theirs = remote(
            src(k, 1 - c, 0, 2), rows[1], sib_send.at[k], sib_recv.at[k], e, z, 1 - c
        )
        theirs.start()
        extra += [mine, theirs]

    def where(side, i):
        return z - 1 - i if side == 0 else z + 1 + i

    def onward(k, side, i):
        slab = dst(k, where(side, i), e)
        step = 1 if side == 0 else -1
        return remote(
            slab, slab, zsend.at[k, side, i], zrecv.at[k, side, i + 1], e, z + step, c
        )

    def near(k, side, i, axis):
        slab = dst(k, where(side, i), e)
        return remote(
            slab, slab, near_send.at[k, side, i, axis], near_recv.at[k, side, i, axis],
            ex if axis == 0 else ey, z, c,
        )

    def near_wait(k, side, i, axis):
        slab = dst(k, where(side, i), ex if axis == 0 else ey)
        remote(
            slab, slab, near_send.at[k, side, i, axis], near_recv.at[k, side, i, axis], ex, z, c
        ).wait_recv()

    def far(k, side, i, axis):
        a = cut(k, Q)
        if axis == 0:
            slab = dst(k, where(side, i), ex, 0, a)
        else:
            slab = dst(k, where(side, i), ey, a, Q - a)
        return remote(
            slab, slab, far_send.at[k, side, i, axis], far_recv.at[k, side, i, axis],
            ey if axis == 0 else ex, z, c,
        )

    def exists(side, i):
        zz = where(side, i)
        return (zz >= 0) & (zz < nz)

    def inside(side):
        return z < nz - 1 if side == 0 else z > 0

    def arrive(k, side, i):
        @pl.when(exists(side, i))
        def _():
            slab = dst(k, where(side, i), e)
            remote(
                slab, slab, zsend.at[k, side, i], zrecv.at[k, side, i], e, z, c
            ).wait_recv()
            if i < nz - 2:

                @pl.when(inside(side))
                def _():
                    onward(k, side, i).start()

            near(k, side, i, 0).start()
            near(k, side, i, 1).start()

    def relay(k, side, i):
        @pl.when(exists(side, i))
        def _():
            for axis in range(2):
                near_wait(k, side, i, axis)
                far(k, side, i, axis).start()

    steps = [(k, side, i) for i in range(nz - 1) for k in range(K) for side in range(2)]
    lag = 2 * K
    blocks = 2 * nz - 1
    beat = len(steps) // blocks
    p_begin, p_arrive, p_relay, p_close, p_end = stream
    for n, step in enumerate(steps):
        arrive(*step)
        if n >= lag:
            relay(*steps[n - lag])
        if n % beat == beat - 1 and n // beat < blocks:
            s = n // beat
            p_arrive(s)
            if s >= 1:
                p_relay(s - 1)
            if s >= 2:
                p_close(s - 2)
    for step in steps[len(steps) - lag :]:
        relay(*step)
    p_relay(blocks - 1)
    p_close(blocks - 2)
    p_close(blocks - 1)
    for s in range(blocks):
        p_end(s)

    for k, side, i in steps:

        @pl.when(exists(side, i))
        def _():
            if i < nz - 2:

                @pl.when(inside(side))
                def _():
                    onward(k, side, i).wait_send()

            a = cut(k, Q)
            zz, diagonal = where(side, i), (ex + 2) % 4
            for axis in range(2):
                near(k, side, i, axis).wait_send()
                far(k, side, i, axis).wait_send()
                slab = dst(k, zz, diagonal, 0, a) if axis == 0 else dst(k, zz, diagonal, a, Q - a)
                remote(
                    slab, slab, far_send.at[k, side, i, axis], far_recv.at[k, side, i, axis],
                    ex, z, c,
                ).wait_recv()

    for k in range(K):
        for step in (1, -1):

            @pl.when((c == holder) & (z + step >= 0) & (z + step < nz))
            def _():
                first_hop(k, step, 0).wait_send()
                first_hop(k, step, 1).wait_send()

    for copy in extra:
        copy.wait()


def gather_attention(nz, weights, small, tokens, lengths, block):
    R, D = weights[0].shape
    Q, H = R // 2, D // 2
    K = len(weights) + 1
    dma = pltpu.SemaphoreType.DMA
    any_ = ANY
    W = small.shape[1]
    sd = jax.ShapeDtypeStruct
    outs = pl.pallas_call(
        functools.partial(gather_kernel, nz, Q, H),
        out_shape=(
            sd((nz * 4 * Q, 3 * H), bf16),
            sd((nz * 4 * Q, H), bf16),
            sd((nz * 4 * Q, W), bf16),
            sd((2,) + tokens.shape, bf16),
            sd((2,) + lengths.shape, lengths.dtype),
            sd((nz, 2, 4) + block.shape, block.dtype),
        ),
        in_specs=[any_] * 8,
        out_specs=(any_,) * 6,
        scratch_shapes=[
            dma((K, 2, nz - 1)),
            dma((K, 2, 2)),
            dma((K, 2, nz - 1)),
            dma((K, 2, nz - 1, 2)),
            dma((K, 2, nz - 1, 2)),
            dma((K, 2, nz - 1, 2)),
            dma((K, 2, nz - 1, 2)),
            dma((K + 2,)),
            dma((K + 2,)),
            dma((K + 2,)),
            *payload_sems(nz),
        ],
        compiler_params=pltpu.CompilerParams(collective_id=0, has_side_effects=True),
        cost_estimate=pl.CostEstimate(
            flops=10**11, bytes_accessed=8 * D * H * 2, transcendentals=0
        ),
        name="gather_attention",
    )(*weights, small, tokens, lengths, block)
    return outs


def reduce_kernel(
    nz, Q, widths,
    *refs,
):
    K = len(widths)
    parts, refs = refs[:K], refs[K:]
    outs, refs = refs[:K], refs[K:]
    (
        mine, mine_x, mine_y, from_x, from_y, via_x, via_y, from_z, result,
        load, via_send, via_recv, plain_send, plain_recv, sum_send, sum_recv,
        zsend, zrecv, fin_send, fin_recv, far_send, far_recv, own,
    ) = refs
    e, z, c, ex, ey = place()
    diagonal = (ex + 2) % 4
    holder, turn = e // 2, e % 2
    offs = [sum(widths[:k]) for k in range(K)]

    def order(i):
        code = 0
        for zz in range(nz):
            far_first = sorted(range(nz), key=lambda t: (-abs(t - zz), t))
            code += far_first[i] * nz**zz
        power = 1
        for zz in range(nz):
            power = power + (nz**zz - 1) * jnp.where(z == zz, 1, 0)
        return (code // power) % nz

    dest = [order(i) for i in range(nz)]

    def cols(k):
        return pl.ds(offs[k], widths[k])

    greet(nz, (False, True))

    def loads(k, i):
        a = cut(k, Q)
        zz = dest[i]
        out = [
            (parts[k].at[zz, e], mine.at[i, :, cols(k)]),
            (parts[k].at[zz, ex, pl.ds(a, Q - a), :], mine_x.at[i, pl.ds(0, Q - a), cols(k)]),
            (parts[k].at[zz, ey, pl.ds(0, a), :], mine_y.at[i, pl.ds(0, a), cols(k)]),
        ]
        return [pltpu.make_async_copy(s, d, load.at[k, i, n]) for n, (s, d) in enumerate(out)]

    def via(k, i, axis):
        a = cut(k, Q)
        zz = dest[i]
        if axis == 0:
            return remote(
                parts[k].at[zz, diagonal, pl.ds(0, a), :], via_x.at[i, pl.ds(0, a), cols(k)],
                via_send.at[k, i, 0], via_recv.at[k, i, 0], ex, z, c,
            )
        return remote(
            parts[k].at[zz, diagonal, pl.ds(a, Q - a), :], via_y.at[i, pl.ds(0, Q - a), cols(k)],
            via_send.at[k, i, 1], via_recv.at[k, i, 1], ey, z, c,
        )

    def plain(k, i, axis):
        a = cut(k, Q)
        zz = dest[i]
        if axis == 0:
            return remote(
                parts[k].at[zz, ex, pl.ds(0, a), :], from_x.at[i, pl.ds(0, a), cols(k)],
                plain_send.at[k, i, 0], plain_recv.at[k, i, 0], ex, z, c,
            )
        return remote(
            parts[k].at[zz, ey, pl.ds(a, Q - a), :], from_y.at[i, pl.ds(a, Q - a), cols(k)],
            plain_send.at[k, i, 1], plain_recv.at[k, i, 1], ey, z, c,
        )

    def summed(k, i, axis):
        a = cut(k, Q)
        if axis == 0:
            return remote(
                mine_x.at[i, pl.ds(0, Q - a), cols(k)], from_x.at[i, pl.ds(a, Q - a), cols(k)],
                sum_send.at[k, i, 0], sum_recv.at[k, i, 0], ex, z, c,
            )
        return remote(
            mine_y.at[i, pl.ds(0, a), cols(k)], from_y.at[i, pl.ds(0, a), cols(k)],
            sum_send.at[k, i, 1], sum_recv.at[k, i, 1], ey, z, c,
        )

    def add(target, others, n, k):
        @pl.loop(0, n // 16)
        def _(b):
            rows = pl.ds(pl.multiple_of(b * 16, 16), 16)
            acc = target[rows, cols(k)].astype(f32)
            for o in others:
                acc = acc + o[rows, cols(k)].astype(f32)
            target[rows, cols(k)] = acc.astype(bf16)

    pairs = [(k, i) for i in range(nz) for k in range(K)]
    def begin(k, i):
        via(k, i, 0).start()
        via(k, i, 1).start()
        for copy in loads(k, i):
            copy.start()
        plain(k, i, 0).start()
        plain(k, i, 1).start()

    ahead = AHEAD * K
    for k, i in pairs[:ahead]:
        begin(k, i)

    def combine(k, i):
        a = cut(k, Q)
        group = loads(k, i)
        group[1].wait()
        group[2].wait()
        via(k, i, 0).wait_recv()
        add(mine_y.at[i], [via_x.at[i]], a, k)
        summed(k, i, 1).start()
        via(k, i, 1).wait_recv()
        add(mine_x.at[i], [via_y.at[i]], Q - a, k)
        summed(k, i, 0).start()

    def zcopy(k, i):
        step = jnp.where(dest[i] > z, 1, -1)
        side = jnp.where(dest[i] > z, 0, 1)
        return remote(
            mine.at[i, :, cols(k)], from_z.at[side, dest[i], :, cols(k)],
            zsend.at[k, i], zrecv.at[k, side, dest[i]], e, z + step, c,
        )

    def zwait(k, side, zz):
        slab = from_z.at[side, zz, :, cols(k)]
        remote(slab, slab, zsend.at[k, 0], zrecv.at[k, side, zz], e, z, c).wait_recv()

    def finish(k, i):
        loads(k, i)[0].wait()
        for axis in range(2):
            plain(k, i, axis).wait_recv()
            summed(k, i, axis).wait_recv()
        add(mine.at[i], [from_x.at[i], from_y.at[i]], Q, k)
        zz = dest[i]
        if i < nz - 1:
            for side in range(2):
                going = zz > z if side == 0 else zz < z
                behind = z > 0 if side == 0 else z < nz - 1

                @pl.when(going & behind)
                def _():
                    zwait(k, side, zz)
                    add(mine.at[i], [from_z.at[side, zz]], Q, k)

            zcopy(k, i).start()

    def fin(k, axis):
        if widths[k] == widths[-1] and k == K - 1:
            land = outs[k].at[turn, c]
        else:
            land = outs[k].at[turn, :, pl.ds(pl.multiple_of(c * widths[k], 128), widths[k])]
        te = (ex, ey, e)[axis]
        return remote(
            result.at[:, cols(k)], land, fin_send.at[k, axis], fin_recv.at[k, axis, c],
            te, z, holder,
        )

    def total(k):
        last = nz - 1
        for side in range(2):
            behind = z > 0 if side == 0 else z < nz - 1

            @pl.when(behind)
            def _():
                zwait(k, side, z)
                add(mine.at[last], [from_z.at[side, z]], Q, k)

        @pl.loop(0, Q // 16)
        def _(b):
            rows = pl.ds(pl.multiple_of(b * 16, 16), 16)
            result[rows, cols(k)] = mine[last, rows, cols(k)]

        fin(k, 0).start()
        fin(k, 1).start()

        @pl.when(c == holder)
        def _():
            pltpu.make_async_copy(result.at[:, cols(k)], fin_own(k), own.at[k]).start()

        @pl.when(c != holder)
        def _():
            fin(k, 2).start()

    def fin_own(k):
        if k == K - 1:
            return outs[k].at[turn, c]
        return outs[k].at[turn, :, pl.ds(pl.multiple_of(c * widths[k], 128), widths[k])]

    lag = K
    for n, (k, i) in enumerate(pairs):
        combine(k, i)
        if n + ahead < len(pairs):
            begin(*pairs[n + ahead])
        if n >= lag:
            k2, i2 = pairs[n - lag]
            finish(k2, i2)
    for k2, i2 in pairs[len(pairs) - lag :]:
        finish(k2, i2)
    for k in range(K):
        total(k)

    def slot(k, j, half, r0=0, n=Q):
        if k == K - 1:
            return outs[k].at[j, half, pl.ds(r0, n), :]
        return outs[k].at[j, pl.ds(r0, n), pl.ds(half * widths[k], widths[k])]

    def got(k, axis, half):
        j = (ex if axis == 0 else ey) % 2
        view = slot(k, j, half)
        return remote(
            view, view, fin_send.at[k, axis], fin_recv.at[k, axis, half], e, z, c
        )

    def passed(k, axis, half, quarter):
        a = cut(k, Q)
        j = quarter % 2
        view = slot(k, j, half, 0, a) if axis == 0 else slot(k, j, half, a, Q - a)
        return remote(
            view, view, far_send.at[k, half], far_recv.at[k, axis, half],
            ey if axis == 0 else ex, z, c,
        )

    for k in range(K):
        for axis in range(2):

            @pl.when((c == holder) if axis == 0 else (c != holder))
            def _():
                for half in range(2):
                    got(k, axis, half).wait_recv()
                    passed(k, axis, half, ex if axis == 0 else ey).start()

    for k in range(K):
        for axis in range(2):

            @pl.when((c == holder) if axis == 0 else (c != holder))
            def _():
                for half in range(2):
                    passed(k, axis, half, ex if axis == 0 else ey).wait_send()

        @pl.when(c != holder)
        def _():
            for half in range(2):
                passed(k, 0, half, diagonal).wait_recv()
                passed(k, 1, half, diagonal).wait_recv()
            fin(k, 2).wait_send()

        @pl.when(c == holder)
        def _():
            pltpu.make_async_copy(result.at[:, cols(k)], fin_own(k), own.at[k]).wait()
            other = slot_of(outs, k, K, turn, 1 - c, widths)
            remote(
                other, other, fin_send.at[k, 2], fin_recv.at[k, 2, 1 - c], e, z, c
            ).wait_recv()

        fin(k, 0).wait_send()
        fin(k, 1).wait_send()
        for i in range(nz):
            for axis in range(2):
                via(k, i, axis).wait_send()
                plain(k, i, axis).wait_send()
                summed(k, i, axis).wait_send()
            if i < nz - 1:
                zcopy(k, i).wait_send()


def slot_of(outs, k, K, j, half, widths):
    if k == K - 1:
        return outs[k].at[j, half]
    return outs[k].at[j, :, pl.ds(pl.multiple_of(half * widths[k], 128), widths[k])]


def reduce_attention(nz, parts):
    Q = parts[0].shape[2]
    widths = tuple(p.shape[3] for p in parts)
    W, K = sum(widths), len(parts)
    big = max(cut(0, Q), cut(1, Q))
    dma = pltpu.SemaphoreType.DMA
    sd = jax.ShapeDtypeStruct
    vm = pltpu.VMEM
    out_shape = tuple(sd((2, Q, 2 * w), bf16) for w in widths[:-1]) + (
        sd((2, 2, Q, widths[-1]), bf16),
    )
    return pl.pallas_call(
        functools.partial(reduce_kernel, nz, Q, widths),
        out_shape=out_shape,
        in_specs=[ANY] * K,
        out_specs=(ANY,) * K,
        scratch_shapes=[
            vm((nz, Q, W), bf16),
            vm((nz, big, W), bf16),
            vm((nz, big, W), bf16),
            vm((nz, Q, W), bf16),
            vm((nz, Q, W), bf16),
            vm((nz, big, W), bf16),
            vm((nz, big, W), bf16),
            vm((2, nz, Q, W), bf16),
            vm((Q, W), bf16),
            dma((K, nz, 3)),
            dma((K, nz, 2)),
            dma((K, nz, 2)),
            dma((K, nz, 2)),
            dma((K, nz, 2)),
            dma((K, nz, 2)),
            dma((K, nz, 2)),
            dma((K, nz)),
            dma((K, 2, nz)),
            dma((K, 3)),
            dma((K, 3, 2)),
            dma((K, 2)),
            dma((K, 2, 2)),
            dma((K,)),
        ],
        compiler_params=pltpu.CompilerParams(
            collective_id=1, has_side_effects=True, vmem_limit_bytes=60 << 20
        ),
        cost_estimate=pl.CostEstimate(
            flops=10**11, bytes_accessed=nz * 4 * Q * W * 2, transcendentals=0
        ),
        name="reduce_attention",
    )(*parts)


def payload_stream(nz, ref, out, sems, split):
    zrecv, zsend, near_recv, near_send, far_recv, far_send, sib_recv, sib_send, own = sems
    e, z, c, ex, ey = place()
    diagonal = (ex + 2) % 4
    T = ref.shape[0]
    S = 2 * nz - 1

    def split_step(s):
        return (s - 1) % 2, (s - 1) // 2

    def where(s):
        if s == 0:
            return z
        side, i = split_step(s)
        return z - 1 - i if side == 0 else z + 1 + i

    def exists(s):
        if s == 0:
            return z >= 0
        zz = where(s)
        return (zz >= 0) & (zz < nz)

    def slab(s, quarter, r0=0, n=T):
        return out.at[where(s), c, quarter, pl.ds(r0, n), :]

    def first(step):
        side = 0 if step > 0 else 1
        return remote(ref, slab(0, e), zsend.at[side, nz - 1], zrecv.at[side, 0], e, z + step, c)

    def onward(s):
        side, i = split_step(s)
        step = 1 if side == 0 else -1
        return remote(
            slab(s, e), slab(s, e), zsend.at[side, i], zrecv.at[side, i + 1], e, z + step, c
        )

    def near(s, axis):
        source = ref if s == 0 else slab(s, e)
        return remote(
            source, slab(s, e), near_send.at[s, axis], near_recv.at[s, axis],
            ex if axis == 0 else ey, z, c,
        )

    def near_wait(s, axis):
        view = slab(s, ex if axis == 0 else ey)
        remote(view, view, near_send.at[s, axis], near_recv.at[s, axis], ex, z, c).wait_recv()

    axes = range(2) if split else range(1)

    def far_view(s, quarter, axis):
        if not split:
            return slab(s, quarter)
        return slab(s, quarter, 0, split) if axis == 0 else slab(s, quarter, split, T - split)

    def far(s, axis):
        view = far_view(s, ex if axis == 0 else ey, axis)
        return remote(
            view, view, far_send.at[s, axis], far_recv.at[s, axis],
            ey if axis == 0 else ex, z, c,
        )

    def far_wait(s, axis):
        view = far_view(s, diagonal, axis)
        remote(view, view, far_send.at[s, axis], far_recv.at[s, axis], ex, z, c).wait_recv()

    def beside(s, n):
        quarter = (e, ex, ey, diagonal)[n]
        source = ref if s == 0 and n == 0 else slab(s, quarter)
        return remote(
            source, slab(s, quarter), sib_send.at[s, n], sib_recv.at[s, n], e, z, 1 - c
        )

    def beside_wait(s, n):
        view = out.at[where(s), 1 - c, (e, ex, ey, diagonal)[n]]
        remote(view, view, sib_send.at[s, n], sib_recv.at[s, n], e, z, c).wait_recv()

    def inside(side):
        return z < nz - 1 if side == 0 else z > 0

    def begin():
        for step in (1, -1):

            @pl.when((z + step >= 0) & (z + step < nz))
            def _():
                first(step).start()

        near(0, 0).start()
        near(0, 1).start()
        beside(0, 0).start()
        pltpu.make_async_copy(ref, slab(0, e), own).start()

    def arrive(s):
        if s == 0:
            return

        @pl.when(exists(s))
        def _():
            side, i = split_step(s)
            remote(
                slab(s, e), slab(s, e), zsend.at[side, i], zrecv.at[side, i], e, z, c
            ).wait_recv()
            if i < nz - 2:

                @pl.when(inside(side))
                def _():
                    onward(s).start()

            near(s, 0).start()
            near(s, 1).start()
            beside(s, 0).start()

    def relay(s):
        @pl.when(exists(s))
        def _():
            near_wait(s, 0)
            far(s, 0).start()
            beside(s, 1).start()
            near_wait(s, 1)
            if split:
                far(s, 1).start()
            beside(s, 2).start()

    def close(s):
        @pl.when(exists(s))
        def _():
            for axis in axes:
                far_wait(s, axis)
            beside(s, 3).start()

    def end(s):
        @pl.when(exists(s))
        def _():
            for axis in range(2):
                near(s, axis).wait_send()
            for axis in axes:
                far(s, axis).wait_send()
            for n in range(4):
                beside(s, n).wait_send()
                beside_wait(s, n)
            if s > 0 and split_step(s)[1] < nz - 2:

                @pl.when(inside(split_step(s)[0]))
                def _():
                    onward(s).wait_send()

        if s == 0:
            for step in (1, -1):

                @pl.when((z + step >= 0) & (z + step < nz))
                def _():
                    first(step).wait_send()

            pltpu.make_async_copy(ref, slab(0, e), own).wait()

    return begin, arrive, relay, close, end


def payload_sems(nz):
    dma = pltpu.SemaphoreType.DMA
    S = 2 * nz - 1
    return [
        dma((2, nz)), dma((2, nz)), dma((S, 2)), dma((S, 2)), dma((S, 2)), dma((S, 2)),
        dma((S, 4)), dma((S, 4)), dma(()),
    ]


def spread_kernel(nz, splits, *refs):
    n = len(splits)
    ins, outs, sems = refs[:n], refs[n : 2 * n], refs[2 * n :]
    greet(nz, (False, False))
    streams = [
        payload_stream(nz, ins[i], outs[i], sems[9 * i : 9 * i + 9], splits[i]) for i in range(n)
    ]
    for t in streams:
        t[0]()
    S = 2 * nz - 1
    for s in range(S):
        for t in streams:
            t[1](s)
        if s >= 1:
            for t in streams:
                t[2](s - 1)
        if s >= 2:
            for t in streams:
                t[3](s - 2)
    for t in streams:
        t[2](S - 1)
    for s in (S - 2, S - 1):
        for t in streams:
            t[3](s)
    for s in range(S):
        for t in streams:
            t[4](s)


def spread_blocks(nz, blocks, collective):
    sd = jax.ShapeDtypeStruct
    splits = tuple(b.shape[0] // 2 if b.shape[0] % 32 == 0 else 0 for b in blocks)
    return pl.pallas_call(
        functools.partial(spread_kernel, nz, splits),
        out_shape=tuple(sd((nz, 2, 4) + b.shape, b.dtype) for b in blocks),
        in_specs=[ANY] * len(blocks),
        out_specs=(ANY,) * len(blocks),
        scratch_shapes=[s for _ in blocks for s in payload_sems(nz)],
        compiler_params=pltpu.CompilerParams(collective_id=collective, has_side_effects=True),
        cost_estimate=pl.CostEstimate(
            flops=5 * 10**10, bytes_accessed=sum(b.size for b in blocks) * 128, transcendentals=0
        ),
        name="spread_blocks",
    )(*blocks)


def pack_kernel(n, F, Fp, x_ref, o_ref):
    half = n * F
    rows = x_ref.shape[0]
    for i in range(n):
        for part in range(2):
            cols = x_ref[:, part * half + i * F : part * half + (i + 1) * F]
            if Fp > F:
                cols = jnp.concatenate([cols, jnp.zeros((rows, Fp - F), cols.dtype)], axis=1)
            o_ref[i, :, part * Fp : (part + 1) * Fp] = cols


def pack_columns(w, n, F, Fp):
    rows = w.shape[0]
    block = 16
    return pl.pallas_call(
        functools.partial(pack_kernel, n, F, Fp),
        grid=(rows // block,),
        in_specs=[pl.BlockSpec((block, w.shape[1]), lambda i: (i, 0))],
        out_specs=pl.BlockSpec((n, block, 2 * Fp), lambda i: (0, i, 0)),
        out_shape=jax.ShapeDtypeStruct((n, rows, 2 * Fp), w.dtype),
        name="pack_columns",
    )(w)


def unpack_kernel(n, F, Fp, x_ref, o_ref, line):
    half = n * F
    rows = line.shape[0]
    for i in range(n):
        for part in range(2):
            cols = x_ref[i, :, part * Fp : part * Fp + F].astype(f32)
            line[:, part * half + i * F : part * half + (i + 1) * F] = cols
    tiles = 2 * half // 128
    for j in range(tiles):
        o_ref[pl.ds(j, rows, stride=tiles), :] = line[:, j * 128 : (j + 1) * 128]


def unpack_columns(x, F):
    n, rows, Fp2 = x.shape
    block = 16
    width = 2 * n * F
    tiles = width // 128
    flat = pl.pallas_call(
        functools.partial(unpack_kernel, n, F, Fp2 // 2),
        grid=(rows // block,),
        in_specs=[pl.BlockSpec((n, block, Fp2), lambda i: (0, i, 0))],
        out_specs=pl.BlockSpec((block * tiles, 128), lambda i: (i, 0)),
        out_shape=jax.ShapeDtypeStruct((rows * tiles, 128), f32),
        scratch_shapes=[pltpu.VMEM((block, width), f32)],
        name="unpack_columns",
    )(x)
    return flat.reshape(rows, 1, width)


def line_kernel(x_ref, o_ref):
    rows, width = x_ref.shape
    tiles = width // 128
    for j in range(tiles):
        o_ref[pl.ds(j, rows, stride=tiles), :] = x_ref[:, j * 128 : (j + 1) * 128]


def lined_up(x):
    rows, width = x.shape
    tiles = width // 128
    block = 80 if rows % 80 == 0 else 8
    flat = pl.pallas_call(
        line_kernel,
        grid=(rows // block,),
        in_specs=[pl.BlockSpec((block, width), lambda i: (i, 0))],
        out_specs=pl.BlockSpec((block * tiles, 128), lambda i: (i, 0)),
        out_shape=jax.ShapeDtypeStruct((rows * tiles, 128), x.dtype),
        name="lined_up",
    )(x)
    return flat.reshape(rows, 1, width)


def gather_plain(nz, weights, small, tokens, lengths, block):
    core, H = lax.axis_index("core"), weights[0].shape[1] // 2
    full = [
        lax.all_gather(swap_core(w, 1, 0), "z", axis=0, tiled=True) for w in weights
    ]
    return (
        jnp.concatenate(full[:3], axis=1),
        full[3],
        lax.all_gather(small, SHARD, axis=0, tiled=True),
        lax.all_gather(tokens, "core", axis=0),
        lax.all_gather(lengths, "core", axis=0),
        spread_plain(nz, (block,), 0)[0],
    )


def spread_plain(nz, blocks, collective):
    out = []
    for block in blocks:
        for axis in ("expert", "core", "z"):
            block = lax.all_gather(block, axis, axis=0)
        out.append(block)
    return out


def reduce_plain(nz, parts):
    n_exp = lax.axis_size("expert")
    out = []
    for k, part in enumerate(parts):
        Q, w = part.shape[2:]
        mine = lax.psum_scatter(part.reshape(nz * 4 * Q, w), "z", scatter_dimension=0, tiled=True)
        mine = lax.psum(mine, "expert")
        if k < len(parts) - 1:
            out.append(swap_core(mine, 0, 1).reshape(2, Q, 2 * w))
        else:
            both = lax.all_to_all(
                mine.reshape(2, 2 * Q, w), "core", split_axis=0, concat_axis=0, tiled=True
            )
            out.append(both.reshape(2, 2, Q, w).transpose(1, 0, 2, 3))
    return out


def rope_tables(positions, head_width):
    half_width = head_width // 2
    exponents = jnp.arange(half_width).astype(f32) * 2.0 / head_width
    frequency = rope_base ** (-exponents)
    angles = positions.astype(f32)[..., None] * frequency
    return (jnp.cos(angles), jnp.sin(angles))


def rotate(values, cosine, sine_table):
    half_width = values.shape[-1] // 2
    leading = values[..., :half_width]
    trailing = values[..., half_width:]
    cos_rows = cosine[:, :, None, :]
    sin_rows = sine_table[:, :, None, :]
    return jnp.concatenate(
        [leading * cos_rows - trailing * sin_rows, trailing * cos_rows + leading * sin_rows],
        axis=-1,
    )


def rms_forward(values, norm_gain):
    inverse = lax.rsqrt(jnp.mean(values * values, axis=-1, keepdims=True) + eps_norm)
    return (values * inverse * norm_gain, inverse)


def rms_backward(values, inverse, norm_gain, upstream):
    weighted = upstream * norm_gain
    gain_grad = jnp.sum(upstream * values * inverse, axis=0)
    inner_mean = jnp.mean(weighted * values, axis=-1, keepdims=True)
    return (inverse * weighted - values * inverse * inverse * inverse * inner_mean, gain_grad)


def dot32(a, b):
    return jnp.dot(a, b, preferred_element_type=f32)


def dot_dims(a, b, da, db):
    return lax.dot_general(a, b, (((da,), (db,)), ((), ())), preferred_element_type=f32)


def ein32(spec, a, b):
    return jnp.einsum(spec, a, b, preferred_element_type=f32)


def swap_core(x, split, concat):
    return lax.all_to_all(x, "core", split_axis=split, concat_axis=concat, tiled=True)


def on_device(
    tokens,
    seq_lengths,
    routes,
    norm_attn,
    w_query,
    w_key,
    w_value,
    w_output,
    norm_ffn,
    w_router,
    w_in,
    w_down,
    cotangent,
):
    T, D = tokens.shape
    R = w_query.shape[0]
    H = D // 2
    head_width = D // HEADS
    heads = HEADS // 2
    n_exp = lax.axis_size("expert")
    n_shard = lax.axis_size("z") * lax.axis_size("core")
    experts = w_router.shape[1]
    F = w_down.shape[0]
    FF = F * n_shard
    capacity = 10 * T // (4 * experts)
    slots = experts * capacity
    highest = lax.Precision.HIGHEST
    e_index = lax.axis_index("expert")
    core = lax.axis_index("core")

    Fp = -(-F // 128) * 128
    packed = pack_columns(w_in.reshape(R, 2 * FF), n_shard, F, Fp)
    moved = lax.all_to_all(packed, SHARD, split_axis=0, concat_axis=0, tiled=True)
    w_pair = moved.reshape(n_shard * R, 2 * Fp)
    down = jnp.pad(w_down.reshape(F, D), ((0, Fp - F), (0, 0)))

    nz = lax.axis_size("z")
    small = jnp.concatenate([w_router, norm_attn[:, None], norm_ffn[:, None]], axis=1)
    small = jnp.pad(small, ((0, 0), (0, 128 - small.shape[1])))
    length_rows = jnp.broadcast_to(seq_lengths[:, :1], (8, 128))
    gather = gather_attention if n_exp == 4 else gather_plain
    full_qkv, full_output, full_small, chip_tokens, chip_lengths, all_cotangent = gather(
        nz, (w_query, w_key, w_value, w_output), small, tokens, length_rows, cotangent
    )
    full_router = full_small[:, :experts]
    gain_attn = full_small[:, experts].astype(f32)
    gain_ffn = full_small[:, experts + 1].astype(f32)

    both = (2, T)
    residual_in = tokens.astype(f32)
    inverse_in = rms_forward(residual_in, gain_attn)[1]
    normed_half = rms_forward(chip_tokens.reshape(2 * T, D).astype(f32), gain_attn)[0].astype(bf16)
    lengths = chip_lengths[:, 0, 0]
    row_index = jnp.arange(T)
    segment = (row_index[None, :] >= lengths[:, None]).astype(jnp.int32)
    positions = row_index[None, :] - lengths[:, None] * segment
    allowed = (segment[:, :, None] == segment[:, None, :]) & (
        row_index[None, None, :] <= row_index[None, :, None]
    )
    cosine, sine_table = rope_tables(positions, head_width)
    head_shape = both + (heads, head_width)
    qkv = dot32(normed_half, full_qkv)
    queries = rotate(qkv[:, :H].reshape(head_shape), cosine, sine_table).astype(bf16)
    keys_rot = rotate(qkv[:, H : 2 * H].reshape(head_shape), cosine, sine_table).astype(bf16)
    values = qkv[:, 2 * H :].astype(bf16).reshape(head_shape)
    score_scale = 1.0 / math.sqrt(head_width)
    scores = ein32("bqhd,bkhd->bhqk", queries, keys_rot) * score_scale
    scores = jnp.where(allowed[:, None], scores, masked_score)
    row_peak = jnp.max(scores, axis=-1, keepdims=True)
    log_total = row_peak + jnp.log(jnp.sum(jnp.exp(scores - row_peak), axis=-1, keepdims=True))
    attn_probs = jnp.exp(scores - log_total)
    probs_half = attn_probs.astype(bf16)
    context = ein32("bhqk,bkhd->bqhd", probs_half, values).astype(bf16)
    context_half = context.reshape(2 * T, H)
    context_full = lax.all_gather(context_half, "core", axis=1, tiled=True)
    mid_half = dot32(context_full, full_output)
    mid_own = swap_core(mid_half, 0, 1)
    residual_mid = residual_in + branch_scale * mid_own
    normed_mid, inverse_mid = rms_forward(residual_mid, gain_ffn)
    normed_mid_half = normed_mid.astype(bf16)

    logits = dot32(normed_mid_half, full_router)
    expert_ids = jnp.arange(experts)
    route_mask = (routes[:, :, None] == expert_ids[None, None, :]).astype(f32)
    chosen = jnp.sum(logits[:, None, :] * route_mask, axis=-1)
    gate_probs = jax.nn.softmax(chosen, axis=-1)
    flat_routes = routes.reshape(2 * T)
    hits = (flat_routes[:, None] == expert_ids[None, :]).astype(bf16)
    order = jnp.arange(2 * T)
    before = (order[:, None] > order[None, :]).astype(bf16)
    earlier = dot32(before, hits)
    slot_index = jnp.sum(earlier * hits.astype(f32), axis=1).astype(jnp.int32)
    target = (flat_routes * capacity + slot_index).reshape(T, 2)
    slot_ids = jnp.arange(slots)
    pick = [(target[:, k][:, None] == slot_ids[None, :]).astype(bf16) for k in range(2)]

    def bring_back(partial_rows):
        mine = lax.psum_scatter(
            partial_rows.astype(bf16), SHARD, scatter_dimension=0, tiled=True
        )
        return at_home(mine)

    def at_home(mine):
        back = lax.all_to_all(mine, "expert", split_axis=0, concat_axis=0, tiled=True)
        return [dot32(pick[k], back) for k in range(2)]

    notes = jnp.concatenate([gate_probs, target.astype(f32), jnp.zeros((T, 4), f32)], axis=1)
    notes = jnp.pad(jnp.transpose(notes), ((0, 0), (0, -T % 128)))
    spread = spread_blocks if n_exp == 4 else spread_plain
    all_normed, all_notes = spread(nz, (normed_mid_half, notes), 2)
    devices = n_shard * n_exp
    all_notes = all_notes.reshape(devices, 8, -1)[:, :, :T]
    wanted = (e_index * capacity + jnp.arange(capacity)).astype(f32)
    found = [
        all_notes[:, 2 + k, None, :] == wanted[None, :, None] for k in range(2)
    ]
    gate_rows = jnp.sum(
        jnp.where(found[0], all_notes[:, 0, None, :], 0.0)
        + jnp.where(found[1], all_notes[:, 1, None, :], 0.0),
        axis=-1,
    ).reshape(devices * capacity, 1)
    chosen_rows = (found[0] | found[1]).astype(bf16)

    def take(blocks):
        rows = ein32("spt,std->spd", chosen_rows, blocks.reshape(devices, T, D))
        return rows.astype(bf16).reshape(devices * capacity, D)

    arrived = take(all_normed)
    grad_arrived = (gate_rows * (branch_scale * take(all_cotangent).astype(f32))).astype(bf16)
    pre = dot32(arrived, w_pair)
    gate_part, up_part = pre[:, :Fp], pre[:, Fp:]
    sigmoid_gate = jax.nn.sigmoid(gate_part)
    silu_gate = gate_part * sigmoid_gate
    activated = (silu_gate * up_part).astype(bf16)
    expert_rows = bring_back(dot32(activated, down))
    upstream = cotangent.astype(f32)
    mixture_grad = branch_scale * upstream
    mixture = gate_probs[:, 0:1] * expert_rows[0] + gate_probs[:, 1:2] * expert_rows[1]
    activations = (residual_mid + branch_scale * mixture).astype(bf16)

    act_grad = dot_dims(grad_arrived, down, 1, 1)
    pre_grad = jnp.concatenate(
        [
            act_grad * up_part * sigmoid_gate * (1.0 + gate_part * (1.0 - sigmoid_gate)),
            act_grad * silu_gate,
        ],
        axis=1,
    ).astype(bf16)
    in_sum = lax.psum_scatter(
        dot_dims(pre_grad, w_pair, 1, 1).astype(bf16), SHARD, scatter_dimension=0, tiled=True
    )
    in_term = dot_dims(arrived, pre_grad, 0, 0).astype(bf16).reshape(n_shard, R, 2 * Fp)
    down_term = dot_dims(activated[:, :F], grad_arrived, 0, 0)
    in_sum, in_term, down_term = lax.optimization_barrier((in_sum, in_term, down_term))
    input_rows = at_home(in_sum)
    in_term = lax.all_to_all(in_term, SHARD, split_axis=0, concat_axis=0, tiled=True)
    grad_w_in = unpack_columns(in_term, F)
    grad_w_down = lined_up(down_term)

    gate_grad = jnp.stack(
        [jnp.sum(mixture_grad * expert_rows[k], axis=-1) for k in range(2)], axis=1
    )
    chosen_grad = gate_probs * (gate_grad - jnp.sum(gate_probs * gate_grad, axis=-1, keepdims=True))
    logit_grad = jnp.sum(chosen_grad[:, :, None] * route_mask, axis=1)
    normed_mid_grad = input_rows[0] + input_rows[1]
    normed_mid_grad = normed_mid_grad + jnp.dot(
        logit_grad, jnp.transpose(full_router.astype(f32)), precision=highest
    )
    router_grad = jnp.dot(
        jnp.transpose(normed_mid_half.astype(f32)), logit_grad, precision=highest
    )
    mid_norm_grad, gain_ffn_grad = rms_backward(
        residual_mid, inverse_mid, gain_ffn, normed_mid_grad
    )
    residual_grad = upstream + mid_norm_grad
    branch_own = (branch_scale * residual_grad).astype(bf16)

    branch_half = swap_core(branch_own, 1, 0)
    context_grad = dot_dims(branch_half, full_output, 1, 1)
    context_grad = lax.psum_scatter(
        context_grad.reshape(2 * T, 2, H).transpose(1, 0, 2).reshape(4 * T, H),
        "core",
        scatter_dimension=0,
        tiled=True,
    ).reshape(head_shape)
    row_delta = jnp.sum(context_grad * context.astype(f32), axis=-1)
    context_grad_half = context_grad.astype(bf16)
    probs_grad = ein32("bqhd,bkhd->bhqk", context_grad_half, values)
    scores_grad = (
        attn_probs * (probs_grad - jnp.transpose(row_delta, (0, 2, 1))[..., None]) * score_scale
    ).astype(bf16)
    queries_grad = ein32("bhqk,bkhd->bqhd", scores_grad, keys_rot)
    keys_grad = ein32("bhqk,bqhd->bkhd", scores_grad, queries)
    values_grad = ein32("bhqk,bqhd->bkhd", probs_half, context_grad_half)
    parts = [
        rotate(queries_grad, cosine, -sine_table).reshape(2 * T, H).astype(bf16),
        rotate(keys_grad, cosine, -sine_table).reshape(2 * T, H).astype(bf16),
        values_grad.reshape(2 * T, H).astype(bf16),
    ]
    weight_grads = [dot_dims(normed_half, p, 0, 0) for p in parts]
    weight_grads.append(dot_dims(context_full, branch_half, 0, 0))
    qkv_grad = jnp.concatenate(parts, axis=1)
    normed_in_grad = lax.psum_scatter(
        dot_dims(qkv_grad, full_qkv, 1, 1), "core", scatter_dimension=0, tiled=True
    )
    in_norm_grad, gain_attn_grad = rms_backward(residual_in, inverse_in, gain_attn, normed_in_grad)
    grad_tokens = residual_grad + in_norm_grad

    small_grad = jnp.concatenate(
        [router_grad, gain_attn_grad[:, None], gain_ffn_grad[:, None]], axis=1
    )
    weight_grads.append(jnp.pad(small_grad, ((0, 0), (0, 128 - small_grad.shape[1]))))
    reduce = reduce_attention if n_exp == 4 else reduce_plain
    sums = reduce(nz, [g.astype(bf16).reshape(nz, 4, -1, g.shape[1]) for g in weight_grads])
    small_sum = jnp.sum(sums[4].astype(f32), axis=1).reshape(R, 128)
    sums = [s.reshape(R, D).astype(f32) for s in sums[:4]]
    return (
        activations,
        grad_tokens,
        small_sum[:, experts],
        sums[0],
        sums[1],
        sums[2],
        sums[3],
        small_sum[:, experts + 1],
        small_sum[:, :experts],
        grad_w_in,
        grad_w_down,
    )


def solution(mesh):
    n_expert, n_shard = mesh.devices.shape
    chips = Mesh(mesh.devices.reshape(n_expert, n_shard // 2, 2), ("expert", "z", "core"))
    rows = P(("expert", "z", "core"), None)
    shard = P(SHARD)
    shard2 = P(SHARD, None)
    shard3 = P(SHARD, "expert", None)
    in_specs = (
        rows,
        rows,
        rows,
        shard,
        shard2,
        shard2,
        shard2,
        shard2,
        shard,
        shard2,
        shard3,
        shard3,
        rows,
    )
    out_specs = (
        rows,
        rows,
        shard,
        shard2,
        shard2,
        shard2,
        shard2,
        shard,
        shard2,
        shard3,
        shard3,
    )
    return jax.shard_map(
        on_device, mesh=chips, in_specs=in_specs, out_specs=out_specs, check_vma=False
    )
```

```python
import functools
import math

import jax
import jax.numpy as jnp
from jax import lax
from jax.experimental import pallas as pl
from jax.experimental.pallas import tpu as pltpu
from jax.sharding import Mesh, PartitionSpec as P

HEADS = 36

eps_norm = 1e-05
branch_scale = 1.4 / math.sqrt(40.0)
rope_base = 10000.0
masked_score = -1e30
bf16 = jnp.bfloat16
f32 = jnp.float32
SHARD = ("z", "core")
AHEAD = 2
ANY = pl.BlockSpec(memory_space=pl.ANY)


def place():
    e, z, c = lax.axis_index("expert"), lax.axis_index("z"), lax.axis_index("core")
    across_x = e + 1 - 2 * (e % 2)
    across_y = (e + 2) % 4
    return e, z, c, across_x, across_y


def remote(src, dst, send, recv, e, z, c):
    return pltpu.make_async_remote_copy(
        src_ref=src,
        dst_ref=dst,
        send_sem=send,
        recv_sem=recv,
        device_id=(e, z, c),
        device_id_type=pl.DeviceIdType.MESH,
    )


def greet(nz, both_cores):
    e, z, c, ex, ey = place()
    barrier = pltpu.get_barrier_semaphore()

    def hail(te, tz, tc):
        pl.semaphore_signal(
            barrier, inc=1, device_id=(te, tz, tc), device_id_type=pl.DeviceIdType.MESH
        )

    cores = (c, 1 - c) if both_cores[0] else (c,)
    plane = (c, 1 - c) if both_cores[1] else (c,)
    for t in plane:
        hail(ex, z, t)
        hail(ey, z, t)
    if both_cores[0]:
        n = 2 * nz
        for d in range(1, n):
            to = (2 * z + c + d) % n
            hail(e, to // 2, to % 2)
        pl.semaphore_wait(barrier, n - 1 + 2 * len(plane))
        return
    hail(e, z, 1 - c)
    for step in (-1, 1):

        @pl.when((z + step >= 0) & (z + step < nz))
        def _():
            for t in cores:
                hail(e, z + step, t)

    ends = jnp.where(z > 0, 1, 0) + jnp.where(z < nz - 1, 1, 0)
    pl.semaphore_wait(barrier, 1 + 2 * len(plane) + len(cores) * ends)


def cut(k, Q):
    big = (Q // 2 + 15) // 16 * 16
    return big if k % 2 == 0 else Q - big


def gather_kernel(
    nz, Q, H,
    q_ref, k_ref, v_ref, o_ref, s_ref, t_ref, l_ref, p_ref, w_ref,
    qkv_out, o_out, s_out, t_out, l_out, p_out, w_out,
    zrecv, zhop, zsend, near_recv, near_send, far_recv, far_send, own, sib_send, sib_recv,
    w_send, w_recv, w_own,
    *payload,
):
    e, z, c, ex, ey = place()
    holder, turn = e // 2, e % 2
    sources = (q_ref, k_ref, v_ref, o_ref, s_ref)
    K = len(sources)

    def src(k, half, j, count=1):
        rows = pl.ds(pl.multiple_of(j * Q, 16), count * Q)
        if k == 4:
            return sources[k].at[rows, :]
        return sources[k].at[rows, pl.ds(pl.multiple_of(half * H, 128), H)]

    def dst(k, zz, quarter, r0=0, n=Q):
        rows = pl.ds(pl.multiple_of((zz * 4 + quarter) * Q + r0, 16), n)
        if k < 3:
            return qkv_out.at[rows, pl.ds(k * H, H)]
        return (o_out if k == 3 else s_out).at[rows, :]

    greet(nz, (True, False))

    pairs = ((t_ref, t_out), (l_ref, l_out))
    extra = []
    for n, (a, b) in enumerate(pairs):
        mine = pltpu.make_async_copy(a, b.at[c], own.at[K + n])
        mine.start()
        theirs = remote(a, b.at[c], sib_send.at[K + n], sib_recv.at[K + n], e, z, 1 - c)
        theirs.start()
        extra += [mine, theirs]

    def first_hop(k, step, half):
        side = 0 if step > 0 else 1
        return remote(
            src(k, half, turn), dst(k, z, e), zhop.at[k, side, half], zrecv.at[k, side, 0],
            e, z + step, half,
        )

    for k in range(K):
        for step in (1, -1):

            @pl.when((c == holder) & (z + step >= 0) & (z + step < nz))
            def _():
                first_hop(k, step, 0).start()
                first_hop(k, step, 1).start()

    stream = payload_stream(nz, p_ref, p_out, payload, p_ref.shape[0] // 2)
    stream[0]()
    for k in range(K):
        rows = src(k, c, 0, 2), dst(k, z, 2 * c, 0, 2 * Q)
        mine = pltpu.make_async_copy(rows[0], rows[1], own.at[k])
        mine.start()
        theirs = remote(
            src(k, 1 - c, 0, 2), rows[1], sib_send.at[k], sib_recv.at[k], e, z, 1 - c
        )
        theirs.start()
        extra += [mine, theirs]

    def where(side, i):
        return z - 1 - i if side == 0 else z + 1 + i

    def onward(k, side, i):
        slab = dst(k, where(side, i), e)
        step = 1 if side == 0 else -1
        return remote(
            slab, slab, zsend.at[k, side, i], zrecv.at[k, side, i + 1], e, z + step, c
        )

    def near(k, side, i, axis):
        slab = dst(k, where(side, i), e)
        return remote(
            slab, slab, near_send.at[k, side, i, axis], near_recv.at[k, side, i, axis],
            ex if axis == 0 else ey, z, c,
        )

    def near_wait(k, side, i, axis):
        slab = dst(k, where(side, i), ex if axis == 0 else ey)
        remote(
            slab, slab, near_send.at[k, side, i, axis], near_recv.at[k, side, i, axis], ex, z, c
        ).wait_recv()

    def far(k, side, i, axis):
        a = cut(k, Q)
        if axis == 0:
            slab = dst(k, where(side, i), ex, 0, a)
        else:
            slab = dst(k, where(side, i), ey, a, Q - a)
        return remote(
            slab, slab, far_send.at[k, side, i, axis], far_recv.at[k, side, i, axis],
            ey if axis == 0 else ex, z, c,
        )

    def exists(side, i):
        zz = where(side, i)
        return (zz >= 0) & (zz < nz)

    def inside(side):
        return z < nz - 1 if side == 0 else z > 0

    def arrive(k, side, i):
        @pl.when(exists(side, i))
        def _():
            slab = dst(k, where(side, i), e)
            remote(
                slab, slab, zsend.at[k, side, i], zrecv.at[k, side, i], e, z, c
            ).wait_recv()
            if i < nz - 2:

                @pl.when(inside(side))
                def _():
                    onward(k, side, i).start()

            near(k, side, i, 0).start()
            near(k, side, i, 1).start()

    def relay(k, side, i):
        @pl.when(exists(side, i))
        def _():
            for axis in range(2):
                near_wait(k, side, i, axis)
                far(k, side, i, axis).start()

    steps = [(k, side, i) for i in range(nz - 1) for k in range(K) for side in range(2)]
    lag = 2 * K
    blocks = 2 * nz - 1
    beat = len(steps) // blocks
    p_begin, p_arrive, p_relay, p_close, p_end = stream
    for n, step in enumerate(steps):
        arrive(*step)
        if n >= lag:
            relay(*steps[n - lag])
        if n % beat == beat - 1 and n // beat < blocks:
            s = n // beat
            p_arrive(s)
            if s >= 1:
                p_relay(s - 1)
            if s >= 2:
                p_close(s - 2)
    w_begin, w_end = scatter_stream(nz, w_ref, w_out, w_send, w_recv, w_own)
    w_begin()
    for step in steps[len(steps) - lag :]:
        relay(*step)
    p_relay(blocks - 1)
    p_close(blocks - 2)
    p_close(blocks - 1)
    for s in range(blocks):
        p_end(s)
    w_end()

    for k, side, i in steps:

        @pl.when(exists(side, i))
        def _():
            if i < nz - 2:

                @pl.when(inside(side))
                def _():
                    onward(k, side, i).wait_send()

            a = cut(k, Q)
            zz, diagonal = where(side, i), (ex + 2) % 4
            for axis in range(2):
                near(k, side, i, axis).wait_send()
                far(k, side, i, axis).wait_send()
                slab = dst(k, zz, diagonal, 0, a) if axis == 0 else dst(k, zz, diagonal, a, Q - a)
                remote(
                    slab, slab, far_send.at[k, side, i, axis], far_recv.at[k, side, i, axis],
                    ex, z, c,
                ).wait_recv()

    for k in range(K):
        for step in (1, -1):

            @pl.when((c == holder) & (z + step >= 0) & (z + step < nz))
            def _():
                first_hop(k, step, 0).wait_send()
                first_hop(k, step, 1).wait_send()

    for copy in extra:
        copy.wait()


def gather_attention(nz, weights, small, tokens, lengths, block, columns):
    R, D = weights[0].shape
    Q, H = R // 2, D // 2
    K = len(weights) + 1
    dma = pltpu.SemaphoreType.DMA
    any_ = ANY
    W = small.shape[1]
    sd = jax.ShapeDtypeStruct
    outs = pl.pallas_call(
        functools.partial(gather_kernel, nz, Q, H),
        out_shape=(
            sd((nz * 4 * Q, 3 * H), bf16),
            sd((nz * 4 * Q, H), bf16),
            sd((nz * 4 * Q, W), bf16),
            sd((2,) + tokens.shape, bf16),
            sd((2,) + lengths.shape, lengths.dtype),
            sd((nz, 2, 4) + block.shape, block.dtype),
            sd(columns.shape, columns.dtype),
        ),
        in_specs=[any_] * 9,
        out_specs=(any_,) * 7,
        scratch_shapes=[
            dma((K, 2, nz - 1)),
            dma((K, 2, 2)),
            dma((K, 2, nz - 1)),
            dma((K, 2, nz - 1, 2)),
            dma((K, 2, nz - 1, 2)),
            dma((K, 2, nz - 1, 2)),
            dma((K, 2, nz - 1, 2)),
            dma((K + 2,)),
            dma((K + 2,)),
            dma((K + 2,)),
            dma((2 * nz,)),
            dma((2 * nz,)),
            dma(()),
            *payload_sems(nz),
        ],
        compiler_params=pltpu.CompilerParams(collective_id=0, has_side_effects=True),
        cost_estimate=pl.CostEstimate(
            flops=10**11, bytes_accessed=8 * D * H * 2, transcendentals=0
        ),
        name="gather_attention",
    )(*weights, small, tokens, lengths, block, columns)
    return outs


def reduce_kernel(
    nz, Q, widths,
    *refs,
):
    K = len(widths)
    parts, refs = refs[:K], refs[K:]
    outs, refs = refs[:K], refs[K:]
    (
        mine, mine_x, mine_y, from_x, from_y, via_x, via_y, from_z, result,
        load, via_send, via_recv, plain_send, plain_recv, sum_send, sum_recv,
        zsend, zrecv, fin_send, fin_recv, far_send, far_recv, own,
    ) = refs
    e, z, c, ex, ey = place()
    diagonal = (ex + 2) % 4
    holder, turn = e // 2, e % 2
    offs = [sum(widths[:k]) for k in range(K)]

    def order(i):
        code = 0
        for zz in range(nz):
            far_first = sorted(range(nz), key=lambda t: (-abs(t - zz), t))
            code += far_first[i] * nz**zz
        power = 1
        for zz in range(nz):
            power = power + (nz**zz - 1) * jnp.where(z == zz, 1, 0)
        return (code // power) % nz

    dest = [order(i) for i in range(nz)]

    def cols(k):
        return pl.ds(offs[k], widths[k])

    greet(nz, (False, True))

    def loads(k, i):
        a = cut(k, Q)
        zz = dest[i]
        out = [
            (parts[k].at[zz, e], mine.at[i, :, cols(k)]),
            (parts[k].at[zz, ex, pl.ds(a, Q - a), :], mine_x.at[i, pl.ds(0, Q - a), cols(k)]),
            (parts[k].at[zz, ey, pl.ds(0, a), :], mine_y.at[i, pl.ds(0, a), cols(k)]),
        ]
        return [pltpu.make_async_copy(s, d, load.at[k, i, n]) for n, (s, d) in enumerate(out)]

    def via(k, i, axis):
        a = cut(k, Q)
        zz = dest[i]
        if axis == 0:
            return remote(
                parts[k].at[zz, diagonal, pl.ds(0, a), :], via_x.at[i, pl.ds(0, a), cols(k)],
                via_send.at[k, i, 0], via_recv.at[k, i, 0], ex, z, c,
            )
        return remote(
            parts[k].at[zz, diagonal, pl.ds(a, Q - a), :], via_y.at[i, pl.ds(0, Q - a), cols(k)],
            via_send.at[k, i, 1], via_recv.at[k, i, 1], ey, z, c,
        )

    def plain(k, i, axis):
        a = cut(k, Q)
        zz = dest[i]
        if axis == 0:
            return remote(
                parts[k].at[zz, ex, pl.ds(0, a), :], from_x.at[i, pl.ds(0, a), cols(k)],
                plain_send.at[k, i, 0], plain_recv.at[k, i, 0], ex, z, c,
            )
        return remote(
            parts[k].at[zz, ey, pl.ds(a, Q - a), :], from_y.at[i, pl.ds(a, Q - a), cols(k)],
            plain_send.at[k, i, 1], plain_recv.at[k, i, 1], ey, z, c,
        )

    def summed(k, i, axis):
        a = cut(k, Q)
        if axis == 0:
            return remote(
                mine_x.at[i, pl.ds(0, Q - a), cols(k)], from_x.at[i, pl.ds(a, Q - a), cols(k)],
                sum_send.at[k, i, 0], sum_recv.at[k, i, 0], ex, z, c,
            )
        return remote(
            mine_y.at[i, pl.ds(0, a), cols(k)], from_y.at[i, pl.ds(0, a), cols(k)],
            sum_send.at[k, i, 1], sum_recv.at[k, i, 1], ey, z, c,
        )

    def add(target, others, n, k):
        @pl.loop(0, n // 16)
        def _(b):
            rows = pl.ds(pl.multiple_of(b * 16, 16), 16)
            acc = target[rows, cols(k)].astype(f32)
            for o in others:
                acc = acc + o[rows, cols(k)].astype(f32)
            target[rows, cols(k)] = acc.astype(bf16)

    pairs = [(k, i) for i in range(nz) for k in range(K)]
    def begin(k, i):
        via(k, i, 0).start()
        via(k, i, 1).start()
        for copy in loads(k, i):
            copy.start()
        plain(k, i, 0).start()
        plain(k, i, 1).start()

    ahead = AHEAD * K
    for k, i in pairs[:ahead]:
        begin(k, i)

    def combine(k, i):
        a = cut(k, Q)
        group = loads(k, i)
        group[1].wait()
        group[2].wait()
        via(k, i, 0).wait_recv()
        add(mine_y.at[i], [via_x.at[i]], a, k)
        summed(k, i, 1).start()
        via(k, i, 1).wait_recv()
        add(mine_x.at[i], [via_y.at[i]], Q - a, k)
        summed(k, i, 0).start()

    def zcopy(k, i):
        step = jnp.where(dest[i] > z, 1, -1)
        side = jnp.where(dest[i] > z, 0, 1)
        return remote(
            mine.at[i, :, cols(k)], from_z.at[side, dest[i], :, cols(k)],
            zsend.at[k, i], zrecv.at[k, side, dest[i]], e, z + step, c,
        )

    def zwait(k, side, zz):
        slab = from_z.at[side, zz, :, cols(k)]
        remote(slab, slab, zsend.at[k, 0], zrecv.at[k, side, zz], e, z, c).wait_recv()

    def finish(k, i):
        loads(k, i)[0].wait()
        for axis in range(2):
            plain(k, i, axis).wait_recv()
            summed(k, i, axis).wait_recv()
        add(mine.at[i], [from_x.at[i], from_y.at[i]], Q, k)
        zz = dest[i]
        if i < nz - 1:
            for side in range(2):
                going = zz > z if side == 0 else zz < z
                behind = z > 0 if side == 0 else z < nz - 1

                @pl.when(going & behind)
                def _():
                    zwait(k, side, zz)
                    add(mine.at[i], [from_z.at[side, zz]], Q, k)

            zcopy(k, i).start()

    def fin(k, axis):
        if widths[k] == widths[-1] and k == K - 1:
            land = outs[k].at[turn, c]
        else:
            land = outs[k].at[turn, :, pl.ds(pl.multiple_of(c * widths[k], 128), widths[k])]
        te = (ex, ey, e)[axis]
        return remote(
            result.at[:, cols(k)], land, fin_send.at[k, axis], fin_recv.at[k, axis, c],
            te, z, holder,
        )

    def total(k):
        last = nz - 1
        for side in range(2):
            behind = z > 0 if side == 0 else z < nz - 1

            @pl.when(behind)
            def _():
                zwait(k, side, z)
                add(mine.at[last], [from_z.at[side, z]], Q, k)

        @pl.loop(0, Q // 16)
        def _(b):
            rows = pl.ds(pl.multiple_of(b * 16, 16), 16)
            result[rows, cols(k)] = mine[last, rows, cols(k)]

        fin(k, 0).start()
        fin(k, 1).start()

        @pl.when(c == holder)
        def _():
            pltpu.make_async_copy(result.at[:, cols(k)], fin_own(k), own.at[k]).start()

        @pl.when(c != holder)
        def _():
            fin(k, 2).start()

    def fin_own(k):
        if k == K - 1:
            return outs[k].at[turn, c]
        return outs[k].at[turn, :, pl.ds(pl.multiple_of(c * widths[k], 128), widths[k])]

    lag = K
    for n, (k, i) in enumerate(pairs):
        combine(k, i)
        if n + ahead < len(pairs):
            begin(*pairs[n + ahead])
        if n >= lag:
            k2, i2 = pairs[n - lag]
            finish(k2, i2)
    for k2, i2 in pairs[len(pairs) - lag :]:
        finish(k2, i2)
    for k in range(K):
        total(k)

    def slot(k, j, half, r0=0, n=Q):
        if k == K - 1:
            return outs[k].at[j, half, pl.ds(r0, n), :]
        return outs[k].at[j, pl.ds(r0, n), pl.ds(half * widths[k], widths[k])]

    def got(k, axis, half):
        j = (ex if axis == 0 else ey) % 2
        view = slot(k, j, half)
        return remote(
            view, view, fin_send.at[k, axis], fin_recv.at[k, axis, half], e, z, c
        )

    def passed(k, axis, half, quarter):
        a = cut(k, Q)
        j = quarter % 2
        view = slot(k, j, half, 0, a) if axis == 0 else slot(k, j, half, a, Q - a)
        return remote(
            view, view, far_send.at[k, half], far_recv.at[k, axis, half],
            ey if axis == 0 else ex, z, c,
        )

    for k in range(K):
        for axis in range(2):

            @pl.when((c == holder) if axis == 0 else (c != holder))
            def _():
                for half in range(2):
                    got(k, axis, half).wait_recv()
                    passed(k, axis, half, ex if axis == 0 else ey).start()

    for k in range(K):
        for axis in range(2):

            @pl.when((c == holder) if axis == 0 else (c != holder))
            def _():
                for half in range(2):
                    passed(k, axis, half, ex if axis == 0 else ey).wait_send()

        @pl.when(c != holder)
        def _():
            for half in range(2):
                passed(k, 0, half, diagonal).wait_recv()
                passed(k, 1, half, diagonal).wait_recv()
            fin(k, 2).wait_send()

        @pl.when(c == holder)
        def _():
            pltpu.make_async_copy(result.at[:, cols(k)], fin_own(k), own.at[k]).wait()
            other = slot_of(outs, k, K, turn, 1 - c, widths)
            remote(
                other, other, fin_send.at[k, 2], fin_recv.at[k, 2, 1 - c], e, z, c
            ).wait_recv()

        fin(k, 0).wait_send()
        fin(k, 1).wait_send()
        for i in range(nz):
            for axis in range(2):
                via(k, i, axis).wait_send()
                plain(k, i, axis).wait_send()
                summed(k, i, axis).wait_send()
            if i < nz - 1:
                zcopy(k, i).wait_send()


def slot_of(outs, k, K, j, half, widths):
    if k == K - 1:
        return outs[k].at[j, half]
    return outs[k].at[j, :, pl.ds(pl.multiple_of(half * widths[k], 128), widths[k])]


def reduce_attention(nz, parts):
    Q = parts[0].shape[2]
    widths = tuple(p.shape[3] for p in parts)
    W, K = sum(widths), len(parts)
    big = max(cut(0, Q), cut(1, Q))
    dma = pltpu.SemaphoreType.DMA
    sd = jax.ShapeDtypeStruct
    vm = pltpu.VMEM
    out_shape = tuple(sd((2, Q, 2 * w), bf16) for w in widths[:-1]) + (
        sd((2, 2, Q, widths[-1]), bf16),
    )
    return pl.pallas_call(
        functools.partial(reduce_kernel, nz, Q, widths),
        out_shape=out_shape,
        in_specs=[ANY] * K,
        out_specs=(ANY,) * K,
        scratch_shapes=[
            vm((nz, Q, W), bf16),
            vm((nz, big, W), bf16),
            vm((nz, big, W), bf16),
            vm((nz, Q, W), bf16),
            vm((nz, Q, W), bf16),
            vm((nz, big, W), bf16),
            vm((nz, big, W), bf16),
            vm((2, nz, Q, W), bf16),
            vm((Q, W), bf16),
            dma((K, nz, 3)),
            dma((K, nz, 2)),
            dma((K, nz, 2)),
            dma((K, nz, 2)),
            dma((K, nz, 2)),
            dma((K, nz, 2)),
            dma((K, nz, 2)),
            dma((K, nz)),
            dma((K, 2, nz)),
            dma((K, 3)),
            dma((K, 3, 2)),
            dma((K, 2)),
            dma((K, 2, 2)),
            dma((K,)),
        ],
        compiler_params=pltpu.CompilerParams(
            collective_id=1, has_side_effects=True, vmem_limit_bytes=60 << 20
        ),
        cost_estimate=pl.CostEstimate(
            flops=10**6, bytes_accessed=10**6, transcendentals=0
        ),
        name="reduce_attention",
    )(*parts)


def payload_stream(nz, ref, out, sems, split):
    zrecv, zsend, near_recv, near_send, far_recv, far_send, sib_recv, sib_send, own = sems
    e, z, c, ex, ey = place()
    diagonal = (ex + 2) % 4
    T = ref.shape[0]
    S = 2 * nz - 1

    def split_step(s):
        return (s - 1) % 2, (s - 1) // 2

    def where(s):
        if s == 0:
            return z
        side, i = split_step(s)
        return z - 1 - i if side == 0 else z + 1 + i

    def exists(s):
        if s == 0:
            return z >= 0
        zz = where(s)
        return (zz >= 0) & (zz < nz)

    def slab(s, quarter, r0=0, n=T):
        return out.at[where(s), c, quarter, pl.ds(r0, n), :]

    def first(step):
        side = 0 if step > 0 else 1
        return remote(ref, slab(0, e), zsend.at[side, nz - 1], zrecv.at[side, 0], e, z + step, c)

    def onward(s):
        side, i = split_step(s)
        step = 1 if side == 0 else -1
        return remote(
            slab(s, e), slab(s, e), zsend.at[side, i], zrecv.at[side, i + 1], e, z + step, c
        )

    def near(s, axis):
        source = ref if s == 0 else slab(s, e)
        return remote(
            source, slab(s, e), near_send.at[s, axis], near_recv.at[s, axis],
            ex if axis == 0 else ey, z, c,
        )

    def near_wait(s, axis):
        view = slab(s, ex if axis == 0 else ey)
        remote(view, view, near_send.at[s, axis], near_recv.at[s, axis], ex, z, c).wait_recv()

    axes = range(2) if split else range(1)

    def far_view(s, quarter, axis):
        if not split:
            return slab(s, quarter)
        return slab(s, quarter, 0, split) if axis == 0 else slab(s, quarter, split, T - split)

    def far(s, axis):
        view = far_view(s, ex if axis == 0 else ey, axis)
        return remote(
            view, view, far_send.at[s, axis], far_recv.at[s, axis],
            ey if axis == 0 else ex, z, c,
        )

    def far_wait(s, axis):
        view = far_view(s, diagonal, axis)
        remote(view, view, far_send.at[s, axis], far_recv.at[s, axis], ex, z, c).wait_recv()

    def beside(s, n):
        quarter = (e, ex, ey, diagonal)[n]
        source = ref if s == 0 and n == 0 else slab(s, quarter)
        return remote(
            source, slab(s, quarter), sib_send.at[s, n], sib_recv.at[s, n], e, z, 1 - c
        )

    def beside_wait(s, n):
        view = out.at[where(s), 1 - c, (e, ex, ey, diagonal)[n]]
        remote(view, view, sib_send.at[s, n], sib_recv.at[s, n], e, z, c).wait_recv()

    def inside(side):
        return z < nz - 1 if side == 0 else z > 0

    def begin():
        for step in (1, -1):

            @pl.when((z + step >= 0) & (z + step < nz))
            def _():
                first(step).start()

        near(0, 0).start()
        near(0, 1).start()
        beside(0, 0).start()
        pltpu.make_async_copy(ref, slab(0, e), own).start()

    def arrive(s):
        if s == 0:
            return

        @pl.when(exists(s))
        def _():
            side, i = split_step(s)
            remote(
                slab(s, e), slab(s, e), zsend.at[side, i], zrecv.at[side, i], e, z, c
            ).wait_recv()
            if i < nz - 2:

                @pl.when(inside(side))
                def _():
                    onward(s).start()

            near(s, 0).start()
            near(s, 1).start()
            beside(s, 0).start()

    def relay(s):
        @pl.when(exists(s))
        def _():
            near_wait(s, 0)
            far(s, 0).start()
            beside(s, 1).start()
            near_wait(s, 1)
            if split:
                far(s, 1).start()
            beside(s, 2).start()

    def close(s):
        @pl.when(exists(s))
        def _():
            for axis in axes:
                far_wait(s, axis)
            beside(s, 3).start()

    def end(s):
        @pl.when(exists(s))
        def _():
            for axis in range(2):
                near(s, axis).wait_send()
            for axis in axes:
                far(s, axis).wait_send()
            for n in range(4):
                beside(s, n).wait_send()
                beside_wait(s, n)
            if s > 0 and split_step(s)[1] < nz - 2:

                @pl.when(inside(split_step(s)[0]))
                def _():
                    onward(s).wait_send()

        if s == 0:
            for step in (1, -1):

                @pl.when((z + step >= 0) & (z + step < nz))
                def _():
                    first(step).wait_send()

            pltpu.make_async_copy(ref, slab(0, e), own).wait()

    return begin, arrive, relay, close, end


def payload_sems(nz):
    dma = pltpu.SemaphoreType.DMA
    S = 2 * nz - 1
    return [
        dma((2, nz)), dma((2, nz)), dma((S, 2)), dma((S, 2)), dma((S, 2)), dma((S, 2)),
        dma((S, 4)), dma((S, 4)), dma(()),
    ]


def spread_kernel(nz, splits, *refs):
    n = len(splits)
    ins, outs, sems = refs[:n], refs[n : 2 * n], refs[2 * n :]
    greet(nz, (False, False))
    streams = [
        payload_stream(nz, ins[i], outs[i], sems[9 * i : 9 * i + 9], splits[i]) for i in range(n)
    ]
    for t in streams:
        t[0]()
    S = 2 * nz - 1
    for s in range(S):
        for t in streams:
            t[1](s)
        if s >= 1:
            for t in streams:
                t[2](s - 1)
        if s >= 2:
            for t in streams:
                t[3](s - 2)
    for t in streams:
        t[2](S - 1)
    for s in (S - 2, S - 1):
        for t in streams:
            t[3](s)
    for s in range(S):
        for t in streams:
            t[4](s)


def spread_blocks(nz, blocks, collective):
    sd = jax.ShapeDtypeStruct
    splits = tuple(b.shape[0] // 2 if b.shape[0] % 32 == 0 else 0 for b in blocks)
    return pl.pallas_call(
        functools.partial(spread_kernel, nz, splits),
        out_shape=tuple(sd((nz, 2, 4) + b.shape, b.dtype) for b in blocks),
        in_specs=[ANY] * len(blocks),
        out_specs=(ANY,) * len(blocks),
        scratch_shapes=[s for _ in blocks for s in payload_sems(nz)],
        compiler_params=pltpu.CompilerParams(collective_id=collective, has_side_effects=True),
        cost_estimate=pl.CostEstimate(
            flops=10**6, bytes_accessed=10**6, transcendentals=0
        ),
        name="spread_blocks",
    )(*blocks)


def scatter_stream(nz, ref, out, send, recv, own):
    e, z, c, ex, ey = place()
    n = 2 * nz
    me = 2 * z + c

    def copy(d):
        to = (me + d) % n
        return remote(ref.at[to], out.at[me], send.at[d], recv.at[d], e, to // 2, to % 2)

    def kept():
        return pltpu.make_async_copy(ref.at[me], out.at[me], own)

    def begin():
        kept().start()
        for d in range(1, n):
            copy(d).start()

    def end():
        kept().wait()
        for d in range(1, n):
            view = out.at[(me + n - d) % n]
            remote(view, view, send.at[d], recv.at[d], e, z, c).wait_recv()
            copy(d).wait_send()

    return begin, end


def line_order(nz, z):
    def order(i):
        code = 0
        for zz in range(nz):
            far_first = sorted(range(nz), key=lambda t: (-abs(t - zz), t))
            code += far_first[i] * nz**zz
        power = 1
        for zz in range(nz):
            power = power + (nz**zz - 1) * jnp.where(z == zz, 1, 0)
        return (code // power) % nz

    return [order(i) for i in range(nz)]


def collect_kernel(
    nz, cap,
    rows_ref, notes_ref, dots_ref,
    out_ref, dots_out,
    dots, notes, mine, theirs, block, from_x, from_y, via_x, via_y, from_z,
    note_sem, load, sib_send, sib_recv, via_send, via_recv, plain_send, plain_recv,
    sum_send, sum_recv, zsend, zrecv, dot_send, dot_recv, dot_own,
):
    e, z, c, ex, ey = place()
    diagonal = (ex + 2) % 4
    T, D = out_ref.shape
    h = T // 2
    dest = line_order(nz, z)
    who = (diagonal, ex, ey, e)

    def others():
        for d in range(1, 8 * nz):
            to = ((e * nz + z) * 2 + c + d) % (8 * nz)
            yield d, to // (2 * nz), to // 2 % nz, to % 2

    barrier = pltpu.get_barrier_semaphore()
    for _, te, tz, tc in others():
        pl.semaphore_signal(
            barrier, inc=1, device_id=(te, tz, tc), device_id_type=pl.DeviceIdType.MESH
        )
    pl.semaphore_wait(barrier, 8 * nz - 1)

    def dot(d, te, tz, tc):
        return remote(
            dots_ref.at[tz, tc, te], dots.at[d], dot_send.at[d], dot_recv.at[d], te, tz, tc
        )

    dot_kept = pltpu.make_async_copy(dots_ref.at[z, c, e], dots.at[0], dot_own)
    dot_kept.start()
    for d, te, tz, tc in others():
        dot(d, te, tz, tc).start()

    note_copy = pltpu.make_async_copy(notes_ref, notes, note_sem)
    note_copy.start()

    def fetch(i, q):
        return pltpu.make_async_copy(
            rows_ref.at[dest[i], c, who[q]], mine.at[i, q], load.at[i, q]
        )

    def hand(i, q):
        return remote(
            rows_ref.at[dest[i], 1 - c, who[q]], theirs.at[i, q],
            sib_send.at[i, q], sib_recv.at[i, q], e, z, 1 - c,
        )

    for i in range(nz):
        for q in range(4):
            hand(i, q).start()
            fetch(i, q).start()
    note_copy.wait()

    def open_out(i, q):
        fetch(i, q).wait()
        hand(i, q).wait_recv()
        places = (lax.broadcasted_iota(jnp.int32, (cap, T), 0) + e * cap).astype(f32)
        note = notes[dest[i], c, who[q]]
        pick = ((note[2:3, :] == places) | (note[3:4, :] == places)).astype(bf16)
        wide = 768 if D % 768 == 0 else 128

        @pl.loop(0, D // wide)
        def _(b):
            cols = pl.ds(pl.multiple_of(b * wide, 128), wide)
            both = mine[i, q, :, cols].astype(f32) + theirs[i, q, :, cols].astype(f32)
            block[i, q, :, cols] = lax.dot_general(
                pick, both.astype(bf16), (((0,), (0,)), ((), ())), preferred_element_type=f32
            ).astype(bf16)

    def via(i, axis):
        if axis == 0:
            return remote(
                block.at[i, 0, pl.ds(0, h), :], via_x.at[i],
                via_send.at[i, 0], via_recv.at[i, 0], ex, z, c,
            )
        return remote(
            block.at[i, 0, pl.ds(h, h), :], via_y.at[i],
            via_send.at[i, 1], via_recv.at[i, 1], ey, z, c,
        )

    def plain(i, axis):
        if axis == 0:
            return remote(
                block.at[i, 1, pl.ds(0, h), :], from_x.at[i, pl.ds(0, h), :],
                plain_send.at[i, 0], plain_recv.at[i, 0], ex, z, c,
            )
        return remote(
            block.at[i, 2, pl.ds(h, h), :], from_y.at[i, pl.ds(h, h), :],
            plain_send.at[i, 1], plain_recv.at[i, 1], ey, z, c,
        )

    def summed(i, axis):
        if axis == 0:
            return remote(
                block.at[i, 1, pl.ds(h, h), :], from_x.at[i, pl.ds(h, h), :],
                sum_send.at[i, 0], sum_recv.at[i, 0], ex, z, c,
            )
        return remote(
            block.at[i, 2, pl.ds(0, h), :], from_y.at[i, pl.ds(0, h), :],
            sum_send.at[i, 1], sum_recv.at[i, 1], ey, z, c,
        )

    def add(target, others, n):
        @pl.loop(0, n // 16)
        def _(b):
            rows = pl.ds(pl.multiple_of(b * 16, 16), 16)
            acc = target[rows, :].astype(f32)
            for o in others:
                acc = acc + o[rows, :].astype(f32)
            target[rows, :] = acc.astype(target.dtype)

    def start(i):
        open_out(i, 0)
        via(i, 0).start()
        via(i, 1).start()
        open_out(i, 1)
        plain(i, 0).start()
        open_out(i, 2)
        plain(i, 1).start()
        open_out(i, 3)

    def combine(i):
        via(i, 0).wait_recv()
        add(block.at[i, 2, pl.ds(0, h), :], [via_x.at[i]], h)
        summed(i, 1).start()
        via(i, 1).wait_recv()
        add(block.at[i, 1, pl.ds(h, h), :], [via_y.at[i]], h)
        summed(i, 0).start()

    def zcopy(i):
        step = jnp.where(dest[i] > z, 1, -1)
        side = jnp.where(dest[i] > z, 0, 1)
        return remote(
            block.at[i, 3], from_z.at[side, dest[i]],
            zsend.at[i], zrecv.at[side, dest[i]], e, z + step, c,
        )

    def zwait(side, zz):
        slab = from_z.at[side, zz]
        remote(slab, slab, zsend.at[0], zrecv.at[side, zz], e, z, c).wait_recv()

    def finish(i):
        for axis in range(2):
            plain(i, axis).wait_recv()
            summed(i, axis).wait_recv()
        zz = dest[i]
        if i < nz - 1:
            add(block.at[i, 3], [from_x.at[i], from_y.at[i]], T)
            for side in range(2):
                going = zz > z if side == 0 else zz < z
                behind = z > 0 if side == 0 else z < nz - 1

                @pl.when(going & behind)
                def _():
                    zwait(side, zz)
                    add(block.at[i, 3], [from_z.at[side, zz]], T)

            zcopy(i).start()
            return

        @pl.loop(0, T // 16)
        def _(b):
            rows = pl.ds(pl.multiple_of(b * 16, 16), 16)
            acc = block[i, 3, rows, :].astype(f32) + from_x[i, rows, :].astype(f32)
            out_ref[rows, :] = acc + from_y[i, rows, :].astype(f32)

        for side in range(2):

            @pl.when(z > 0 if side == 0 else z < nz - 1)
            def _():
                zwait(side, z)
                add(out_ref, [from_z.at[side, z]], T)

    for i in range(nz):
        start(i)
        if i >= 1:
            combine(i - 1)
        if i >= 2:
            finish(i - 2)
    combine(nz - 1)
    if nz >= 2:
        finish(nz - 2)
    finish(nz - 1)

    dot_kept.wait()
    for d, te, tz, tc in others():
        dot(d, te, tz, tc).wait_recv()
        dot(d, te, tz, tc).wait_send()
    dots_out[...] = jnp.sum(dots[...], axis=0)

    for i in range(nz):
        for q in range(4):
            hand(i, q).wait_send()
        for axis in range(2):
            via(i, axis).wait_send()
            plain(i, axis).wait_send()
            summed(i, axis).wait_send()
        if i < nz - 1:
            zcopy(i).wait_send()


def collect_rows(nz, rows, notes, dots, T):
    cap, D = rows.shape[3:]
    dma = pltpu.SemaphoreType.DMA
    vm = pltpu.VMEM
    return pl.pallas_call(
        functools.partial(collect_kernel, nz, cap),
        out_shape=(
            jax.ShapeDtypeStruct((T, D), f32),
            jax.ShapeDtypeStruct(dots.shape[3:], f32),
        ),
        in_specs=[ANY] * 3,
        out_specs=(pl.BlockSpec(memory_space=pltpu.VMEM),) * 2,
        scratch_shapes=[
            vm((8 * nz,) + dots.shape[3:], f32),
            vm(notes.shape, f32),
            vm((nz, 4, cap, D), bf16),
            vm((nz, 4, cap, D), bf16),
            vm((nz, 4, T, D), bf16),
            vm((nz, T, D), bf16),
            vm((nz, T, D), bf16),
            vm((nz, T // 2, D), bf16),
            vm((nz, T // 2, D), bf16),
            vm((2, nz, T, D), bf16),
            dma(()),
            dma((nz, 4)),
            dma((nz, 4)),
            dma((nz, 4)),
            dma((nz, 2)),
            dma((nz, 2)),
            dma((nz, 2)),
            dma((nz, 2)),
            dma((nz, 2)),
            dma((nz, 2)),
            dma((nz,)),
            dma((2, nz)),
            dma((8 * nz,)),
            dma((8 * nz,)),
            dma(()),
        ],
        compiler_params=pltpu.CompilerParams(
            collective_id=3, has_side_effects=True, vmem_limit_bytes=56 << 20
        ),
        cost_estimate=pl.CostEstimate(
            flops=5 * 10**10, bytes_accessed=2 * rows.size, transcendentals=0
        ),
        name="collect_rows",
    )(rows, notes, dots)


def pack_kernel(n, F, Fp, x_ref, *o_refs):
    half = n * F
    rows = x_ref.shape[0]
    for i in range(n):
        for part in range(2):
            cols = x_ref[:, part * half + i * F : part * half + (i + 1) * F]
            if Fp > F:
                cols = jnp.concatenate([cols, jnp.zeros((rows, Fp - F), cols.dtype)], axis=1)
            o_refs[part][i] = cols


def pack_columns(w, n, F, Fp):
    rows = w.shape[0]
    block = 16
    return pl.pallas_call(
        functools.partial(pack_kernel, n, F, Fp),
        grid=(rows // block,),
        in_specs=[pl.BlockSpec((block, w.shape[1]), lambda i: (i, 0))],
        out_specs=(pl.BlockSpec((n, block, Fp), lambda i: (0, i, 0)),) * 2,
        out_shape=(jax.ShapeDtypeStruct((n, rows, Fp), w.dtype),) * 2,
        name="pack_columns",
    )(w)


def unpack_kernel(n, F, Fp, x_ref, o_ref, line):
    half = n * F
    rows = line.shape[0]
    for i in range(n):
        for part in range(2):
            cols = x_ref[i, :, part * Fp : part * Fp + F].astype(f32)
            line[:, part * half + i * F : part * half + (i + 1) * F] = cols
    tiles = 2 * half // 128
    for j in range(tiles):
        o_ref[pl.ds(j, rows, stride=tiles), :] = line[:, j * 128 : (j + 1) * 128]


def unpack_columns(x, F):
    n, rows, Fp2 = x.shape
    block = 16
    width = 2 * n * F
    tiles = width // 128
    flat = pl.pallas_call(
        functools.partial(unpack_kernel, n, F, Fp2 // 2),
        grid=(rows // block,),
        in_specs=[pl.BlockSpec((n, block, Fp2), lambda i: (0, i, 0))],
        out_specs=pl.BlockSpec((block * tiles, 128), lambda i: (i, 0)),
        out_shape=jax.ShapeDtypeStruct((rows * tiles, 128), f32),
        scratch_shapes=[pltpu.VMEM((block, width), f32)],
        name="unpack_columns",
    )(x)
    return flat.reshape(rows, 1, width)


def line_kernel(x_ref, o_ref):
    rows, width = x_ref.shape
    tiles = width // 128
    for j in range(tiles):
        o_ref[pl.ds(j, rows, stride=tiles), :] = x_ref[:, j * 128 : (j + 1) * 128]


def lined_up(x):
    rows, width = x.shape
    tiles = width // 128
    block = 80 if rows % 80 == 0 else 8
    flat = pl.pallas_call(
        line_kernel,
        grid=(rows // block,),
        in_specs=[pl.BlockSpec((block, width), lambda i: (i, 0))],
        out_specs=pl.BlockSpec((block * tiles, 128), lambda i: (i, 0)),
        out_shape=jax.ShapeDtypeStruct((rows * tiles, 128), x.dtype),
        name="lined_up",
    )(x)
    return flat.reshape(rows, 1, width)


def gather_plain(nz, weights, small, tokens, lengths, block, columns):
    core, H = lax.axis_index("core"), weights[0].shape[1] // 2
    full = [
        lax.all_gather(swap_core(w, 1, 0), "z", axis=0, tiled=True) for w in weights
    ]
    return (
        jnp.concatenate(full[:3], axis=1),
        full[3],
        lax.all_gather(small, SHARD, axis=0, tiled=True),
        lax.all_gather(tokens, "core", axis=0),
        lax.all_gather(lengths, "core", axis=0),
        spread_plain(nz, (block,), 0)[0],
        lax.all_to_all(columns, SHARD, split_axis=0, concat_axis=0, tiled=True),
    )


def spread_plain(nz, blocks, collective):
    out = []
    for block in blocks:
        for axis in ("expert", "core", "z"):
            block = lax.all_gather(block, axis, axis=0)
        out.append(block)
    return out


def collect_plain(nz, rows, notes, dots, T):
    n_exp, cap, D = rows.shape[2:]
    places = (lax.axis_index("expert") * cap + jnp.arange(cap)).astype(f32)
    notes = notes[..., :T]
    pick = (notes[..., 2, None, :] == places[:, None]) | (notes[..., 3, None, :] == places[:, None])
    part = jnp.einsum(
        "zceps,zcepd->zcesd", pick.astype(bf16), rows, preferred_element_type=f32
    ).astype(bf16)
    part = part.transpose(2, 0, 1, 3, 4).reshape(n_exp * nz * 2 * T, D)
    part = lax.psum_scatter(part, "expert", scatter_dimension=0, tiled=True)
    part = lax.psum_scatter(part, SHARD, scatter_dimension=0, tiled=True).astype(f32)
    z, core, e = lax.axis_index("z"), lax.axis_index("core"), lax.axis_index("expert")
    return part, lax.psum(dots, ("expert",) + SHARD)[z, core, e]


def reduce_plain(nz, parts):
    n_exp = lax.axis_size("expert")
    out = []
    for k, part in enumerate(parts):
        Q, w = part.shape[2:]
        mine = lax.psum_scatter(part.reshape(nz * 4 * Q, w), "z", scatter_dimension=0, tiled=True)
        mine = lax.psum(mine, "expert")
        if k < len(parts) - 1:
            out.append(swap_core(mine, 0, 1).reshape(2, Q, 2 * w))
        else:
            both = lax.all_to_all(
                mine.reshape(2, 2 * Q, w), "core", split_axis=0, concat_axis=0, tiled=True
            )
            out.append(both.reshape(2, 2, Q, w).transpose(1, 0, 2, 3))
    return out


def rope_tables(positions, head_width):
    half_width = head_width // 2
    exponents = jnp.arange(half_width).astype(f32) * 2.0 / head_width
    frequency = rope_base ** (-exponents)
    angles = positions.astype(f32)[..., None] * frequency
    return (jnp.cos(angles), jnp.sin(angles))


def rotate(values, cosine, sine_table):
    half_width = values.shape[-1] // 2
    leading = values[..., :half_width]
    trailing = values[..., half_width:]
    cos_rows = cosine[:, :, None, :]
    sin_rows = sine_table[:, :, None, :]
    return jnp.concatenate(
        [leading * cos_rows - trailing * sin_rows, trailing * cos_rows + leading * sin_rows],
        axis=-1,
    )


def rms_forward(values, norm_gain):
    inverse = lax.rsqrt(jnp.mean(values * values, axis=-1, keepdims=True) + eps_norm)
    return (values * inverse * norm_gain, inverse)


def rms_backward(values, inverse, norm_gain, upstream):
    weighted = upstream * norm_gain
    gain_grad = jnp.sum(upstream * values * inverse, axis=0)
    inner_mean = jnp.mean(weighted * values, axis=-1, keepdims=True)
    return (inverse * weighted - values * inverse * inverse * inverse * inner_mean, gain_grad)


def dot32(a, b):
    return jnp.dot(a, b, preferred_element_type=f32)


def dot_dims(a, b, da, db):
    return lax.dot_general(a, b, (((da,), (db,)), ((), ())), preferred_element_type=f32)


def ein32(spec, a, b):
    return jnp.einsum(spec, a, b, preferred_element_type=f32)


def swap_core(x, split, concat):
    return lax.all_to_all(x, "core", split_axis=split, concat_axis=concat, tiled=True)


def on_device(
    tokens,
    seq_lengths,
    routes,
    norm_attn,
    w_query,
    w_key,
    w_value,
    w_output,
    norm_ffn,
    w_router,
    w_in,
    w_down,
    cotangent,
):
    T, D = tokens.shape
    R = w_query.shape[0]
    H = D // 2
    head_width = D // HEADS
    heads = HEADS // 2
    n_exp = lax.axis_size("expert")
    n_shard = lax.axis_size("z") * lax.axis_size("core")
    experts = w_router.shape[1]
    F = w_down.shape[0]
    FF = F * n_shard
    capacity = 10 * T // (4 * experts)
    slots = experts * capacity
    highest = lax.Precision.HIGHEST
    e_index = lax.axis_index("expert")
    core = lax.axis_index("core")

    Fp = -(-F // 128) * 128
    packed_gate, packed_up = pack_columns(w_in.reshape(R, 2 * FF), n_shard, F, Fp)
    moved_up = lax.all_to_all(packed_up, SHARD, split_axis=0, concat_axis=0, tiled=True)
    down = jnp.pad(w_down.reshape(F, D), ((0, Fp - F), (0, 0)))

    nz = lax.axis_size("z")
    small = jnp.concatenate([w_router, norm_attn[:, None], norm_ffn[:, None]], axis=1)
    small = jnp.pad(small, ((0, 0), (0, 128 - small.shape[1])))
    length_rows = jnp.broadcast_to(seq_lengths[:, :1], (8, 128))
    gather = gather_attention if n_exp == 4 else gather_plain
    full_qkv, full_output, full_small, chip_tokens, chip_lengths, all_cotangent, moved_gate = gather(
        nz, (w_query, w_key, w_value, w_output), small, tokens, length_rows, cotangent, packed_gate
    )
    w_gate, w_up = moved_gate.reshape(n_shard * R, Fp), moved_up.reshape(n_shard * R, Fp)
    full_router = full_small[:, :experts]
    gain_attn = full_small[:, experts].astype(f32)
    gain_ffn = full_small[:, experts + 1].astype(f32)

    both = (2, T)
    residual_in = tokens.astype(f32)
    inverse_in = rms_forward(residual_in, gain_attn)[1]
    normed_half = rms_forward(chip_tokens.reshape(2 * T, D).astype(f32), gain_attn)[0].astype(bf16)
    lengths = chip_lengths[:, 0, 0]
    row_index = jnp.arange(T)
    segment = (row_index[None, :] >= lengths[:, None]).astype(jnp.int32)
    positions = row_index[None, :] - lengths[:, None] * segment
    allowed = (segment[:, :, None] == segment[:, None, :]) & (
        row_index[None, None, :] <= row_index[None, :, None]
    )
    cosine, sine_table = rope_tables(positions, head_width)
    head_shape = both + (heads, head_width)
    qkv = dot32(normed_half, full_qkv)
    queries = rotate(qkv[:, :H].reshape(head_shape), cosine, sine_table).astype(bf16)
    keys_rot = rotate(qkv[:, H : 2 * H].reshape(head_shape), cosine, sine_table).astype(bf16)
    values = qkv[:, 2 * H :].astype(bf16).reshape(head_shape)
    score_scale = 1.0 / math.sqrt(head_width)
    scores = ein32("bqhd,bkhd->bhqk", queries, keys_rot) * score_scale
    scores = jnp.where(allowed[:, None], scores, masked_score)
    row_peak = jnp.max(scores, axis=-1, keepdims=True)
    log_total = row_peak + jnp.log(jnp.sum(jnp.exp(scores - row_peak), axis=-1, keepdims=True))
    attn_probs = jnp.exp(scores - log_total)
    probs_half = attn_probs.astype(bf16)
    context = ein32("bhqk,bkhd->bqhd", probs_half, values).astype(bf16)
    context_half = context.reshape(2 * T, H)
    core = lax.axis_index("core")

    def beside(x):
        return lax.ppermute(x, "core", [(0, 1), (1, 0)])

    def side_by_side(mine, theirs, axis):
        first = jnp.where(core == 0, mine, theirs)
        return jnp.concatenate([first, jnp.where(core == 0, theirs, mine)], axis=axis)

    def halves(x, axis):
        size = x.shape[axis] // 2
        mine = lax.dynamic_slice_in_dim(x, core * size, size, axis)
        return mine, lax.dynamic_slice_in_dim(x, (1 - core) * size, size, axis)

    context_full = side_by_side(context_half, beside(context_half), 1)
    mid_half = dot32(context_full, full_output)
    mid_mine, mid_other = halves(mid_half, 0)
    mid_own = side_by_side(mid_mine, beside(mid_other), 1)
    residual_mid = residual_in + branch_scale * mid_own
    normed_mid, inverse_mid = rms_forward(residual_mid, gain_ffn)
    normed_mid_half = normed_mid.astype(bf16)

    logits = dot32(normed_mid_half, full_router)
    expert_ids = jnp.arange(experts)
    route_mask = (routes[:, :, None] == expert_ids[None, None, :]).astype(f32)
    chosen = jnp.sum(logits[:, None, :] * route_mask, axis=-1)
    gate_probs = jax.nn.softmax(chosen, axis=-1)
    flat_routes = routes.reshape(2 * T)
    hits = (flat_routes[:, None] == expert_ids[None, :]).astype(bf16)
    order = jnp.arange(2 * T)
    before = (order[:, None] > order[None, :]).astype(bf16)
    earlier = dot32(before, hits)
    slot_index = jnp.sum(earlier * hits.astype(f32), axis=1).astype(jnp.int32)
    target = (flat_routes * capacity + slot_index).reshape(T, 2)
    slot_ids = jnp.arange(slots)
    pick = [(target[:, k][:, None] == slot_ids[None, :]).astype(bf16) for k in range(2)]

    def bring_back(partial_rows):
        mine = lax.psum_scatter(
            partial_rows.astype(bf16), SHARD, scatter_dimension=0, tiled=True
        )
        return at_home(mine)

    def at_home(mine):
        back = lax.all_to_all(mine, "expert", split_axis=0, concat_axis=0, tiled=True)
        return [dot32(pick[k], back) for k in range(2)]

    notes = jnp.concatenate([gate_probs, target.astype(f32), jnp.zeros((T, 4), f32)], axis=1)
    notes = jnp.pad(jnp.transpose(notes), ((0, 0), (0, -T % 128)))
    spread = spread_blocks if n_exp == 4 else spread_plain
    all_normed, all_notes = spread(nz, (normed_mid_half, notes), 2)
    devices = n_shard * n_exp
    flat_notes = all_notes.reshape(devices, 8, -1)[:, :, :T]
    wanted = (e_index * capacity + jnp.arange(capacity)).astype(f32)
    found = [
        flat_notes[:, 2 + k, None, :] == wanted[None, :, None] for k in range(2)
    ]
    gate_rows = jnp.sum(
        jnp.where(found[0], flat_notes[:, 0, None, :], 0.0)
        + jnp.where(found[1], flat_notes[:, 1, None, :], 0.0),
        axis=-1,
    ).reshape(devices * capacity, 1)
    chosen_rows = (found[0] | found[1]).astype(bf16)

    def take(blocks):
        rows = ein32("spt,std->spd", chosen_rows, blocks.reshape(devices, T, D))
        return rows.reshape(devices * capacity, D)

    arrived = take(all_normed).astype(bf16)
    cotangent_rows = take(all_cotangent)
    grad_scale = gate_rows * branch_scale
    grad_arrived = (gate_rows * (branch_scale * cotangent_rows)).astype(bf16)
    gate_part, up_part = dot32(arrived, w_gate), dot32(arrived, w_up)
    sigmoid_gate = jax.nn.sigmoid(gate_part)
    silu_gate = gate_part * sigmoid_gate
    activated = (silu_gate * up_part).astype(bf16)
    expert_rows = bring_back(dot32(activated, down))
    upstream = cotangent.astype(f32)
    mixture = gate_probs[:, 0:1] * expert_rows[0] + gate_probs[:, 1:2] * expert_rows[1]
    activations = (residual_mid + branch_scale * mixture).astype(bf16)

    raw_grad = dot_dims(cotangent_rows.astype(bf16), down, 1, 1)
    row_dots = branch_scale * jnp.sum(raw_grad * activated.astype(f32), axis=1)
    row_dots = row_dots.reshape(devices, capacity, 1)
    token_dots = [jnp.sum(jnp.where(found[k], row_dots, 0.0), axis=1) for k in range(2)]
    token_dots = jnp.stack(token_dots, axis=1).reshape(nz, 2, n_exp, 2, T)
    token_dots = jnp.pad(token_dots, ((0, 0),) * 3 + ((0, 6), (0, -T % 128)))
    act_grad = grad_scale * raw_grad
    pre_grad = jnp.concatenate(
        [
            act_grad * up_part * sigmoid_gate * (1.0 + gate_part * (1.0 - sigmoid_gate)),
            act_grad * silu_gate,
        ],
        axis=1,
    ).astype(bf16)
    w_pair = jnp.concatenate([w_gate, w_up], axis=1)
    in_rows = dot_dims(pre_grad, w_pair, 1, 1).astype(bf16)
    in_rows = in_rows.reshape(nz, 2, n_exp, capacity, D)
    collect = collect_rows if n_exp == 4 else collect_plain
    normed_mid_grad, gate_grad = collect(nz, in_rows, all_notes, token_dots, T)
    gate_grad = jnp.transpose(gate_grad[:2, :T])
    in_term = dot_dims(arrived, pre_grad, 0, 0).astype(bf16).reshape(n_shard, R, 2 * Fp)
    in_term, normed_mid_grad = lax.optimization_barrier((in_term, normed_mid_grad))
    in_term = lax.all_to_all(in_term, SHARD, split_axis=0, concat_axis=0, tiled=True)
    down_term = dot_dims(activated[:, :F], grad_arrived, 0, 0)
    grad_w_in = unpack_columns(in_term, F)
    grad_w_down = lined_up(down_term)

    chosen_grad = gate_probs * (gate_grad - jnp.sum(gate_probs * gate_grad, axis=-1, keepdims=True))
    logit_grad = jnp.sum(chosen_grad[:, :, None] * route_mask, axis=1)
    normed_mid_grad = normed_mid_grad + jnp.dot(
        logit_grad, jnp.transpose(full_router.astype(f32)), precision=highest
    )
    router_grad = jnp.dot(
        jnp.transpose(normed_mid_half.astype(f32)), logit_grad, precision=highest
    )
    mid_norm_grad, gain_ffn_grad = rms_backward(
        residual_mid, inverse_mid, gain_ffn, normed_mid_grad
    )
    residual_grad = upstream + mid_norm_grad
    branch_own = (branch_scale * residual_grad).astype(bf16)

    branch_mine, branch_other = halves(branch_own, 1)
    branch_half = side_by_side(branch_mine, beside(branch_other), 0)
    context_grad = dot_dims(branch_half, full_output, 1, 1)
    grad_mine, grad_other = halves(context_grad, 1)
    context_grad = (grad_mine + beside(grad_other)).reshape(head_shape)
    row_delta = jnp.sum(context_grad * context.astype(f32), axis=-1)
    context_grad_half = context_grad.astype(bf16)
    probs_grad = ein32("bqhd,bkhd->bhqk", context_grad_half, values)
    scores_grad = (
        attn_probs * (probs_grad - jnp.transpose(row_delta, (0, 2, 1))[..., None]) * score_scale
    ).astype(bf16)
    queries_grad = ein32("bhqk,bkhd->bqhd", scores_grad, keys_rot)
    keys_grad = ein32("bhqk,bqhd->bkhd", scores_grad, queries)
    values_grad = ein32("bhqk,bqhd->bkhd", probs_half, context_grad_half)
    parts = [
        rotate(queries_grad, cosine, -sine_table).reshape(2 * T, H).astype(bf16),
        rotate(keys_grad, cosine, -sine_table).reshape(2 * T, H).astype(bf16),
        values_grad.reshape(2 * T, H).astype(bf16),
    ]
    weight_grads = [dot_dims(normed_half, p, 0, 0) for p in parts]
    weight_grads.append(dot_dims(context_full, branch_half, 0, 0))
    qkv_grad = jnp.concatenate(parts, axis=1)
    grad_mine, grad_other = halves(dot_dims(qkv_grad, full_qkv, 1, 1), 0)
    normed_in_grad = grad_mine + beside(grad_other)
    in_norm_grad, gain_attn_grad = rms_backward(residual_in, inverse_in, gain_attn, normed_in_grad)
    grad_tokens = residual_grad + in_norm_grad

    small_grad = jnp.concatenate(
        [router_grad, gain_attn_grad[:, None], gain_ffn_grad[:, None]], axis=1
    )
    weight_grads.append(jnp.pad(small_grad, ((0, 0), (0, 128 - small_grad.shape[1]))))
    reduce = reduce_attention if n_exp == 4 else reduce_plain
    sums = reduce(nz, [g.astype(bf16).reshape(nz, 4, -1, g.shape[1]) for g in weight_grads])
    small_sum = jnp.sum(sums[4].astype(f32), axis=1).reshape(R, 128)
    sums = [s.reshape(R, D).astype(f32) for s in sums[:4]]
    return (
        activations,
        grad_tokens,
        small_sum[:, experts],
        sums[0],
        sums[1],
        sums[2],
        sums[3],
        small_sum[:, experts + 1],
        small_sum[:, :experts],
        grad_w_in,
        grad_w_down,
    )


def solution(mesh):
    n_expert, n_shard = mesh.devices.shape
    chips = Mesh(mesh.devices.reshape(n_expert, n_shard // 2, 2), ("expert", "z", "core"))
    rows = P(("expert", "z", "core"), None)
    shard = P(SHARD)
    shard2 = P(SHARD, None)
    shard3 = P(SHARD, "expert", None)
    in_specs = (
        rows,
        rows,
        rows,
        shard,
        shard2,
        shard2,
        shard2,
        shard2,
        shard,
        shard2,
        shard3,
        shard3,
        rows,
    )
    out_specs = (
        rows,
        rows,
        shard,
        shard2,
        shard2,
        shard2,
        shard2,
        shard,
        shard2,
        shard3,
        shard3,
    )
    return jax.shard_map(
        on_device, mesh=chips, in_specs=in_specs, out_specs=out_specs, check_vma=False
    )
```

```python
import functools
import math

import jax
import jax.numpy as jnp
from jax import lax
from jax.experimental import pallas as pl
from jax.experimental.pallas import tpu as pltpu
from jax.sharding import Mesh, PartitionSpec as P

HEADS = 36

eps_norm = 1e-05
branch_scale = 1.4 / math.sqrt(40.0)
rope_base = 10000.0
masked_score = -1e30
bf16 = jnp.bfloat16
f32 = jnp.float32
SHARD = ("z", "core")
ANY = pl.BlockSpec(memory_space=pl.ANY)


def place():
    e, z, c = lax.axis_index("expert"), lax.axis_index("z"), lax.axis_index("core")
    across_x = e + 1 - 2 * (e % 2)
    across_y = (e + 2) % 4
    return e, z, c, across_x, across_y


def remote(src, dst, send, recv, e, z, c):
    return pltpu.make_async_remote_copy(
        src_ref=src,
        dst_ref=dst,
        send_sem=send,
        recv_sem=recv,
        device_id=(e, z, c),
        device_id_type=pl.DeviceIdType.MESH,
    )


def payload_stream(nz, ref, out, sems, split):
    zrecv, zsend, near_recv, near_send, far_recv, far_send, sib_recv, sib_send, own = sems
    e, z, c, ex, ey = place()
    diagonal = (ex + 2) % 4
    T = ref.shape[0]
    S = 2 * nz - 1

    def split_step(s):
        return (s - 1) % 2, (s - 1) // 2

    def where(s):
        if s == 0:
            return z
        side, i = split_step(s)
        return z - 1 - i if side == 0 else z + 1 + i

    def exists(s):
        if s == 0:
            return z >= 0
        zz = where(s)
        return (zz >= 0) & (zz < nz)

    def slab(s, quarter, r0=0, n=T):
        return out.at[where(s), c, quarter, pl.ds(r0, n), :]

    def first(step):
        side = 0 if step > 0 else 1
        return remote(ref, slab(0, e), zsend.at[side, nz - 1], zrecv.at[side, 0], e, z + step, c)

    def onward(s):
        side, i = split_step(s)
        step = 1 if side == 0 else -1
        return remote(
            slab(s, e), slab(s, e), zsend.at[side, i], zrecv.at[side, i + 1], e, z + step, c
        )

    def near(s, axis):
        source = ref if s == 0 else slab(s, e)
        return remote(
            source, slab(s, e), near_send.at[s, axis], near_recv.at[s, axis],
            ex if axis == 0 else ey, z, c,
        )

    def near_wait(s, axis):
        view = slab(s, ex if axis == 0 else ey)
        remote(view, view, near_send.at[s, axis], near_recv.at[s, axis], ex, z, c).wait_recv()

    axes = range(2) if split else range(1)

    def far_view(s, quarter, axis):
        if not split:
            return slab(s, quarter)
        return slab(s, quarter, 0, split) if axis == 0 else slab(s, quarter, split, T - split)

    def far(s, axis):
        view = far_view(s, ex if axis == 0 else ey, axis)
        return remote(
            view, view, far_send.at[s, axis], far_recv.at[s, axis],
            ey if axis == 0 else ex, z, c,
        )

    def far_wait(s, axis):
        view = far_view(s, diagonal, axis)
        remote(view, view, far_send.at[s, axis], far_recv.at[s, axis], ex, z, c).wait_recv()

    def beside(s, n):
        quarter = (e, ex, ey, diagonal)[n]
        source = ref if s == 0 and n == 0 else slab(s, quarter)
        return remote(
            source, slab(s, quarter), sib_send.at[s, n], sib_recv.at[s, n], e, z, 1 - c
        )

    def beside_wait(s, n):
        view = out.at[where(s), 1 - c, (e, ex, ey, diagonal)[n]]
        remote(view, view, sib_send.at[s, n], sib_recv.at[s, n], e, z, c).wait_recv()

    def inside(side):
        return z < nz - 1 if side == 0 else z > 0

    def begin():
        for step in (1, -1):

            @pl.when((z + step >= 0) & (z + step < nz))
            def _():
                first(step).start()

        near(0, 0).start()
        near(0, 1).start()
        beside(0, 0).start()
        pltpu.make_async_copy(ref, slab(0, e), own).start()

    def arrive(s):
        if s == 0:
            return

        @pl.when(exists(s))
        def _():
            side, i = split_step(s)
            remote(
                slab(s, e), slab(s, e), zsend.at[side, i], zrecv.at[side, i], e, z, c
            ).wait_recv()
            if i < nz - 2:

                @pl.when(inside(side))
                def _():
                    onward(s).start()

            near(s, 0).start()
            near(s, 1).start()
            beside(s, 0).start()

    def relay(s):
        @pl.when(exists(s))
        def _():
            near_wait(s, 0)
            far(s, 0).start()
            beside(s, 1).start()
            near_wait(s, 1)
            if split:
                far(s, 1).start()
            beside(s, 2).start()

    def close(s):
        @pl.when(exists(s))
        def _():
            for axis in axes:
                far_wait(s, axis)
            beside(s, 3).start()

    def end(s):
        @pl.when(exists(s))
        def _():
            for axis in range(2):
                near(s, axis).wait_send()
            for axis in axes:
                far(s, axis).wait_send()
            for n in range(4):
                beside(s, n).wait_send()
                beside_wait(s, n)
            if s > 0 and split_step(s)[1] < nz - 2:

                @pl.when(inside(split_step(s)[0]))
                def _():
                    onward(s).wait_send()

        if s == 0:
            for step in (1, -1):

                @pl.when((z + step >= 0) & (z + step < nz))
                def _():
                    first(step).wait_send()

            pltpu.make_async_copy(ref, slab(0, e), own).wait()

    return begin, arrive, relay, close, end


def payload_sems(nz):
    dma = pltpu.SemaphoreType.DMA
    S = 2 * nz - 1
    return [
        dma((2, nz)), dma((2, nz)), dma((S, 2)), dma((S, 2)), dma((S, 2)), dma((S, 2)),
        dma((S, 4)), dma((S, 4)), dma(()),
    ]


def spread_kernel(nz, splits, *refs):
    n = len(splits)
    ins, outs, sems = refs[:n], refs[n : 2 * n], refs[2 * n :]
    greet_cross(nz)
    streams = [
        payload_stream(nz, ins[i], outs[i], sems[9 * i : 9 * i + 9], splits[i]) for i in range(n)
    ]
    for t in streams:
        t[0]()
    S = 2 * nz - 1
    for s in range(S):
        for t in streams:
            t[1](s)
        if s >= 1:
            for t in streams:
                t[2](s - 1)
        if s >= 2:
            for t in streams:
                t[3](s - 2)
    for t in streams:
        t[2](S - 1)
    for s in (S - 2, S - 1):
        for t in streams:
            t[3](s)
    for s in range(S):
        for t in streams:
            t[4](s)


def spread_blocks(nz, blocks, collective):
    sd = jax.ShapeDtypeStruct
    splits = tuple(b.shape[0] // 2 if b.shape[0] % 32 == 0 else 0 for b in blocks)
    return pl.pallas_call(
        functools.partial(spread_kernel, nz, splits),
        out_shape=tuple(sd((nz, 2, 4) + b.shape, b.dtype) for b in blocks),
        in_specs=[ANY] * len(blocks),
        out_specs=(ANY,) * len(blocks),
        scratch_shapes=[s for _ in blocks for s in payload_sems(nz)],
        compiler_params=pltpu.CompilerParams(collective_id=collective, has_side_effects=True),
        cost_estimate=pl.CostEstimate(
            flops=10**6, bytes_accessed=10**6, transcendentals=0
        ),
        name="spread_blocks",
    )(*blocks)


def line_order(nz, z):
    def order(i):
        code = 0
        for zz in range(nz):
            far_first = sorted(range(nz), key=lambda t: (-abs(t - zz), t))
            code += far_first[i] * nz**zz
        power = 1
        for zz in range(nz):
            power = power + (nz**zz - 1) * jnp.where(z == zz, 1, 0)
        return (code // power) % nz

    return [order(i) for i in range(nz)]


def collect_kernel(
    nz, cap,
    rows_ref, notes_ref, dots_ref,
    out_ref, dots_out,
    dots, notes, mine, theirs, block, from_x, from_y, via_x, via_y, from_z,
    note_sem, load, sib_send, sib_recv, via_send, via_recv, plain_send, plain_recv,
    sum_send, sum_recv, zsend, zrecv, dot_send, dot_recv, dot_own,
):
    e, z, c, ex, ey = place()
    diagonal = (ex + 2) % 4
    T, D = out_ref.shape
    h = T // 2
    dest = line_order(nz, z)
    who = (diagonal, ex, ey, e)

    def others():
        for d in range(1, 8 * nz):
            to = ((e * nz + z) * 2 + c + d) % (8 * nz)
            yield d, to // (2 * nz), to // 2 % nz, to % 2

    barrier = pltpu.get_barrier_semaphore()
    for _, te, tz, tc in others():
        pl.semaphore_signal(
            barrier, inc=1, device_id=(te, tz, tc), device_id_type=pl.DeviceIdType.MESH
        )
    pl.semaphore_wait(barrier, 8 * nz - 1)

    def dot(d, te, tz, tc):
        return remote(
            dots_ref.at[tz, tc, te], dots.at[d], dot_send.at[d], dot_recv.at[d], te, tz, tc
        )

    dot_kept = pltpu.make_async_copy(dots_ref.at[z, c, e], dots.at[0], dot_own)
    dot_kept.start()
    for d, te, tz, tc in others():
        dot(d, te, tz, tc).start()

    note_copy = pltpu.make_async_copy(notes_ref, notes, note_sem)
    note_copy.start()

    def fetch(i, q):
        return pltpu.make_async_copy(
            rows_ref.at[dest[i], c, who[q]], mine.at[i, q], load.at[i, q]
        )

    def hand(i, q):
        return remote(
            rows_ref.at[dest[i], 1 - c, who[q]], theirs.at[i, q],
            sib_send.at[i, q], sib_recv.at[i, q], e, z, 1 - c,
        )

    for i in range(nz):
        for q in range(4):
            hand(i, q).start()
            fetch(i, q).start()
    note_copy.wait()

    def open_out(i, q):
        fetch(i, q).wait()
        hand(i, q).wait_recv()
        places = (lax.broadcasted_iota(jnp.int32, (cap, T), 0) + e * cap).astype(f32)
        note = notes[dest[i], c, who[q]]
        pick = ((note[2:3, :] == places) | (note[3:4, :] == places)).astype(bf16)
        wide = 768 if D % 768 == 0 else 128

        @pl.loop(0, D // wide)
        def _(b):
            cols = pl.ds(pl.multiple_of(b * wide, 128), wide)
            both = mine[i, q, :, cols].astype(f32) + theirs[i, q, :, cols].astype(f32)
            block[i, q, :, cols] = lax.dot_general(
                pick, both.astype(bf16), (((0,), (0,)), ((), ())), preferred_element_type=f32
            ).astype(bf16)

    def via(i, axis):
        if axis == 0:
            return remote(
                block.at[i, 0, pl.ds(0, h), :], via_x.at[i],
                via_send.at[i, 0], via_recv.at[i, 0], ex, z, c,
            )
        return remote(
            block.at[i, 0, pl.ds(h, h), :], via_y.at[i],
            via_send.at[i, 1], via_recv.at[i, 1], ey, z, c,
        )

    def plain(i, axis):
        if axis == 0:
            return remote(
                block.at[i, 1, pl.ds(0, h), :], from_x.at[i, pl.ds(0, h), :],
                plain_send.at[i, 0], plain_recv.at[i, 0], ex, z, c,
            )
        return remote(
            block.at[i, 2, pl.ds(h, h), :], from_y.at[i, pl.ds(h, h), :],
            plain_send.at[i, 1], plain_recv.at[i, 1], ey, z, c,
        )

    def summed(i, axis):
        if axis == 0:
            return remote(
                block.at[i, 1, pl.ds(h, h), :], from_x.at[i, pl.ds(h, h), :],
                sum_send.at[i, 0], sum_recv.at[i, 0], ex, z, c,
            )
        return remote(
            block.at[i, 2, pl.ds(0, h), :], from_y.at[i, pl.ds(0, h), :],
            sum_send.at[i, 1], sum_recv.at[i, 1], ey, z, c,
        )

    def add(target, others, n):
        @pl.loop(0, n // 16)
        def _(b):
            rows = pl.ds(pl.multiple_of(b * 16, 16), 16)
            acc = target[rows, :].astype(f32)
            for o in others:
                acc = acc + o[rows, :].astype(f32)
            target[rows, :] = acc.astype(target.dtype)

    def start(i):
        open_out(i, 0)
        via(i, 0).start()
        via(i, 1).start()
        open_out(i, 1)
        plain(i, 0).start()
        open_out(i, 2)
        plain(i, 1).start()
        open_out(i, 3)

    def combine(i):
        via(i, 0).wait_recv()
        add(block.at[i, 2, pl.ds(0, h), :], [via_x.at[i]], h)
        summed(i, 1).start()
        via(i, 1).wait_recv()
        add(block.at[i, 1, pl.ds(h, h), :], [via_y.at[i]], h)
        summed(i, 0).start()

    def zcopy(i):
        step = jnp.where(dest[i] > z, 1, -1)
        side = jnp.where(dest[i] > z, 0, 1)
        return remote(
            block.at[i, 3], from_z.at[side, dest[i]],
            zsend.at[i], zrecv.at[side, dest[i]], e, z + step, c,
        )

    def zwait(side, zz):
        slab = from_z.at[side, zz]
        remote(slab, slab, zsend.at[0], zrecv.at[side, zz], e, z, c).wait_recv()

    def finish(i):
        for axis in range(2):
            plain(i, axis).wait_recv()
            summed(i, axis).wait_recv()
        zz = dest[i]
        if i < nz - 1:
            add(block.at[i, 3], [from_x.at[i], from_y.at[i]], T)
            for side in range(2):
                going = zz > z if side == 0 else zz < z
                behind = z > 0 if side == 0 else z < nz - 1

                @pl.when(going & behind)
                def _():
                    zwait(side, zz)
                    add(block.at[i, 3], [from_z.at[side, zz]], T)

            zcopy(i).start()
            return

        @pl.loop(0, T // 16)
        def _(b):
            rows = pl.ds(pl.multiple_of(b * 16, 16), 16)
            acc = block[i, 3, rows, :].astype(f32) + from_x[i, rows, :].astype(f32)
            out_ref[rows, :] = acc + from_y[i, rows, :].astype(f32)

        for side in range(2):

            @pl.when(z > 0 if side == 0 else z < nz - 1)
            def _():
                zwait(side, z)
                add(out_ref, [from_z.at[side, z]], T)

    for i in range(nz):
        start(i)
        if i >= 1:
            combine(i - 1)
        if i >= 2:
            finish(i - 2)
    combine(nz - 1)
    if nz >= 2:
        finish(nz - 2)
    finish(nz - 1)

    dot_kept.wait()
    for d, te, tz, tc in others():
        dot(d, te, tz, tc).wait_recv()
        dot(d, te, tz, tc).wait_send()
    dots_out[...] = jnp.sum(dots[...], axis=0)

    for i in range(nz):
        for q in range(4):
            hand(i, q).wait_send()
        for axis in range(2):
            via(i, axis).wait_send()
            plain(i, axis).wait_send()
            summed(i, axis).wait_send()
        if i < nz - 1:
            zcopy(i).wait_send()


def collect_rows(nz, rows, notes, dots, T):
    cap, D = rows.shape[3:]
    dma = pltpu.SemaphoreType.DMA
    vm = pltpu.VMEM
    return pl.pallas_call(
        functools.partial(collect_kernel, nz, cap),
        out_shape=(
            jax.ShapeDtypeStruct((T, D), f32),
            jax.ShapeDtypeStruct(dots.shape[3:], f32),
        ),
        in_specs=[ANY] * 3,
        out_specs=(pl.BlockSpec(memory_space=pltpu.VMEM),) * 2,
        scratch_shapes=[
            vm((8 * nz,) + dots.shape[3:], f32),
            vm(notes.shape, f32),
            vm((nz, 4, cap, D), bf16),
            vm((nz, 4, cap, D), bf16),
            vm((nz, 4, T, D), bf16),
            vm((nz, T, D), bf16),
            vm((nz, T, D), bf16),
            vm((nz, T // 2, D), bf16),
            vm((nz, T // 2, D), bf16),
            vm((2, nz, T, D), bf16),
            dma(()),
            dma((nz, 4)),
            dma((nz, 4)),
            dma((nz, 4)),
            dma((nz, 2)),
            dma((nz, 2)),
            dma((nz, 2)),
            dma((nz, 2)),
            dma((nz, 2)),
            dma((nz, 2)),
            dma((nz,)),
            dma((2, nz)),
            dma((8 * nz,)),
            dma((8 * nz,)),
            dma(()),
        ],
        compiler_params=pltpu.CompilerParams(
            collective_id=3, has_side_effects=True, vmem_limit_bytes=56 << 20
        ),
        cost_estimate=pl.CostEstimate(
            flops=5 * 10**10, bytes_accessed=2 * rows.size, transcendentals=0
        ),
        name="collect_rows",
    )(rows, notes, dots)


def pack_kernel(n, F, Fp, x_ref, o_ref):
    half = n * F
    rows = x_ref.shape[0]
    for i in range(n):
        for part in range(2):
            cols = x_ref[:, part * half + i * F : part * half + (i + 1) * F]
            if Fp > F:
                cols = jnp.concatenate([cols, jnp.zeros((rows, Fp - F), cols.dtype)], axis=1)
            o_ref[i, :, part * Fp : (part + 1) * Fp] = cols


def pack_columns(w, n, F, Fp):
    rows = w.shape[0]
    block = 16
    return pl.pallas_call(
        functools.partial(pack_kernel, n, F, Fp),
        grid=(rows // block,),
        in_specs=[pl.BlockSpec((block, w.shape[1]), lambda i: (i, 0))],
        out_specs=pl.BlockSpec((n, block, 2 * Fp), lambda i: (0, i, 0)),
        out_shape=jax.ShapeDtypeStruct((n, rows, 2 * Fp), w.dtype),
        name="pack_columns",
    )(w)


def unpack_kernel(n, F, Fp, x_ref, o_ref, line):
    half = n * F
    rows = line.shape[0]
    for i in range(n):
        for part in range(2):
            cols = x_ref[i, :, part * Fp : part * Fp + F].astype(f32)
            line[:, part * half + i * F : part * half + (i + 1) * F] = cols
    tiles = 2 * half // 128
    for j in range(tiles):
        o_ref[pl.ds(j, rows, stride=tiles), :] = line[:, j * 128 : (j + 1) * 128]


def unpack_columns(x, F):
    n, rows, Fp2 = x.shape
    block = 16
    width = 2 * n * F
    tiles = width // 128
    flat = pl.pallas_call(
        functools.partial(unpack_kernel, n, F, Fp2 // 2),
        grid=(rows // block,),
        in_specs=[pl.BlockSpec((n, block, Fp2), lambda i: (0, i, 0))],
        out_specs=pl.BlockSpec((block * tiles, 128), lambda i: (i, 0)),
        out_shape=jax.ShapeDtypeStruct((rows * tiles, 128), f32),
        scratch_shapes=[pltpu.VMEM((block, width), f32)],
        name="unpack_columns",
    )(x)
    return flat.reshape(rows, 1, width)


def line_kernel(x_ref, o_ref):
    rows, width = x_ref.shape
    tiles = width // 128
    for j in range(tiles):
        o_ref[pl.ds(j, rows, stride=tiles), :] = x_ref[:, j * 128 : (j + 1) * 128]


def lined_up(x):
    rows, width = x.shape
    tiles = width // 128
    block = 80 if rows % 80 == 0 else 8
    flat = pl.pallas_call(
        line_kernel,
        grid=(rows // block,),
        in_specs=[pl.BlockSpec((block, width), lambda i: (i, 0))],
        out_specs=pl.BlockSpec((block * tiles, 128), lambda i: (i, 0)),
        out_shape=jax.ShapeDtypeStruct((rows * tiles, 128), x.dtype),
        name="lined_up",
    )(x)
    return flat.reshape(rows, 1, width)


def greet_cross(nz):
    e, z, c, ex, ey = place()
    barrier = pltpu.get_barrier_semaphore()

    def hail(te, tz, tc):
        pl.semaphore_signal(
            barrier, inc=1, device_id=(te, tz, tc), device_id_type=pl.DeviceIdType.MESH
        )

    hail(e, z, 1 - c)
    for te in (ex, ey, (ex + 2) % 4):
        hail(te, z, c)
    for step in (-1, 1):

        @pl.when((z + step >= 0) & (z + step < nz))
        def _():
            hail(e, z + step, c)

    pl.semaphore_wait(barrier, 4 + jnp.where(z > 0, 1, 0) + jnp.where(z < nz - 1, 1, 0))


def line_stream(nz, ref, out, zrecv, zsend, sib_recv, sib_send, own):
    e, z, c, _, _ = place()

    def split_step(s):
        return (s - 1) % 2, (s - 1) // 2

    def where(s):
        if s == 0:
            return z
        side, i = split_step(s)
        return z - 1 - i if side == 0 else z + 1 + i

    def exists(s):
        return (where(s) >= 0) & (where(s) < nz)

    def inside(side):
        return z < nz - 1 if side == 0 else z > 0

    def slab(s):
        return out.at[where(s), c]

    def first(side):
        step = 1 if side == 0 else -1
        return remote(ref, slab(0), zsend.at[side, nz - 1], zrecv.at[side, 0], e, z + step, c)

    def onward(s):
        side, i = split_step(s)
        step = 1 if side == 0 else -1
        return remote(
            slab(s), slab(s), zsend.at[side, i], zrecv.at[side, i + 1], e, z + step, c
        )

    def beside(s):
        return remote(
            ref if s == 0 else slab(s), slab(s), sib_send.at[s], sib_recv.at[s], e, z, 1 - c
        )

    def begin():
        for side in range(2):

            @pl.when(inside(side))
            def _():
                first(side).start()

        beside(0).start()
        pltpu.make_async_copy(ref, slab(0), own).start()

    def arrive(s):
        side, i = split_step(s)

        @pl.when(exists(s))
        def _():
            remote(slab(s), slab(s), zsend.at[side, i], zrecv.at[side, i], e, z, c).wait_recv()
            if i < nz - 2:

                @pl.when(inside(side))
                def _():
                    onward(s).start()

            beside(s).start()

    def end():
        for s in range(2 * nz - 1):

            @pl.when(exists(s))
            def _():
                beside(s).wait_send()
                view = out.at[where(s), 1 - c]
                remote(view, view, sib_send.at[s], sib_recv.at[s], e, z, c).wait_recv()
                if s > 0 and split_step(s)[1] < nz - 2:

                    @pl.when(inside(split_step(s)[0]))
                    def _():
                        onward(s).wait_send()

        for side in range(2):

            @pl.when(inside(side))
            def _():
                first(side).wait_send()

        pltpu.make_async_copy(ref, slab(0), own).wait()

    return begin, arrive, end


def line_sems(nz):
    dma = pltpu.SemaphoreType.DMA
    S = 2 * nz - 1
    return [dma((2, nz)), dma((2, nz)), dma((S,)), dma((S,)), dma(())]


def plane_stream(source, views, send, recv, own):
    e, z, c, ex, ey = place()
    peers = (ex, ey, (ex + 2) % 4)

    def copy(n):
        return remote(source, views(e), send.at[n], recv.at[n], peers[n], z, c)

    def kept():
        return pltpu.make_async_copy(source, views(e), own)

    def begin():
        for n in range(3):
            copy(n).start()
        kept().start()

    def end():
        kept().wait()
        for n in range(3):
            view = views(peers[n])
            remote(view, view, send.at[n], recv.at[n], e, z, c).wait_recv()
            copy(n).wait_send()

    return begin, end


def plane_sems():
    dma = pltpu.SemaphoreType.DMA
    return [dma((3,)), dma((3,)), dma(())]


def fetch_kernel(
    nz,
    w_ref, s_ref, o_ref, t_ref, l_ref, p_ref,
    w_out, s_out, o_out, t_out, l_out, p_out,
    *sems,
):
    e, z, c, ex, ey = place()
    w_sems, sems = sems[:5], sems[5:]
    s_sems, sems = sems[:5], sems[5:]
    t_sems, sems = sems[:3], sems[3:]
    l_sems, sems = sems[:3], sems[3:]
    p_sems, sems = sems[:9], sems[9:]
    orecv, osend, sib_recv, sib_send, own = sems
    greet_cross(nz)
    w_begin, w_arrive, w_end = line_stream(nz, w_ref, w_out, *w_sems)
    s_begin, s_arrive, s_end = line_stream(nz, s_ref, s_out, *s_sems)
    t_begin, t_end = plane_stream(t_ref, lambda q: t_out.at[q], *t_sems)
    l_begin, l_end = plane_stream(l_ref, lambda q: l_out.at[q], *l_sems)
    p_begin, p_arrive, p_relay, p_close, p_end = payload_stream(
        nz, p_ref, p_out, p_sems, p_ref.shape[0] // 2
    )

    def o_copy(side, source):
        step = 1 if side == 0 else -1
        return remote(source, o_out.at[c], osend.at[side], orecv, e, z + step, c)

    def o_beside(source):
        return remote(source, o_out.at[c], sib_send, sib_recv, e, z, 1 - c)

    def o_goes(side):
        return (z >= e) & (z < nz - 1) if side == 0 else (z <= e) & (z > 0)

    w_begin()
    s_begin()

    @pl.when(z == e)
    def _():
        for side in range(2):

            @pl.when(o_goes(side))
            def _():
                o_copy(side, o_ref).start()

        o_beside(o_ref).start()
        pltpu.make_async_copy(o_ref, o_out.at[c], own).start()

    t_begin()
    l_begin()
    p_begin()

    def o_arrive():
        @pl.when(z != e)
        def _():
            remote(o_out.at[c], o_out.at[c], sib_send, orecv, e, z, c).wait_recv()
            for side in range(2):

                @pl.when(o_goes(side))
                def _():
                    o_copy(side, o_out.at[c]).start()

            o_beside(o_out.at[c]).start()

    blocks = 2 * nz - 1
    for s in range(1, blocks):
        w_arrive(s)
        s_arrive(s)
        p_arrive(s)
        p_relay(s - 1)
        if s >= 2:
            p_close(s - 2)
        if s == 4:
            o_arrive()
    p_relay(blocks - 1)
    p_close(blocks - 2)
    p_close(blocks - 1)
    for s in range(blocks):
        p_end(s)
    w_end()
    s_end()
    t_end()
    l_end()
    view = o_out.at[1 - c]
    remote(view, view, sib_send, sib_recv, e, z, c).wait_recv()
    o_beside(o_out.at[c]).wait_send()
    for side in range(2):

        @pl.when(o_goes(side))
        def _():
            o_copy(side, o_out.at[c]).wait_send()

    @pl.when(z == e)
    def _():
        pltpu.make_async_copy(o_ref, o_out.at[c], own).wait()


def fetch_weights(nz, columns, small, rows, tokens, lengths, block):
    dma = pltpu.SemaphoreType.DMA
    sd = jax.ShapeDtypeStruct
    return pl.pallas_call(
        functools.partial(fetch_kernel, nz),
        out_shape=(
            sd((nz, 2) + columns.shape, bf16),
            sd((nz, 2) + small.shape, bf16),
            sd((2,) + rows.shape, bf16),
            sd((4,) + tokens.shape, bf16),
            sd((4,) + lengths.shape, lengths.dtype),
            sd((nz, 2, 4) + block.shape, block.dtype),
        ),
        in_specs=[ANY] * 6,
        out_specs=(ANY,) * 6,
        scratch_shapes=[
            *line_sems(nz), *line_sems(nz), *plane_sems(), *plane_sems(), *payload_sems(nz),
            dma(()), dma((2,)), dma(()), dma(()), dma(()),
        ],
        compiler_params=pltpu.CompilerParams(collective_id=0, has_side_effects=True),
        cost_estimate=pl.CostEstimate(
            flops=10**11, bytes_accessed=8 * columns.size, transcendentals=0
        ),
        name="fetch_weights",
    )(columns, small, rows, tokens, lengths, block)


def plane_gather_kernel(x_ref, out_ref, send, recv, own):
    e, z, c, ex, ey = place()
    greet_plane()
    begin, end = plane_stream(x_ref, lambda q: out_ref.at[q], send, recv, own)
    begin()
    end()


def greet_plane():
    e, z, c, ex, ey = place()
    barrier = pltpu.get_barrier_semaphore()
    for te in (ex, ey, (ex + 2) % 4):
        pl.semaphore_signal(
            barrier, inc=1, device_id=(te, z, c), device_id_type=pl.DeviceIdType.MESH
        )
    pl.semaphore_wait(barrier, 3)


def plane_gather(x, collective):
    return pl.pallas_call(
        plane_gather_kernel,
        out_shape=jax.ShapeDtypeStruct((4,) + x.shape, x.dtype),
        in_specs=[ANY],
        out_specs=ANY,
        scratch_shapes=plane_sems(),
        compiler_params=pltpu.CompilerParams(collective_id=collective, has_side_effects=True),
        cost_estimate=pl.CostEstimate(flops=10**6, bytes_accessed=10**6, transcendentals=0),
        name="plane_gather",
    )(x)


def plane_sum_kernel(x_ref, out_ref, held, send, recv, own):
    e, z, c, ex, ey = place()
    peers = (ex, ey, (ex + 2) % 4)
    greet_plane()

    def copy(n):
        return remote(x_ref.at[peers[n]], held.at[n], send.at[n], recv.at[n], peers[n], z, c)

    for n in (2, 0, 1):
        copy(n).start()
    kept = pltpu.make_async_copy(x_ref.at[e], held.at[3], own)
    kept.start()
    kept.wait()
    for n in range(3):
        copy(n).wait_recv()

    @pl.loop(0, out_ref.shape[0] // 16)
    def _(b):
        rows = pl.ds(pl.multiple_of(b * 16, 16), 16)
        acc = held[3, rows, :].astype(f32) + held[0, rows, :].astype(f32)
        acc = acc + held[1, rows, :].astype(f32)
        out_ref[rows, :] = acc + held[2, rows, :].astype(f32)

    for n in range(3):
        copy(n).wait_send()


def plane_sum(x, collective):
    vm = pltpu.VMEM
    return pl.pallas_call(
        plane_sum_kernel,
        out_shape=jax.ShapeDtypeStruct(x.shape[1:], f32),
        in_specs=[ANY],
        out_specs=pl.BlockSpec(memory_space=vm),
        scratch_shapes=[vm(x.shape, bf16), *plane_sems()],
        compiler_params=pltpu.CompilerParams(collective_id=collective, has_side_effects=True),
        cost_estimate=pl.CostEstimate(flops=10**6, bytes_accessed=10**6, transcendentals=0),
        name="plane_sum",
    )(x)


def settle_kernel(
    nz,
    g_ref, s_ref, o_ref,
    g_out, s_out, o_out,
    g_mine, g_sib, g_z, s_mine, s_sib, s_z, o_mine, o_sib, o_z,
    load, sib_send, sib_recv, zsend, zrecv,
    o_load, o_sib_send, o_sib_recv, o_zsend, o_zrecv,
    o_send, o_recv, o_own,
    *sems,
):
    e, z, c, ex, ey = place()
    peers = (ex, ey, (ex + 2) % 4)
    dest = line_order(nz, z)
    greet_cross(nz)
    groups = ((g_ref, g_mine, g_sib, g_z, g_out), (s_ref, s_mine, s_sib, s_z, s_out))

    def fetch(k, i):
        ref, mine = groups[k][0], groups[k][1]
        return pltpu.make_async_copy(ref.at[dest[i], c], mine.at[i], load.at[k, i])

    def hand(k, i):
        ref, theirs = groups[k][0], groups[k][2]
        return remote(
            ref.at[dest[i], 1 - c], theirs.at[i], sib_send.at[k, i], sib_recv.at[k, i], e, z, 1 - c
        )

    def zcopy(k, i):
        mine, from_z = groups[k][1], groups[k][3]
        step = jnp.where(dest[i] > z, 1, -1)
        side = jnp.where(dest[i] > z, 0, 1)
        return remote(
            mine.at[i], from_z.at[side, dest[i]],
            zsend.at[k, i], zrecv.at[k, side, dest[i]], e, z + step, c,
        )

    def zwait(k, side, zz):
        slab = groups[k][3].at[side, zz]
        remote(slab, slab, zsend.at[k, 0], zrecv.at[k, side, zz], e, z, c).wait_recv()

    def add(target, others):
        @pl.loop(0, target.shape[0] // 16)
        def _(b):
            rows = pl.ds(pl.multiple_of(b * 16, 16), 16)
            acc = target[rows, :].astype(f32)
            for o in others:
                acc = acc + o[rows, :].astype(f32)
            target[rows, :] = acc.astype(target.dtype)

    def o_fetch():
        return pltpu.make_async_copy(o_ref.at[c], o_mine, o_load)

    def o_hand():
        return remote(o_ref.at[1 - c], o_sib, o_sib_send, o_sib_recv, e, z, 1 - c)

    def o_line():
        step, side = jnp.where(z < e, 1, -1), jnp.where(z < e, 0, 1)
        return remote(o_mine, o_z.at[side], o_zsend, o_zrecv.at[side], e, z + step, c)

    def o_wait(side):
        slab = o_z.at[side]
        remote(slab, slab, o_zsend, o_zrecv.at[side], e, z, c).wait_recv()
        add(o_mine, [slab])

    def o_peer(n):
        return remote(o_mine, o_out, o_send.at[n], o_recv, peers[n], z, c)

    def o_kept():
        return pltpu.make_async_copy(o_mine, o_out, o_own)

    o_fetch().start()
    o_hand().start()
    for i in range(nz):
        for k in range(2):
            hand(k, i).start()
            fetch(k, i).start()

    def finish(k, i):
        mine, theirs, from_z = groups[k][1:4]
        fetch(k, i).wait()
        hand(k, i).wait_recv()
        zz = dest[i]
        add(mine.at[i], [theirs.at[i]])
        if i < nz - 1:
            for side in range(2):
                going = zz > z if side == 0 else zz < z
                behind = z > 0 if side == 0 else z < nz - 1

                @pl.when(going & behind)
                def _():
                    zwait(k, side, zz)
                    add(mine.at[i], [from_z.at[side, zz]])

            zcopy(k, i).start()
            return
        for side in range(2):

            @pl.when(z > 0 if side == 0 else z < nz - 1)
            def _():
                zwait(k, side, z)
                add(mine.at[i], [from_z.at[side, z]])

    def o_flow():
        o_fetch().wait()
        o_hand().wait_recv()
        add(o_mine, [o_sib])
        for side in range(2):
            behind = (z > 0) & (z <= e) if side == 0 else (z < nz - 1) & (z >= e)

            @pl.when(behind)
            def _():
                o_wait(side)

        @pl.when(z != e)
        def _():
            o_line().start()

        @pl.when(z == e)
        def _():
            for n in range(3):
                o_peer(n).start()
            o_kept().start()

    for i in range(nz - 1):
        for k in range(2):
            finish(k, i)
        if i == 0:
            o_flow()
    for k in range(2):
        finish(k, nz - 1)
    spread = [
        plane_stream(
            groups[k][1].at[nz - 1], lambda q, k=k: groups[k][4].at[q], *sems[3 * k : 3 * k + 3]
        )
        for k in range(2)
    ]
    for begin, _ in spread:
        begin()

    @pl.when(z == e)
    def _():
        o_kept().wait()
        for n in range(3):
            o_peer(n).wait_send()

    @pl.when(z != e)
    def _():
        remote(o_out, o_out, o_send.at[0], o_recv, e, z, c).wait_recv()
        o_line().wait_send()

    o_hand().wait_send()
    for i in range(nz):
        for k in range(2):
            hand(k, i).wait_send()
            if i < nz - 1:
                zcopy(k, i).wait_send()
    for _, end in spread:
        end()


def settle_weights(nz, grads, small, rows):
    R, W = grads.shape[2:]
    D = rows.shape[2]
    dma = pltpu.SemaphoreType.DMA
    sd = jax.ShapeDtypeStruct
    vm = pltpu.VMEM
    Ws = small.shape[3]
    return pl.pallas_call(
        functools.partial(settle_kernel, nz),
        out_shape=(sd((4, R, W), bf16), sd((4, R, Ws), bf16), sd((R, D), bf16)),
        in_specs=[ANY] * 3,
        out_specs=(ANY,) * 3,
        scratch_shapes=[
            vm((nz, R, W), bf16), vm((nz, R, W), bf16), vm((2, nz, R, W), bf16),
            vm((nz, R, Ws), bf16), vm((nz, R, Ws), bf16), vm((2, nz, R, Ws), bf16),
            vm((R, D), bf16), vm((R, D), bf16), vm((2, R, D), bf16),
            dma((2, nz)), dma((2, nz)), dma((2, nz)), dma((2, nz)), dma((2, 2, nz)),
            dma(()), dma(()), dma(()), dma(()), dma((2,)),
            dma((3,)), dma(()), dma(()),
            *plane_sems(), *plane_sems(),
        ],
        compiler_params=pltpu.CompilerParams(
            collective_id=1, has_side_effects=True, vmem_limit_bytes=56 << 20
        ),
        cost_estimate=pl.CostEstimate(flops=10**6, bytes_accessed=10**6, transcendentals=0),
        name="settle_weights",
    )(grads, small, rows)


def pick_kernel(width, q_ref, k_ref, v_ref, o_ref):
    e = lax.axis_index("expert")
    for n in range(4):

        @pl.when(e == n)
        def _():
            for i, ref in enumerate((q_ref, k_ref, v_ref)):
                o_ref[:, i * width : (i + 1) * width] = ref[:, n * width : (n + 1) * width]


def pick_columns(weights, width):
    vm = pl.BlockSpec(memory_space=pltpu.VMEM)
    return pl.pallas_call(
        functools.partial(pick_kernel, width),
        in_specs=[vm] * 3,
        out_specs=vm,
        out_shape=jax.ShapeDtypeStruct((weights[0].shape[0], 3 * width), bf16),
        name="pick_columns",
    )(*weights)


def assemble_kernel(width, x_ref, *o_refs):
    for n in range(4):
        for i in range(3):
            cols = x_ref[n, :, i * width : (i + 1) * width]
            o_refs[i][:, n * width : (n + 1) * width] = cols.astype(f32)


def assemble_columns(x, width):
    R = x.shape[1]
    block = 32
    return pl.pallas_call(
        functools.partial(assemble_kernel, width),
        grid=(R // block,),
        in_specs=[pl.BlockSpec((4, block, 3 * width), lambda i: (0, i, 0))],
        out_specs=(pl.BlockSpec((block, 4 * width), lambda i: (i, 0)),) * 3,
        out_shape=(jax.ShapeDtypeStruct((R, 4 * width), f32),) * 3,
        name="assemble_columns",
    )(x)


def sum_shard(x, axis=0):
    mine = lax.psum_scatter(x, SHARD, scatter_dimension=axis, tiled=True)
    return lax.psum(mine, "expert")


def fetch(nz, fast, weights, w_output, small, tokens, lengths, block):
    D = tokens.shape[1]
    if fast:
        width = D // 4
        columns, full_small, rows, tokens, lengths, blocks = fetch_weights(
            nz, pick_columns(weights, width), small, w_output, tokens, lengths, block
        )
        columns, rows = columns.reshape(D, 3 * width), rows.reshape(width, D)
        return columns, rows, full_small.reshape(D, -1), tokens, lengths, blocks
    full = [lax.all_gather(w, SHARD, axis=0, tiled=True) for w in weights + (w_output, small)]
    blocks = spread_plain(nz, (block,), 0)[0]
    return jnp.concatenate(full[:3], axis=1), full[3], full[4], tokens[None], lengths[None], blocks


def settle(nz, fast, columns, rows, small):
    D, width = rows.shape[1], rows.shape[0]
    if fast:
        R = D // (2 * nz)
        parts = [x.astype(bf16).reshape(nz, 2, R, -1) for x in (columns, small)]
        sums, small, out = settle_weights(nz, *parts, rows.astype(bf16).reshape(2, R, D))
        return *assemble_columns(sums, width), out.astype(f32), jnp.sum(small.astype(f32), axis=0)
    parts = [columns[:, i * width : (i + 1) * width] for i in range(3)] + [rows, small]
    return [sum_shard(x) for x in parts]


def spread_plain(nz, blocks, collective):
    out = []
    for block in blocks:
        for axis in ("expert", "core", "z"):
            block = lax.all_gather(block, axis, axis=0)
        out.append(block)
    return out


def collect_plain(nz, rows, notes, dots, T):
    n_exp, cap, D = rows.shape[2:]
    places = (lax.axis_index("expert") * cap + jnp.arange(cap)).astype(f32)
    notes = notes[..., :T]
    pick = (notes[..., 2, None, :] == places[:, None]) | (notes[..., 3, None, :] == places[:, None])
    part = jnp.einsum(
        "zceps,zcepd->zcesd", pick.astype(bf16), rows, preferred_element_type=f32
    ).astype(bf16)
    part = part.transpose(2, 0, 1, 3, 4).reshape(n_exp * nz * 2 * T, D)
    part = lax.psum_scatter(part, "expert", scatter_dimension=0, tiled=True)
    part = lax.psum_scatter(part, SHARD, scatter_dimension=0, tiled=True).astype(f32)
    z, core, e = lax.axis_index("z"), lax.axis_index("core"), lax.axis_index("expert")
    return part, lax.psum(dots, ("expert",) + SHARD)[z, core, e]


def rope_tables(positions, head_width):
    half_width = head_width // 2
    exponents = jnp.arange(half_width).astype(f32) * 2.0 / head_width
    frequency = rope_base ** (-exponents)
    angles = positions.astype(f32)[..., None] * frequency
    return (jnp.cos(angles), jnp.sin(angles))


def rotate(values, cosine, sine_table):
    half_width = values.shape[-1] // 2
    leading = values[..., :half_width]
    trailing = values[..., half_width:]
    cos_rows = cosine[:, :, None, :]
    sin_rows = sine_table[:, :, None, :]
    return jnp.concatenate(
        [leading * cos_rows - trailing * sin_rows, trailing * cos_rows + leading * sin_rows],
        axis=-1,
    )


def rms_forward(values, norm_gain):
    inverse = lax.rsqrt(jnp.mean(values * values, axis=-1, keepdims=True) + eps_norm)
    return (values * inverse * norm_gain, inverse)


def rms_backward(values, inverse, norm_gain, upstream):
    weighted = upstream * norm_gain
    gain_grad = jnp.sum(upstream * values * inverse, axis=0)
    inner_mean = jnp.mean(weighted * values, axis=-1, keepdims=True)
    return (inverse * weighted - values * inverse * inverse * inverse * inner_mean, gain_grad)


def dot32(a, b):
    return jnp.dot(a, b, preferred_element_type=f32)


def dot_dims(a, b, da, db):
    return lax.dot_general(a, b, (((da,), (db,)), ((), ())), preferred_element_type=f32)


def ein32(spec, a, b):
    return jnp.einsum(spec, a, b, preferred_element_type=f32)


def on_device(
    tokens,
    seq_lengths,
    routes,
    norm_attn,
    w_query,
    w_key,
    w_value,
    w_output,
    norm_ffn,
    w_router,
    w_in,
    w_down,
    cotangent,
):
    T, D = tokens.shape
    R = w_query.shape[0]
    head_width = D // HEADS
    n_exp = lax.axis_size("expert")
    nz = lax.axis_size("z")
    n_shard = nz * lax.axis_size("core")
    experts = w_router.shape[1]
    F = w_down.shape[0]
    FF = F * n_shard
    capacity = 10 * T // (4 * experts)
    slots = experts * capacity
    highest = lax.Precision.HIGHEST
    e_index = lax.axis_index("expert")
    fast = n_exp == 4 and nz == 4

    small = jnp.concatenate([w_router, norm_attn[:, None], norm_ffn[:, None]], axis=1)
    small = jnp.pad(small, ((0, 0), (0, 128 - small.shape[1])))
    length_rows = jnp.broadcast_to(seq_lengths[:, :1], (8, 128))
    full_qkv, full_output, full_small, near_tokens, near_lengths, all_cotangent = fetch(
        nz, fast, (w_query, w_key, w_value), w_output, small, tokens, length_rows, cotangent
    )
    full_router = full_small[:, :experts]
    gain_attn = full_small[:, experts].astype(f32)
    gain_ffn = full_small[:, experts + 1].astype(f32)

    Fp = -(-F // 128) * 128
    packed = pack_columns(w_in.reshape(R, 2 * FF), n_shard, F, Fp)
    packed, full_qkv = lax.optimization_barrier((packed, full_qkv))
    moved = lax.all_to_all(packed, SHARD, split_axis=0, concat_axis=0, tiled=True)
    w_pair = moved.reshape(n_shard * R, 2 * Fp)
    down = jnp.pad(w_down.reshape(F, D), ((0, Fp - F), (0, 0)))

    B, H = near_tokens.shape[0], full_output.shape[0]
    heads = H // head_width
    residual_in = tokens.astype(f32)
    inverse_in = rms_forward(residual_in, gain_attn)[1]
    near_in = near_tokens.reshape(B * T, D).astype(f32)
    near_normed, near_inverse = rms_forward(near_in, gain_attn)
    normed_half = near_normed.astype(bf16)
    lengths = near_lengths[:, 0, 0]
    row_index = jnp.arange(T)
    segment = (row_index[None, :] >= lengths[:, None]).astype(jnp.int32)
    positions = row_index[None, :] - lengths[:, None] * segment
    allowed = (segment[:, :, None] == segment[:, None, :]) & (
        row_index[None, None, :] <= row_index[None, :, None]
    )
    cosine, sine_table = rope_tables(positions, head_width)
    head_shape = (B, T, heads, head_width)
    qkv = dot32(normed_half, full_qkv)
    queries = rotate(qkv[:, :H].reshape(head_shape), cosine, sine_table).astype(bf16)
    keys_rot = rotate(qkv[:, H : 2 * H].reshape(head_shape), cosine, sine_table).astype(bf16)
    values = qkv[:, 2 * H :].astype(bf16).reshape(head_shape)
    score_scale = 1.0 / math.sqrt(head_width)
    scores = ein32("bqhd,bkhd->bhqk", queries, keys_rot) * score_scale
    scores = jnp.where(allowed[:, None], scores, masked_score)
    row_peak = jnp.max(scores, axis=-1, keepdims=True)
    log_total = row_peak + jnp.log(jnp.sum(jnp.exp(scores - row_peak), axis=-1, keepdims=True))
    attn_probs = jnp.exp(scores - log_total)
    probs_half = attn_probs.astype(bf16)
    context = ein32("bhqk,bkhd->bqhd", probs_half, values).astype(bf16)
    context_flat = context.reshape(B * T, H)

    def at_home(partial_rows, collective):
        if not fast:
            return partial_rows
        return plane_sum(partial_rows.astype(bf16).reshape(B, T, D), collective)

    residual_mid = residual_in + branch_scale * at_home(dot32(context_flat, full_output), 4)
    normed_mid, inverse_mid = rms_forward(residual_mid, gain_ffn)
    normed_mid_half = normed_mid.astype(bf16)

    logits = dot32(normed_mid_half, full_router)
    expert_ids = jnp.arange(experts)
    route_mask = (routes[:, :, None] == expert_ids[None, None, :]).astype(f32)
    chosen = jnp.sum(logits[:, None, :] * route_mask, axis=-1)
    gate_probs = jax.nn.softmax(chosen, axis=-1)
    flat_routes = routes.reshape(2 * T)
    hits = (flat_routes[:, None] == expert_ids[None, :]).astype(bf16)
    order = jnp.arange(2 * T)
    before = (order[:, None] > order[None, :]).astype(bf16)
    earlier = dot32(before, hits)
    slot_index = jnp.sum(earlier * hits.astype(f32), axis=1).astype(jnp.int32)
    target = (flat_routes * capacity + slot_index).reshape(T, 2)
    slot_ids = jnp.arange(slots)
    pick = [(target[:, k][:, None] == slot_ids[None, :]).astype(bf16) for k in range(2)]

    notes = jnp.concatenate([gate_probs, target.astype(f32), jnp.zeros((T, 4), f32)], axis=1)
    notes = jnp.pad(jnp.transpose(notes), ((0, 0), (0, -T % 128)))
    spread = spread_blocks if fast else spread_plain
    all_normed, all_notes = spread(nz, (normed_mid_half, notes), 2)
    devices = n_shard * n_exp
    flat_notes = all_notes.reshape(devices, 8, -1)[:, :, :T]
    wanted = (e_index * capacity + jnp.arange(capacity)).astype(f32)
    found = [flat_notes[:, 2 + k, None, :] == wanted[None, :, None] for k in range(2)]
    gate_rows = jnp.sum(
        jnp.where(found[0], flat_notes[:, 0, None, :], 0.0)
        + jnp.where(found[1], flat_notes[:, 1, None, :], 0.0),
        axis=-1,
    ).reshape(devices * capacity, 1)
    chosen_rows = (found[0] | found[1]).astype(bf16)

    def take(blocks):
        rows = ein32("spt,std->spd", chosen_rows, blocks.reshape(devices, T, D))
        return rows.astype(bf16).reshape(devices * capacity, D)

    arrived = take(all_normed)
    cotangent_rows = take(all_cotangent)
    grad_scale = gate_rows * branch_scale
    pre = dot32(arrived, w_pair)
    gate_part, up_part = pre[:, :Fp], pre[:, Fp:]
    sigmoid_gate = jax.nn.sigmoid(gate_part)
    silu_gate = gate_part * sigmoid_gate
    activated = (silu_gate * up_part).astype(bf16)
    out_sum = lax.psum_scatter(
        dot32(activated, down).astype(bf16), SHARD, scatter_dimension=0, tiled=True
    )
    back = lax.all_to_all(out_sum, "expert", split_axis=0, concat_axis=0, tiled=True)
    mixture = gate_probs[:, 0:1] * dot32(pick[0], back) + gate_probs[:, 1:2] * dot32(pick[1], back)
    activations = (residual_mid + branch_scale * mixture).astype(bf16)

    raw_grad = dot_dims(cotangent_rows, down, 1, 1)
    row_dots = branch_scale * jnp.sum(raw_grad * activated.astype(f32), axis=1)
    row_dots = row_dots.reshape(devices, capacity, 1)
    token_dots = [jnp.sum(jnp.where(found[k], row_dots, 0.0), axis=1) for k in range(2)]
    token_dots = jnp.stack(token_dots, axis=1).reshape(nz, 2, n_exp, 2, T)
    token_dots = jnp.pad(token_dots, ((0, 0),) * 3 + ((0, 6), (0, -T % 128)))
    act_grad = grad_scale * raw_grad
    pre_grad = jnp.concatenate(
        [
            act_grad * up_part * sigmoid_gate * (1.0 + gate_part * (1.0 - sigmoid_gate)),
            act_grad * silu_gate,
        ],
        axis=1,
    ).astype(bf16)
    in_rows = dot_dims(pre_grad, w_pair, 1, 1).astype(bf16)
    in_rows = in_rows.reshape(nz, 2, n_exp, capacity, D)
    collect = collect_rows if fast else collect_plain
    normed_mid_grad, gate_grad = collect(nz, in_rows, all_notes, token_dots, T)
    gate_grad = jnp.transpose(gate_grad[:2, :T])
    in_term = dot_dims(arrived, pre_grad, 0, 0).astype(bf16).reshape(n_shard, R, 2 * Fp)
    in_term, normed_mid_grad = lax.optimization_barrier((in_term, normed_mid_grad))
    in_term = lax.all_to_all(in_term, SHARD, split_axis=0, concat_axis=0, tiled=True)
    grad_w_in = unpack_columns(in_term, F)
    scaled = (grad_scale * activated.astype(f32)).astype(bf16)
    grad_w_down = lined_up(dot_dims(scaled[:, :F], cotangent_rows, 0, 0))

    upstream = cotangent.astype(f32)
    chosen_grad = gate_probs * (gate_grad - jnp.sum(gate_probs * gate_grad, axis=-1, keepdims=True))
    logit_grad = jnp.sum(chosen_grad[:, :, None] * route_mask, axis=1)
    normed_mid_grad = normed_mid_grad + jnp.dot(
        logit_grad, jnp.transpose(full_router.astype(f32)), precision=highest
    )
    router_grad = jnp.dot(
        jnp.transpose(normed_mid_half.astype(f32)), logit_grad, precision=highest
    )
    mid_norm_grad, gain_ffn_grad = rms_backward(
        residual_mid, inverse_mid, gain_ffn, normed_mid_grad
    )
    residual_grad = upstream + mid_norm_grad
    branch_grad = (branch_scale * residual_grad).astype(bf16)

    if fast:
        branch_grad = plane_gather(branch_grad, 5).reshape(B * T, D)
    output_grad = dot_dims(context_flat, branch_grad, 0, 0)
    context_grad = dot_dims(branch_grad, full_output, 1, 1).reshape(head_shape)
    row_delta = jnp.sum(context_grad * context.astype(f32), axis=-1)
    context_grad_half = context_grad.astype(bf16)
    probs_grad = ein32("bqhd,bkhd->bhqk", context_grad_half, values)
    scores_grad = (
        attn_probs * (probs_grad - jnp.transpose(row_delta, (0, 2, 1))[..., None]) * score_scale
    ).astype(bf16)
    queries_grad = ein32("bhqk,bkhd->bqhd", scores_grad, keys_rot)
    keys_grad = ein32("bhqk,bqhd->bkhd", scores_grad, queries)
    values_grad = ein32("bhqk,bqhd->bkhd", probs_half, context_grad_half)
    qkv_grad = jnp.concatenate(
        [
            rotate(queries_grad, cosine, -sine_table).reshape(B * T, H).astype(bf16),
            rotate(keys_grad, cosine, -sine_table).reshape(B * T, H).astype(bf16),
            values_grad.reshape(B * T, H).astype(bf16),
        ],
        axis=1,
    )
    qkv_weight_grad = dot_dims(normed_half, qkv_grad, 0, 0)
    near_grad = dot_dims(qkv_grad, full_qkv, 1, 1)
    gain_attn_grad = jnp.sum(near_grad * near_in * near_inverse, axis=0)
    in_norm_grad = rms_backward(residual_in, inverse_in, gain_attn, at_home(near_grad, 6))[0]
    grad_tokens = residual_grad + in_norm_grad

    small_grad = jnp.concatenate(
        [router_grad, gain_attn_grad[:, None], gain_ffn_grad[:, None]], axis=1
    )
    small_grad = jnp.pad(small_grad, ((0, 0), (0, 128 - small_grad.shape[1])))
    sum_query, sum_key, sum_value, sum_output, small_sum = settle(
        nz, fast, qkv_weight_grad, output_grad, small_grad
    )
    return (
        activations,
        grad_tokens,
        small_sum[:, experts],
        sum_query,
        sum_key,
        sum_value,
        sum_output,
        small_sum[:, experts + 1],
        small_sum[:, :experts],
        grad_w_in,
        grad_w_down,
    )


def solution(mesh):
    n_expert, n_shard = mesh.devices.shape
    chips = Mesh(mesh.devices.reshape(n_expert, n_shard // 2, 2), ("expert", "z", "core"))
    rows = P(("expert", "z", "core"), None)
    shard = P(SHARD)
    shard2 = P(SHARD, None)
    shard3 = P(SHARD, "expert", None)
    in_specs = (
        rows,
        rows,
        rows,
        shard,
        shard2,
        shard2,
        shard2,
        shard2,
        shard,
        shard2,
        shard3,
        shard3,
        rows,
    )
    out_specs = (
        rows,
        rows,
        shard,
        shard2,
        shard2,
        shard2,
        shard2,
        shard,
        shard2,
        shard3,
        shard3,
    )
    return jax.shard_map(
        on_device, mesh=chips, in_specs=in_specs, out_specs=out_specs, check_vma=False
    )
```

```python
import functools
import math

import jax
import jax.numpy as jnp
from jax import lax
from jax.experimental import pallas as pl
from jax.experimental.pallas import tpu as pltpu
from jax.sharding import Mesh, PartitionSpec as P

HEADS = 36

eps_norm = 1e-05
branch_scale = 1.4 / math.sqrt(40.0)
rope_base = 10000.0
masked_score = -1e30
bf16 = jnp.bfloat16
f32 = jnp.float32
SHARD = ("z", "core")
ANY = pl.BlockSpec(memory_space=pl.ANY)


def place():
    e, z, c = lax.axis_index("expert"), lax.axis_index("z"), lax.axis_index("core")
    across_x = e + 1 - 2 * (e % 2)
    across_y = (e + 2) % 4
    return e, z, c, across_x, across_y


def remote(src, dst, send, recv, e, z, c):
    return pltpu.make_async_remote_copy(
        src_ref=src,
        dst_ref=dst,
        send_sem=send,
        recv_sem=recv,
        device_id=(e, z, c),
        device_id_type=pl.DeviceIdType.MESH,
    )


def payload_stream(nz, ref, out, sems, split):
    zrecv, zsend, near_recv, near_send, far_recv, far_send, sib_recv, sib_send, own = sems
    e, z, c, ex, ey = place()
    diagonal = (ex + 2) % 4
    T = ref.shape[0]
    S = 2 * nz - 1

    def split_step(s):
        return (s - 1) % 2, (s - 1) // 2

    def where(s):
        if s == 0:
            return z
        side, i = split_step(s)
        return z - 1 - i if side == 0 else z + 1 + i

    def exists(s):
        if s == 0:
            return z >= 0
        zz = where(s)
        return (zz >= 0) & (zz < nz)

    def slab(s, quarter, r0=0, n=T):
        return out.at[where(s), c, quarter, pl.ds(r0, n), :]

    def first(step):
        side = 0 if step > 0 else 1
        return remote(ref, slab(0, e), zsend.at[side, nz - 1], zrecv.at[side, 0], e, z + step, c)

    def onward(s):
        side, i = split_step(s)
        step = 1 if side == 0 else -1
        return remote(
            slab(s, e), slab(s, e), zsend.at[side, i], zrecv.at[side, i + 1], e, z + step, c
        )

    def near(s, axis):
        source = ref if s == 0 else slab(s, e)
        return remote(
            source, slab(s, e), near_send.at[s, axis], near_recv.at[s, axis],
            ex if axis == 0 else ey, z, c,
        )

    def near_wait(s, axis):
        view = slab(s, ex if axis == 0 else ey)
        remote(view, view, near_send.at[s, axis], near_recv.at[s, axis], ex, z, c).wait_recv()

    axes = range(2) if split else range(1)

    def far_view(s, quarter, axis):
        if not split:
            return slab(s, quarter)
        return slab(s, quarter, 0, split) if axis == 0 else slab(s, quarter, split, T - split)

    def far(s, axis):
        view = far_view(s, ex if axis == 0 else ey, axis)
        return remote(
            view, view, far_send.at[s, axis], far_recv.at[s, axis],
            ey if axis == 0 else ex, z, c,
        )

    def far_wait(s, axis):
        view = far_view(s, diagonal, axis)
        remote(view, view, far_send.at[s, axis], far_recv.at[s, axis], ex, z, c).wait_recv()

    def beside(s, n):
        quarter = (e, ex, ey, diagonal)[n]
        source = ref if s == 0 and n == 0 else slab(s, quarter)
        return remote(
            source, slab(s, quarter), sib_send.at[s, n], sib_recv.at[s, n], e, z, 1 - c
        )

    def beside_wait(s, n):
        view = out.at[where(s), 1 - c, (e, ex, ey, diagonal)[n]]
        remote(view, view, sib_send.at[s, n], sib_recv.at[s, n], e, z, c).wait_recv()

    def inside(side):
        return z < nz - 1 if side == 0 else z > 0

    def begin():
        for step in (1, -1):

            @pl.when((z + step >= 0) & (z + step < nz))
            def _():
                first(step).start()

        near(0, 0).start()
        near(0, 1).start()
        beside(0, 0).start()
        pltpu.make_async_copy(ref, slab(0, e), own).start()

    def arrive(s):
        if s == 0:
            return

        @pl.when(exists(s))
        def _():
            side, i = split_step(s)
            remote(
                slab(s, e), slab(s, e), zsend.at[side, i], zrecv.at[side, i], e, z, c
            ).wait_recv()
            if i < nz - 2:

                @pl.when(inside(side))
                def _():
                    onward(s).start()

            near(s, 0).start()
            near(s, 1).start()
            beside(s, 0).start()

    def relay(s):
        @pl.when(exists(s))
        def _():
            near_wait(s, 0)
            far(s, 0).start()
            beside(s, 1).start()
            near_wait(s, 1)
            if split:
                far(s, 1).start()
            beside(s, 2).start()

    def close(s):
        @pl.when(exists(s))
        def _():
            for axis in axes:
                far_wait(s, axis)
            beside(s, 3).start()

    def end(s):
        @pl.when(exists(s))
        def _():
            for axis in range(2):
                near(s, axis).wait_send()
            for axis in axes:
                far(s, axis).wait_send()
            for n in range(4):
                beside(s, n).wait_send()
                beside_wait(s, n)
            if s > 0 and split_step(s)[1] < nz - 2:

                @pl.when(inside(split_step(s)[0]))
                def _():
                    onward(s).wait_send()

        if s == 0:
            for step in (1, -1):

                @pl.when((z + step >= 0) & (z + step < nz))
                def _():
                    first(step).wait_send()

            pltpu.make_async_copy(ref, slab(0, e), own).wait()

    return begin, arrive, relay, close, end


def payload_sems(nz):
    dma = pltpu.SemaphoreType.DMA
    S = 2 * nz - 1
    return [
        dma((2, nz)), dma((2, nz)), dma((S, 2)), dma((S, 2)), dma((S, 2)), dma((S, 2)),
        dma((S, 4)), dma((S, 4)), dma(()),
    ]


def spread_kernel(nz, splits, *refs):
    n = len(splits)
    ins, outs, sems = refs[:n], refs[n : 2 * n], refs[2 * n :]
    greet_cross(nz)
    streams = [
        payload_stream(nz, ins[i], outs[i], sems[9 * i : 9 * i + 9], splits[i]) for i in range(n)
    ]
    for t in streams:
        t[0]()
    S = 2 * nz - 1
    for s in range(S):
        for t in streams:
            t[1](s)
        if s >= 1:
            for t in streams:
                t[2](s - 1)
        if s >= 2:
            for t in streams:
                t[3](s - 2)
    for t in streams:
        t[2](S - 1)
    for s in (S - 2, S - 1):
        for t in streams:
            t[3](s)
    for s in range(S):
        for t in streams:
            t[4](s)


def spread_blocks(nz, blocks, collective):
    sd = jax.ShapeDtypeStruct
    splits = tuple(b.shape[0] // 2 if b.shape[0] % 32 == 0 else 0 for b in blocks)
    return pl.pallas_call(
        functools.partial(spread_kernel, nz, splits),
        out_shape=tuple(sd((nz, 2, 4) + b.shape, b.dtype) for b in blocks),
        in_specs=[ANY] * len(blocks),
        out_specs=(ANY,) * len(blocks),
        scratch_shapes=[s for _ in blocks for s in payload_sems(nz)],
        compiler_params=pltpu.CompilerParams(collective_id=collective, has_side_effects=True),
        cost_estimate=pl.CostEstimate(
            flops=10**6, bytes_accessed=10**6, transcendentals=0
        ),
        name="spread_blocks",
    )(*blocks)


def line_order(nz, z):
    def order(i):
        code = 0
        for zz in range(nz):
            far_first = sorted(range(nz), key=lambda t: (-abs(t - zz), t))
            code += far_first[i] * nz**zz
        power = 1
        for zz in range(nz):
            power = power + (nz**zz - 1) * jnp.where(z == zz, 1, 0)
        return (code // power) % nz

    return [order(i) for i in range(nz)]


def collect_kernel(
    nz, cap,
    rows_ref, notes_ref, dots_ref,
    out_ref, dots_out,
    dots, notes, mine, theirs, block, from_x, from_y, via_x, via_y, from_z,
    note_sem, load, sib_send, sib_recv, via_send, via_recv, plain_send, plain_recv,
    sum_send, sum_recv, zsend, zrecv, dot_send, dot_recv, dot_own,
):
    e, z, c, ex, ey = place()
    diagonal = (ex + 2) % 4
    T, D = out_ref.shape
    h = T // 2
    dest = line_order(nz, z)
    who = (diagonal, ex, ey, e)

    def others():
        for d in range(1, 8 * nz):
            to = ((e * nz + z) * 2 + c + d) % (8 * nz)
            yield d, to // (2 * nz), to // 2 % nz, to % 2

    barrier = pltpu.get_barrier_semaphore()
    for _, te, tz, tc in others():
        pl.semaphore_signal(
            barrier, inc=1, device_id=(te, tz, tc), device_id_type=pl.DeviceIdType.MESH
        )
    pl.semaphore_wait(barrier, 8 * nz - 1)

    def dot(d, te, tz, tc):
        return remote(
            dots_ref.at[tz, tc, te], dots.at[d], dot_send.at[d], dot_recv.at[d], te, tz, tc
        )

    dot_kept = pltpu.make_async_copy(dots_ref.at[z, c, e], dots.at[0], dot_own)
    dot_kept.start()
    for d, te, tz, tc in others():
        dot(d, te, tz, tc).start()

    note_copy = pltpu.make_async_copy(notes_ref, notes, note_sem)
    note_copy.start()

    def fetch(i, q):
        return pltpu.make_async_copy(
            rows_ref.at[dest[i], c, who[q]], mine.at[i, q], load.at[i, q]
        )

    def hand(i, q):
        return remote(
            rows_ref.at[dest[i], 1 - c, who[q]], theirs.at[i, q],
            sib_send.at[i, q], sib_recv.at[i, q], e, z, 1 - c,
        )

    for i in range(nz):
        for q in range(4):
            hand(i, q).start()
            fetch(i, q).start()
    note_copy.wait()

    def open_out(i, q):
        fetch(i, q).wait()
        hand(i, q).wait_recv()
        places = (lax.broadcasted_iota(jnp.int32, (cap, T), 0) + e * cap).astype(f32)
        note = notes[dest[i], c, who[q]]
        pick = ((note[2:3, :] == places) | (note[3:4, :] == places)).astype(bf16)
        wide = 768 if D % 768 == 0 else 128

        @pl.loop(0, D // wide)
        def _(b):
            cols = pl.ds(pl.multiple_of(b * wide, 128), wide)
            both = mine[i, q, :, cols].astype(f32) + theirs[i, q, :, cols].astype(f32)
            block[i, q, :, cols] = lax.dot_general(
                pick, both.astype(bf16), (((0,), (0,)), ((), ())), preferred_element_type=f32
            ).astype(bf16)

    def via(i, axis):
        if axis == 0:
            return remote(
                block.at[i, 0, pl.ds(0, h), :], via_x.at[i],
                via_send.at[i, 0], via_recv.at[i, 0], ex, z, c,
            )
        return remote(
            block.at[i, 0, pl.ds(h, h), :], via_y.at[i],
            via_send.at[i, 1], via_recv.at[i, 1], ey, z, c,
        )

    def plain(i, axis):
        if axis == 0:
            return remote(
                block.at[i, 1, pl.ds(0, h), :], from_x.at[i, pl.ds(0, h), :],
                plain_send.at[i, 0], plain_recv.at[i, 0], ex, z, c,
            )
        return remote(
            block.at[i, 2, pl.ds(h, h), :], from_y.at[i, pl.ds(h, h), :],
            plain_send.at[i, 1], plain_recv.at[i, 1], ey, z, c,
        )

    def summed(i, axis):
        if axis == 0:
            return remote(
                block.at[i, 1, pl.ds(h, h), :], from_x.at[i, pl.ds(h, h), :],
                sum_send.at[i, 0], sum_recv.at[i, 0], ex, z, c,
            )
        return remote(
            block.at[i, 2, pl.ds(0, h), :], from_y.at[i, pl.ds(0, h), :],
            sum_send.at[i, 1], sum_recv.at[i, 1], ey, z, c,
        )

    def add(target, others, n):
        @pl.loop(0, n // 16)
        def _(b):
            rows = pl.ds(pl.multiple_of(b * 16, 16), 16)
            acc = target[rows, :].astype(f32)
            for o in others:
                acc = acc + o[rows, :].astype(f32)
            target[rows, :] = acc.astype(target.dtype)

    def start(i):
        open_out(i, 0)
        via(i, 0).start()
        via(i, 1).start()
        open_out(i, 1)
        plain(i, 0).start()
        open_out(i, 2)
        plain(i, 1).start()
        open_out(i, 3)

    def combine(i):
        via(i, 0).wait_recv()
        add(block.at[i, 2, pl.ds(0, h), :], [via_x.at[i]], h)
        summed(i, 1).start()
        via(i, 1).wait_recv()
        add(block.at[i, 1, pl.ds(h, h), :], [via_y.at[i]], h)
        summed(i, 0).start()

    def zcopy(i):
        step = jnp.where(dest[i] > z, 1, -1)
        side = jnp.where(dest[i] > z, 0, 1)
        return remote(
            block.at[i, 3], from_z.at[side, dest[i]],
            zsend.at[i], zrecv.at[side, dest[i]], e, z + step, c,
        )

    def zwait(side, zz):
        slab = from_z.at[side, zz]
        remote(slab, slab, zsend.at[0], zrecv.at[side, zz], e, z, c).wait_recv()

    def finish(i):
        for axis in range(2):
            plain(i, axis).wait_recv()
            summed(i, axis).wait_recv()
        zz = dest[i]
        if i < nz - 1:
            add(block.at[i, 3], [from_x.at[i], from_y.at[i]], T)
            for side in range(2):
                going = zz > z if side == 0 else zz < z
                behind = z > 0 if side == 0 else z < nz - 1

                @pl.when(going & behind)
                def _():
                    zwait(side, zz)
                    add(block.at[i, 3], [from_z.at[side, zz]], T)

            zcopy(i).start()
            return

        @pl.loop(0, T // 16)
        def _(b):
            rows = pl.ds(pl.multiple_of(b * 16, 16), 16)
            acc = block[i, 3, rows, :].astype(f32) + from_x[i, rows, :].astype(f32)
            out_ref[rows, :] = acc + from_y[i, rows, :].astype(f32)

        for side in range(2):

            @pl.when(z > 0 if side == 0 else z < nz - 1)
            def _():
                zwait(side, z)
                add(out_ref, [from_z.at[side, z]], T)

    for i in range(nz):
        start(i)
        if i >= 1:
            combine(i - 1)
        if i >= 2:
            finish(i - 2)
    combine(nz - 1)
    if nz >= 2:
        finish(nz - 2)
    finish(nz - 1)

    dot_kept.wait()
    for d, te, tz, tc in others():
        dot(d, te, tz, tc).wait_recv()
        dot(d, te, tz, tc).wait_send()
    dots_out[...] = jnp.sum(dots[...], axis=0)

    for i in range(nz):
        for q in range(4):
            hand(i, q).wait_send()
        for axis in range(2):
            via(i, axis).wait_send()
            plain(i, axis).wait_send()
            summed(i, axis).wait_send()
        if i < nz - 1:
            zcopy(i).wait_send()


def collect_rows(nz, rows, notes, dots, T):
    cap, D = rows.shape[3:]
    dma = pltpu.SemaphoreType.DMA
    vm = pltpu.VMEM
    return pl.pallas_call(
        functools.partial(collect_kernel, nz, cap),
        out_shape=(
            jax.ShapeDtypeStruct((T, D), f32),
            jax.ShapeDtypeStruct(dots.shape[3:], f32),
        ),
        in_specs=[ANY] * 3,
        out_specs=(pl.BlockSpec(memory_space=pltpu.VMEM),) * 2,
        scratch_shapes=[
            vm((8 * nz,) + dots.shape[3:], f32),
            vm(notes.shape, f32),
            vm((nz, 4, cap, D), bf16),
            vm((nz, 4, cap, D), bf16),
            vm((nz, 4, T, D), bf16),
            vm((nz, T, D), bf16),
            vm((nz, T, D), bf16),
            vm((nz, T // 2, D), bf16),
            vm((nz, T // 2, D), bf16),
            vm((2, nz, T, D), bf16),
            dma(()),
            dma((nz, 4)),
            dma((nz, 4)),
            dma((nz, 4)),
            dma((nz, 2)),
            dma((nz, 2)),
            dma((nz, 2)),
            dma((nz, 2)),
            dma((nz, 2)),
            dma((nz, 2)),
            dma((nz,)),
            dma((2, nz)),
            dma((8 * nz,)),
            dma((8 * nz,)),
            dma(()),
        ],
        compiler_params=pltpu.CompilerParams(
            collective_id=3, has_side_effects=True, vmem_limit_bytes=56 << 20
        ),
        cost_estimate=pl.CostEstimate(
            flops=5 * 10**10, bytes_accessed=2 * rows.size, transcendentals=0
        ),
        name="collect_rows",
    )(rows, notes, dots)


def pack_kernel(n, F, Fp, x_ref, o_ref):
    half = n * F
    rows = x_ref.shape[0]
    for i in range(n):
        for part in range(2):
            cols = x_ref[:, part * half + i * F : part * half + (i + 1) * F]
            if Fp > F:
                cols = jnp.concatenate([cols, jnp.zeros((rows, Fp - F), cols.dtype)], axis=1)
            o_ref[i, :, part * Fp : (part + 1) * Fp] = cols


def pack_columns(w, n, F, Fp):
    rows = w.shape[0]
    block = 16
    return pl.pallas_call(
        functools.partial(pack_kernel, n, F, Fp),
        grid=(rows // block,),
        in_specs=[pl.BlockSpec((block, w.shape[1]), lambda i: (i, 0))],
        out_specs=pl.BlockSpec((n, block, 2 * Fp), lambda i: (0, i, 0)),
        out_shape=jax.ShapeDtypeStruct((n, rows, 2 * Fp), w.dtype),
        name="pack_columns",
    )(w)


def unpack_kernel(n, F, Fp, x_ref, o_ref, line):
    half = n * F
    rows = line.shape[0]
    for i in range(n):
        for part in range(2):
            cols = x_ref[i, :, part * Fp : part * Fp + F].astype(f32)
            line[:, part * half + i * F : part * half + (i + 1) * F] = cols
    tiles = 2 * half // 128
    for j in range(tiles):
        o_ref[pl.ds(j, rows, stride=tiles), :] = line[:, j * 128 : (j + 1) * 128]


def unpack_columns(x, F):
    n, rows, Fp2 = x.shape
    block = 16
    width = 2 * n * F
    tiles = width // 128
    flat = pl.pallas_call(
        functools.partial(unpack_kernel, n, F, Fp2 // 2),
        grid=(rows // block,),
        in_specs=[pl.BlockSpec((n, block, Fp2), lambda i: (0, i, 0))],
        out_specs=pl.BlockSpec((block * tiles, 128), lambda i: (i, 0)),
        out_shape=jax.ShapeDtypeStruct((rows * tiles, 128), f32),
        scratch_shapes=[pltpu.VMEM((block, width), f32)],
        name="unpack_columns",
    )(x)
    return flat.reshape(rows, 1, width)


def line_kernel(x_ref, o_ref):
    rows, width = x_ref.shape
    tiles = width // 128
    for j in range(tiles):
        o_ref[pl.ds(j, rows, stride=tiles), :] = x_ref[:, j * 128 : (j + 1) * 128]


def lined_up(x):
    rows, width = x.shape
    tiles = width // 128
    block = 80 if rows % 80 == 0 else 8
    flat = pl.pallas_call(
        line_kernel,
        grid=(rows // block,),
        in_specs=[pl.BlockSpec((block, width), lambda i: (i, 0))],
        out_specs=pl.BlockSpec((block * tiles, 128), lambda i: (i, 0)),
        out_shape=jax.ShapeDtypeStruct((rows * tiles, 128), x.dtype),
        name="lined_up",
    )(x)
    return flat.reshape(rows, 1, width)


def greet_cross(nz):
    e, z, c, ex, ey = place()
    barrier = pltpu.get_barrier_semaphore()

    def hail(te, tz, tc):
        pl.semaphore_signal(
            barrier, inc=1, device_id=(te, tz, tc), device_id_type=pl.DeviceIdType.MESH
        )

    hail(e, z, 1 - c)
    for te in (ex, ey, (ex + 2) % 4):
        hail(te, z, c)
    for step in (-1, 1):

        @pl.when((z + step >= 0) & (z + step < nz))
        def _():
            hail(e, z + step, c)

    pl.semaphore_wait(barrier, 4 + jnp.where(z > 0, 1, 0) + jnp.where(z < nz - 1, 1, 0))


def line_stream(nz, ref, out, zrecv, zsend, sib_recv, sib_send, own):
    e, z, c, _, _ = place()

    def split_step(s):
        return (s - 1) % 2, (s - 1) // 2

    def where(s):
        if s == 0:
            return z
        side, i = split_step(s)
        return z - 1 - i if side == 0 else z + 1 + i

    def exists(s):
        return (where(s) >= 0) & (where(s) < nz)

    def inside(side):
        return z < nz - 1 if side == 0 else z > 0

    def slab(s):
        return out.at[where(s), c]

    def first(side):
        step = 1 if side == 0 else -1
        return remote(ref, slab(0), zsend.at[side, nz - 1], zrecv.at[side, 0], e, z + step, c)

    def onward(s):
        side, i = split_step(s)
        step = 1 if side == 0 else -1
        return remote(
            slab(s), slab(s), zsend.at[side, i], zrecv.at[side, i + 1], e, z + step, c
        )

    def beside(s):
        return remote(
            ref if s == 0 else slab(s), slab(s), sib_send.at[s], sib_recv.at[s], e, z, 1 - c
        )

    def begin():
        for side in range(2):

            @pl.when(inside(side))
            def _():
                first(side).start()

        beside(0).start()
        pltpu.make_async_copy(ref, slab(0), own).start()

    def arrive(s):
        side, i = split_step(s)

        @pl.when(exists(s))
        def _():
            remote(slab(s), slab(s), zsend.at[side, i], zrecv.at[side, i], e, z, c).wait_recv()
            if i < nz - 2:

                @pl.when(inside(side))
                def _():
                    onward(s).start()

            beside(s).start()

    def end():
        for s in range(2 * nz - 1):

            @pl.when(exists(s))
            def _():
                beside(s).wait_send()
                view = out.at[where(s), 1 - c]
                remote(view, view, sib_send.at[s], sib_recv.at[s], e, z, c).wait_recv()
                if s > 0 and split_step(s)[1] < nz - 2:

                    @pl.when(inside(split_step(s)[0]))
                    def _():
                        onward(s).wait_send()

        for side in range(2):

            @pl.when(inside(side))
            def _():
                first(side).wait_send()

        pltpu.make_async_copy(ref, slab(0), own).wait()

    return begin, arrive, end


def line_sems(nz):
    dma = pltpu.SemaphoreType.DMA
    S = 2 * nz - 1
    return [dma((2, nz)), dma((2, nz)), dma((S,)), dma((S,)), dma(())]


def plane_stream(source, views, send, recv, own):
    e, z, c, ex, ey = place()
    peers = (ex, ey, (ex + 2) % 4)

    def copy(n):
        return remote(source, views(e), send.at[n], recv.at[n], peers[n], z, c)

    def kept():
        return pltpu.make_async_copy(source, views(e), own)

    def begin():
        for n in range(3):
            copy(n).start()
        kept().start()

    def end():
        kept().wait()
        for n in range(3):
            view = views(peers[n])
            remote(view, view, send.at[n], recv.at[n], e, z, c).wait_recv()
            copy(n).wait_send()

    return begin, end


def plane_sems():
    dma = pltpu.SemaphoreType.DMA
    return [dma((3,)), dma((3,)), dma(())]


def fetch_kernel(
    nz,
    w_ref, s_ref, o_ref, t_ref, l_ref, p_ref,
    w_out, s_out, o_out, t_out, l_out, p_out,
    *sems,
):
    e, z, c, ex, ey = place()
    w_sems, sems = sems[:5], sems[5:]
    s_sems, sems = sems[:5], sems[5:]
    t_sems, sems = sems[:3], sems[3:]
    l_sems, sems = sems[:3], sems[3:]
    p_sems, sems = sems[:9], sems[9:]
    orecv, osend, sib_recv, sib_send, own = sems
    greet_cross(nz)
    w_begin, w_arrive, w_end = line_stream(nz, w_ref, w_out, *w_sems)
    s_begin, s_arrive, s_end = line_stream(nz, s_ref, s_out, *s_sems)
    t_begin, t_end = plane_stream(t_ref, lambda q: t_out.at[q], *t_sems)
    l_begin, l_end = plane_stream(l_ref, lambda q: l_out.at[q], *l_sems)
    p_begin, p_arrive, p_relay, p_close, p_end = payload_stream(
        nz, p_ref, p_out, p_sems, p_ref.shape[0] // 2
    )

    pieces = orecv.shape[0]
    height = o_ref.shape[0] // pieces

    def o_part(n):
        return pl.ds(n * height, height)

    def o_view(n):
        return o_out.at[c, o_part(n), :]

    def o_copy(side, n, source):
        step = 1 if side == 0 else -1
        return remote(source, o_view(n), osend.at[side, n], orecv.at[n], e, z + step, c)

    def o_beside(n, source):
        return remote(source, o_view(n), sib_send.at[n], sib_recv.at[n], e, z, 1 - c)

    def o_goes(side):
        return (z >= e) & (z < nz - 1) if side == 0 else (z <= e) & (z > 0)

    def o_pass(n, source):
        for side in range(2):

            @pl.when(o_goes(side))
            def _():
                o_copy(side, n, source).start()

        o_beside(n, source).start()

    def o_arrive(n):
        @pl.when(z != e)
        def _():
            remote(o_view(n), o_view(n), sib_send.at[n], orecv.at[n], e, z, c).wait_recv()
            o_pass(n, o_view(n))

    p_begin()

    @pl.when(z == e)
    def _():
        for n in range(pieces):
            o_pass(n, o_ref.at[o_part(n), :])
        pltpu.make_async_copy(o_ref, o_out.at[c], own).start()

    s_begin()
    w_begin()
    t_begin()
    l_begin()

    blocks = 2 * nz - 1
    for s in range(1, blocks):
        p_arrive(s)
        s_arrive(s)
        if s <= pieces:
            o_arrive(s - 1)
    for n in range(blocks - 1, pieces):
        o_arrive(n)
    for s in range(1, blocks):
        p_relay(s - 1)
        w_arrive(s)
        if s >= 2:
            p_close(s - 2)
    p_relay(blocks - 1)
    p_close(blocks - 2)
    p_close(blocks - 1)
    for s in range(blocks):
        p_end(s)
    w_end()
    s_end()
    t_end()
    l_end()
    for n in range(pieces):
        view = o_out.at[1 - c, o_part(n), :]
        remote(view, view, sib_send.at[n], sib_recv.at[n], e, z, c).wait_recv()
        o_beside(n, o_view(n)).wait_send()
        for side in range(2):

            @pl.when(o_goes(side))
            def _():
                o_copy(side, n, o_view(n)).wait_send()

    @pl.when(z == e)
    def _():
        pltpu.make_async_copy(o_ref, o_out.at[c], own).wait()


def fetch_weights(nz, columns, small, rows, tokens, lengths, block):
    dma = pltpu.SemaphoreType.DMA
    sd = jax.ShapeDtypeStruct
    return pl.pallas_call(
        functools.partial(fetch_kernel, nz),
        out_shape=(
            sd((nz, 2) + columns.shape, bf16),
            sd((nz, 2) + small.shape, bf16),
            sd((2,) + rows.shape, bf16),
            sd((4,) + tokens.shape, bf16),
            sd((4,) + lengths.shape, lengths.dtype),
            sd((nz, 2, 4) + block.shape, block.dtype),
        ),
        in_specs=[ANY] * 6,
        out_specs=(ANY,) * 6,
        scratch_shapes=[
            *line_sems(nz), *line_sems(nz), *plane_sems(), *plane_sems(), *payload_sems(nz),
            dma((6,)), dma((2, 6)), dma((6,)), dma((6,)), dma(()),
        ],
        compiler_params=pltpu.CompilerParams(collective_id=0, has_side_effects=True),
        cost_estimate=pl.CostEstimate(
            flops=10**11, bytes_accessed=8 * columns.size, transcendentals=0
        ),
        name="fetch_weights",
    )(columns, small, rows, tokens, lengths, block)


def plane_gather_kernel(x_ref, out_ref, send, recv, own):
    e, z, c, ex, ey = place()
    greet_plane()
    begin, end = plane_stream(x_ref, lambda q: out_ref.at[q], send, recv, own)
    begin()
    end()


def greet_plane():
    e, z, c, ex, ey = place()
    barrier = pltpu.get_barrier_semaphore()
    for te in (ex, ey, (ex + 2) % 4):
        pl.semaphore_signal(
            barrier, inc=1, device_id=(te, z, c), device_id_type=pl.DeviceIdType.MESH
        )
    pl.semaphore_wait(barrier, 3)


def plane_gather(x, collective):
    return pl.pallas_call(
        plane_gather_kernel,
        out_shape=jax.ShapeDtypeStruct((4,) + x.shape, x.dtype),
        in_specs=[ANY],
        out_specs=ANY,
        scratch_shapes=plane_sems(),
        compiler_params=pltpu.CompilerParams(collective_id=collective, has_side_effects=True),
        cost_estimate=pl.CostEstimate(flops=10**6, bytes_accessed=10**6, transcendentals=0),
        name="plane_gather",
    )(x)


def plane_sum_kernel(x_ref, out_ref, held, send, recv, own):
    e, z, c, ex, ey = place()
    peers = (ex, ey, (ex + 2) % 4)
    greet_plane()

    def copy(n):
        return remote(x_ref.at[peers[n]], held.at[n], send.at[n], recv.at[n], peers[n], z, c)

    for n in (2, 0, 1):
        copy(n).start()
    kept = pltpu.make_async_copy(x_ref.at[e], held.at[3], own)
    kept.start()
    kept.wait()
    for n in range(3):
        copy(n).wait_recv()

    @pl.loop(0, out_ref.shape[0] // 16)
    def _(b):
        rows = pl.ds(pl.multiple_of(b * 16, 16), 16)
        acc = held[3, rows, :].astype(f32) + held[0, rows, :].astype(f32)
        acc = acc + held[1, rows, :].astype(f32)
        out_ref[rows, :] = acc + held[2, rows, :].astype(f32)

    for n in range(3):
        copy(n).wait_send()


def plane_sum(x, collective):
    vm = pltpu.VMEM
    return pl.pallas_call(
        plane_sum_kernel,
        out_shape=jax.ShapeDtypeStruct(x.shape[1:], f32),
        in_specs=[ANY],
        out_specs=pl.BlockSpec(memory_space=vm),
        scratch_shapes=[vm(x.shape, bf16), *plane_sems()],
        compiler_params=pltpu.CompilerParams(collective_id=collective, has_side_effects=True),
        cost_estimate=pl.CostEstimate(flops=10**6, bytes_accessed=10**6, transcendentals=0),
        name="plane_sum",
    )(x)


def settle_kernel(
    nz,
    g_ref, s_ref, o_ref,
    g_out, s_out, o_out,
    g_mine, g_sib, g_z, s_mine, s_sib, s_z, o_mine, o_sib, o_z,
    load, sib_send, sib_recv, zsend, zrecv,
    o_load, o_sib_send, o_sib_recv, o_zsend, o_zrecv,
    o_send, o_recv, o_own,
    *sems,
):
    e, z, c, ex, ey = place()
    peers = (ex, ey, (ex + 2) % 4)
    dest = line_order(nz, z)
    greet_cross(nz)
    W = g_ref.shape[3]
    first = W // 256 * 128
    groups = (
        (g_ref, g_mine, g_sib, g_z, g_out, pl.ds(0, first)),
        (g_ref, g_mine, g_sib, g_z, g_out, pl.ds(first, W - first)),
        (s_ref, s_mine, s_sib, s_z, s_out, pl.ds(0, s_ref.shape[3])),
    )
    K = len(groups)

    def part(k, which, *index):
        return groups[k][which].at[(*index, slice(None), groups[k][5])]

    def fetch(k, i):
        return pltpu.make_async_copy(
            part(k, 0, dest[i], c), part(k, 1, i), load.at[k, i]
        )

    def hand(k, i):
        return remote(
            part(k, 0, dest[i], 1 - c), part(k, 2, i),
            sib_send.at[k, i], sib_recv.at[k, i], e, z, 1 - c,
        )

    def zcopy(k, i):
        step = jnp.where(dest[i] > z, 1, -1)
        side = jnp.where(dest[i] > z, 0, 1)
        return remote(
            part(k, 1, i), part(k, 3, side, dest[i]),
            zsend.at[k, i], zrecv.at[k, side, dest[i]], e, z + step, c,
        )

    def zwait(k, side, zz):
        slab = part(k, 3, side, zz)
        remote(slab, slab, zsend.at[k, 0], zrecv.at[k, side, zz], e, z, c).wait_recv()

    def add(target, others):
        @pl.loop(0, target.shape[0] // 16)
        def _(b):
            rows = pl.ds(pl.multiple_of(b * 16, 16), 16)
            acc = target[rows, :].astype(f32)
            for o in others:
                acc = acc + o[rows, :].astype(f32)
            target[rows, :] = acc.astype(target.dtype)

    pieces = o_load.shape[0]
    height = o_mine.shape[0] // pieces

    def o_part(n):
        return pl.ds(n * height, height)

    def o_fetch(n):
        return pltpu.make_async_copy(o_ref.at[c, o_part(n), :], o_mine.at[o_part(n), :], o_load.at[n])

    def o_hand(n):
        return remote(
            o_ref.at[1 - c, o_part(n), :], o_sib.at[o_part(n), :],
            o_sib_send.at[n], o_sib_recv.at[n], e, z, 1 - c,
        )

    def o_line(n):
        step, side = jnp.where(z < e, 1, -1), jnp.where(z < e, 0, 1)
        return remote(
            o_mine.at[o_part(n), :], o_z.at[side, o_part(n), :],
            o_zsend.at[n], o_zrecv.at[side, n], e, z + step, c,
        )

    def o_wait(side, n):
        slab = o_z.at[side, o_part(n), :]
        remote(slab, slab, o_zsend.at[n], o_zrecv.at[side, n], e, z, c).wait_recv()
        add(o_mine.at[o_part(n), :], [slab])

    def o_peer(p, n):
        view = o_out.at[o_part(n), :]
        return remote(
            o_mine.at[o_part(n), :], view, o_send.at[p, n], o_recv.at[n], peers[p], z, c
        )

    def o_kept():
        return pltpu.make_async_copy(o_mine, o_out, o_own)

    for i in range(nz):
        for k in range(K):
            hand(k, i).start()
            fetch(k, i).start()
        if i == 0:
            for n in range(pieces):
                o_fetch(n).start()
                o_hand(n).start()

    def finish(k, i):
        fetch(k, i).wait()
        hand(k, i).wait_recv()
        zz = dest[i]
        add(part(k, 1, i), [part(k, 2, i)])
        if i < nz - 1:
            for side in range(2):
                going = zz > z if side == 0 else zz < z
                behind = z > 0 if side == 0 else z < nz - 1

                @pl.when(going & behind)
                def _():
                    zwait(k, side, zz)
                    add(part(k, 1, i), [part(k, 3, side, zz)])

            zcopy(k, i).start()
            return
        for side in range(2):

            @pl.when(z > 0 if side == 0 else z < nz - 1)
            def _():
                zwait(k, side, z)
                add(part(k, 1, i), [part(k, 3, side, z)])

        streams[k][0]()

    def o_flow(n):
        o_fetch(n).wait()
        o_hand(n).wait_recv()
        add(o_mine.at[o_part(n), :], [o_sib.at[o_part(n), :]])
        for side in range(2):
            behind = (z > 0) & (z <= e) if side == 0 else (z < nz - 1) & (z >= e)

            @pl.when(behind)
            def _():
                o_wait(side, n)

        @pl.when(z != e)
        def _():
            o_line(n).start()

        @pl.when(z == e)
        def _():
            for p in range(3):
                o_peer(p, n).start()

    streams = [
        plane_stream(
            part(k, 1, nz - 1), lambda q, k=k: part(k, 4, q), *sems[3 * k : 3 * k + 3]
        )
        for k in range(K)
    ]
    order = []
    for k in range(K):
        order += [(k, i) for i in range(1 if k else 0, nz - 1)]
        if k + 1 < K:
            order.append((k + 1, 0))
        order.append((k, nz - 1))
    for n, (k, i) in enumerate(order):
        finish(k, i)
        if n == 0:
            for m in range(pieces):
                o_flow(m)

    @pl.when(z == e)
    def _():
        o_kept().start()
        o_kept().wait()
        for n in range(pieces):
            for p in range(3):
                o_peer(p, n).wait_send()

    @pl.when(z != e)
    def _():
        for n in range(pieces):
            view = o_out.at[o_part(n), :]
            remote(view, view, o_send.at[0, n], o_recv.at[n], e, z, c).wait_recv()
            o_line(n).wait_send()

    for n in range(pieces):
        o_hand(n).wait_send()
    for i in range(nz):
        for k in range(K):
            hand(k, i).wait_send()
            if i < nz - 1:
                zcopy(k, i).wait_send()
    for _, end in streams:
        end()


def settle_weights(nz, grads, small, rows):
    R, W = grads.shape[2:]
    D = rows.shape[2]
    dma = pltpu.SemaphoreType.DMA
    sd = jax.ShapeDtypeStruct
    vm = pltpu.VMEM
    Ws = small.shape[3]
    return pl.pallas_call(
        functools.partial(settle_kernel, nz),
        out_shape=(sd((4, R, W), bf16), sd((4, R, Ws), bf16), sd((R, D), bf16)),
        in_specs=[ANY] * 3,
        out_specs=(ANY,) * 3,
        scratch_shapes=[
            vm((nz, R, W), bf16), vm((nz, R, W), bf16), vm((2, nz, R, W), bf16),
            vm((nz, R, Ws), bf16), vm((nz, R, Ws), bf16), vm((2, nz, R, Ws), bf16),
            vm((R, D), bf16), vm((R, D), bf16), vm((2, R, D), bf16),
            dma((3, nz)), dma((3, nz)), dma((3, nz)), dma((3, nz)), dma((3, 2, nz)),
            dma((6,)), dma((6,)), dma((6,)), dma((6,)), dma((2, 6)),
            dma((3, 6)), dma((6,)), dma(()),
            *plane_sems(), *plane_sems(), *plane_sems(),
        ],
        compiler_params=pltpu.CompilerParams(
            collective_id=1, has_side_effects=True, vmem_limit_bytes=56 << 20
        ),
        cost_estimate=pl.CostEstimate(flops=10**6, bytes_accessed=10**6, transcendentals=0),
        name="settle_weights",
    )(grads, small, rows)


def pick_kernel(width, q_ref, k_ref, v_ref, o_ref):
    e = lax.axis_index("expert")
    spare = o_ref.shape[1] - 3 * width
    if spare:
        o_ref[:, 3 * width :] = jnp.zeros((o_ref.shape[0], spare), o_ref.dtype)
    for n in range(4):

        @pl.when(e == n)
        def _():
            for i, ref in enumerate((q_ref, k_ref, v_ref)):
                o_ref[:, i * width : (i + 1) * width] = ref[:, n * width : (n + 1) * width]


def pick_columns(weights, width):
    vm = pl.BlockSpec(memory_space=pltpu.VMEM)
    return pl.pallas_call(
        functools.partial(pick_kernel, width),
        in_specs=[vm] * 3,
        out_specs=vm,
        out_shape=jax.ShapeDtypeStruct((weights[0].shape[0], -(-3 * width // 128) * 128), bf16),
        name="pick_columns",
    )(*weights)


def assemble_kernel(width, x_ref, *o_refs):
    for n in range(4):
        for i in range(3):
            cols = x_ref[n, :, i * width : (i + 1) * width]
            o_refs[i][:, n * width : (n + 1) * width] = cols.astype(f32)


def assemble_columns(x, width):
    R = x.shape[1]
    block = 32
    return pl.pallas_call(
        functools.partial(assemble_kernel, width),
        grid=(R // block,),
        in_specs=[pl.BlockSpec((4, block, x.shape[2]), lambda i: (0, i, 0))],
        out_specs=(pl.BlockSpec((block, 4 * width), lambda i: (i, 0)),) * 3,
        out_shape=(jax.ShapeDtypeStruct((R, 4 * width), f32),) * 3,
        name="assemble_columns",
    )(x)


def sum_shard(x, axis=0):
    mine = lax.psum_scatter(x, SHARD, scatter_dimension=axis, tiled=True)
    return lax.psum(mine, "expert")


def fetch(nz, fast, weights, w_output, small, tokens, lengths, block):
    D = tokens.shape[1]
    if fast:
        width = D // 4
        columns, full_small, rows, tokens, lengths, blocks = fetch_weights(
            nz, pick_columns(weights, width), small, w_output, tokens, lengths, block
        )
        columns, rows = columns.reshape(D, -1), rows.reshape(width, D)
        return columns, rows, full_small.reshape(D, -1), tokens, lengths, blocks
    full = [lax.all_gather(w, SHARD, axis=0, tiled=True) for w in weights + (w_output, small)]
    blocks = spread_plain(nz, (block,), 0)[0]
    return jnp.concatenate(full[:3], axis=1), full[3], full[4], tokens[None], lengths[None], blocks


def settle(nz, fast, columns, rows, small):
    D, width = rows.shape[1], rows.shape[0]
    if fast:
        R = D // (2 * nz)
        parts = [x.astype(bf16).reshape(nz, 2, R, -1) for x in (columns, small)]
        sums, small, out = settle_weights(nz, *parts, rows.astype(bf16).reshape(2, R, D))
        return *assemble_columns(sums, width), out.astype(f32), jnp.sum(small.astype(f32), axis=0)
    parts = [columns[:, i * width : (i + 1) * width] for i in range(3)] + [rows, small]
    return [sum_shard(x) for x in parts]


def spread_plain(nz, blocks, collective):
    out = []
    for block in blocks:
        for axis in ("expert", "core", "z"):
            block = lax.all_gather(block, axis, axis=0)
        out.append(block)
    return out


def collect_plain(nz, rows, notes, dots, T):
    n_exp, cap, D = rows.shape[2:]
    places = (lax.axis_index("expert") * cap + jnp.arange(cap)).astype(f32)
    notes = notes[..., :T]
    pick = (notes[..., 2, None, :] == places[:, None]) | (notes[..., 3, None, :] == places[:, None])
    part = jnp.einsum(
        "zceps,zcepd->zcesd", pick.astype(bf16), rows, preferred_element_type=f32
    ).astype(bf16)
    part = part.transpose(2, 0, 1, 3, 4).reshape(n_exp * nz * 2 * T, D)
    part = lax.psum_scatter(part, "expert", scatter_dimension=0, tiled=True)
    part = lax.psum_scatter(part, SHARD, scatter_dimension=0, tiled=True).astype(f32)
    z, core, e = lax.axis_index("z"), lax.axis_index("core"), lax.axis_index("expert")
    return part, lax.psum(dots, ("expert",) + SHARD)[z, core, e]


def rope_tables(positions, head_width):
    half_width = head_width // 2
    exponents = jnp.arange(half_width).astype(f32) * 2.0 / head_width
    frequency = rope_base ** (-exponents)
    angles = positions.astype(f32)[..., None] * frequency
    return (jnp.cos(angles), jnp.sin(angles))


def rotate(values, cosine, sine_table):
    half_width = values.shape[-1] // 2
    leading = values[..., :half_width]
    trailing = values[..., half_width:]
    cos_rows = cosine[:, :, None, :]
    sin_rows = sine_table[:, :, None, :]
    return jnp.concatenate(
        [leading * cos_rows - trailing * sin_rows, trailing * cos_rows + leading * sin_rows],
        axis=-1,
    )


def rms_forward(values, norm_gain):
    inverse = lax.rsqrt(jnp.mean(values * values, axis=-1, keepdims=True) + eps_norm)
    return (values * inverse * norm_gain, inverse)


def rms_backward(values, inverse, norm_gain, upstream):
    weighted = upstream * norm_gain
    gain_grad = jnp.sum(upstream * values * inverse, axis=0)
    inner_mean = jnp.mean(weighted * values, axis=-1, keepdims=True)
    return (inverse * weighted - values * inverse * inverse * inverse * inner_mean, gain_grad)


def dot32(a, b):
    return jnp.dot(a, b, preferred_element_type=f32)


def dot_dims(a, b, da, db):
    return lax.dot_general(a, b, (((da,), (db,)), ((), ())), preferred_element_type=f32)


def ein32(spec, a, b):
    return jnp.einsum(spec, a, b, preferred_element_type=f32)


def on_device(
    tokens,
    seq_lengths,
    routes,
    norm_attn,
    w_query,
    w_key,
    w_value,
    w_output,
    norm_ffn,
    w_router,
    w_in,
    w_down,
    cotangent,
):
    T, D = tokens.shape
    R = w_query.shape[0]
    head_width = D // HEADS
    n_exp = lax.axis_size("expert")
    nz = lax.axis_size("z")
    n_shard = nz * lax.axis_size("core")
    experts = w_router.shape[1]
    F = w_down.shape[0]
    FF = F * n_shard
    capacity = 10 * T // (4 * experts)
    slots = experts * capacity
    highest = lax.Precision.HIGHEST
    e_index = lax.axis_index("expert")
    fast = n_exp == 4 and nz == 4

    small = jnp.concatenate([w_router, norm_attn[:, None], norm_ffn[:, None]], axis=1)
    small = jnp.pad(small, ((0, 0), (0, 128 - small.shape[1])))
    length_rows = jnp.broadcast_to(seq_lengths[:, :1], (8, 128))
    full_qkv, full_output, full_small, near_tokens, near_lengths, all_cotangent = fetch(
        nz, fast, (w_query, w_key, w_value), w_output, small, tokens, length_rows, cotangent
    )
    full_router = full_small[:, :experts]
    gain_attn = full_small[:, experts].astype(f32)
    gain_ffn = full_small[:, experts + 1].astype(f32)

    Fp = -(-F // 128) * 128
    packed = pack_columns(w_in.reshape(R, 2 * FF), n_shard, F, Fp)
    packed, full_qkv = lax.optimization_barrier((packed, full_qkv))
    moved = lax.all_to_all(packed, SHARD, split_axis=0, concat_axis=0, tiled=True)
    w_pair = moved.reshape(n_shard * R, 2 * Fp)
    down = jnp.pad(w_down.reshape(F, D), ((0, Fp - F), (0, 0)))

    B, H = near_tokens.shape[0], full_output.shape[0]
    heads = H // head_width
    residual_in = tokens.astype(f32)
    inverse_in = rms_forward(residual_in, gain_attn)[1]
    near_in = near_tokens.reshape(B * T, D).astype(f32)
    near_normed, near_inverse = rms_forward(near_in, gain_attn)
    normed_half = near_normed.astype(bf16)
    lengths = near_lengths[:, 0, 0]
    row_index = jnp.arange(T)
    segment = (row_index[None, :] >= lengths[:, None]).astype(jnp.int32)
    positions = row_index[None, :] - lengths[:, None] * segment
    allowed = (segment[:, :, None] == segment[:, None, :]) & (
        row_index[None, None, :] <= row_index[None, :, None]
    )
    cosine, sine_table = rope_tables(positions, head_width)
    head_shape = (B, T, heads, head_width)
    qkv = dot32(normed_half, full_qkv)
    queries = rotate(qkv[:, :H].reshape(head_shape), cosine, sine_table).astype(bf16)
    keys_rot = rotate(qkv[:, H : 2 * H].reshape(head_shape), cosine, sine_table).astype(bf16)
    values = qkv[:, 2 * H : 3 * H].astype(bf16).reshape(head_shape)
    score_scale = 1.0 / math.sqrt(head_width)
    scores = ein32("bqhd,bkhd->bhqk", queries, keys_rot) * score_scale
    scores = jnp.where(allowed[:, None], scores, masked_score)
    row_peak = jnp.max(scores, axis=-1, keepdims=True)
    log_total = row_peak + jnp.log(jnp.sum(jnp.exp(scores - row_peak), axis=-1, keepdims=True))
    attn_probs = jnp.exp(scores - log_total)
    probs_half = attn_probs.astype(bf16)
    context = ein32("bhqk,bkhd->bqhd", probs_half, values).astype(bf16)
    context_flat = context.reshape(B * T, H)

    def at_home(partial_rows, collective):
        if not fast:
            return partial_rows
        return plane_sum(partial_rows.astype(bf16).reshape(B, T, D), collective)

    residual_mid = residual_in + branch_scale * at_home(dot32(context_flat, full_output), 4)
    normed_mid, inverse_mid = rms_forward(residual_mid, gain_ffn)
    normed_mid_half = normed_mid.astype(bf16)

    logits = dot32(normed_mid_half, full_router)
    expert_ids = jnp.arange(experts)
    route_mask = (routes[:, :, None] == expert_ids[None, None, :]).astype(f32)
    chosen = jnp.sum(logits[:, None, :] * route_mask, axis=-1)
    gate_probs = jax.nn.softmax(chosen, axis=-1)
    flat_routes = routes.reshape(2 * T)
    hits = (flat_routes[:, None] == expert_ids[None, :]).astype(bf16)
    order = jnp.arange(2 * T)
    before = (order[:, None] > order[None, :]).astype(bf16)
    earlier = dot32(before, hits)
    slot_index = jnp.sum(earlier * hits.astype(f32), axis=1).astype(jnp.int32)
    target = (flat_routes * capacity + slot_index).reshape(T, 2)
    slot_ids = jnp.arange(slots)
    pick = [(target[:, k][:, None] == slot_ids[None, :]).astype(bf16) for k in range(2)]

    notes = jnp.concatenate([gate_probs, target.astype(f32), jnp.zeros((T, 4), f32)], axis=1)
    notes = jnp.pad(jnp.transpose(notes), ((0, 0), (0, -T % 128)))
    spread = spread_blocks if fast else spread_plain
    all_normed, all_notes = spread(nz, (normed_mid_half, notes), 2)
    devices = n_shard * n_exp
    flat_notes = all_notes.reshape(devices, 8, -1)[:, :, :T]
    wanted = (e_index * capacity + jnp.arange(capacity)).astype(f32)
    found = [flat_notes[:, 2 + k, None, :] == wanted[None, :, None] for k in range(2)]
    gate_rows = jnp.sum(
        jnp.where(found[0], flat_notes[:, 0, None, :], 0.0)
        + jnp.where(found[1], flat_notes[:, 1, None, :], 0.0),
        axis=-1,
    ).reshape(devices * capacity, 1)
    chosen_rows = (found[0] | found[1]).astype(bf16)

    def take(blocks):
        rows = ein32("spt,std->spd", chosen_rows, blocks.reshape(devices, T, D))
        return rows.astype(bf16).reshape(devices * capacity, D)

    arrived = take(all_normed)
    cotangent_rows = take(all_cotangent)
    grad_scale = gate_rows * branch_scale
    pre = dot32(arrived, w_pair)
    gate_part, up_part = pre[:, :Fp], pre[:, Fp:]
    sigmoid_gate = jax.nn.sigmoid(gate_part)
    silu_gate = gate_part * sigmoid_gate
    activated = (silu_gate * up_part).astype(bf16)
    out_sum = lax.psum_scatter(
        dot32(activated, down).astype(bf16), SHARD, scatter_dimension=0, tiled=True
    )
    back = lax.all_to_all(out_sum, "expert", split_axis=0, concat_axis=0, tiled=True)
    mixture = gate_probs[:, 0:1] * dot32(pick[0], back) + gate_probs[:, 1:2] * dot32(pick[1], back)
    activations = (residual_mid + branch_scale * mixture).astype(bf16)

    raw_grad = dot_dims(cotangent_rows, down, 1, 1)
    row_dots = branch_scale * jnp.sum(raw_grad * activated.astype(f32), axis=1)
    row_dots = row_dots.reshape(devices, capacity, 1)
    token_dots = [jnp.sum(jnp.where(found[k], row_dots, 0.0), axis=1) for k in range(2)]
    token_dots = jnp.stack(token_dots, axis=1).reshape(nz, 2, n_exp, 2, T)
    token_dots = jnp.pad(token_dots, ((0, 0),) * 3 + ((0, 6), (0, -T % 128)))
    act_grad = grad_scale * raw_grad
    pre_grad = jnp.concatenate(
        [
            act_grad * up_part * sigmoid_gate * (1.0 + gate_part * (1.0 - sigmoid_gate)),
            act_grad * silu_gate,
        ],
        axis=1,
    ).astype(bf16)
    in_rows = dot_dims(pre_grad, w_pair, 1, 1).astype(bf16)
    in_rows = in_rows.reshape(nz, 2, n_exp, capacity, D)
    collect = collect_rows if fast else collect_plain
    normed_mid_grad, gate_grad = collect(nz, in_rows, all_notes, token_dots, T)
    gate_grad = jnp.transpose(gate_grad[:2, :T])
    in_term = dot_dims(arrived, pre_grad, 0, 0).astype(bf16).reshape(n_shard, R, 2 * Fp)
    in_term, normed_mid_grad = lax.optimization_barrier((in_term, normed_mid_grad))
    in_term = lax.all_to_all(in_term, SHARD, split_axis=0, concat_axis=0, tiled=True)
    grad_w_in = unpack_columns(in_term, F)
    scaled = (grad_scale * activated.astype(f32)).astype(bf16)
    grad_w_down = lined_up(dot_dims(scaled[:, :F], cotangent_rows, 0, 0))

    upstream = cotangent.astype(f32)
    chosen_grad = gate_probs * (gate_grad - jnp.sum(gate_probs * gate_grad, axis=-1, keepdims=True))
    logit_grad = jnp.sum(chosen_grad[:, :, None] * route_mask, axis=1)
    normed_mid_grad = normed_mid_grad + jnp.dot(
        logit_grad, jnp.transpose(full_router.astype(f32)), precision=highest
    )
    router_grad = jnp.dot(
        jnp.transpose(normed_mid_half.astype(f32)), logit_grad, precision=highest
    )
    mid_norm_grad, gain_ffn_grad = rms_backward(
        residual_mid, inverse_mid, gain_ffn, normed_mid_grad
    )
    residual_grad = upstream + mid_norm_grad
    branch_grad = (branch_scale * residual_grad).astype(bf16)

    if fast:
        branch_grad = plane_gather(branch_grad, 5).reshape(B * T, D)
    output_grad = dot_dims(context_flat, branch_grad, 0, 0)
    context_grad = dot_dims(branch_grad, full_output, 1, 1).reshape(head_shape)
    row_delta = jnp.sum(context_grad * context.astype(f32), axis=-1)
    context_grad_half = context_grad.astype(bf16)
    probs_grad = ein32("bqhd,bkhd->bhqk", context_grad_half, values)
    scores_grad = (
        attn_probs * (probs_grad - jnp.transpose(row_delta, (0, 2, 1))[..., None]) * score_scale
    ).astype(bf16)
    queries_grad = ein32("bhqk,bkhd->bqhd", scores_grad, keys_rot)
    keys_grad = ein32("bhqk,bqhd->bkhd", scores_grad, queries)
    values_grad = ein32("bhqk,bqhd->bkhd", probs_half, context_grad_half)
    qkv_grad = jnp.concatenate(
        [
            rotate(queries_grad, cosine, -sine_table).reshape(B * T, H).astype(bf16),
            rotate(keys_grad, cosine, -sine_table).reshape(B * T, H).astype(bf16),
            values_grad.reshape(B * T, H).astype(bf16),
            jnp.zeros((B * T, full_qkv.shape[1] - 3 * H), bf16),
        ],
        axis=1,
    )
    qkv_weight_grad = dot_dims(normed_half, qkv_grad, 0, 0)
    near_grad = dot_dims(qkv_grad, full_qkv, 1, 1)
    gain_attn_grad = jnp.sum(near_grad * near_in * near_inverse, axis=0)
    in_norm_grad = rms_backward(residual_in, inverse_in, gain_attn, at_home(near_grad, 6))[0]
    grad_tokens = residual_grad + in_norm_grad

    small_grad = jnp.concatenate(
        [router_grad, gain_attn_grad[:, None], gain_ffn_grad[:, None]], axis=1
    )
    small_grad = jnp.pad(small_grad, ((0, 0), (0, 128 - small_grad.shape[1])))
    sum_query, sum_key, sum_value, sum_output, small_sum = settle(
        nz, fast, qkv_weight_grad, output_grad, small_grad
    )
    return (
        activations,
        grad_tokens,
        small_sum[:, experts],
        sum_query,
        sum_key,
        sum_value,
        sum_output,
        small_sum[:, experts + 1],
        small_sum[:, :experts],
        grad_w_in,
        grad_w_down,
    )


def solution(mesh):
    n_expert, n_shard = mesh.devices.shape
    chips = Mesh(mesh.devices.reshape(n_expert, n_shard // 2, 2), ("expert", "z", "core"))
    rows = P(("expert", "z", "core"), None)
    shard = P(SHARD)
    shard2 = P(SHARD, None)
    shard3 = P(SHARD, "expert", None)
    in_specs = (
        rows,
        rows,
        rows,
        shard,
        shard2,
        shard2,
        shard2,
        shard2,
        shard,
        shard2,
        shard3,
        shard3,
        rows,
    )
    out_specs = (
        rows,
        rows,
        shard,
        shard2,
        shard2,
        shard2,
        shard2,
        shard,
        shard2,
        shard3,
        shard3,
    )
    return jax.shard_map(
        on_device, mesh=chips, in_specs=in_specs, out_specs=out_specs, check_vma=False
    )
```

```python
import functools
import math

import jax
import jax.numpy as jnp
from jax import lax
from jax.experimental import pallas as pl
from jax.experimental.pallas import tpu as pltpu
from jax.sharding import Mesh, PartitionSpec as P

HEADS = 36

eps_norm = 1e-05
branch_scale = 1.4 / math.sqrt(40.0)
rope_base = 10000.0
masked_score = -1e30
bf16 = jnp.bfloat16
f32 = jnp.float32
SHARD = ("z", "core")
ANY = pl.BlockSpec(memory_space=pl.ANY)


def place():
    e, z, c = lax.axis_index("expert"), lax.axis_index("z"), lax.axis_index("core")
    across_x = e + 1 - 2 * (e % 2)
    across_y = (e + 2) % 4
    return e, z, c, across_x, across_y


def remote(src, dst, send, recv, e, z, c):
    return pltpu.make_async_remote_copy(
        src_ref=src,
        dst_ref=dst,
        send_sem=send,
        recv_sem=recv,
        device_id=(e, z, c),
        device_id_type=pl.DeviceIdType.MESH,
    )


def payload_stream(nz, ref, out, sems, split):
    zrecv, zsend, near_recv, near_send, far_recv, far_send, sib_recv, sib_send, own = sems
    e, z, c, ex, ey = place()
    diagonal = (ex + 2) % 4
    T = ref.shape[0]
    S = 2 * nz - 1

    def split_step(s):
        return (s - 1) % 2, (s - 1) // 2

    def where(s):
        if s == 0:
            return z
        side, i = split_step(s)
        return z - 1 - i if side == 0 else z + 1 + i

    def exists(s):
        if s == 0:
            return z >= 0
        zz = where(s)
        return (zz >= 0) & (zz < nz)

    def slab(s, quarter, r0=0, n=T):
        return out.at[where(s), c, quarter, pl.ds(r0, n), :]

    def first(step):
        side = 0 if step > 0 else 1
        return remote(ref, slab(0, e), zsend.at[side, nz - 1], zrecv.at[side, 0], e, z + step, c)

    def onward(s):
        side, i = split_step(s)
        step = 1 if side == 0 else -1
        return remote(
            slab(s, e), slab(s, e), zsend.at[side, i], zrecv.at[side, i + 1], e, z + step, c
        )

    def near(s, axis):
        source = ref if s == 0 else slab(s, e)
        return remote(
            source, slab(s, e), near_send.at[s, axis], near_recv.at[s, axis],
            ex if axis == 0 else ey, z, c,
        )

    def near_wait(s, axis):
        view = slab(s, ex if axis == 0 else ey)
        remote(view, view, near_send.at[s, axis], near_recv.at[s, axis], ex, z, c).wait_recv()

    axes = range(2) if split else range(1)

    def far_view(s, quarter, axis):
        if not split:
            return slab(s, quarter)
        return slab(s, quarter, 0, split) if axis == 0 else slab(s, quarter, split, T - split)

    def far(s, axis):
        view = far_view(s, ex if axis == 0 else ey, axis)
        return remote(
            view, view, far_send.at[s, axis], far_recv.at[s, axis],
            ey if axis == 0 else ex, z, c,
        )

    def far_wait(s, axis):
        view = far_view(s, diagonal, axis)
        remote(view, view, far_send.at[s, axis], far_recv.at[s, axis], ex, z, c).wait_recv()

    def beside(s, n):
        quarter = (e, ex, ey, diagonal)[n]
        source = ref if s == 0 and n == 0 else slab(s, quarter)
        return remote(
            source, slab(s, quarter), sib_send.at[s, n], sib_recv.at[s, n], e, z, 1 - c
        )

    def beside_wait(s, n):
        view = out.at[where(s), 1 - c, (e, ex, ey, diagonal)[n]]
        remote(view, view, sib_send.at[s, n], sib_recv.at[s, n], e, z, c).wait_recv()

    def inside(side):
        return z < nz - 1 if side == 0 else z > 0

    def begin():
        for step in (1, -1):

            @pl.when((z + step >= 0) & (z + step < nz))
            def _():
                first(step).start()

        near(0, 0).start()
        near(0, 1).start()
        beside(0, 0).start()
        pltpu.make_async_copy(ref, slab(0, e), own).start()

    def arrive(s):
        if s == 0:
            return

        @pl.when(exists(s))
        def _():
            side, i = split_step(s)
            remote(
                slab(s, e), slab(s, e), zsend.at[side, i], zrecv.at[side, i], e, z, c
            ).wait_recv()
            if i < nz - 2:

                @pl.when(inside(side))
                def _():
                    onward(s).start()

            near(s, 0).start()
            near(s, 1).start()
            beside(s, 0).start()

    def relay(s):
        @pl.when(exists(s))
        def _():
            near_wait(s, 0)
            far(s, 0).start()
            beside(s, 1).start()
            near_wait(s, 1)
            if split:
                far(s, 1).start()
            beside(s, 2).start()

    def close(s):
        @pl.when(exists(s))
        def _():
            for axis in axes:
                far_wait(s, axis)
            beside(s, 3).start()

    def end(s):
        @pl.when(exists(s))
        def _():
            for axis in range(2):
                near(s, axis).wait_send()
            for axis in axes:
                far(s, axis).wait_send()
            for n in range(4):
                beside(s, n).wait_send()
                beside_wait(s, n)
            if s > 0 and split_step(s)[1] < nz - 2:

                @pl.when(inside(split_step(s)[0]))
                def _():
                    onward(s).wait_send()

        if s == 0:
            for step in (1, -1):

                @pl.when((z + step >= 0) & (z + step < nz))
                def _():
                    first(step).wait_send()

            pltpu.make_async_copy(ref, slab(0, e), own).wait()

    return begin, arrive, relay, close, end


def payload_sems(nz):
    dma = pltpu.SemaphoreType.DMA
    S = 2 * nz - 1
    return [
        dma((2, nz)), dma((2, nz)), dma((S, 2)), dma((S, 2)), dma((S, 2)), dma((S, 2)),
        dma((S, 4)), dma((S, 4)), dma(()),
    ]


def spread_kernel(nz, splits, *refs):
    n = len(splits)
    ins, outs, sems = refs[:n], refs[n : 2 * n], refs[2 * n :]
    greet_cross(nz)
    streams = [
        payload_stream(nz, ins[i], outs[i], sems[9 * i : 9 * i + 9], splits[i]) for i in range(n)
    ]
    for t in streams:
        t[0]()
    S = 2 * nz - 1
    for s in range(S):
        for t in streams:
            t[1](s)
        if s >= 1:
            for t in streams:
                t[2](s - 1)
        if s >= 2:
            for t in streams:
                t[3](s - 2)
    for t in streams:
        t[2](S - 1)
    for s in (S - 2, S - 1):
        for t in streams:
            t[3](s)
    for s in range(S):
        for t in streams:
            t[4](s)


def spread_blocks(nz, blocks, collective):
    sd = jax.ShapeDtypeStruct
    splits = tuple(b.shape[0] // 2 if b.shape[0] % 32 == 0 else 0 for b in blocks)
    return pl.pallas_call(
        functools.partial(spread_kernel, nz, splits),
        out_shape=tuple(sd((nz, 2, 4) + b.shape, b.dtype) for b in blocks),
        in_specs=[ANY] * len(blocks),
        out_specs=(ANY,) * len(blocks),
        scratch_shapes=[s for _ in blocks for s in payload_sems(nz)],
        compiler_params=pltpu.CompilerParams(collective_id=collective, has_side_effects=True),
        cost_estimate=pl.CostEstimate(
            flops=10**6, bytes_accessed=10**6, transcendentals=0
        ),
        name="spread_blocks",
    )(*blocks)


def line_order(nz, z):
    def order(i):
        code = 0
        for zz in range(nz):
            far_first = sorted(range(nz), key=lambda t: (-abs(t - zz), t))
            code += far_first[i] * nz**zz
        power = 1
        for zz in range(nz):
            power = power + (nz**zz - 1) * jnp.where(z == zz, 1, 0)
        return (code // power) % nz

    return [order(i) for i in range(nz)]


def collect_kernel(
    nz, cap,
    rows_ref, notes_ref, dots_ref,
    out_ref, dots_out,
    dots, notes, mine, theirs, block, from_x, from_y, via_x, via_y, from_z,
    note_sem, load, sib_send, sib_recv, via_send, via_recv, plain_send, plain_recv,
    sum_send, sum_recv, zsend, zrecv, dot_send, dot_recv, dot_own,
):
    e, z, c, ex, ey = place()
    diagonal = (ex + 2) % 4
    T, D = out_ref.shape
    h = T // 2
    dest = line_order(nz, z)
    who = (diagonal, ex, ey, e)

    def others():
        for d in range(1, 8 * nz):
            to = ((e * nz + z) * 2 + c + d) % (8 * nz)
            yield d, to // (2 * nz), to // 2 % nz, to % 2

    barrier = pltpu.get_barrier_semaphore()
    for _, te, tz, tc in others():
        pl.semaphore_signal(
            barrier, inc=1, device_id=(te, tz, tc), device_id_type=pl.DeviceIdType.MESH
        )
    pl.semaphore_wait(barrier, 8 * nz - 1)

    def dot(d, te, tz, tc):
        return remote(
            dots_ref.at[tz, tc, te], dots.at[d], dot_send.at[d], dot_recv.at[d], te, tz, tc
        )

    dot_kept = pltpu.make_async_copy(dots_ref.at[z, c, e], dots.at[0], dot_own)
    dot_kept.start()
    for d, te, tz, tc in others():
        dot(d, te, tz, tc).start()

    note_copy = pltpu.make_async_copy(notes_ref, notes, note_sem)
    note_copy.start()

    def fetch(i, q):
        return pltpu.make_async_copy(
            rows_ref.at[dest[i], c, who[q]], mine.at[i, q], load.at[i, q]
        )

    def hand(i, q):
        return remote(
            rows_ref.at[dest[i], 1 - c, who[q]], theirs.at[i, q],
            sib_send.at[i, q], sib_recv.at[i, q], e, z, 1 - c,
        )

    for i in range(nz):
        for q in range(4):
            hand(i, q).start()
            fetch(i, q).start()
    note_copy.wait()

    def open_out(i, q):
        fetch(i, q).wait()
        hand(i, q).wait_recv()
        places = (lax.broadcasted_iota(jnp.int32, (cap, T), 0) + e * cap).astype(f32)
        note = notes[dest[i], c, who[q]]
        pick = ((note[2:3, :] == places) | (note[3:4, :] == places)).astype(bf16)
        wide = 768 if D % 768 == 0 else 128

        @pl.loop(0, D // wide)
        def _(b):
            cols = pl.ds(pl.multiple_of(b * wide, 128), wide)
            both = mine[i, q, :, cols].astype(f32) + theirs[i, q, :, cols].astype(f32)
            block[i, q, :, cols] = lax.dot_general(
                pick, both.astype(bf16), (((0,), (0,)), ((), ())), preferred_element_type=f32
            ).astype(bf16)

    def via(i, axis):
        if axis == 0:
            return remote(
                block.at[i, 0, pl.ds(0, h), :], via_x.at[i],
                via_send.at[i, 0], via_recv.at[i, 0], ex, z, c,
            )
        return remote(
            block.at[i, 0, pl.ds(h, h), :], via_y.at[i],
            via_send.at[i, 1], via_recv.at[i, 1], ey, z, c,
        )

    def plain(i, axis):
        if axis == 0:
            return remote(
                block.at[i, 1, pl.ds(0, h), :], from_x.at[i, pl.ds(0, h), :],
                plain_send.at[i, 0], plain_recv.at[i, 0], ex, z, c,
            )
        return remote(
            block.at[i, 2, pl.ds(h, h), :], from_y.at[i, pl.ds(h, h), :],
            plain_send.at[i, 1], plain_recv.at[i, 1], ey, z, c,
        )

    def summed(i, axis):
        if axis == 0:
            return remote(
                block.at[i, 1, pl.ds(h, h), :], from_x.at[i, pl.ds(h, h), :],
                sum_send.at[i, 0], sum_recv.at[i, 0], ex, z, c,
            )
        return remote(
            block.at[i, 2, pl.ds(0, h), :], from_y.at[i, pl.ds(0, h), :],
            sum_send.at[i, 1], sum_recv.at[i, 1], ey, z, c,
        )

    def add(target, others, n):
        @pl.loop(0, n // 16)
        def _(b):
            rows = pl.ds(pl.multiple_of(b * 16, 16), 16)
            acc = target[rows, :].astype(f32)
            for o in others:
                acc = acc + o[rows, :].astype(f32)
            target[rows, :] = acc.astype(target.dtype)

    def start(i):
        open_out(i, 0)
        via(i, 0).start()
        via(i, 1).start()
        open_out(i, 1)
        plain(i, 0).start()
        open_out(i, 2)
        plain(i, 1).start()
        open_out(i, 3)

    def combine(i):
        via(i, 0).wait_recv()
        add(block.at[i, 2, pl.ds(0, h), :], [via_x.at[i]], h)
        summed(i, 1).start()
        via(i, 1).wait_recv()
        add(block.at[i, 1, pl.ds(h, h), :], [via_y.at[i]], h)
        summed(i, 0).start()

    def zcopy(i):
        step = jnp.where(dest[i] > z, 1, -1)
        side = jnp.where(dest[i] > z, 0, 1)
        return remote(
            block.at[i, 3], from_z.at[side, dest[i]],
            zsend.at[i], zrecv.at[side, dest[i]], e, z + step, c,
        )

    def zwait(side, zz):
        slab = from_z.at[side, zz]
        remote(slab, slab, zsend.at[0], zrecv.at[side, zz], e, z, c).wait_recv()

    def finish(i):
        for axis in range(2):
            plain(i, axis).wait_recv()
            summed(i, axis).wait_recv()
        zz = dest[i]
        if i < nz - 1:
            add(block.at[i, 3], [from_x.at[i], from_y.at[i]], T)
            for side in range(2):
                going = zz > z if side == 0 else zz < z
                behind = z > 0 if side == 0 else z < nz - 1

                @pl.when(going & behind)
                def _():
                    zwait(side, zz)
                    add(block.at[i, 3], [from_z.at[side, zz]], T)

            zcopy(i).start()
            return

        @pl.loop(0, T // 16)
        def _(b):
            rows = pl.ds(pl.multiple_of(b * 16, 16), 16)
            acc = block[i, 3, rows, :].astype(f32) + from_x[i, rows, :].astype(f32)
            out_ref[rows, :] = acc + from_y[i, rows, :].astype(f32)

        for side in range(2):

            @pl.when(z > 0 if side == 0 else z < nz - 1)
            def _():
                zwait(side, z)
                add(out_ref, [from_z.at[side, z]], T)

    for i in range(nz):
        start(i)
        if i >= 1:
            combine(i - 1)
        if i >= 2:
            finish(i - 2)
    combine(nz - 1)
    if nz >= 2:
        finish(nz - 2)
    finish(nz - 1)

    dot_kept.wait()
    for d, te, tz, tc in others():
        dot(d, te, tz, tc).wait_recv()
        dot(d, te, tz, tc).wait_send()
    dots_out[...] = jnp.sum(dots[...], axis=0)

    for i in range(nz):
        for q in range(4):
            hand(i, q).wait_send()
        for axis in range(2):
            via(i, axis).wait_send()
            plain(i, axis).wait_send()
            summed(i, axis).wait_send()
        if i < nz - 1:
            zcopy(i).wait_send()


def collect_rows(nz, rows, notes, dots, T):
    cap, D = rows.shape[3:]
    dma = pltpu.SemaphoreType.DMA
    vm = pltpu.VMEM
    return pl.pallas_call(
        functools.partial(collect_kernel, nz, cap),
        out_shape=(
            jax.ShapeDtypeStruct((T, D), f32),
            jax.ShapeDtypeStruct(dots.shape[3:], f32),
        ),
        in_specs=[ANY] * 3,
        out_specs=(pl.BlockSpec(memory_space=pltpu.VMEM),) * 2,
        scratch_shapes=[
            vm((8 * nz,) + dots.shape[3:], f32),
            vm(notes.shape, f32),
            vm((nz, 4, cap, D), bf16),
            vm((nz, 4, cap, D), bf16),
            vm((nz, 4, T, D), bf16),
            vm((nz, T, D), bf16),
            vm((nz, T, D), bf16),
            vm((nz, T // 2, D), bf16),
            vm((nz, T // 2, D), bf16),
            vm((2, nz, T, D), bf16),
            dma(()),
            dma((nz, 4)),
            dma((nz, 4)),
            dma((nz, 4)),
            dma((nz, 2)),
            dma((nz, 2)),
            dma((nz, 2)),
            dma((nz, 2)),
            dma((nz, 2)),
            dma((nz, 2)),
            dma((nz,)),
            dma((2, nz)),
            dma((8 * nz,)),
            dma((8 * nz,)),
            dma(()),
        ],
        compiler_params=pltpu.CompilerParams(
            collective_id=3, has_side_effects=True, vmem_limit_bytes=56 << 20
        ),
        cost_estimate=pl.CostEstimate(
            flops=10**6, bytes_accessed=10**6, transcendentals=0
        ),
        name="collect_rows",
    )(rows, notes, dots)


def pack_rows(n, F, Fp, x_ref, o_ref):
    half = n * F
    rows = x_ref.shape[0]
    for i in range(n):
        for part in range(2):
            cols = x_ref[:, part * half + i * F : part * half + (i + 1) * F]
            if Fp > F:
                cols = jnp.concatenate([cols, jnp.zeros((rows, Fp - F), cols.dtype)], axis=1)
            o_ref[i, :, part * Fp : (part + 1) * Fp] = cols


def pack_columns(w, n, F, Fp):
    rows = w.shape[0]
    block = 16
    return pl.pallas_call(
        functools.partial(pack_rows, n, F, Fp),
        grid=(rows // block,),
        in_specs=[pl.BlockSpec((block, w.shape[1]), lambda i: (i, 0))],
        out_specs=pl.BlockSpec((n, block, 2 * Fp), lambda i: (0, i, 0)),
        out_shape=jax.ShapeDtypeStruct((n, rows, 2 * Fp), w.dtype),
        name="pack_columns",
    )(w)


def unpack_kernel(n, F, Fp, x_ref, o_ref, line):
    half = n * F
    rows = line.shape[0]
    for i in range(n):
        for part in range(2):
            cols = x_ref[i, :, part * Fp : part * Fp + F].astype(f32)
            line[:, part * half + i * F : part * half + (i + 1) * F] = cols
    tiles = 2 * half // 128
    for j in range(tiles):
        o_ref[pl.ds(j, rows, stride=tiles), :] = line[:, j * 128 : (j + 1) * 128]


def unpack_columns(x, F):
    n, rows, Fp2 = x.shape
    block = 16
    width = 2 * n * F
    tiles = width // 128
    flat = pl.pallas_call(
        functools.partial(unpack_kernel, n, F, Fp2 // 2),
        grid=(rows // block,),
        in_specs=[pl.BlockSpec((n, block, Fp2), lambda i: (0, i, 0))],
        out_specs=pl.BlockSpec((block * tiles, 128), lambda i: (i, 0)),
        out_shape=jax.ShapeDtypeStruct((rows * tiles, 128), f32),
        scratch_shapes=[pltpu.VMEM((block, width), f32)],
        name="unpack_columns",
    )(x)
    return flat.reshape(rows, 1, width)


def line_kernel(x_ref, o_ref):
    rows, width = x_ref.shape
    tiles = width // 128
    for j in range(tiles):
        o_ref[pl.ds(j, rows, stride=tiles), :] = x_ref[:, j * 128 : (j + 1) * 128]


def lined_up(x):
    rows, width = x.shape
    tiles = width // 128
    block = 80 if rows % 80 == 0 else 8
    flat = pl.pallas_call(
        line_kernel,
        grid=(rows // block,),
        in_specs=[pl.BlockSpec((block, width), lambda i: (i, 0))],
        out_specs=pl.BlockSpec((block * tiles, 128), lambda i: (i, 0)),
        out_shape=jax.ShapeDtypeStruct((rows * tiles, 128), x.dtype),
        name="lined_up",
    )(x)
    return flat.reshape(rows, 1, width)


def greet_cross(nz):
    e, z, c, ex, ey = place()
    barrier = pltpu.get_barrier_semaphore()

    def hail(te, tz, tc):
        pl.semaphore_signal(
            barrier, inc=1, device_id=(te, tz, tc), device_id_type=pl.DeviceIdType.MESH
        )

    hail(e, z, 1 - c)
    for te in (ex, ey, (ex + 2) % 4):
        hail(te, z, c)
    for step in (-1, 1):

        @pl.when((z + step >= 0) & (z + step < nz))
        def _():
            hail(e, z + step, c)

    pl.semaphore_wait(barrier, 4 + jnp.where(z > 0, 1, 0) + jnp.where(z < nz - 1, 1, 0))


def line_stream(nz, ref, out, zrecv, zsend, sib_recv, sib_send, own):
    e, z, c, _, _ = place()

    def split_step(s):
        return (s - 1) % 2, (s - 1) // 2

    def where(s):
        if s == 0:
            return z
        side, i = split_step(s)
        return z - 1 - i if side == 0 else z + 1 + i

    def exists(s):
        return (where(s) >= 0) & (where(s) < nz)

    def inside(side):
        return z < nz - 1 if side == 0 else z > 0

    def slab(s):
        return out.at[where(s), c]

    def first(side):
        step = 1 if side == 0 else -1
        return remote(ref, slab(0), zsend.at[side, nz - 1], zrecv.at[side, 0], e, z + step, c)

    def onward(s):
        side, i = split_step(s)
        step = 1 if side == 0 else -1
        return remote(
            slab(s), slab(s), zsend.at[side, i], zrecv.at[side, i + 1], e, z + step, c
        )

    def beside(s):
        return remote(
            ref if s == 0 else slab(s), slab(s), sib_send.at[s], sib_recv.at[s], e, z, 1 - c
        )

    def begin():
        for side in range(2):

            @pl.when(inside(side))
            def _():
                first(side).start()

        beside(0).start()
        pltpu.make_async_copy(ref, slab(0), own).start()

    def arrive(s):
        side, i = split_step(s)

        @pl.when(exists(s))
        def _():
            remote(slab(s), slab(s), zsend.at[side, i], zrecv.at[side, i], e, z, c).wait_recv()
            if i < nz - 2:

                @pl.when(inside(side))
                def _():
                    onward(s).start()

            beside(s).start()

    def end():
        for s in range(2 * nz - 1):

            @pl.when(exists(s))
            def _():
                beside(s).wait_send()
                view = out.at[where(s), 1 - c]
                remote(view, view, sib_send.at[s], sib_recv.at[s], e, z, c).wait_recv()
                if s > 0 and split_step(s)[1] < nz - 2:

                    @pl.when(inside(split_step(s)[0]))
                    def _():
                        onward(s).wait_send()

        for side in range(2):

            @pl.when(inside(side))
            def _():
                first(side).wait_send()

        pltpu.make_async_copy(ref, slab(0), own).wait()

    return begin, arrive, end


def line_sems(nz):
    dma = pltpu.SemaphoreType.DMA
    S = 2 * nz - 1
    return [dma((2, nz)), dma((2, nz)), dma((S,)), dma((S,)), dma(())]


def plane_stream(source, views, send, recv, own):
    e, z, c, ex, ey = place()
    peers = (ex, ey, (ex + 2) % 4)

    def copy(n):
        return remote(source, views(e), send.at[n], recv.at[n], peers[n], z, c)

    def kept():
        return pltpu.make_async_copy(source, views(e), own)

    def begin():
        for n in range(3):
            copy(n).start()
        kept().start()

    def end():
        kept().wait()
        for n in range(3):
            view = views(peers[n])
            remote(view, view, send.at[n], recv.at[n], e, z, c).wait_recv()
            copy(n).wait_send()

    return begin, end


def plane_sems():
    dma = pltpu.SemaphoreType.DMA
    return [dma((3,)), dma((3,)), dma(())]


def fetch_kernel(
    nz,
    F, w_ref, s_ref, o_ref, t_ref, l_ref, p_ref, x_ref,
    w_out, s_out, o_out, t_out, l_out, p_out, x_out,
    wide, packed, wide_sem, packed_sem,
    *sems,
):
    e, z, c, ex, ey = place()
    w_sems, sems = sems[:5], sems[5:]
    s_sems, sems = sems[:5], sems[5:]
    t_sems, sems = sems[:3], sems[3:]
    l_sems, sems = sems[:3], sems[3:]
    p_sems, sems = sems[:9], sems[9:]
    orecv, osend, sib_recv, sib_send, own = sems
    wide_copy = pltpu.make_async_copy(x_ref, wide, wide_sem)
    wide_copy.start()
    greet_cross(nz)
    w_begin, w_arrive, w_end = line_stream(nz, w_ref, w_out, *w_sems)
    s_begin, s_arrive, s_end = line_stream(nz, s_ref, s_out, *s_sems)
    t_begin, t_end = plane_stream(t_ref, lambda q: t_out.at[q], *t_sems)
    l_begin, l_end = plane_stream(l_ref, lambda q: l_out.at[q], *l_sems)
    p_begin, p_arrive, p_relay, p_close, p_end = payload_stream(
        nz, p_ref, p_out, p_sems, p_ref.shape[0] // 2
    )

    pieces = orecv.shape[0]
    height = o_ref.shape[0] // pieces

    def o_part(n):
        return pl.ds(n * height, height)

    def o_view(n):
        return o_out.at[c, o_part(n), :]

    def o_copy(side, n, source):
        step = 1 if side == 0 else -1
        return remote(source, o_view(n), osend.at[side, n], orecv.at[n], e, z + step, c)

    def o_beside(n, source):
        return remote(source, o_view(n), sib_send.at[n], sib_recv.at[n], e, z, 1 - c)

    def o_goes(side):
        return (z >= e) & (z < nz - 1) if side == 0 else (z <= e) & (z > 0)

    def o_pass(n, source):
        for side in range(2):

            @pl.when(o_goes(side))
            def _():
                o_copy(side, n, source).start()

        o_beside(n, source).start()

    def o_arrive(n):
        @pl.when(z != e)
        def _():
            remote(o_view(n), o_view(n), sib_send.at[n], orecv.at[n], e, z, c).wait_recv()
            o_pass(n, o_view(n))

    p_begin()

    @pl.when(z == e)
    def _():
        for n in range(pieces):
            o_pass(n, o_ref.at[o_part(n), :])
        pltpu.make_async_copy(o_ref, o_out.at[c], own).start()

    s_begin()
    w_begin()
    t_begin()
    l_begin()

    wide_copy.wait()

    @pl.loop(0, wide.shape[0] // 16)
    def _(b):
        rows = pl.ds(pl.multiple_of(b * 16, 16), 16)
        pack_rows(packed.shape[0], F, packed.shape[2] // 2, wide.at[rows, :], packed.at[:, rows, :])

    packed_copy = pltpu.make_async_copy(packed, x_out, packed_sem)
    packed_copy.start()

    blocks = 2 * nz - 1
    for s in range(1, blocks):
        p_arrive(s)
        s_arrive(s)
        if s <= pieces:
            o_arrive(s - 1)
    for n in range(blocks - 1, pieces):
        o_arrive(n)
    for s in range(1, blocks):
        p_relay(s - 1)
        w_arrive(s)
        if s >= 2:
            p_close(s - 2)
    p_relay(blocks - 1)
    p_close(blocks - 2)
    p_close(blocks - 1)
    for s in range(blocks):
        p_end(s)
    w_end()
    s_end()
    t_end()
    l_end()
    for n in range(pieces):
        view = o_out.at[1 - c, o_part(n), :]
        remote(view, view, sib_send.at[n], sib_recv.at[n], e, z, c).wait_recv()
        o_beside(n, o_view(n)).wait_send()
        for side in range(2):

            @pl.when(o_goes(side))
            def _():
                o_copy(side, n, o_view(n)).wait_send()

    @pl.when(z == e)
    def _():
        pltpu.make_async_copy(o_ref, o_out.at[c], own).wait()

    packed_copy.wait()


def fetch_weights(nz, columns, small, rows, tokens, lengths, block, wide, F):
    dma = pltpu.SemaphoreType.DMA
    packed = (2 * nz, wide.shape[0], 2 * (-(-F // 128) * 128))
    sd = jax.ShapeDtypeStruct
    return pl.pallas_call(
        functools.partial(fetch_kernel, nz, F),
        out_shape=(
            sd((nz, 2) + columns.shape, bf16),
            sd((nz, 2) + small.shape, bf16),
            sd((2,) + rows.shape, bf16),
            sd((4,) + tokens.shape, bf16),
            sd((4,) + lengths.shape, lengths.dtype),
            sd((nz, 2, 4) + block.shape, block.dtype),
            sd(packed, wide.dtype),
        ),
        in_specs=[ANY] * 7,
        out_specs=(ANY,) * 7,
        scratch_shapes=[
            pltpu.VMEM(wide.shape, wide.dtype), pltpu.VMEM(packed, wide.dtype), dma(()), dma(()),
            *line_sems(nz), *line_sems(nz), *plane_sems(), *plane_sems(), *payload_sems(nz),
            dma((6,)), dma((2, 6)), dma((6,)), dma((6,)), dma(()),
        ],
        compiler_params=pltpu.CompilerParams(
            collective_id=0, has_side_effects=True, vmem_limit_bytes=32 << 20
        ),
        cost_estimate=pl.CostEstimate(
            flops=10**11, bytes_accessed=8 * columns.size, transcendentals=0
        ),
        name="fetch_weights",
    )(columns, small, rows, tokens, lengths, block, wide)


def plane_gather_kernel(x_ref, out_ref, send, recv, own):
    e, z, c, ex, ey = place()
    greet_plane()
    begin, end = plane_stream(x_ref, lambda q: out_ref.at[q], send, recv, own)
    begin()
    end()


def greet_plane():
    e, z, c, ex, ey = place()
    barrier = pltpu.get_barrier_semaphore()
    for te in (ex, ey, (ex + 2) % 4):
        pl.semaphore_signal(
            barrier, inc=1, device_id=(te, z, c), device_id_type=pl.DeviceIdType.MESH
        )
    pl.semaphore_wait(barrier, 3)


def plane_gather(x, collective):
    return pl.pallas_call(
        plane_gather_kernel,
        out_shape=jax.ShapeDtypeStruct((4,) + x.shape, x.dtype),
        in_specs=[ANY],
        out_specs=ANY,
        scratch_shapes=plane_sems(),
        compiler_params=pltpu.CompilerParams(collective_id=collective, has_side_effects=True),
        cost_estimate=pl.CostEstimate(flops=10**6, bytes_accessed=10**6, transcendentals=0),
        name="plane_gather",
    )(x)


def plane_sum_parts(x_ref, out_ref, held, send, recv, own):
    e, z, c, ex, ey = place()
    peers = (ex, ey, (ex + 2) % 4)

    def copy(n):
        return remote(x_ref.at[peers[n]], held.at[n], send.at[n], recv.at[n], peers[n], z, c)

    kept = pltpu.make_async_copy(x_ref.at[e], held.at[3], own)

    def total():
        kept.wait()
        for n in range(3):
            copy(n).wait_recv()

        @pl.loop(0, out_ref.shape[0] // 16)
        def _(b):
            rows = pl.ds(pl.multiple_of(b * 16, 16), 16)
            acc = held[3, rows, :].astype(f32) + held[0, rows, :].astype(f32)
            acc = acc + held[1, rows, :].astype(f32)
            out_ref[rows, :] = acc + held[2, rows, :].astype(f32)

    return copy, kept, total


def plane_sum_kernel(x_ref, out_ref, held, send, recv, own):
    greet_plane()
    copy, kept, total = plane_sum_parts(x_ref, out_ref, held, send, recv, own)
    for n in (2, 0, 1):
        copy(n).start()
    kept.start()
    total()
    for n in range(3):
        copy(n).wait_send()


def plane_sum(x, collective):
    vm = pltpu.VMEM
    return pl.pallas_call(
        plane_sum_kernel,
        out_shape=jax.ShapeDtypeStruct(x.shape[1:], f32),
        in_specs=[ANY],
        out_specs=pl.BlockSpec(memory_space=vm),
        scratch_shapes=[vm(x.shape, bf16), *plane_sems()],
        compiler_params=pltpu.CompilerParams(collective_id=collective, has_side_effects=True),
        cost_estimate=pl.CostEstimate(flops=10**6, bytes_accessed=10**6, transcendentals=0),
        name="plane_sum",
    )(x)


def settle_kernel(
    nz,
    g_ref, s_ref, o_ref, x_ref, y_ref,
    g_out, s_out, o_out, x_out, y_out,
    x_held, x_send, x_recv, x_own, y_send, y_recv, y_own,
    g_mine, g_sib, g_z, s_mine, s_sib, s_z, o_mine, o_sib, o_z,
    load, sib_send, sib_recv, zsend, zrecv,
    o_load, o_sib_send, o_sib_recv, o_zsend, o_zrecv,
    o_send, o_recv, o_own,
    *sems,
):
    e, z, c, ex, ey = place()
    peers = (ex, ey, (ex + 2) % 4)
    dest = line_order(nz, z)
    greet_cross(nz)
    W = g_ref.shape[3]
    first = W // 256 * 128
    groups = (
        (g_ref, g_mine, g_sib, g_z, g_out, pl.ds(0, first)),
        (g_ref, g_mine, g_sib, g_z, g_out, pl.ds(first, W - first)),
        (s_ref, s_mine, s_sib, s_z, s_out, pl.ds(0, s_ref.shape[3])),
    )
    K = len(groups)

    def part(k, which, *index):
        return groups[k][which].at[(*index, slice(None), groups[k][5])]

    def fetch(k, i):
        return pltpu.make_async_copy(
            part(k, 0, dest[i], c), part(k, 1, i), load.at[k, i]
        )

    def hand(k, i):
        return remote(
            part(k, 0, dest[i], 1 - c), part(k, 2, i),
            sib_send.at[k, i], sib_recv.at[k, i], e, z, 1 - c,
        )

    def zcopy(k, i):
        step = jnp.where(dest[i] > z, 1, -1)
        side = jnp.where(dest[i] > z, 0, 1)
        return remote(
            part(k, 1, i), part(k, 3, side, dest[i]),
            zsend.at[k, i], zrecv.at[k, side, dest[i]], e, z + step, c,
        )

    def zwait(k, side, zz):
        slab = part(k, 3, side, zz)
        remote(slab, slab, zsend.at[k, 0], zrecv.at[k, side, zz], e, z, c).wait_recv()

    def add(target, others):
        @pl.loop(0, target.shape[0] // 16)
        def _(b):
            rows = pl.ds(pl.multiple_of(b * 16, 16), 16)
            acc = target[rows, :].astype(f32)
            for o in others:
                acc = acc + o[rows, :].astype(f32)
            target[rows, :] = acc.astype(target.dtype)

    pieces = o_load.shape[0]
    height = o_mine.shape[0] // pieces

    def o_part(n):
        return pl.ds(n * height, height)

    def o_fetch(n):
        return pltpu.make_async_copy(o_ref.at[c, o_part(n), :], o_mine.at[o_part(n), :], o_load.at[n])

    def o_hand(n):
        return remote(
            o_ref.at[1 - c, o_part(n), :], o_sib.at[o_part(n), :],
            o_sib_send.at[n], o_sib_recv.at[n], e, z, 1 - c,
        )

    def o_line(n):
        step, side = jnp.where(z < e, 1, -1), jnp.where(z < e, 0, 1)
        return remote(
            o_mine.at[o_part(n), :], o_z.at[side, o_part(n), :],
            o_zsend.at[n], o_zrecv.at[side, n], e, z + step, c,
        )

    def o_wait(side, n):
        slab = o_z.at[side, o_part(n), :]
        remote(slab, slab, o_zsend.at[n], o_zrecv.at[side, n], e, z, c).wait_recv()
        add(o_mine.at[o_part(n), :], [slab])

    def o_peer(p, n):
        view = o_out.at[o_part(n), :]
        return remote(
            o_mine.at[o_part(n), :], view, o_send.at[p, n], o_recv.at[n], peers[p], z, c
        )

    def o_kept():
        return pltpu.make_async_copy(o_mine, o_out, o_own)

    for i in range(nz):
        for k in range(K):
            hand(k, i).start()
            fetch(k, i).start()
        if i == 0:
            for n in range(pieces):
                o_fetch(n).start()
                o_hand(n).start()

    def finish(k, i):
        fetch(k, i).wait()
        hand(k, i).wait_recv()
        zz = dest[i]
        add(part(k, 1, i), [part(k, 2, i)])
        if i < nz - 1:
            for side in range(2):
                going = zz > z if side == 0 else zz < z
                behind = z > 0 if side == 0 else z < nz - 1

                @pl.when(going & behind)
                def _():
                    zwait(k, side, zz)
                    add(part(k, 1, i), [part(k, 3, side, zz)])

            zcopy(k, i).start()
            return
        for side in range(2):

            @pl.when(z > 0 if side == 0 else z < nz - 1)
            def _():
                zwait(k, side, z)
                add(part(k, 1, i), [part(k, 3, side, z)])

        streams[k][0]()

    x_copy, x_kept, x_total = plane_sum_parts(x_ref, x_out, x_held, x_send, x_recv, x_own)
    for p in (2, 0, 1):
        x_copy(p).start()
    x_kept.start()

    def y_copy(p):
        return remote(
            y_ref.at[peers[p]], y_out.at[e], y_send.at[p], y_recv.at[p], peers[p], z, c
        )

    y_kept = pltpu.make_async_copy(y_ref.at[e], y_out.at[e], y_own)
    y_kept.start()
    for p in range(3):
        y_copy(p).start()

    def o_flow(n):
        o_fetch(n).wait()
        o_hand(n).wait_recv()
        add(o_mine.at[o_part(n), :], [o_sib.at[o_part(n), :]])
        for side in range(2):
            behind = (z > 0) & (z <= e) if side == 0 else (z < nz - 1) & (z >= e)

            @pl.when(behind)
            def _():
                o_wait(side, n)

        @pl.when(z != e)
        def _():
            o_line(n).start()

        @pl.when(z == e)
        def _():
            for p in range(3):
                o_peer(p, n).start()

    streams = [
        plane_stream(
            part(k, 1, nz - 1), lambda q, k=k: part(k, 4, q), *sems[3 * k : 3 * k + 3]
        )
        for k in range(K)
    ]
    turn = K * nz // 2
    order = []
    for k in range(K):
        order += [(k, i) for i in range(1 if k else 0, nz - 1)]
        if k + 1 < K:
            order.append((k + 1, 0))
        order.append((k, nz - 1))
    for n, (k, i) in enumerate(order):
        finish(k, i)
        if n == 0:
            for m in range(pieces):
                o_flow(m)
        if n == turn:
            x_total()

    @pl.when(z == e)
    def _():
        o_kept().start()
        o_kept().wait()
        for n in range(pieces):
            for p in range(3):
                o_peer(p, n).wait_send()

    @pl.when(z != e)
    def _():
        for n in range(pieces):
            view = o_out.at[o_part(n), :]
            remote(view, view, o_send.at[0, n], o_recv.at[n], e, z, c).wait_recv()
            o_line(n).wait_send()

    y_kept.wait()
    for p in range(3):
        x_copy(p).wait_send()
        view = y_out.at[peers[p]]
        remote(view, view, y_send.at[p], y_recv.at[p], e, z, c).wait_recv()
        y_copy(p).wait_send()
    for n in range(pieces):
        o_hand(n).wait_send()
    for i in range(nz):
        for k in range(K):
            hand(k, i).wait_send()
            if i < nz - 1:
                zcopy(k, i).wait_send()
    for _, end in streams:
        end()


def settle_weights(nz, grads, small, rows, near, blocks):
    R, W = grads.shape[2:]
    D = rows.shape[2]
    dma = pltpu.SemaphoreType.DMA
    sd = jax.ShapeDtypeStruct
    vm = pltpu.VMEM
    Ws = small.shape[3]
    return pl.pallas_call(
        functools.partial(settle_kernel, nz),
        out_shape=(
            sd((4, R, W), bf16),
            sd((4, R, Ws), bf16),
            sd((R, D), bf16),
            sd(near.shape[1:], f32),
            sd(blocks.shape, bf16),
        ),
        in_specs=[ANY] * 5,
        out_specs=(ANY,) * 3 + (pl.BlockSpec(memory_space=vm), ANY),
        scratch_shapes=[
            vm(near.shape, bf16), *plane_sems(), *plane_sems(),
            vm((nz, R, W), bf16), vm((nz, R, W), bf16), vm((2, nz, R, W), bf16),
            vm((nz, R, Ws), bf16), vm((nz, R, Ws), bf16), vm((2, nz, R, Ws), bf16),
            vm((R, D), bf16), vm((R, D), bf16), vm((2, R, D), bf16),
            dma((3, nz)), dma((3, nz)), dma((3, nz)), dma((3, nz)), dma((3, 2, nz)),
            dma((6,)), dma((6,)), dma((6,)), dma((6,)), dma((2, 6)),
            dma((3, 6)), dma((6,)), dma(()),
            *plane_sems(), *plane_sems(), *plane_sems(),
        ],
        compiler_params=pltpu.CompilerParams(
            collective_id=1, has_side_effects=True, vmem_limit_bytes=56 << 20
        ),
        cost_estimate=pl.CostEstimate(flops=10**6, bytes_accessed=10**6, transcendentals=0),
        name="settle_weights",
    )(grads, small, rows, near, blocks)


def pick_kernel(width, q_ref, k_ref, v_ref, o_ref):
    e = lax.axis_index("expert")
    spare = o_ref.shape[1] - 3 * width
    if spare:
        o_ref[:, 3 * width :] = jnp.zeros((o_ref.shape[0], spare), o_ref.dtype)
    for n in range(4):

        @pl.when(e == n)
        def _():
            for i, ref in enumerate((q_ref, k_ref, v_ref)):
                o_ref[:, i * width : (i + 1) * width] = ref[:, n * width : (n + 1) * width]


def pick_columns(weights, width):
    vm = pl.BlockSpec(memory_space=pltpu.VMEM)
    return pl.pallas_call(
        functools.partial(pick_kernel, width),
        in_specs=[vm] * 3,
        out_specs=vm,
        out_shape=jax.ShapeDtypeStruct((weights[0].shape[0], -(-3 * width // 128) * 128), bf16),
        name="pick_columns",
    )(*weights)


def assemble_kernel(width, x_ref, *o_refs):
    for n in range(4):
        for i in range(3):
            cols = x_ref[n, :, i * width : (i + 1) * width]
            o_refs[i][:, n * width : (n + 1) * width] = cols.astype(f32)


def assemble_columns(x, width):
    R = x.shape[1]
    block = 32
    return pl.pallas_call(
        functools.partial(assemble_kernel, width),
        grid=(R // block,),
        in_specs=[pl.BlockSpec((4, block, x.shape[2]), lambda i: (0, i, 0))],
        out_specs=(pl.BlockSpec((block, 4 * width), lambda i: (i, 0)),) * 3,
        out_shape=(jax.ShapeDtypeStruct((R, 4 * width), f32),) * 3,
        name="assemble_columns",
    )(x)


def sum_shard(x, axis=0):
    mine = lax.psum_scatter(x, SHARD, scatter_dimension=axis, tiled=True)
    return lax.psum(mine, "expert")


def fetch(nz, fast, weights, w_output, small, tokens, lengths, block, wide, F):
    D = tokens.shape[1]
    if fast:
        width = D // 4
        columns, full_small, rows, tokens, lengths, blocks, packed = fetch_weights(
            nz, pick_columns(weights, width), small, w_output, tokens, lengths, block, wide, F
        )
        columns, rows = columns.reshape(D, -1), rows.reshape(width, D)
        return columns, rows, full_small.reshape(D, -1), tokens, lengths, blocks, packed
    full = [lax.all_gather(w, SHARD, axis=0, tiled=True) for w in weights + (w_output, small)]
    blocks = spread_plain(nz, (block,), 0)[0]
    packed = pack_columns(wide, 2 * nz, F, -(-F // 128) * 128)
    columns = jnp.concatenate(full[:3], axis=1)
    return columns, full[3], full[4], tokens[None], lengths[None], blocks, packed


def settle(nz, fast, columns, rows, small, near, blocks):
    D, width = rows.shape[1], rows.shape[0]
    if fast:
        R = D // (2 * nz)
        parts = [x.astype(bf16).reshape(nz, 2, R, -1) for x in (columns, small)]
        near = near.astype(bf16).reshape(4, -1, D)
        blocks = blocks.reshape(4, -1, D)
        sums, small, out, near, blocks = settle_weights(
            nz, *parts, rows.astype(bf16).reshape(2, R, D), near, blocks
        )
        small, blocks = jnp.sum(small.astype(f32), axis=0), blocks.reshape(-1, D)
        return *assemble_columns(sums, width), out.astype(f32), small, near, blocks
    parts = [columns[:, i * width : (i + 1) * width] for i in range(3)] + [rows, small]
    blocks = lax.all_to_all(blocks, "expert", split_axis=0, concat_axis=0, tiled=True)
    return [sum_shard(x) for x in parts] + [near, blocks]


def spread_plain(nz, blocks, collective):
    out = []
    for block in blocks:
        for axis in ("expert", "core", "z"):
            block = lax.all_gather(block, axis, axis=0)
        out.append(block)
    return out


def collect_plain(nz, rows, notes, dots, T):
    n_exp, cap, D = rows.shape[2:]
    places = (lax.axis_index("expert") * cap + jnp.arange(cap)).astype(f32)
    notes = notes[..., :T]
    pick = (notes[..., 2, None, :] == places[:, None]) | (notes[..., 3, None, :] == places[:, None])
    part = jnp.einsum(
        "zceps,zcepd->zcesd", pick.astype(bf16), rows, preferred_element_type=f32
    ).astype(bf16)
    part = part.transpose(2, 0, 1, 3, 4).reshape(n_exp * nz * 2 * T, D)
    part = lax.psum_scatter(part, "expert", scatter_dimension=0, tiled=True)
    part = lax.psum_scatter(part, SHARD, scatter_dimension=0, tiled=True).astype(f32)
    z, core, e = lax.axis_index("z"), lax.axis_index("core"), lax.axis_index("expert")
    return part, lax.psum(dots, ("expert",) + SHARD)[z, core, e]


def rope_tables(positions, head_width):
    half_width = head_width // 2
    exponents = jnp.arange(half_width).astype(f32) * 2.0 / head_width
    frequency = rope_base ** (-exponents)
    angles = positions.astype(f32)[..., None] * frequency
    return (jnp.cos(angles), jnp.sin(angles))


def rotate(values, cosine, sine_table):
    half_width = values.shape[-1] // 2
    leading = values[..., :half_width]
    trailing = values[..., half_width:]
    cos_rows = cosine[:, :, None, :]
    sin_rows = sine_table[:, :, None, :]
    return jnp.concatenate(
        [leading * cos_rows - trailing * sin_rows, trailing * cos_rows + leading * sin_rows],
        axis=-1,
    )


def rms_forward(values, norm_gain):
    inverse = lax.rsqrt(jnp.mean(values * values, axis=-1, keepdims=True) + eps_norm)
    return (values * inverse * norm_gain, inverse)


def rms_backward(values, inverse, norm_gain, upstream):
    weighted = upstream * norm_gain
    gain_grad = jnp.sum(upstream * values * inverse, axis=0)
    inner_mean = jnp.mean(weighted * values, axis=-1, keepdims=True)
    return (inverse * weighted - values * inverse * inverse * inverse * inner_mean, gain_grad)


def dot32(a, b):
    return jnp.dot(a, b, preferred_element_type=f32)


def dot_dims(a, b, da, db):
    return lax.dot_general(a, b, (((da,), (db,)), ((), ())), preferred_element_type=f32)


def ein32(spec, a, b):
    return jnp.einsum(spec, a, b, preferred_element_type=f32)


def on_device(
    tokens,
    seq_lengths,
    routes,
    norm_attn,
    w_query,
    w_key,
    w_value,
    w_output,
    norm_ffn,
    w_router,
    w_in,
    w_down,
    cotangent,
):
    T, D = tokens.shape
    R = w_query.shape[0]
    head_width = D // HEADS
    n_exp = lax.axis_size("expert")
    nz = lax.axis_size("z")
    n_shard = nz * lax.axis_size("core")
    experts = w_router.shape[1]
    F = w_down.shape[0]
    FF = F * n_shard
    capacity = 10 * T // (4 * experts)
    slots = experts * capacity
    highest = lax.Precision.HIGHEST
    e_index = lax.axis_index("expert")
    fast = n_exp == 4 and nz == 4

    small = jnp.concatenate([w_router, norm_attn[:, None], norm_ffn[:, None]], axis=1)
    small = jnp.pad(small, ((0, 0), (0, 128 - small.shape[1])))
    length_rows = jnp.broadcast_to(seq_lengths[:, :1], (8, 128))
    full_qkv, full_output, full_small, near_tokens, near_lengths, all_cotangent, packed = fetch(
        nz,
        fast,
        (w_query, w_key, w_value),
        w_output,
        small,
        tokens,
        length_rows,
        cotangent,
        w_in.reshape(R, 2 * FF),
        F,
    )
    full_router = full_small[:, :experts]
    gain_attn = full_small[:, experts].astype(f32)
    gain_ffn = full_small[:, experts + 1].astype(f32)

    Fp = -(-F // 128) * 128
    moved = lax.all_to_all(packed, SHARD, split_axis=0, concat_axis=0, tiled=True)
    w_pair = moved.reshape(n_shard * R, 2 * Fp)
    down = jnp.pad(w_down.reshape(F, D), ((0, Fp - F), (0, 0)))

    B, H = near_tokens.shape[0], full_output.shape[0]
    heads = H // head_width
    residual_in = tokens.astype(f32)
    inverse_in = rms_forward(residual_in, gain_attn)[1]
    near_in = near_tokens.reshape(B * T, D).astype(f32)
    near_normed, near_inverse = rms_forward(near_in, gain_attn)
    normed_half = near_normed.astype(bf16)
    lengths = near_lengths[:, 0, 0]
    row_index = jnp.arange(T)
    segment = (row_index[None, :] >= lengths[:, None]).astype(jnp.int32)
    positions = row_index[None, :] - lengths[:, None] * segment
    allowed = (segment[:, :, None] == segment[:, None, :]) & (
        row_index[None, None, :] <= row_index[None, :, None]
    )
    cosine, sine_table = rope_tables(positions, head_width)
    head_shape = (B, T, heads, head_width)
    qkv = dot32(normed_half, full_qkv)
    queries = rotate(qkv[:, :H].reshape(head_shape), cosine, sine_table).astype(bf16)
    keys_rot = rotate(qkv[:, H : 2 * H].reshape(head_shape), cosine, sine_table).astype(bf16)
    values = qkv[:, 2 * H : 3 * H].astype(bf16).reshape(head_shape)
    score_scale = 1.0 / math.sqrt(head_width)
    scores = ein32("bqhd,bkhd->bhqk", queries, keys_rot) * score_scale
    scores = jnp.where(allowed[:, None], scores, masked_score)
    row_peak = jnp.max(scores, axis=-1, keepdims=True)
    log_total = row_peak + jnp.log(jnp.sum(jnp.exp(scores - row_peak), axis=-1, keepdims=True))
    attn_probs = jnp.exp(scores - log_total)
    probs_half = attn_probs.astype(bf16)
    context = ein32("bhqk,bkhd->bqhd", probs_half, values).astype(bf16)
    context_flat = context.reshape(B * T, H)

    def at_home(partial_rows, collective):
        if not fast:
            return partial_rows
        return plane_sum(partial_rows.astype(bf16).reshape(B, T, D), collective)

    residual_mid = residual_in + branch_scale * at_home(dot32(context_flat, full_output), 4)
    normed_mid, inverse_mid = rms_forward(residual_mid, gain_ffn)
    normed_mid_half = normed_mid.astype(bf16)

    logits = dot32(normed_mid_half, full_router)
    expert_ids = jnp.arange(experts)
    route_mask = (routes[:, :, None] == expert_ids[None, None, :]).astype(f32)
    chosen = jnp.sum(logits[:, None, :] * route_mask, axis=-1)
    gate_probs = jax.nn.softmax(chosen, axis=-1)
    flat_routes = routes.reshape(2 * T)
    hits = (flat_routes[:, None] == expert_ids[None, :]).astype(bf16)
    order = jnp.arange(2 * T)
    before = (order[:, None] > order[None, :]).astype(bf16)
    earlier = dot32(before, hits)
    slot_index = jnp.sum(earlier * hits.astype(f32), axis=1).astype(jnp.int32)
    target = (flat_routes * capacity + slot_index).reshape(T, 2)
    slot_ids = jnp.arange(slots)
    pick = [(target[:, k][:, None] == slot_ids[None, :]).astype(bf16) for k in range(2)]

    notes = jnp.concatenate([gate_probs, target.astype(f32), jnp.zeros((T, 4), f32)], axis=1)
    notes = jnp.pad(jnp.transpose(notes), ((0, 0), (0, -T % 128)))
    spread = spread_blocks if fast else spread_plain
    all_normed, all_notes = spread(nz, (normed_mid_half, notes), 2)
    devices = n_shard * n_exp
    flat_notes = all_notes.reshape(devices, 8, -1)[:, :, :T]
    wanted = (e_index * capacity + jnp.arange(capacity)).astype(f32)
    found = [flat_notes[:, 2 + k, None, :] == wanted[None, :, None] for k in range(2)]
    gate_rows = jnp.sum(
        jnp.where(found[0], flat_notes[:, 0, None, :], 0.0)
        + jnp.where(found[1], flat_notes[:, 1, None, :], 0.0),
        axis=-1,
    ).reshape(devices * capacity, 1)
    chosen_rows = (found[0] | found[1]).astype(bf16)

    def take(blocks):
        rows = ein32("spt,std->spd", chosen_rows, blocks.reshape(devices, T, D))
        return rows.astype(bf16).reshape(devices * capacity, D)

    arrived = take(all_normed)
    cotangent_rows = take(all_cotangent)
    grad_scale = gate_rows * branch_scale
    pre = dot32(arrived, w_pair)
    gate_part, up_part = pre[:, :Fp], pre[:, Fp:]
    sigmoid_gate = jax.nn.sigmoid(gate_part)
    silu_gate = gate_part * sigmoid_gate
    activated = (silu_gate * up_part).astype(bf16)
    out_sum = lax.psum_scatter(
        dot32(activated, down).astype(bf16), SHARD, scatter_dimension=0, tiled=True
    )

    raw_grad = dot_dims(cotangent_rows, down, 1, 1)
    row_dots = branch_scale * jnp.sum(raw_grad * activated.astype(f32), axis=1)
    row_dots = row_dots.reshape(devices, capacity, 1)
    token_dots = [jnp.sum(jnp.where(found[k], row_dots, 0.0), axis=1) for k in range(2)]
    token_dots = jnp.stack(token_dots, axis=1).reshape(nz, 2, n_exp, 2, T)
    token_dots = jnp.pad(token_dots, ((0, 0),) * 3 + ((0, 6), (0, -T % 128)))
    act_grad = grad_scale * raw_grad
    pre_grad = jnp.concatenate(
        [
            act_grad * up_part * sigmoid_gate * (1.0 + gate_part * (1.0 - sigmoid_gate)),
            act_grad * silu_gate,
        ],
        axis=1,
    ).astype(bf16)
    in_rows = dot_dims(pre_grad, w_pair, 1, 1).astype(bf16)
    scaled = (grad_scale * activated.astype(f32)).astype(bf16)
    grad_w_down = lined_up(dot_dims(scaled[:, :F], cotangent_rows, 0, 0))
    in_term = dot_dims(arrived, pre_grad, 0, 0).astype(bf16).reshape(n_shard, R, 2 * Fp)
    in_rows, in_term, grad_w_down = lax.optimization_barrier((in_rows, in_term, grad_w_down))
    in_rows = in_rows.reshape(nz, 2, n_exp, capacity, D)
    collect = collect_rows if fast else collect_plain
    normed_mid_grad, gate_grad = collect(nz, in_rows, all_notes, token_dots, T)
    gate_grad = jnp.transpose(gate_grad[:2, :T])
    in_term, normed_mid_grad, out_sum = lax.optimization_barrier(
        (in_term, normed_mid_grad, out_sum)
    )
    in_term = lax.all_to_all(in_term, SHARD, split_axis=0, concat_axis=0, tiled=True)
    grad_w_in = unpack_columns(in_term, F)

    upstream = cotangent.astype(f32)
    chosen_grad = gate_probs * (gate_grad - jnp.sum(gate_probs * gate_grad, axis=-1, keepdims=True))
    logit_grad = jnp.sum(chosen_grad[:, :, None] * route_mask, axis=1)
    normed_mid_grad = normed_mid_grad + jnp.dot(
        logit_grad, jnp.transpose(full_router.astype(f32)), precision=highest
    )
    router_grad = jnp.dot(
        jnp.transpose(normed_mid_half.astype(f32)), logit_grad, precision=highest
    )
    mid_norm_grad, gain_ffn_grad = rms_backward(
        residual_mid, inverse_mid, gain_ffn, normed_mid_grad
    )
    residual_grad = upstream + mid_norm_grad
    branch_grad = (branch_scale * residual_grad).astype(bf16)

    if fast:
        branch_grad = plane_gather(branch_grad, 5).reshape(B * T, D)
    output_grad = dot_dims(context_flat, branch_grad, 0, 0)
    context_grad = dot_dims(branch_grad, full_output, 1, 1).reshape(head_shape)
    row_delta = jnp.sum(context_grad * context.astype(f32), axis=-1)
    context_grad_half = context_grad.astype(bf16)
    probs_grad = ein32("bqhd,bkhd->bhqk", context_grad_half, values)
    scores_grad = (
        attn_probs * (probs_grad - jnp.transpose(row_delta, (0, 2, 1))[..., None]) * score_scale
    ).astype(bf16)
    queries_grad = ein32("bhqk,bkhd->bqhd", scores_grad, keys_rot)
    keys_grad = ein32("bhqk,bqhd->bkhd", scores_grad, queries)
    values_grad = ein32("bhqk,bqhd->bkhd", probs_half, context_grad_half)
    qkv_grad = jnp.concatenate(
        [
            rotate(queries_grad, cosine, -sine_table).reshape(B * T, H).astype(bf16),
            rotate(keys_grad, cosine, -sine_table).reshape(B * T, H).astype(bf16),
            values_grad.reshape(B * T, H).astype(bf16),
            jnp.zeros((B * T, full_qkv.shape[1] - 3 * H), bf16),
        ],
        axis=1,
    )
    qkv_weight_grad = dot_dims(normed_half, qkv_grad, 0, 0)
    near_grad = dot_dims(qkv_grad, full_qkv, 1, 1)
    gain_attn_grad = jnp.sum(near_grad * near_in * near_inverse, axis=0)

    small_grad = jnp.concatenate(
        [router_grad, gain_attn_grad[:, None], gain_ffn_grad[:, None]], axis=1
    )
    small_grad = jnp.pad(small_grad, ((0, 0), (0, 128 - small_grad.shape[1])))
    sum_query, sum_key, sum_value, sum_output, small_sum, normed_in_grad, back = settle(
        nz, fast, qkv_weight_grad, output_grad, small_grad, near_grad, out_sum
    )
    mixture = gate_probs[:, 0:1] * dot32(pick[0], back) + gate_probs[:, 1:2] * dot32(pick[1], back)
    activations = (residual_mid + branch_scale * mixture).astype(bf16)
    in_norm_grad = rms_backward(residual_in, inverse_in, gain_attn, normed_in_grad)[0]
    grad_tokens = residual_grad + in_norm_grad
    return (
        activations,
        grad_tokens,
        small_sum[:, experts],
        sum_query,
        sum_key,
        sum_value,
        sum_output,
        small_sum[:, experts + 1],
        small_sum[:, :experts],
        grad_w_in,
        grad_w_down,
    )


def solution(mesh):
    n_expert, n_shard = mesh.devices.shape
    chips = Mesh(mesh.devices.reshape(n_expert, n_shard // 2, 2), ("expert", "z", "core"))
    rows = P(("expert", "z", "core"), None)
    shard = P(SHARD)
    shard2 = P(SHARD, None)
    shard3 = P(SHARD, "expert", None)
    in_specs = (
        rows,
        rows,
        rows,
        shard,
        shard2,
        shard2,
        shard2,
        shard2,
        shard,
        shard2,
        shard3,
        shard3,
        rows,
    )
    out_specs = (
        rows,
        rows,
        shard,
        shard2,
        shard2,
        shard2,
        shard2,
        shard,
        shard2,
        shard3,
        shard3,
    )
    return jax.shard_map(
        on_device, mesh=chips, in_specs=in_specs, out_specs=out_specs, check_vma=False
    )
```

```python
import functools
import math

import jax
import jax.numpy as jnp
from jax import lax
from jax.experimental import pallas as pl
from jax.experimental.pallas import tpu as pltpu
from jax.sharding import Mesh, PartitionSpec as P

HEADS = 36

eps_norm = 1e-05
branch_scale = 1.4 / math.sqrt(40.0)
rope_base = 10000.0
masked_score = -1e30
bf16 = jnp.bfloat16
f32 = jnp.float32
SHARD = ("z", "core")
ANY = pl.BlockSpec(memory_space=pl.ANY)


def place():
    e, z, c = lax.axis_index("expert"), lax.axis_index("z"), lax.axis_index("core")
    across_x = e + 1 - 2 * (e % 2)
    across_y = (e + 2) % 4
    return e, z, c, across_x, across_y


def remote(src, dst, send, recv, e, z, c):
    return pltpu.make_async_remote_copy(
        src_ref=src,
        dst_ref=dst,
        send_sem=send,
        recv_sem=recv,
        device_id=(e, z, c),
        device_id_type=pl.DeviceIdType.MESH,
    )


def payload_stream(nz, ref, out, sems, split):
    zrecv, zsend, near_recv, near_send, far_recv, far_send, sib_recv, sib_send, own = sems
    e, z, c, ex, ey = place()
    diagonal = (ex + 2) % 4
    T = ref.shape[0]
    S = 2 * nz - 1

    def split_step(s):
        return (s - 1) % 2, (s - 1) // 2

    def where(s):
        if s == 0:
            return z
        side, i = split_step(s)
        return z - 1 - i if side == 0 else z + 1 + i

    def exists(s):
        if s == 0:
            return z >= 0
        zz = where(s)
        return (zz >= 0) & (zz < nz)

    def slab(s, quarter, r0=0, n=T):
        return out.at[where(s), c, quarter, pl.ds(r0, n), :]

    def first(step):
        side = 0 if step > 0 else 1
        return remote(ref, slab(0, e), zsend.at[side, nz - 1], zrecv.at[side, 0], e, z + step, c)

    def onward(s):
        side, i = split_step(s)
        step = 1 if side == 0 else -1
        return remote(
            slab(s, e), slab(s, e), zsend.at[side, i], zrecv.at[side, i + 1], e, z + step, c
        )

    def near(s, axis):
        source = ref if s == 0 else slab(s, e)
        return remote(
            source, slab(s, e), near_send.at[s, axis], near_recv.at[s, axis],
            ex if axis == 0 else ey, z, c,
        )

    def near_wait(s, axis):
        view = slab(s, ex if axis == 0 else ey)
        remote(view, view, near_send.at[s, axis], near_recv.at[s, axis], ex, z, c).wait_recv()

    axes = range(2) if split else range(1)

    def far_view(s, quarter, axis):
        if not split:
            return slab(s, quarter)
        return slab(s, quarter, 0, split) if axis == 0 else slab(s, quarter, split, T - split)

    def far(s, axis):
        view = far_view(s, ex if axis == 0 else ey, axis)
        return remote(
            view, view, far_send.at[s, axis], far_recv.at[s, axis],
            ey if axis == 0 else ex, z, c,
        )

    def far_wait(s, axis):
        view = far_view(s, diagonal, axis)
        remote(view, view, far_send.at[s, axis], far_recv.at[s, axis], ex, z, c).wait_recv()

    def beside(s, n):
        quarter = (e, ex, ey, diagonal)[n]
        source = ref if s == 0 and n == 0 else slab(s, quarter)
        return remote(
            source, slab(s, quarter), sib_send.at[s, n], sib_recv.at[s, n], e, z, 1 - c
        )

    def beside_wait(s, n):
        view = out.at[where(s), 1 - c, (e, ex, ey, diagonal)[n]]
        remote(view, view, sib_send.at[s, n], sib_recv.at[s, n], e, z, c).wait_recv()

    def inside(side):
        return z < nz - 1 if side == 0 else z > 0

    def begin():
        for step in (1, -1):

            @pl.when((z + step >= 0) & (z + step < nz))
            def _():
                first(step).start()

        near(0, 0).start()
        near(0, 1).start()
        beside(0, 0).start()
        pltpu.make_async_copy(ref, slab(0, e), own).start()

    def arrive(s):
        if s == 0:
            return

        @pl.when(exists(s))
        def _():
            side, i = split_step(s)
            remote(
                slab(s, e), slab(s, e), zsend.at[side, i], zrecv.at[side, i], e, z, c
            ).wait_recv()
            if i < nz - 2:

                @pl.when(inside(side))
                def _():
                    onward(s).start()

            near(s, 0).start()
            near(s, 1).start()
            beside(s, 0).start()

    def relay(s):
        @pl.when(exists(s))
        def _():
            near_wait(s, 0)
            far(s, 0).start()
            beside(s, 1).start()
            near_wait(s, 1)
            if split:
                far(s, 1).start()
            beside(s, 2).start()

    def close(s):
        @pl.when(exists(s))
        def _():
            for axis in axes:
                far_wait(s, axis)
            beside(s, 3).start()

    def end(s):
        @pl.when(exists(s))
        def _():
            for axis in range(2):
                near(s, axis).wait_send()
            for axis in axes:
                far(s, axis).wait_send()
            for n in range(4):
                beside(s, n).wait_send()
                beside_wait(s, n)
            if s > 0 and split_step(s)[1] < nz - 2:

                @pl.when(inside(split_step(s)[0]))
                def _():
                    onward(s).wait_send()

        if s == 0:
            for step in (1, -1):

                @pl.when((z + step >= 0) & (z + step < nz))
                def _():
                    first(step).wait_send()

            pltpu.make_async_copy(ref, slab(0, e), own).wait()

    return begin, arrive, relay, close, end


def payload_sems(nz):
    dma = pltpu.SemaphoreType.DMA
    S = 2 * nz - 1
    return [
        dma((2, nz)), dma((2, nz)), dma((S, 2)), dma((S, 2)), dma((S, 2)), dma((S, 2)),
        dma((S, 4)), dma((S, 4)), dma(()),
    ]


def spread_kernel(nz, splits, *refs):
    n = len(splits)
    (gate_ref, up_ref), refs = refs[:2], refs[2:]
    ins, refs = refs[:n], refs[n:]
    pair, outs, sems = refs[0], refs[1 : n + 1], refs[n + 1 :]
    v_sems, beside_sem, sems = sems[:3], sems[3], sems[4:]
    width = gate_ref.shape[2]
    greet_shard(nz)
    streams = [
        payload_stream(nz, ins[i], outs[i], sems[9 * i : 9 * i + 9], splits[i]) for i in range(n)
    ]
    v_begin, v_end = scatter_stream(
        nz, gate_ref, lambda i: pair.at[i, :, pl.ds(0, width)], *v_sems
    )
    beside = pltpu.make_async_copy(up_ref, pair.at[:, :, pl.ds(width, width)], beside_sem)
    for t in streams:
        t[0]()
    beside.start()
    S = 2 * nz - 1
    for s in range(1, S):
        for t in streams:
            t[1](s)
    v_begin()
    for s in range(S):
        for t in streams:
            t[2](s)
        if s >= 1:
            for t in streams:
                t[3](s - 1)
    for t in streams:
        t[3](S - 1)
    for s in range(S):
        for t in streams:
            t[4](s)
    beside.wait()
    v_end()


def spread_blocks(nz, blocks, gate, up, collective):
    sd = jax.ShapeDtypeStruct
    splits = tuple(b.shape[0] // 2 if b.shape[0] % 32 == 0 else 0 for b in blocks)
    pair = sd(gate.shape[:2] + (2 * gate.shape[2],), gate.dtype)
    return pl.pallas_call(
        functools.partial(spread_kernel, nz, splits),
        out_shape=(pair,) + tuple(sd((nz, 2, 4) + b.shape, b.dtype) for b in blocks),
        in_specs=[ANY] * (len(blocks) + 2),
        out_specs=(ANY,) * (len(blocks) + 1),
        scratch_shapes=[
            *scatter_sems(nz), pltpu.SemaphoreType.DMA(()),
            *[s for _ in blocks for s in payload_sems(nz)],
        ],
        compiler_params=pltpu.CompilerParams(collective_id=collective, has_side_effects=True),
        cost_estimate=pl.CostEstimate(flops=10**6, bytes_accessed=10**6, transcendentals=0),
        name="spread_blocks",
    )(gate, up, *blocks)


def line_order(nz, z):
    def order(i):
        code = 0
        for zz in range(nz):
            far_first = sorted(range(nz), key=lambda t: (-abs(t - zz), t))
            code += far_first[i] * nz**zz
        power = 1
        for zz in range(nz):
            power = power + (nz**zz - 1) * jnp.where(z == zz, 1, 0)
        return (code // power) % nz

    return [order(i) for i in range(nz)]


def collect_kernel(
    nz, cap,
    rows_ref, notes_ref, dots_ref,
    out_ref, dots_out,
    dots, notes, mine, theirs, block, from_x, from_y, via_x, via_y, from_z,
    note_sem, load, sib_send, sib_recv, via_send, via_recv, plain_send, plain_recv,
    sum_send, sum_recv, zsend, zrecv, dot_send, dot_recv, dot_own,
):
    e, z, c, ex, ey = place()
    diagonal = (ex + 2) % 4
    T, D = out_ref.shape
    h = T // 2
    dest = line_order(nz, z)
    who = (diagonal, ex, ey, e)

    def others():
        for d in range(1, 8 * nz):
            to = ((e * nz + z) * 2 + c + d) % (8 * nz)
            yield d, to // (2 * nz), to // 2 % nz, to % 2

    barrier = pltpu.get_barrier_semaphore()
    for _, te, tz, tc in others():
        pl.semaphore_signal(
            barrier, inc=1, device_id=(te, tz, tc), device_id_type=pl.DeviceIdType.MESH
        )
    pl.semaphore_wait(barrier, 8 * nz - 1)

    def dot(d, te, tz, tc):
        return remote(
            dots_ref.at[tz, tc, te], dots.at[d], dot_send.at[d], dot_recv.at[d], te, tz, tc
        )

    dot_kept = pltpu.make_async_copy(dots_ref.at[z, c, e], dots.at[0], dot_own)
    dot_kept.start()
    for d, te, tz, tc in others():
        dot(d, te, tz, tc).start()

    note_copy = pltpu.make_async_copy(notes_ref, notes, note_sem)
    note_copy.start()

    def fetch(i, q):
        return pltpu.make_async_copy(
            rows_ref.at[dest[i], c, who[q]], mine.at[i, q], load.at[i, q]
        )

    def hand(i, q):
        return remote(
            rows_ref.at[dest[i], 1 - c, who[q]], theirs.at[i, q],
            sib_send.at[i, q], sib_recv.at[i, q], e, z, 1 - c,
        )

    for i in range(nz):
        for q in range(4):
            hand(i, q).start()
            fetch(i, q).start()
    note_copy.wait()

    def open_out(i, q):
        fetch(i, q).wait()
        hand(i, q).wait_recv()
        places = (lax.broadcasted_iota(jnp.int32, (cap, T), 0) + e * cap).astype(f32)
        note = notes[dest[i], c, who[q]]
        pick = ((note[2:3, :] == places) | (note[3:4, :] == places)).astype(bf16)
        wide = 768 if D % 768 == 0 else 128

        @pl.loop(0, D // wide)
        def _(b):
            cols = pl.ds(pl.multiple_of(b * wide, 128), wide)
            both = mine[i, q, :, cols].astype(f32) + theirs[i, q, :, cols].astype(f32)
            block[i, q, :, cols] = lax.dot_general(
                pick, both.astype(bf16), (((0,), (0,)), ((), ())), preferred_element_type=f32
            ).astype(bf16)

    def via(i, axis):
        if axis == 0:
            return remote(
                block.at[i, 0, pl.ds(0, h), :], via_x.at[i],
                via_send.at[i, 0], via_recv.at[i, 0], ex, z, c,
            )
        return remote(
            block.at[i, 0, pl.ds(h, h), :], via_y.at[i],
            via_send.at[i, 1], via_recv.at[i, 1], ey, z, c,
        )

    def plain(i, axis):
        if axis == 0:
            return remote(
                block.at[i, 1, pl.ds(0, h), :], from_x.at[i, pl.ds(0, h), :],
                plain_send.at[i, 0], plain_recv.at[i, 0], ex, z, c,
            )
        return remote(
            block.at[i, 2, pl.ds(h, h), :], from_y.at[i, pl.ds(h, h), :],
            plain_send.at[i, 1], plain_recv.at[i, 1], ey, z, c,
        )

    def summed(i, axis):
        if axis == 0:
            return remote(
                block.at[i, 1, pl.ds(h, h), :], from_x.at[i, pl.ds(h, h), :],
                sum_send.at[i, 0], sum_recv.at[i, 0], ex, z, c,
            )
        return remote(
            block.at[i, 2, pl.ds(0, h), :], from_y.at[i, pl.ds(0, h), :],
            sum_send.at[i, 1], sum_recv.at[i, 1], ey, z, c,
        )

    def add(target, others, n):
        @pl.loop(0, n // 16)
        def _(b):
            rows = pl.ds(pl.multiple_of(b * 16, 16), 16)
            acc = target[rows, :].astype(f32)
            for o in others:
                acc = acc + o[rows, :].astype(f32)
            target[rows, :] = acc.astype(target.dtype)

    def start(i):
        open_out(i, 0)
        via(i, 0).start()
        via(i, 1).start()
        open_out(i, 1)
        plain(i, 0).start()
        open_out(i, 2)
        plain(i, 1).start()
        open_out(i, 3)

    def combine(i):
        via(i, 0).wait_recv()
        add(block.at[i, 2, pl.ds(0, h), :], [via_x.at[i]], h)
        summed(i, 1).start()
        via(i, 1).wait_recv()
        add(block.at[i, 1, pl.ds(h, h), :], [via_y.at[i]], h)
        summed(i, 0).start()

    def zcopy(i):
        step = jnp.where(dest[i] > z, 1, -1)
        side = jnp.where(dest[i] > z, 0, 1)
        return remote(
            block.at[i, 3], from_z.at[side, dest[i]],
            zsend.at[i], zrecv.at[side, dest[i]], e, z + step, c,
        )

    def zwait(side, zz):
        slab = from_z.at[side, zz]
        remote(slab, slab, zsend.at[0], zrecv.at[side, zz], e, z, c).wait_recv()

    def finish(i):
        for axis in range(2):
            plain(i, axis).wait_recv()
            summed(i, axis).wait_recv()
        zz = dest[i]
        if i < nz - 1:
            add(block.at[i, 3], [from_x.at[i], from_y.at[i]], T)
            for side in range(2):
                going = zz > z if side == 0 else zz < z
                behind = z > 0 if side == 0 else z < nz - 1

                @pl.when(going & behind)
                def _():
                    zwait(side, zz)
                    add(block.at[i, 3], [from_z.at[side, zz]], T)

            zcopy(i).start()
            return

        @pl.loop(0, T // 16)
        def _(b):
            rows = pl.ds(pl.multiple_of(b * 16, 16), 16)
            acc = block[i, 3, rows, :].astype(f32) + from_x[i, rows, :].astype(f32)
            out_ref[rows, :] = acc + from_y[i, rows, :].astype(f32)

        for side in range(2):

            @pl.when(z > 0 if side == 0 else z < nz - 1)
            def _():
                zwait(side, z)
                add(out_ref, [from_z.at[side, z]], T)

    for i in range(nz):
        start(i)
        if i >= 1:
            combine(i - 1)
        if i >= 2:
            finish(i - 2)
    combine(nz - 1)
    if nz >= 2:
        finish(nz - 2)
    finish(nz - 1)

    dot_kept.wait()
    for d, te, tz, tc in others():
        dot(d, te, tz, tc).wait_recv()
        dot(d, te, tz, tc).wait_send()
    dots_out[...] = jnp.sum(dots[...], axis=0)

    for i in range(nz):
        for q in range(4):
            hand(i, q).wait_send()
        for axis in range(2):
            via(i, axis).wait_send()
            plain(i, axis).wait_send()
            summed(i, axis).wait_send()
        if i < nz - 1:
            zcopy(i).wait_send()


def collect_rows(nz, rows, notes, dots, T):
    cap, D = rows.shape[3:]
    dma = pltpu.SemaphoreType.DMA
    vm = pltpu.VMEM
    return pl.pallas_call(
        functools.partial(collect_kernel, nz, cap),
        out_shape=(
            jax.ShapeDtypeStruct((T, D), f32),
            jax.ShapeDtypeStruct(dots.shape[3:], f32),
        ),
        in_specs=[ANY] * 3,
        out_specs=(pl.BlockSpec(memory_space=pltpu.VMEM),) * 2,
        scratch_shapes=[
            vm((8 * nz,) + dots.shape[3:], f32),
            vm(notes.shape, f32),
            vm((nz, 4, cap, D), bf16),
            vm((nz, 4, cap, D), bf16),
            vm((nz, 4, T, D), bf16),
            vm((nz, T, D), bf16),
            vm((nz, T, D), bf16),
            vm((nz, T // 2, D), bf16),
            vm((nz, T // 2, D), bf16),
            vm((2, nz, T, D), bf16),
            dma(()),
            dma((nz, 4)),
            dma((nz, 4)),
            dma((nz, 4)),
            dma((nz, 2)),
            dma((nz, 2)),
            dma((nz, 2)),
            dma((nz, 2)),
            dma((nz, 2)),
            dma((nz, 2)),
            dma((nz,)),
            dma((2, nz)),
            dma((8 * nz,)),
            dma((8 * nz,)),
            dma(()),
        ],
        compiler_params=pltpu.CompilerParams(
            collective_id=3, has_side_effects=True, vmem_limit_bytes=56 << 20
        ),
        cost_estimate=pl.CostEstimate(
            flops=10**6, bytes_accessed=10**6, transcendentals=0
        ),
        name="collect_rows",
    )(rows, notes, dots)


def pack_rows(n, F, Fp, x_ref, *o_refs):
    half = n * F
    rows = x_ref.shape[0]
    for i in range(n):
        for part in range(2):
            cols = x_ref[:, part * half + i * F : part * half + (i + 1) * F]
            if Fp > F:
                cols = jnp.concatenate([cols, jnp.zeros((rows, Fp - F), cols.dtype)], axis=1)
            o_refs[part][i] = cols


def pack_columns(w, n, F, Fp):
    rows = w.shape[0]
    block = 16
    return pl.pallas_call(
        functools.partial(pack_rows, n, F, Fp),
        grid=(rows // block,),
        in_specs=[pl.BlockSpec((block, w.shape[1]), lambda i: (i, 0))],
        out_specs=(pl.BlockSpec((n, block, Fp), lambda i: (0, i, 0)),) * 2,
        out_shape=(jax.ShapeDtypeStruct((n, rows, Fp), w.dtype),) * 2,
        name="pack_columns",
    )(w)


def unpack_kernel(n, F, gate_ref, up_ref, o_ref, line):
    half = n * F
    rows = line.shape[0]
    for i in range(n):
        for part in range(2):
            cols = (up_ref if part else gate_ref)[i, :, :F].astype(f32)
            line[:, part * half + i * F : part * half + (i + 1) * F] = cols
    tiles = 2 * half // 128
    for j in range(tiles):
        o_ref[pl.ds(j, rows, stride=tiles), :] = line[:, j * 128 : (j + 1) * 128]


def unpack_columns(gate, up, F):
    n, rows, Fp = gate.shape
    block = 16
    width = 2 * n * F
    tiles = width // 128
    flat = pl.pallas_call(
        functools.partial(unpack_kernel, n, F),
        grid=(rows // block,),
        in_specs=[pl.BlockSpec((n, block, Fp), lambda i: (0, i, 0))] * 2,
        out_specs=pl.BlockSpec((block * tiles, 128), lambda i: (i, 0)),
        out_shape=jax.ShapeDtypeStruct((rows * tiles, 128), f32),
        scratch_shapes=[pltpu.VMEM((block, width), f32)],
        name="unpack_columns",
    )(gate, up)
    return flat.reshape(rows, 1, width)


def line_kernel(x_ref, o_ref):
    rows, width = x_ref.shape
    tiles = width // 128
    for j in range(tiles):
        o_ref[pl.ds(j, rows, stride=tiles), :] = x_ref[:, j * 128 : (j + 1) * 128]


def lined_up(x):
    rows, width = x.shape
    tiles = width // 128
    block = 80 if rows % 80 == 0 else 8
    flat = pl.pallas_call(
        line_kernel,
        grid=(rows // block,),
        in_specs=[pl.BlockSpec((block, width), lambda i: (i, 0))],
        out_specs=pl.BlockSpec((block * tiles, 128), lambda i: (i, 0)),
        out_shape=jax.ShapeDtypeStruct((rows * tiles, 128), x.dtype),
        name="lined_up",
    )(x)
    return flat.reshape(rows, 1, width)


def greet_cross(nz):
    e, z, c, ex, ey = place()
    barrier = pltpu.get_barrier_semaphore()

    def hail(te, tz, tc):
        pl.semaphore_signal(
            barrier, inc=1, device_id=(te, tz, tc), device_id_type=pl.DeviceIdType.MESH
        )

    hail(e, z, 1 - c)
    for te in (ex, ey, (ex + 2) % 4):
        hail(te, z, c)
    for step in (-1, 1):

        @pl.when((z + step >= 0) & (z + step < nz))
        def _():
            hail(e, z + step, c)

    pl.semaphore_wait(barrier, 4 + jnp.where(z > 0, 1, 0) + jnp.where(z < nz - 1, 1, 0))


def greet_shard(nz):
    e, z, c, ex, ey = place()
    barrier = pltpu.get_barrier_semaphore()
    n = 2 * nz
    peers = [(te, z, c) for te in (ex, ey, (ex + 2) % 4)]
    for d in range(1, n):
        to = (2 * z + c + d) % n
        peers.append((e, to // 2, to % 2))
    for peer in peers:
        pl.semaphore_signal(barrier, inc=1, device_id=peer, device_id_type=pl.DeviceIdType.MESH)
    pl.semaphore_wait(barrier, n + 2)


def scatter_stream(nz, ref, view, send, recv, own):
    e, z, c, _, _ = place()
    n = 2 * nz
    me = 2 * z + c

    def copy(d):
        to = (me + d) % n
        return remote(ref.at[to], view(me), send.at[d], recv.at[d], e, to // 2, to % 2)

    kept = pltpu.make_async_copy(ref.at[me], view(me), own)

    def begin():
        for d in range(1, n):
            copy(d).start()
        kept.start()

    def end():
        kept.wait()
        for d in range(1, n):
            land = view((me + n - d) % n)
            remote(land, land, send.at[d], recv.at[d], e, z, c).wait_recv()
            copy(d).wait_send()

    return begin, end


def scatter_sems(nz):
    dma = pltpu.SemaphoreType.DMA
    return [dma((2 * nz,)), dma((2 * nz,)), dma(())]


def line_stream(nz, ref, out, zrecv, zsend, sib_recv, sib_send, own):
    e, z, c, _, _ = place()

    def split_step(s):
        return (s - 1) % 2, (s - 1) // 2

    def where(s):
        if s == 0:
            return z
        side, i = split_step(s)
        return z - 1 - i if side == 0 else z + 1 + i

    def exists(s):
        return (where(s) >= 0) & (where(s) < nz)

    def inside(side):
        return z < nz - 1 if side == 0 else z > 0

    def slab(s):
        return out.at[where(s), c]

    def first(side):
        step = 1 if side == 0 else -1
        return remote(ref, slab(0), zsend.at[side, nz - 1], zrecv.at[side, 0], e, z + step, c)

    def onward(s):
        side, i = split_step(s)
        step = 1 if side == 0 else -1
        return remote(
            slab(s), slab(s), zsend.at[side, i], zrecv.at[side, i + 1], e, z + step, c
        )

    def beside(s):
        return remote(
            ref if s == 0 else slab(s), slab(s), sib_send.at[s], sib_recv.at[s], e, z, 1 - c
        )

    def begin():
        for side in range(2):

            @pl.when(inside(side))
            def _():
                first(side).start()

        beside(0).start()
        pltpu.make_async_copy(ref, slab(0), own).start()

    def arrive(s):
        side, i = split_step(s)

        @pl.when(exists(s))
        def _():
            remote(slab(s), slab(s), zsend.at[side, i], zrecv.at[side, i], e, z, c).wait_recv()
            if i < nz - 2:

                @pl.when(inside(side))
                def _():
                    onward(s).start()

            beside(s).start()

    def end():
        for s in range(2 * nz - 1):

            @pl.when(exists(s))
            def _():
                beside(s).wait_send()
                view = out.at[where(s), 1 - c]
                remote(view, view, sib_send.at[s], sib_recv.at[s], e, z, c).wait_recv()
                if s > 0 and split_step(s)[1] < nz - 2:

                    @pl.when(inside(split_step(s)[0]))
                    def _():
                        onward(s).wait_send()

        for side in range(2):

            @pl.when(inside(side))
            def _():
                first(side).wait_send()

        pltpu.make_async_copy(ref, slab(0), own).wait()

    return begin, arrive, end


def line_sems(nz):
    dma = pltpu.SemaphoreType.DMA
    S = 2 * nz - 1
    return [dma((2, nz)), dma((2, nz)), dma((S,)), dma((S,)), dma(())]


def plane_stream(source, views, send, recv, own):
    e, z, c, ex, ey = place()
    peers = (ex, ey, (ex + 2) % 4)

    def copy(n):
        return remote(source, views(e), send.at[n], recv.at[n], peers[n], z, c)

    def kept():
        return pltpu.make_async_copy(source, views(e), own)

    def begin():
        for n in range(3):
            copy(n).start()
        kept().start()

    def end():
        kept().wait()
        for n in range(3):
            view = views(peers[n])
            remote(view, view, send.at[n], recv.at[n], e, z, c).wait_recv()
            copy(n).wait_send()

    return begin, end


def plane_sems():
    dma = pltpu.SemaphoreType.DMA
    return [dma((3,)), dma((3,)), dma(())]


def fetch_kernel(
    nz,
    F, w_ref, s_ref, o_ref, t_ref, l_ref, p_ref, x_ref,
    w_out, s_out, o_out, t_out, l_out, p_out, gate_out, up_out,
    wide, gate, up, wide_sem, packed_sem,
    *sems,
):
    e, z, c, ex, ey = place()
    w_sems, sems = sems[:5], sems[5:]
    s_sems, sems = sems[:5], sems[5:]
    t_sems, sems = sems[:3], sems[3:]
    l_sems, sems = sems[:3], sems[3:]
    p_sems, sems = sems[:9], sems[9:]
    orecv, osend, sib_recv, sib_send, own = sems
    wide_copy = pltpu.make_async_copy(x_ref, wide, wide_sem)
    wide_copy.start()
    greet_cross(nz)
    w_begin, w_arrive, w_end = line_stream(nz, w_ref, w_out, *w_sems)
    s_begin, s_arrive, s_end = line_stream(nz, s_ref, s_out, *s_sems)
    t_begin, t_end = plane_stream(t_ref, lambda q: t_out.at[q], *t_sems)
    l_begin, l_end = plane_stream(l_ref, lambda q: l_out.at[q], *l_sems)
    p_begin, p_arrive, p_relay, p_close, p_end = payload_stream(
        nz, p_ref, p_out, p_sems, p_ref.shape[0] // 2
    )

    pieces = orecv.shape[0]
    height = o_ref.shape[0] // pieces

    def o_part(n):
        return pl.ds(n * height, height)

    def o_view(n):
        return o_out.at[c, o_part(n), :]

    def o_copy(side, n, source):
        step = 1 if side == 0 else -1
        return remote(source, o_view(n), osend.at[side, n], orecv.at[n], e, z + step, c)

    def o_beside(n, source):
        return remote(source, o_view(n), sib_send.at[n], sib_recv.at[n], e, z, 1 - c)

    def o_goes(side):
        return (z >= e) & (z < nz - 1) if side == 0 else (z <= e) & (z > 0)

    def o_pass(n, source):
        for side in range(2):

            @pl.when(o_goes(side))
            def _():
                o_copy(side, n, source).start()

        o_beside(n, source).start()

    def o_arrive(n):
        @pl.when(z != e)
        def _():
            remote(o_view(n), o_view(n), sib_send.at[n], orecv.at[n], e, z, c).wait_recv()
            o_pass(n, o_view(n))

    p_begin()

    @pl.when(z == e)
    def _():
        for n in range(pieces):
            o_pass(n, o_ref.at[o_part(n), :])
        pltpu.make_async_copy(o_ref, o_out.at[c], own).start()

    s_begin()
    w_begin()
    t_begin()
    l_begin()

    wide_copy.wait()

    @pl.loop(0, wide.shape[0] // 16)
    def _(b):
        rows = pl.ds(pl.multiple_of(b * 16, 16), 16)
        pack_rows(
            gate.shape[0], F, gate.shape[2], wide.at[rows, :], gate.at[:, rows, :], up.at[:, rows, :]
        )

    packed_copies = [
        pltpu.make_async_copy(a, b, packed_sem.at[n])
        for n, (a, b) in enumerate(((gate, gate_out), (up, up_out)))
    ]
    for copy in packed_copies:
        copy.start()

    blocks = 2 * nz - 1
    for s in range(1, blocks):
        p_arrive(s)
        s_arrive(s)
        if s <= pieces:
            o_arrive(s - 1)
    for n in range(blocks - 1, pieces):
        o_arrive(n)
    for s in range(1, blocks):
        p_relay(s - 1)
        w_arrive(s)
        if s >= 2:
            p_close(s - 2)
    p_relay(blocks - 1)
    p_close(blocks - 2)
    p_close(blocks - 1)
    for s in range(blocks):
        p_end(s)
    w_end()
    s_end()
    t_end()
    l_end()
    for n in range(pieces):
        view = o_out.at[1 - c, o_part(n), :]
        remote(view, view, sib_send.at[n], sib_recv.at[n], e, z, c).wait_recv()
        o_beside(n, o_view(n)).wait_send()
        for side in range(2):

            @pl.when(o_goes(side))
            def _():
                o_copy(side, n, o_view(n)).wait_send()

    @pl.when(z == e)
    def _():
        pltpu.make_async_copy(o_ref, o_out.at[c], own).wait()

    for copy in packed_copies:
        copy.wait()


def fetch_weights(nz, columns, small, rows, tokens, lengths, block, wide, F):
    dma = pltpu.SemaphoreType.DMA
    packed = (2 * nz, wide.shape[0], -(-F // 128) * 128)
    sd = jax.ShapeDtypeStruct
    return pl.pallas_call(
        functools.partial(fetch_kernel, nz, F),
        out_shape=(
            sd((nz, 2) + columns.shape, bf16),
            sd((nz, 2) + small.shape, bf16),
            sd((2,) + rows.shape, bf16),
            sd((4,) + tokens.shape, bf16),
            sd((4,) + lengths.shape, lengths.dtype),
            sd((nz, 2, 4) + block.shape, block.dtype),
            sd(packed, wide.dtype),
            sd(packed, wide.dtype),
        ),
        in_specs=[ANY] * 7,
        out_specs=(ANY,) * 8,
        scratch_shapes=[
            pltpu.VMEM(wide.shape, wide.dtype), pltpu.VMEM(packed, wide.dtype),
            pltpu.VMEM(packed, wide.dtype), dma(()), dma((2,)),
            *line_sems(nz), *line_sems(nz), *plane_sems(), *plane_sems(), *payload_sems(nz),
            dma((6,)), dma((2, 6)), dma((6,)), dma((6,)), dma(()),
        ],
        compiler_params=pltpu.CompilerParams(
            collective_id=0, has_side_effects=True, vmem_limit_bytes=32 << 20
        ),
        cost_estimate=pl.CostEstimate(
            flops=10**11, bytes_accessed=8 * columns.size, transcendentals=0
        ),
        name="fetch_weights",
    )(columns, small, rows, tokens, lengths, block, wide)


def plane_gather_kernel(x_ref, out_ref, send, recv, own):
    e, z, c, ex, ey = place()
    greet_plane()
    begin, end = plane_stream(x_ref, lambda q: out_ref.at[q], send, recv, own)
    begin()
    end()


def greet_plane():
    e, z, c, ex, ey = place()
    barrier = pltpu.get_barrier_semaphore()
    for te in (ex, ey, (ex + 2) % 4):
        pl.semaphore_signal(
            barrier, inc=1, device_id=(te, z, c), device_id_type=pl.DeviceIdType.MESH
        )
    pl.semaphore_wait(barrier, 3)


def plane_gather(x, collective):
    return pl.pallas_call(
        plane_gather_kernel,
        out_shape=jax.ShapeDtypeStruct((4,) + x.shape, x.dtype),
        in_specs=[ANY],
        out_specs=ANY,
        scratch_shapes=plane_sems(),
        compiler_params=pltpu.CompilerParams(collective_id=collective, has_side_effects=True),
        cost_estimate=pl.CostEstimate(flops=10**6, bytes_accessed=10**6, transcendentals=0),
        name="plane_gather",
    )(x)


def plane_sum_parts(x_ref, out_ref, held, send, recv, own):
    e, z, c, ex, ey = place()
    peers = (ex, ey, (ex + 2) % 4)

    def copy(n):
        return remote(x_ref.at[peers[n]], held.at[n], send.at[n], recv.at[n], peers[n], z, c)

    kept = pltpu.make_async_copy(x_ref.at[e], held.at[3], own)

    def total():
        kept.wait()
        for n in range(3):
            copy(n).wait_recv()

        @pl.loop(0, out_ref.shape[0] // 16)
        def _(b):
            rows = pl.ds(pl.multiple_of(b * 16, 16), 16)
            acc = held[3, rows, :].astype(f32) + held[0, rows, :].astype(f32)
            acc = acc + held[1, rows, :].astype(f32)
            out_ref[rows, :] = acc + held[2, rows, :].astype(f32)

    return copy, kept, total


def plane_sum_kernel(x_ref, out_ref, held, send, recv, own):
    greet_plane()
    copy, kept, total = plane_sum_parts(x_ref, out_ref, held, send, recv, own)
    for n in (2, 0, 1):
        copy(n).start()
    kept.start()
    total()
    for n in range(3):
        copy(n).wait_send()


def plane_sum(x, collective):
    vm = pltpu.VMEM
    return pl.pallas_call(
        plane_sum_kernel,
        out_shape=jax.ShapeDtypeStruct(x.shape[1:], f32),
        in_specs=[ANY],
        out_specs=pl.BlockSpec(memory_space=vm),
        scratch_shapes=[vm(x.shape, bf16), *plane_sems()],
        compiler_params=pltpu.CompilerParams(collective_id=collective, has_side_effects=True),
        cost_estimate=pl.CostEstimate(flops=10**6, bytes_accessed=10**6, transcendentals=0),
        name="plane_sum",
    )(x)


def settle_kernel(
    nz,
    g_ref, s_ref, o_ref, x_ref, y_ref, v_ref,
    g_out, s_out, o_out, x_out, y_out, v_out,
    v_send, v_recv, v_own,
    x_held, x_send, x_recv, x_own, y_send, y_recv, y_own,
    g_mine, g_sib, g_z, s_mine, s_sib, s_z, o_mine, o_sib, o_z,
    load, sib_send, sib_recv, zsend, zrecv,
    o_load, o_sib_send, o_sib_recv, o_zsend, o_zrecv,
    o_send, o_recv, o_own,
    *sems,
):
    e, z, c, ex, ey = place()
    peers = (ex, ey, (ex + 2) % 4)
    dest = line_order(nz, z)
    greet_shard(nz)
    v_begin, v_end = scatter_stream(nz, v_ref, lambda i: v_out.at[i], v_send, v_recv, v_own)
    W = g_ref.shape[3]
    first = W // 256 * 128
    groups = (
        (g_ref, g_mine, g_sib, g_z, g_out, pl.ds(0, first)),
        (g_ref, g_mine, g_sib, g_z, g_out, pl.ds(first, W - first)),
        (s_ref, s_mine, s_sib, s_z, s_out, pl.ds(0, s_ref.shape[3])),
    )
    K = len(groups)

    def part(k, which, *index):
        return groups[k][which].at[(*index, slice(None), groups[k][5])]

    def fetch(k, i):
        return pltpu.make_async_copy(
            part(k, 0, dest[i], c), part(k, 1, i), load.at[k, i]
        )

    def hand(k, i):
        return remote(
            part(k, 0, dest[i], 1 - c), part(k, 2, i),
            sib_send.at[k, i], sib_recv.at[k, i], e, z, 1 - c,
        )

    def zcopy(k, i):
        step = jnp.where(dest[i] > z, 1, -1)
        side = jnp.where(dest[i] > z, 0, 1)
        return remote(
            part(k, 1, i), part(k, 3, side, dest[i]),
            zsend.at[k, i], zrecv.at[k, side, dest[i]], e, z + step, c,
        )

    def zwait(k, side, zz):
        slab = part(k, 3, side, zz)
        remote(slab, slab, zsend.at[k, 0], zrecv.at[k, side, zz], e, z, c).wait_recv()

    def add(target, others):
        @pl.loop(0, target.shape[0] // 16)
        def _(b):
            rows = pl.ds(pl.multiple_of(b * 16, 16), 16)
            acc = target[rows, :].astype(f32)
            for o in others:
                acc = acc + o[rows, :].astype(f32)
            target[rows, :] = acc.astype(target.dtype)

    pieces = o_load.shape[0]
    height = o_mine.shape[0] // pieces

    def o_part(n):
        return pl.ds(n * height, height)

    def o_fetch(n):
        return pltpu.make_async_copy(o_ref.at[c, o_part(n), :], o_mine.at[o_part(n), :], o_load.at[n])

    def o_hand(n):
        return remote(
            o_ref.at[1 - c, o_part(n), :], o_sib.at[o_part(n), :],
            o_sib_send.at[n], o_sib_recv.at[n], e, z, 1 - c,
        )

    def o_line(n):
        step, side = jnp.where(z < e, 1, -1), jnp.where(z < e, 0, 1)
        return remote(
            o_mine.at[o_part(n), :], o_z.at[side, o_part(n), :],
            o_zsend.at[n], o_zrecv.at[side, n], e, z + step, c,
        )

    def o_wait(side, n):
        slab = o_z.at[side, o_part(n), :]
        remote(slab, slab, o_zsend.at[n], o_zrecv.at[side, n], e, z, c).wait_recv()
        add(o_mine.at[o_part(n), :], [slab])

    def o_peer(p, n):
        view = o_out.at[o_part(n), :]
        return remote(
            o_mine.at[o_part(n), :], view, o_send.at[p, n], o_recv.at[n], peers[p], z, c
        )

    def o_kept():
        return pltpu.make_async_copy(o_mine, o_out, o_own)

    for i in range(nz):
        for k in range(K):
            hand(k, i).start()
            fetch(k, i).start()
        if i == 0:
            for n in range(pieces):
                o_fetch(n).start()
                o_hand(n).start()

    def finish(k, i):
        fetch(k, i).wait()
        hand(k, i).wait_recv()
        zz = dest[i]
        add(part(k, 1, i), [part(k, 2, i)])
        if i < nz - 1:
            for side in range(2):
                going = zz > z if side == 0 else zz < z
                behind = z > 0 if side == 0 else z < nz - 1

                @pl.when(going & behind)
                def _():
                    zwait(k, side, zz)
                    add(part(k, 1, i), [part(k, 3, side, zz)])

            zcopy(k, i).start()
            return
        for side in range(2):

            @pl.when(z > 0 if side == 0 else z < nz - 1)
            def _():
                zwait(k, side, z)
                add(part(k, 1, i), [part(k, 3, side, z)])

        streams[k][0]()

    x_copy, x_kept, x_total = plane_sum_parts(x_ref, x_out, x_held, x_send, x_recv, x_own)
    for p in (2, 0, 1):
        x_copy(p).start()
    x_kept.start()

    def y_copy(p):
        return remote(
            y_ref.at[peers[p]], y_out.at[e], y_send.at[p], y_recv.at[p], peers[p], z, c
        )

    y_kept = pltpu.make_async_copy(y_ref.at[e], y_out.at[e], y_own)
    y_kept.start()
    for p in range(3):
        y_copy(p).start()

    def o_flow(n):
        o_fetch(n).wait()
        o_hand(n).wait_recv()
        add(o_mine.at[o_part(n), :], [o_sib.at[o_part(n), :]])
        for side in range(2):
            behind = (z > 0) & (z <= e) if side == 0 else (z < nz - 1) & (z >= e)

            @pl.when(behind)
            def _():
                o_wait(side, n)

        @pl.when(z != e)
        def _():
            o_line(n).start()

        @pl.when(z == e)
        def _():
            for p in range(3):
                o_peer(p, n).start()

    streams = [
        plane_stream(
            part(k, 1, nz - 1), lambda q, k=k: part(k, 4, q), *sems[3 * k : 3 * k + 3]
        )
        for k in range(K)
    ]
    turn = K * nz // 2
    order = []
    for k in range(K):
        order += [(k, i) for i in range(1 if k else 0, nz - 1)]
        if k + 1 < K:
            order.append((k + 1, 0))
        order.append((k, nz - 1))
    for n, (k, i) in enumerate(order):
        finish(k, i)
        if n == 0:
            for m in range(pieces):
                o_flow(m)
        if n == turn:
            x_total()
        if (k, i) == (1, nz - 2):
            v_begin()

    @pl.when(z == e)
    def _():
        o_kept().start()
        o_kept().wait()
        for n in range(pieces):
            for p in range(3):
                o_peer(p, n).wait_send()

    @pl.when(z != e)
    def _():
        for n in range(pieces):
            view = o_out.at[o_part(n), :]
            remote(view, view, o_send.at[0, n], o_recv.at[n], e, z, c).wait_recv()
            o_line(n).wait_send()

    y_kept.wait()
    for p in range(3):
        x_copy(p).wait_send()
        view = y_out.at[peers[p]]
        remote(view, view, y_send.at[p], y_recv.at[p], e, z, c).wait_recv()
        y_copy(p).wait_send()
    for n in range(pieces):
        o_hand(n).wait_send()
    for i in range(nz):
        for k in range(K):
            hand(k, i).wait_send()
            if i < nz - 1:
                zcopy(k, i).wait_send()
    for _, end in streams:
        end()
    v_end()


def settle_weights(nz, grads, small, rows, near, blocks, columns):
    R, W = grads.shape[2:]
    D = rows.shape[2]
    dma = pltpu.SemaphoreType.DMA
    sd = jax.ShapeDtypeStruct
    vm = pltpu.VMEM
    Ws = small.shape[3]
    return pl.pallas_call(
        functools.partial(settle_kernel, nz),
        out_shape=(
            sd((4, R, W), bf16),
            sd((4, R, Ws), bf16),
            sd((R, D), bf16),
            sd(near.shape[1:], f32),
            sd(blocks.shape, bf16),
            sd(columns.shape, bf16),
        ),
        in_specs=[ANY] * 6,
        out_specs=(ANY,) * 3 + (pl.BlockSpec(memory_space=vm), ANY, ANY),
        scratch_shapes=[
            *scatter_sems(nz),
            vm(near.shape, bf16), *plane_sems(), *plane_sems(),
            vm((nz, R, W), bf16), vm((nz, R, W), bf16), vm((2, nz, R, W), bf16),
            vm((nz, R, Ws), bf16), vm((nz, R, Ws), bf16), vm((2, nz, R, Ws), bf16),
            vm((R, D), bf16), vm((R, D), bf16), vm((2, R, D), bf16),
            dma((3, nz)), dma((3, nz)), dma((3, nz)), dma((3, nz)), dma((3, 2, nz)),
            dma((6,)), dma((6,)), dma((6,)), dma((6,)), dma((2, 6)),
            dma((3, 6)), dma((6,)), dma(()),
            *plane_sems(), *plane_sems(), *plane_sems(),
        ],
        compiler_params=pltpu.CompilerParams(
            collective_id=1, has_side_effects=True, vmem_limit_bytes=56 << 20
        ),
        cost_estimate=pl.CostEstimate(flops=10**6, bytes_accessed=10**6, transcendentals=0),
        name="settle_weights",
    )(grads, small, rows, near, blocks, columns)


def pick_kernel(width, q_ref, k_ref, v_ref, o_ref):
    e = lax.axis_index("expert")
    spare = o_ref.shape[1] - 3 * width
    if spare:
        o_ref[:, 3 * width :] = jnp.zeros((o_ref.shape[0], spare), o_ref.dtype)
    for n in range(4):

        @pl.when(e == n)
        def _():
            for i, ref in enumerate((q_ref, k_ref, v_ref)):
                o_ref[:, i * width : (i + 1) * width] = ref[:, n * width : (n + 1) * width]


def pick_columns(weights, width):
    vm = pl.BlockSpec(memory_space=pltpu.VMEM)
    return pl.pallas_call(
        functools.partial(pick_kernel, width),
        in_specs=[vm] * 3,
        out_specs=vm,
        out_shape=jax.ShapeDtypeStruct((weights[0].shape[0], -(-3 * width // 128) * 128), bf16),
        name="pick_columns",
    )(*weights)


def assemble_kernel(width, x_ref, *o_refs):
    for n in range(4):
        for i in range(3):
            cols = x_ref[n, :, i * width : (i + 1) * width]
            o_refs[i][:, n * width : (n + 1) * width] = cols.astype(f32)


def assemble_columns(x, width):
    R = x.shape[1]
    block = 32
    return pl.pallas_call(
        functools.partial(assemble_kernel, width),
        grid=(R // block,),
        in_specs=[pl.BlockSpec((4, block, x.shape[2]), lambda i: (0, i, 0))],
        out_specs=(pl.BlockSpec((block, 4 * width), lambda i: (i, 0)),) * 3,
        out_shape=(jax.ShapeDtypeStruct((R, 4 * width), f32),) * 3,
        name="assemble_columns",
    )(x)


def sum_shard(x, axis=0):
    mine = lax.psum_scatter(x, SHARD, scatter_dimension=axis, tiled=True)
    return lax.psum(mine, "expert")


def fetch(nz, fast, weights, w_output, small, tokens, lengths, block, wide, F):
    D = tokens.shape[1]
    if fast:
        width = D // 4
        columns, full_small, rows, tokens, lengths, blocks, *packed = fetch_weights(
            nz, pick_columns(weights, width), small, w_output, tokens, lengths, block, wide, F
        )
        columns, rows = columns.reshape(D, -1), rows.reshape(width, D)
        return columns, rows, full_small.reshape(D, -1), tokens, lengths, blocks, packed
    full = [lax.all_gather(w, SHARD, axis=0, tiled=True) for w in weights + (w_output, small)]
    blocks = spread_plain(nz, (block,), 0)[0]
    packed = pack_columns(wide, 2 * nz, F, -(-F // 128) * 128)
    columns = jnp.concatenate(full[:3], axis=1)
    return columns, full[3], full[4], tokens[None], lengths[None], blocks, packed


def settle(nz, fast, columns, rows, small, near, blocks, term):
    D, width = rows.shape[1], rows.shape[0]
    if fast:
        R = D // (2 * nz)
        parts = [x.astype(bf16).reshape(nz, 2, R, -1) for x in (columns, small)]
        near = near.astype(bf16).reshape(4, -1, D)
        blocks = blocks.reshape(4, -1, D)
        sums, small, out, near, blocks, term = settle_weights(
            nz, *parts, rows.astype(bf16).reshape(2, R, D), near, blocks, term
        )
        small, blocks = jnp.sum(small.astype(f32), axis=0), blocks.reshape(-1, D)
        return *assemble_columns(sums, width), out.astype(f32), small, near, blocks, term
    parts = [columns[:, i * width : (i + 1) * width] for i in range(3)] + [rows, small]
    blocks = lax.all_to_all(blocks, "expert", split_axis=0, concat_axis=0, tiled=True)
    term = lax.all_to_all(term, SHARD, split_axis=0, concat_axis=0, tiled=True)
    return [sum_shard(x) for x in parts] + [near, blocks, term]


def spread_plain(nz, blocks, collective):
    out = []
    for block in blocks:
        for axis in ("expert", "core", "z"):
            block = lax.all_gather(block, axis, axis=0)
        out.append(block)
    return out


def spread_pair(nz, blocks, gate, up, collective):
    gate = lax.all_to_all(gate, SHARD, split_axis=0, concat_axis=0, tiled=True)
    return jnp.concatenate([gate, up], axis=2), *spread_plain(nz, blocks, collective)


def collect_plain(nz, rows, notes, dots, T):
    n_exp, cap, D = rows.shape[2:]
    places = (lax.axis_index("expert") * cap + jnp.arange(cap)).astype(f32)
    notes = notes[..., :T]
    pick = (notes[..., 2, None, :] == places[:, None]) | (notes[..., 3, None, :] == places[:, None])
    part = jnp.einsum(
        "zceps,zcepd->zcesd", pick.astype(bf16), rows, preferred_element_type=f32
    ).astype(bf16)
    part = part.transpose(2, 0, 1, 3, 4).reshape(n_exp * nz * 2 * T, D)
    part = lax.psum_scatter(part, "expert", scatter_dimension=0, tiled=True)
    part = lax.psum_scatter(part, SHARD, scatter_dimension=0, tiled=True).astype(f32)
    z, core, e = lax.axis_index("z"), lax.axis_index("core"), lax.axis_index("expert")
    return part, lax.psum(dots, ("expert",) + SHARD)[z, core, e]


def rope_tables(positions, head_width):
    half_width = head_width // 2
    exponents = jnp.arange(half_width).astype(f32) * 2.0 / head_width
    frequency = rope_base ** (-exponents)
    angles = positions.astype(f32)[..., None] * frequency
    return (jnp.cos(angles), jnp.sin(angles))


def rotate(values, cosine, sine_table):
    half_width = values.shape[-1] // 2
    leading = values[..., :half_width]
    trailing = values[..., half_width:]
    cos_rows = cosine[:, :, None, :]
    sin_rows = sine_table[:, :, None, :]
    return jnp.concatenate(
        [leading * cos_rows - trailing * sin_rows, trailing * cos_rows + leading * sin_rows],
        axis=-1,
    )


def rms_forward(values, norm_gain):
    inverse = lax.rsqrt(jnp.mean(values * values, axis=-1, keepdims=True) + eps_norm)
    return (values * inverse * norm_gain, inverse)


def rms_backward(values, inverse, norm_gain, upstream):
    weighted = upstream * norm_gain
    gain_grad = jnp.sum(upstream * values * inverse, axis=0)
    inner_mean = jnp.mean(weighted * values, axis=-1, keepdims=True)
    return (inverse * weighted - values * inverse * inverse * inverse * inner_mean, gain_grad)


def dot32(a, b):
    return jnp.dot(a, b, preferred_element_type=f32)


def dot_dims(a, b, da, db):
    return lax.dot_general(a, b, (((da,), (db,)), ((), ())), preferred_element_type=f32)


def ein32(spec, a, b):
    return jnp.einsum(spec, a, b, preferred_element_type=f32)


def on_device(
    tokens,
    seq_lengths,
    routes,
    norm_attn,
    w_query,
    w_key,
    w_value,
    w_output,
    norm_ffn,
    w_router,
    w_in,
    w_down,
    cotangent,
):
    T, D = tokens.shape
    R = w_query.shape[0]
    head_width = D // HEADS
    n_exp = lax.axis_size("expert")
    nz = lax.axis_size("z")
    n_shard = nz * lax.axis_size("core")
    experts = w_router.shape[1]
    F = w_down.shape[0]
    FF = F * n_shard
    capacity = 10 * T // (4 * experts)
    slots = experts * capacity
    highest = lax.Precision.HIGHEST
    e_index = lax.axis_index("expert")
    fast = n_exp == 4 and nz == 4

    small = jnp.concatenate([w_router, norm_attn[:, None], norm_ffn[:, None]], axis=1)
    small = jnp.pad(small, ((0, 0), (0, 128 - small.shape[1])))
    length_rows = jnp.broadcast_to(seq_lengths[:, :1], (8, 128))
    full_qkv, full_output, full_small, near_tokens, near_lengths, all_cotangent, packed = fetch(
        nz,
        fast,
        (w_query, w_key, w_value),
        w_output,
        small,
        tokens,
        length_rows,
        cotangent,
        w_in.reshape(R, 2 * FF),
        F,
    )
    full_router = full_small[:, :experts]
    gain_attn = full_small[:, experts].astype(f32)
    gain_ffn = full_small[:, experts + 1].astype(f32)

    Fp = -(-F // 128) * 128
    moved_up = lax.all_to_all(packed[1], SHARD, split_axis=0, concat_axis=0, tiled=True)
    down = jnp.pad(w_down.reshape(F, D), ((0, Fp - F), (0, 0)))

    B, H = near_tokens.shape[0], full_output.shape[0]
    heads = H // head_width
    residual_in = tokens.astype(f32)
    inverse_in = rms_forward(residual_in, gain_attn)[1]
    near_in = near_tokens.reshape(B * T, D).astype(f32)
    near_normed, near_inverse = rms_forward(near_in, gain_attn)
    normed_half = near_normed.astype(bf16)
    lengths = near_lengths[:, 0, 0]
    row_index = jnp.arange(T)
    segment = (row_index[None, :] >= lengths[:, None]).astype(jnp.int32)
    positions = row_index[None, :] - lengths[:, None] * segment
    allowed = (segment[:, :, None] == segment[:, None, :]) & (
        row_index[None, None, :] <= row_index[None, :, None]
    )
    cosine, sine_table = rope_tables(positions, head_width)
    head_shape = (B, T, heads, head_width)
    qkv = dot32(normed_half, full_qkv)
    queries = rotate(qkv[:, :H].reshape(head_shape), cosine, sine_table).astype(bf16)
    keys_rot = rotate(qkv[:, H : 2 * H].reshape(head_shape), cosine, sine_table).astype(bf16)
    values = qkv[:, 2 * H : 3 * H].astype(bf16).reshape(head_shape)
    score_scale = 1.0 / math.sqrt(head_width)
    scores = ein32("bqhd,bkhd->bhqk", queries, keys_rot) * score_scale
    scores = jnp.where(allowed[:, None], scores, masked_score)
    row_peak = jnp.max(scores, axis=-1, keepdims=True)
    log_total = row_peak + jnp.log(jnp.sum(jnp.exp(scores - row_peak), axis=-1, keepdims=True))
    attn_probs = jnp.exp(scores - log_total)
    probs_half = attn_probs.astype(bf16)
    context = ein32("bhqk,bkhd->bqhd", probs_half, values).astype(bf16)
    context_flat = context.reshape(B * T, H)

    def at_home(partial_rows, collective):
        if not fast:
            return partial_rows
        return plane_sum(partial_rows.astype(bf16).reshape(B, T, D), collective)

    residual_mid = residual_in + branch_scale * at_home(dot32(context_flat, full_output), 4)
    normed_mid, inverse_mid = rms_forward(residual_mid, gain_ffn)
    normed_mid_half = normed_mid.astype(bf16)

    logits = dot32(normed_mid_half, full_router)
    expert_ids = jnp.arange(experts)
    route_mask = (routes[:, :, None] == expert_ids[None, None, :]).astype(f32)
    chosen = jnp.sum(logits[:, None, :] * route_mask, axis=-1)
    gate_probs = jax.nn.softmax(chosen, axis=-1)
    flat_routes = routes.reshape(2 * T)
    hits = (flat_routes[:, None] == expert_ids[None, :]).astype(bf16)
    order = jnp.arange(2 * T)
    before = (order[:, None] > order[None, :]).astype(bf16)
    earlier = dot32(before, hits)
    slot_index = jnp.sum(earlier * hits.astype(f32), axis=1).astype(jnp.int32)
    target = (flat_routes * capacity + slot_index).reshape(T, 2)
    slot_ids = jnp.arange(slots)
    pick = [(target[:, k][:, None] == slot_ids[None, :]).astype(bf16) for k in range(2)]

    notes = jnp.concatenate([gate_probs, target.astype(f32), jnp.zeros((T, 4), f32)], axis=1)
    notes = jnp.pad(jnp.transpose(notes), ((0, 0), (0, -T % 128)))
    spread = spread_blocks if fast else spread_pair
    w_pair, all_normed, all_notes = spread(nz, (normed_mid_half, notes), packed[0], moved_up, 2)
    w_pair = w_pair.reshape(n_shard * R, 2 * Fp)
    devices = n_shard * n_exp
    flat_notes = all_notes.reshape(devices, 8, -1)[:, :, :T]
    wanted = (e_index * capacity + jnp.arange(capacity)).astype(f32)
    found = [flat_notes[:, 2 + k, None, :] == wanted[None, :, None] for k in range(2)]
    gate_rows = jnp.sum(
        jnp.where(found[0], flat_notes[:, 0, None, :], 0.0)
        + jnp.where(found[1], flat_notes[:, 1, None, :], 0.0),
        axis=-1,
    ).reshape(devices * capacity, 1)
    chosen_rows = (found[0] | found[1]).astype(bf16)

    def take(blocks):
        rows = ein32("spt,std->spd", chosen_rows, blocks.reshape(devices, T, D))
        return rows.astype(bf16).reshape(devices * capacity, D)

    arrived = take(all_normed)
    cotangent_rows = take(all_cotangent)
    grad_scale = gate_rows * branch_scale
    pre = dot32(arrived, w_pair)
    gate_part, up_part = pre[:, :Fp], pre[:, Fp:]
    sigmoid_gate = jax.nn.sigmoid(gate_part)
    silu_gate = gate_part * sigmoid_gate
    activated = (silu_gate * up_part).astype(bf16)
    out_sum = lax.psum_scatter(
        dot32(activated, down).astype(bf16), SHARD, scatter_dimension=0, tiled=True
    )

    raw_grad = dot_dims(cotangent_rows, down, 1, 1)
    row_dots = branch_scale * jnp.sum(raw_grad * activated.astype(f32), axis=1)
    row_dots = row_dots.reshape(devices, capacity, 1)
    token_dots = [jnp.sum(jnp.where(found[k], row_dots, 0.0), axis=1) for k in range(2)]
    token_dots = jnp.stack(token_dots, axis=1).reshape(nz, 2, n_exp, 2, T)
    token_dots = jnp.pad(token_dots, ((0, 0),) * 3 + ((0, 6), (0, -T % 128)))
    act_grad = grad_scale * raw_grad
    gate_grads = act_grad * up_part * sigmoid_gate * (1.0 + gate_part * (1.0 - sigmoid_gate))
    gate_grads, up_grads = gate_grads.astype(bf16), (act_grad * silu_gate).astype(bf16)
    pre_grad = jnp.concatenate([gate_grads, up_grads], axis=1)
    in_rows = dot_dims(pre_grad, w_pair, 1, 1).astype(bf16)
    scaled = (grad_scale * activated.astype(f32)).astype(bf16)
    grad_w_down = lined_up(dot_dims(scaled[:, :F], cotangent_rows, 0, 0))
    gate_term, up_term = [
        dot_dims(arrived, x, 0, 0).astype(bf16).reshape(n_shard, R, Fp)
        for x in (gate_grads, up_grads)
    ]
    in_rows, up_term = lax.optimization_barrier((in_rows, up_term))
    in_rows = in_rows.reshape(nz, 2, n_exp, capacity, D)
    collect = collect_rows if fast else collect_plain
    normed_mid_grad, gate_grad = collect(nz, in_rows, all_notes, token_dots, T)
    gate_grad = jnp.transpose(gate_grad[:2, :T])
    up_term, normed_mid_grad, out_sum = lax.optimization_barrier(
        (up_term, normed_mid_grad, out_sum)
    )
    up_term = lax.all_to_all(up_term, SHARD, split_axis=0, concat_axis=0, tiled=True)

    upstream = cotangent.astype(f32)
    chosen_grad = gate_probs * (gate_grad - jnp.sum(gate_probs * gate_grad, axis=-1, keepdims=True))
    logit_grad = jnp.sum(chosen_grad[:, :, None] * route_mask, axis=1)
    normed_mid_grad = normed_mid_grad + jnp.dot(
        logit_grad, jnp.transpose(full_router.astype(f32)), precision=highest
    )
    router_grad = jnp.dot(
        jnp.transpose(normed_mid_half.astype(f32)), logit_grad, precision=highest
    )
    mid_norm_grad, gain_ffn_grad = rms_backward(
        residual_mid, inverse_mid, gain_ffn, normed_mid_grad
    )
    residual_grad = upstream + mid_norm_grad
    branch_grad = (branch_scale * residual_grad).astype(bf16)

    if fast:
        branch_grad = plane_gather(branch_grad, 5).reshape(B * T, D)
    output_grad = dot_dims(context_flat, branch_grad, 0, 0)
    context_grad = dot_dims(branch_grad, full_output, 1, 1).reshape(head_shape)
    row_delta = jnp.sum(context_grad * context.astype(f32), axis=-1)
    context_grad_half = context_grad.astype(bf16)
    probs_grad = ein32("bqhd,bkhd->bhqk", context_grad_half, values)
    scores_grad = (
        attn_probs * (probs_grad - jnp.transpose(row_delta, (0, 2, 1))[..., None]) * score_scale
    ).astype(bf16)
    queries_grad = ein32("bhqk,bkhd->bqhd", scores_grad, keys_rot)
    keys_grad = ein32("bhqk,bqhd->bkhd", scores_grad, queries)
    values_grad = ein32("bhqk,bqhd->bkhd", probs_half, context_grad_half)
    qkv_grad = jnp.concatenate(
        [
            rotate(queries_grad, cosine, -sine_table).reshape(B * T, H).astype(bf16),
            rotate(keys_grad, cosine, -sine_table).reshape(B * T, H).astype(bf16),
            values_grad.reshape(B * T, H).astype(bf16),
            jnp.zeros((B * T, full_qkv.shape[1] - 3 * H), bf16),
        ],
        axis=1,
    )
    qkv_weight_grad = dot_dims(normed_half, qkv_grad, 0, 0)
    near_grad = dot_dims(qkv_grad, full_qkv, 1, 1)
    gain_attn_grad = jnp.sum(near_grad * near_in * near_inverse, axis=0)

    small_grad = jnp.concatenate(
        [router_grad, gain_attn_grad[:, None], gain_ffn_grad[:, None]], axis=1
    )
    small_grad = jnp.pad(small_grad, ((0, 0), (0, 128 - small_grad.shape[1])))
    small_grad, up_term = lax.optimization_barrier((small_grad, up_term))
    sum_query, sum_key, sum_value, sum_output, small_sum, normed_in_grad, back, gate_term = settle(
        nz, fast, qkv_weight_grad, output_grad, small_grad, near_grad, out_sum, gate_term
    )
    grad_w_in = unpack_columns(gate_term, up_term, F)
    mixture = gate_probs[:, 0:1] * dot32(pick[0], back) + gate_probs[:, 1:2] * dot32(pick[1], back)
    activations = (residual_mid + branch_scale * mixture).astype(bf16)
    in_norm_grad = rms_backward(residual_in, inverse_in, gain_attn, normed_in_grad)[0]
    grad_tokens = residual_grad + in_norm_grad
    return (
        activations,
        grad_tokens,
        small_sum[:, experts],
        sum_query,
        sum_key,
        sum_value,
        sum_output,
        small_sum[:, experts + 1],
        small_sum[:, :experts],
        grad_w_in,
        grad_w_down,
    )


def solution(mesh):
    n_expert, n_shard = mesh.devices.shape
    chips = Mesh(mesh.devices.reshape(n_expert, n_shard // 2, 2), ("expert", "z", "core"))
    rows = P(("expert", "z", "core"), None)
    shard = P(SHARD)
    shard2 = P(SHARD, None)
    shard3 = P(SHARD, "expert", None)
    in_specs = (
        rows,
        rows,
        rows,
        shard,
        shard2,
        shard2,
        shard2,
        shard2,
        shard,
        shard2,
        shard3,
        shard3,
        rows,
    )
    out_specs = (
        rows,
        rows,
        shard,
        shard2,
        shard2,
        shard2,
        shard2,
        shard,
        shard2,
        shard3,
        shard3,
    )
    return jax.shard_map(
        on_device, mesh=chips, in_specs=in_specs, out_specs=out_specs, check_vma=False
    )
```

```python
import functools
import math

import jax
import jax.numpy as jnp
from jax import lax
from jax.experimental import pallas as pl
from jax.experimental.pallas import tpu as pltpu
from jax.sharding import Mesh, PartitionSpec as P

HEADS = 36

eps_norm = 1e-05
branch_scale = 1.4 / math.sqrt(40.0)
rope_base = 10000.0
masked_score = -1e30
bf16 = jnp.bfloat16
f32 = jnp.float32
SHARD = ("z", "core")
ANY = pl.BlockSpec(memory_space=pl.ANY)


def place():
    e, z, c = lax.axis_index("expert"), lax.axis_index("z"), lax.axis_index("core")
    across_x = e + 1 - 2 * (e % 2)
    across_y = (e + 2) % 4
    return e, z, c, across_x, across_y


def remote(src, dst, send, recv, e, z, c):
    return pltpu.make_async_remote_copy(
        src_ref=src,
        dst_ref=dst,
        send_sem=send,
        recv_sem=recv,
        device_id=(e, z, c),
        device_id_type=pl.DeviceIdType.MESH,
    )


def payload_stream(nz, ref, out, sems, split):
    zrecv, zsend, near_recv, near_send, far_recv, far_send, sib_recv, sib_send, own = sems
    e, z, c, ex, ey = place()
    diagonal = (ex + 2) % 4
    T = ref.shape[0]
    S = 2 * nz - 1

    def split_step(s):
        return (s - 1) % 2, (s - 1) // 2

    def where(s):
        if s == 0:
            return z
        side, i = split_step(s)
        return z - 1 - i if side == 0 else z + 1 + i

    def exists(s):
        if s == 0:
            return z >= 0
        zz = where(s)
        return (zz >= 0) & (zz < nz)

    def slab(s, quarter, r0=0, n=T):
        return out.at[where(s), c, quarter, pl.ds(r0, n), :]

    def first(step):
        side = 0 if step > 0 else 1
        return remote(ref, slab(0, e), zsend.at[side, nz - 1], zrecv.at[side, 0], e, z + step, c)

    def onward(s):
        side, i = split_step(s)
        step = 1 if side == 0 else -1
        return remote(
            slab(s, e), slab(s, e), zsend.at[side, i], zrecv.at[side, i + 1], e, z + step, c
        )

    def near(s, axis):
        source = ref if s == 0 else slab(s, e)
        return remote(
            source, slab(s, e), near_send.at[s, axis], near_recv.at[s, axis],
            ex if axis == 0 else ey, z, c,
        )

    def near_wait(s, axis):
        view = slab(s, ex if axis == 0 else ey)
        remote(view, view, near_send.at[s, axis], near_recv.at[s, axis], ex, z, c).wait_recv()

    axes = range(2) if split else range(1)

    def far_view(s, quarter, axis):
        if not split:
            return slab(s, quarter)
        return slab(s, quarter, 0, split) if axis == 0 else slab(s, quarter, split, T - split)

    def far(s, axis):
        view = far_view(s, ex if axis == 0 else ey, axis)
        return remote(
            view, view, far_send.at[s, axis], far_recv.at[s, axis],
            ey if axis == 0 else ex, z, c,
        )

    def far_wait(s, axis):
        view = far_view(s, diagonal, axis)
        remote(view, view, far_send.at[s, axis], far_recv.at[s, axis], ex, z, c).wait_recv()

    def beside(s, n):
        quarter = (e, ex, ey, diagonal)[n]
        source = ref if s == 0 and n == 0 else slab(s, quarter)
        return remote(
            source, slab(s, quarter), sib_send.at[s, n], sib_recv.at[s, n], e, z, 1 - c
        )

    def beside_wait(s, n):
        view = out.at[where(s), 1 - c, (e, ex, ey, diagonal)[n]]
        remote(view, view, sib_send.at[s, n], sib_recv.at[s, n], e, z, c).wait_recv()

    def inside(side):
        return z < nz - 1 if side == 0 else z > 0

    def begin():
        for step in (1, -1):

            @pl.when((z + step >= 0) & (z + step < nz))
            def _():
                first(step).start()

        near(0, 0).start()
        near(0, 1).start()
        beside(0, 0).start()
        pltpu.make_async_copy(ref, slab(0, e), own).start()

    def arrive(s):
        if s == 0:
            return

        @pl.when(exists(s))
        def _():
            side, i = split_step(s)
            remote(
                slab(s, e), slab(s, e), zsend.at[side, i], zrecv.at[side, i], e, z, c
            ).wait_recv()
            if i < nz - 2:

                @pl.when(inside(side))
                def _():
                    onward(s).start()

            near(s, 0).start()
            near(s, 1).start()
            beside(s, 0).start()

    def relay(s):
        @pl.when(exists(s))
        def _():
            near_wait(s, 0)
            far(s, 0).start()
            beside(s, 1).start()
            near_wait(s, 1)
            if split:
                far(s, 1).start()
            beside(s, 2).start()

    def close(s):
        @pl.when(exists(s))
        def _():
            for axis in axes:
                far_wait(s, axis)
            beside(s, 3).start()

    def end(s):
        @pl.when(exists(s))
        def _():
            for axis in range(2):
                near(s, axis).wait_send()
            for axis in axes:
                far(s, axis).wait_send()
            for n in range(4):
                beside(s, n).wait_send()
                beside_wait(s, n)
            if s > 0 and split_step(s)[1] < nz - 2:

                @pl.when(inside(split_step(s)[0]))
                def _():
                    onward(s).wait_send()

        if s == 0:
            for step in (1, -1):

                @pl.when((z + step >= 0) & (z + step < nz))
                def _():
                    first(step).wait_send()

            pltpu.make_async_copy(ref, slab(0, e), own).wait()

    return begin, arrive, relay, close, end


def payload_sems(nz):
    dma = pltpu.SemaphoreType.DMA
    S = 2 * nz - 1
    return [
        dma((2, nz)), dma((2, nz)), dma((S, 2)), dma((S, 2)), dma((S, 2)), dma((S, 2)),
        dma((S, 4)), dma((S, 4)), dma(()),
    ]


def spread_kernel(nz, splits, *refs):
    n = len(splits)
    (gate_ref, up_ref), refs = refs[:2], refs[2:]
    ins, refs = refs[:n], refs[n:]
    pair, outs, sems = refs[0], refs[1 : n + 1], refs[n + 1 :]
    v_sems, beside_sem, sems = sems[:3], sems[3], sems[4:]
    width = gate_ref.shape[2]
    greet_shard(nz)
    streams = [
        payload_stream(nz, ins[i], outs[i], sems[9 * i : 9 * i + 9], splits[i]) for i in range(n)
    ]
    v_begin, v_end = scatter_stream(
        nz, gate_ref, lambda i: pair.at[i, :, pl.ds(0, width)], *v_sems
    )
    beside = pltpu.make_async_copy(up_ref, pair.at[:, :, pl.ds(width, width)], beside_sem)
    for t in streams:
        t[0]()
    beside.start()
    S = 2 * nz - 1
    for s in range(1, S):
        for t in streams:
            t[1](s)
    v_begin()
    for s in range(S):
        for t in streams:
            t[2](s)
        if s >= 1:
            for t in streams:
                t[3](s - 1)
    for t in streams:
        t[3](S - 1)
    for s in range(S):
        for t in streams:
            t[4](s)
    beside.wait()
    v_end()


def spread_blocks(nz, blocks, gate, up, collective):
    sd = jax.ShapeDtypeStruct
    splits = tuple(b.shape[0] // 2 if b.shape[0] % 32 == 0 else 0 for b in blocks)
    pair = sd(gate.shape[:2] + (2 * gate.shape[2],), gate.dtype)
    return pl.pallas_call(
        functools.partial(spread_kernel, nz, splits),
        out_shape=(pair,) + tuple(sd((nz, 2, 4) + b.shape, b.dtype) for b in blocks),
        in_specs=[ANY] * (len(blocks) + 2),
        out_specs=(ANY,) * (len(blocks) + 1),
        scratch_shapes=[
            *scatter_sems(nz), pltpu.SemaphoreType.DMA(()),
            *[s for _ in blocks for s in payload_sems(nz)],
        ],
        compiler_params=pltpu.CompilerParams(collective_id=collective, has_side_effects=True),
        cost_estimate=pl.CostEstimate(flops=10**6, bytes_accessed=10**6, transcendentals=0),
        name="spread_blocks",
    )(gate, up, *blocks)


def line_order(nz, z):
    def order(i):
        code = 0
        for zz in range(nz):
            far_first = sorted(range(nz), key=lambda t: (-abs(t - zz), t))
            code += far_first[i] * nz**zz
        power = 1
        for zz in range(nz):
            power = power + (nz**zz - 1) * jnp.where(z == zz, 1, 0)
        return (code // power) % nz

    return [order(i) for i in range(nz)]


def collect_kernel(
    nz, cap,
    rows_ref, notes_ref, dots_ref,
    out_ref, dots_out,
    dots, notes, mine, theirs, block, from_x, from_y, via_x, via_y, from_z,
    note_sem, load, sib_send, sib_recv, via_send, via_recv, plain_send, plain_recv,
    sum_send, sum_recv, zsend, zrecv, dot_send, dot_recv, dot_own,
):
    e, z, c, ex, ey = place()
    diagonal = (ex + 2) % 4
    T, D = out_ref.shape
    h = T // 2
    dest = line_order(nz, z)
    who = (diagonal, ex, ey, e)

    def others():
        for d in range(1, 8 * nz):
            to = ((e * nz + z) * 2 + c + d) % (8 * nz)
            yield d, to // (2 * nz), to // 2 % nz, to % 2

    barrier = pltpu.get_barrier_semaphore()
    for _, te, tz, tc in others():
        pl.semaphore_signal(
            barrier, inc=1, device_id=(te, tz, tc), device_id_type=pl.DeviceIdType.MESH
        )
    pl.semaphore_wait(barrier, 8 * nz - 1)

    def dot(d, te, tz, tc):
        return remote(
            dots_ref.at[tz, tc, te], dots.at[d], dot_send.at[d], dot_recv.at[d], te, tz, tc
        )

    dot_kept = pltpu.make_async_copy(dots_ref.at[z, c, e], dots.at[0], dot_own)
    dot_kept.start()
    for d, te, tz, tc in others():
        dot(d, te, tz, tc).start()

    note_copy = pltpu.make_async_copy(notes_ref, notes, note_sem)
    note_copy.start()

    def fetch(i, q):
        return pltpu.make_async_copy(
            rows_ref.at[dest[i], c, who[q]], mine.at[i, q], load.at[i, q]
        )

    def hand(i, q):
        return remote(
            rows_ref.at[dest[i], 1 - c, who[q]], theirs.at[i, q],
            sib_send.at[i, q], sib_recv.at[i, q], e, z, 1 - c,
        )

    for i in range(nz):
        for q in range(4):
            hand(i, q).start()
            fetch(i, q).start()
    note_copy.wait()

    def open_out(i, q):
        fetch(i, q).wait()
        hand(i, q).wait_recv()
        places = (lax.broadcasted_iota(jnp.int32, (cap, T), 0) + e * cap).astype(f32)
        note = notes[dest[i], c, who[q]]
        pick = ((note[2:3, :] == places) | (note[3:4, :] == places)).astype(bf16)
        wide = 768 if D % 768 == 0 else 128

        @pl.loop(0, D // wide)
        def _(b):
            cols = pl.ds(pl.multiple_of(b * wide, 128), wide)
            both = mine[i, q, :, cols].astype(f32) + theirs[i, q, :, cols].astype(f32)
            block[i, q, :, cols] = lax.dot_general(
                pick, both.astype(bf16), (((0,), (0,)), ((), ())), preferred_element_type=f32
            ).astype(bf16)

    def via(i, axis):
        if axis == 0:
            return remote(
                block.at[i, 0, pl.ds(0, h), :], via_x.at[i],
                via_send.at[i, 0], via_recv.at[i, 0], ex, z, c,
            )
        return remote(
            block.at[i, 0, pl.ds(h, h), :], via_y.at[i],
            via_send.at[i, 1], via_recv.at[i, 1], ey, z, c,
        )

    def plain(i, axis):
        if axis == 0:
            return remote(
                block.at[i, 1, pl.ds(0, h), :], from_x.at[i, pl.ds(0, h), :],
                plain_send.at[i, 0], plain_recv.at[i, 0], ex, z, c,
            )
        return remote(
            block.at[i, 2, pl.ds(h, h), :], from_y.at[i, pl.ds(h, h), :],
            plain_send.at[i, 1], plain_recv.at[i, 1], ey, z, c,
        )

    def summed(i, axis):
        if axis == 0:
            return remote(
                block.at[i, 1, pl.ds(h, h), :], from_x.at[i, pl.ds(h, h), :],
                sum_send.at[i, 0], sum_recv.at[i, 0], ex, z, c,
            )
        return remote(
            block.at[i, 2, pl.ds(0, h), :], from_y.at[i, pl.ds(0, h), :],
            sum_send.at[i, 1], sum_recv.at[i, 1], ey, z, c,
        )

    def add(target, others, n):
        @pl.loop(0, n // 16)
        def _(b):
            rows = pl.ds(pl.multiple_of(b * 16, 16), 16)
            acc = target[rows, :].astype(f32)
            for o in others:
                acc = acc + o[rows, :].astype(f32)
            target[rows, :] = acc.astype(target.dtype)

    def start(i):
        open_out(i, 0)
        via(i, 0).start()
        via(i, 1).start()
        open_out(i, 1)
        plain(i, 0).start()
        open_out(i, 2)
        plain(i, 1).start()
        open_out(i, 3)

    def combine(i):
        via(i, 0).wait_recv()
        add(block.at[i, 2, pl.ds(0, h), :], [via_x.at[i]], h)
        summed(i, 1).start()
        via(i, 1).wait_recv()
        add(block.at[i, 1, pl.ds(h, h), :], [via_y.at[i]], h)
        summed(i, 0).start()

    def zcopy(i):
        step = jnp.where(dest[i] > z, 1, -1)
        side = jnp.where(dest[i] > z, 0, 1)
        return remote(
            block.at[i, 3], from_z.at[side, dest[i]],
            zsend.at[i], zrecv.at[side, dest[i]], e, z + step, c,
        )

    def zwait(side, zz):
        slab = from_z.at[side, zz]
        remote(slab, slab, zsend.at[0], zrecv.at[side, zz], e, z, c).wait_recv()

    def finish(i):
        for axis in range(2):
            plain(i, axis).wait_recv()
            summed(i, axis).wait_recv()
        zz = dest[i]
        if i < nz - 1:
            add(block.at[i, 3], [from_x.at[i], from_y.at[i]], T)
            for side in range(2):
                going = zz > z if side == 0 else zz < z
                behind = z > 0 if side == 0 else z < nz - 1

                @pl.when(going & behind)
                def _():
                    zwait(side, zz)
                    add(block.at[i, 3], [from_z.at[side, zz]], T)

            zcopy(i).start()
            return

        @pl.loop(0, T // 16)
        def _(b):
            rows = pl.ds(pl.multiple_of(b * 16, 16), 16)
            acc = block[i, 3, rows, :].astype(f32) + from_x[i, rows, :].astype(f32)
            out_ref[rows, :] = acc + from_y[i, rows, :].astype(f32)

        for side in range(2):

            @pl.when(z > 0 if side == 0 else z < nz - 1)
            def _():
                zwait(side, z)
                add(out_ref, [from_z.at[side, z]], T)

    for i in range(nz):
        start(i)
        if i >= 1:
            combine(i - 1)
        if i >= 2:
            finish(i - 2)
    combine(nz - 1)
    if nz >= 2:
        finish(nz - 2)
    finish(nz - 1)

    dot_kept.wait()
    for d, te, tz, tc in others():
        dot(d, te, tz, tc).wait_recv()
        dot(d, te, tz, tc).wait_send()
    dots_out[...] = jnp.sum(dots[...], axis=0)

    for i in range(nz):
        for q in range(4):
            hand(i, q).wait_send()
        for axis in range(2):
            via(i, axis).wait_send()
            plain(i, axis).wait_send()
            summed(i, axis).wait_send()
        if i < nz - 1:
            zcopy(i).wait_send()


def collect_rows(nz, rows, notes, dots, T):
    cap, D = rows.shape[3:]
    dma = pltpu.SemaphoreType.DMA
    vm = pltpu.VMEM
    return pl.pallas_call(
        functools.partial(collect_kernel, nz, cap),
        out_shape=(
            jax.ShapeDtypeStruct((T, D), f32),
            jax.ShapeDtypeStruct(dots.shape[3:], f32),
        ),
        in_specs=[ANY] * 3,
        out_specs=(pl.BlockSpec(memory_space=pltpu.VMEM),) * 2,
        scratch_shapes=[
            vm((8 * nz,) + dots.shape[3:], f32),
            vm(notes.shape, f32),
            vm((nz, 4, cap, D), bf16),
            vm((nz, 4, cap, D), bf16),
            vm((nz, 4, T, D), bf16),
            vm((nz, T, D), bf16),
            vm((nz, T, D), bf16),
            vm((nz, T // 2, D), bf16),
            vm((nz, T // 2, D), bf16),
            vm((2, nz, T, D), bf16),
            dma(()),
            dma((nz, 4)),
            dma((nz, 4)),
            dma((nz, 4)),
            dma((nz, 2)),
            dma((nz, 2)),
            dma((nz, 2)),
            dma((nz, 2)),
            dma((nz, 2)),
            dma((nz, 2)),
            dma((nz,)),
            dma((2, nz)),
            dma((8 * nz,)),
            dma((8 * nz,)),
            dma(()),
        ],
        compiler_params=pltpu.CompilerParams(
            collective_id=3, has_side_effects=True, vmem_limit_bytes=56 << 20
        ),
        cost_estimate=pl.CostEstimate(
            flops=10**6, bytes_accessed=10**6, transcendentals=0
        ),
        name="collect_rows",
    )(rows, notes, dots)


def pack_rows(n, F, Fp, x_ref, *o_refs):
    half = n * F
    rows = x_ref.shape[0]
    for i in range(n):
        for part in range(2):
            cols = x_ref[:, part * half + i * F : part * half + (i + 1) * F]
            if Fp > F:
                cols = jnp.concatenate([cols, jnp.zeros((rows, Fp - F), cols.dtype)], axis=1)
            o_refs[part][i] = cols


def pack_columns(w, n, F, Fp):
    rows = w.shape[0]
    block = 16
    return pl.pallas_call(
        functools.partial(pack_rows, n, F, Fp),
        grid=(rows // block,),
        in_specs=[pl.BlockSpec((block, w.shape[1]), lambda i: (i, 0))],
        out_specs=(pl.BlockSpec((n, block, Fp), lambda i: (0, i, 0)),) * 2,
        out_shape=(jax.ShapeDtypeStruct((n, rows, Fp), w.dtype),) * 2,
        name="pack_columns",
    )(w)


def unpack_kernel(n, F, gate_ref, up_ref, o_ref, line):
    half = n * F
    rows = line.shape[0]
    for i in range(n):
        for part in range(2):
            cols = (up_ref if part else gate_ref)[i, :, :F].astype(f32)
            line[:, part * half + i * F : part * half + (i + 1) * F] = cols
    tiles = 2 * half // 128
    for j in range(tiles):
        o_ref[pl.ds(j, rows, stride=tiles), :] = line[:, j * 128 : (j + 1) * 128]


def unpack_columns(gate, up, F):
    n, rows, Fp = gate.shape
    block = 16
    width = 2 * n * F
    tiles = width // 128
    flat = pl.pallas_call(
        functools.partial(unpack_kernel, n, F),
        grid=(rows // block,),
        in_specs=[pl.BlockSpec((n, block, Fp), lambda i: (0, i, 0))] * 2,
        out_specs=pl.BlockSpec((block * tiles, 128), lambda i: (i, 0)),
        out_shape=jax.ShapeDtypeStruct((rows * tiles, 128), f32),
        scratch_shapes=[pltpu.VMEM((block, width), f32)],
        name="unpack_columns",
    )(gate, up)
    return flat.reshape(rows, 1, width)


def line_kernel(x_ref, o_ref):
    rows, width = x_ref.shape
    tiles = width // 128
    for j in range(tiles):
        o_ref[pl.ds(j, rows, stride=tiles), :] = x_ref[:, j * 128 : (j + 1) * 128]


def lined_up(x):
    rows, width = x.shape
    tiles = width // 128
    block = 80 if rows % 80 == 0 else 8
    flat = pl.pallas_call(
        line_kernel,
        grid=(rows // block,),
        in_specs=[pl.BlockSpec((block, width), lambda i: (i, 0))],
        out_specs=pl.BlockSpec((block * tiles, 128), lambda i: (i, 0)),
        out_shape=jax.ShapeDtypeStruct((rows * tiles, 128), x.dtype),
        name="lined_up",
    )(x)
    return flat.reshape(rows, 1, width)


def greet_cross(nz):
    e, z, c, ex, ey = place()
    barrier = pltpu.get_barrier_semaphore()

    def hail(te, tz, tc):
        pl.semaphore_signal(
            barrier, inc=1, device_id=(te, tz, tc), device_id_type=pl.DeviceIdType.MESH
        )

    hail(e, z, 1 - c)
    for te in (ex, ey, (ex + 2) % 4):
        hail(te, z, c)
    for step in (-1, 1):

        @pl.when((z + step >= 0) & (z + step < nz))
        def _():
            hail(e, z + step, c)

    pl.semaphore_wait(barrier, 4 + jnp.where(z > 0, 1, 0) + jnp.where(z < nz - 1, 1, 0))


def greet_shard(nz):
    e, z, c, ex, ey = place()
    barrier = pltpu.get_barrier_semaphore()
    n = 2 * nz
    peers = [(te, z, c) for te in (ex, ey, (ex + 2) % 4)]
    for d in range(1, n):
        to = (2 * z + c + d) % n
        peers.append((e, to // 2, to % 2))
    for peer in peers:
        pl.semaphore_signal(barrier, inc=1, device_id=peer, device_id_type=pl.DeviceIdType.MESH)
    pl.semaphore_wait(barrier, n + 2)


def scatter_stream(nz, ref, view, send, recv, own):
    e, z, c, _, _ = place()
    n = 2 * nz
    me = 2 * z + c

    def copy(d):
        to = (me + d) % n
        return remote(ref.at[to], view(me), send.at[d], recv.at[d], e, to // 2, to % 2)

    kept = pltpu.make_async_copy(ref.at[me], view(me), own)

    def begin():
        for d in range(1, n):
            copy(d).start()
        kept.start()

    def end():
        kept.wait()
        for d in range(1, n):
            land = view((me + n - d) % n)
            remote(land, land, send.at[d], recv.at[d], e, z, c).wait_recv()
            copy(d).wait_send()

    return begin, end


def scatter_sems(nz):
    dma = pltpu.SemaphoreType.DMA
    return [dma((2 * nz,)), dma((2 * nz,)), dma(())]


def line_stream(nz, ref, out, zrecv, zsend, sib_recv, sib_send, own):
    e, z, c, _, _ = place()

    def split_step(s):
        return (s - 1) % 2, (s - 1) // 2

    def where(s):
        if s == 0:
            return z
        side, i = split_step(s)
        return z - 1 - i if side == 0 else z + 1 + i

    def exists(s):
        return (where(s) >= 0) & (where(s) < nz)

    def inside(side):
        return z < nz - 1 if side == 0 else z > 0

    def slab(s):
        return out.at[where(s), c]

    def first(side):
        step = 1 if side == 0 else -1
        return remote(ref, slab(0), zsend.at[side, nz - 1], zrecv.at[side, 0], e, z + step, c)

    def onward(s):
        side, i = split_step(s)
        step = 1 if side == 0 else -1
        return remote(
            slab(s), slab(s), zsend.at[side, i], zrecv.at[side, i + 1], e, z + step, c
        )

    def beside(s):
        return remote(
            ref if s == 0 else slab(s), slab(s), sib_send.at[s], sib_recv.at[s], e, z, 1 - c
        )

    def begin():
        for side in range(2):

            @pl.when(inside(side))
            def _():
                first(side).start()

        beside(0).start()
        pltpu.make_async_copy(ref, slab(0), own).start()

    def arrive(s):
        side, i = split_step(s)

        @pl.when(exists(s))
        def _():
            remote(slab(s), slab(s), zsend.at[side, i], zrecv.at[side, i], e, z, c).wait_recv()
            if i < nz - 2:

                @pl.when(inside(side))
                def _():
                    onward(s).start()

            beside(s).start()

    def end():
        for s in range(2 * nz - 1):

            @pl.when(exists(s))
            def _():
                beside(s).wait_send()
                view = out.at[where(s), 1 - c]
                remote(view, view, sib_send.at[s], sib_recv.at[s], e, z, c).wait_recv()
                if s > 0 and split_step(s)[1] < nz - 2:

                    @pl.when(inside(split_step(s)[0]))
                    def _():
                        onward(s).wait_send()

        for side in range(2):

            @pl.when(inside(side))
            def _():
                first(side).wait_send()

        pltpu.make_async_copy(ref, slab(0), own).wait()

    return begin, arrive, end


def line_sems(nz):
    dma = pltpu.SemaphoreType.DMA
    S = 2 * nz - 1
    return [dma((2, nz)), dma((2, nz)), dma((S,)), dma((S,)), dma(())]


def plane_stream(source, views, send, recv, own):
    e, z, c, ex, ey = place()
    peers = (ex, ey, (ex + 2) % 4)

    def copy(n):
        return remote(source, views(e), send.at[n], recv.at[n], peers[n], z, c)

    def kept():
        return pltpu.make_async_copy(source, views(e), own)

    def begin():
        for n in range(3):
            copy(n).start()
        kept().start()

    def end():
        kept().wait()
        for n in range(3):
            view = views(peers[n])
            remote(view, view, send.at[n], recv.at[n], e, z, c).wait_recv()
            copy(n).wait_send()

    return begin, end


def plane_sems():
    dma = pltpu.SemaphoreType.DMA
    return [dma((3,)), dma((3,)), dma(())]


def fetch_kernel(
    nz,
    F, w_ref, s_ref, o_ref, t_ref, l_ref, p_ref, x_ref,
    w_out, s_out, o_out, t_out, l_out, p_out, gate_out, up_out,
    wide, gate, up, wide_sem, packed_sem,
    *sems,
):
    e, z, c, ex, ey = place()
    w_sems, sems = sems[:5], sems[5:]
    s_sems, sems = sems[:5], sems[5:]
    t_sems, sems = sems[:3], sems[3:]
    l_sems, sems = sems[:3], sems[3:]
    p_sems, sems = sems[:9], sems[9:]
    orecv, osend, sib_recv, sib_send, own = sems
    wide_copy = pltpu.make_async_copy(x_ref, wide, wide_sem)
    wide_copy.start()
    greet_cross(nz)
    w_begin, w_arrive, w_end = line_stream(nz, w_ref, w_out, *w_sems)
    s_begin, s_arrive, s_end = line_stream(nz, s_ref, s_out, *s_sems)
    t_begin, t_end = plane_stream(t_ref, lambda q: t_out.at[q], *t_sems)
    l_begin, l_end = plane_stream(l_ref, lambda q: l_out.at[q], *l_sems)
    p_begin, p_arrive, p_relay, p_close, p_end = payload_stream(
        nz, p_ref, p_out, p_sems, p_ref.shape[0] // 2
    )

    pieces = orecv.shape[0]
    height = o_ref.shape[0] // pieces

    def o_part(n):
        return pl.ds(n * height, height)

    def o_view(n):
        return o_out.at[c, o_part(n), :]

    def o_copy(side, n, source):
        step = 1 if side == 0 else -1
        return remote(source, o_view(n), osend.at[side, n], orecv.at[n], e, z + step, c)

    def o_beside(n, source):
        return remote(source, o_view(n), sib_send.at[n], sib_recv.at[n], e, z, 1 - c)

    def o_goes(side):
        return (z >= e) & (z < nz - 1) if side == 0 else (z <= e) & (z > 0)

    def o_pass(n, source):
        for side in range(2):

            @pl.when(o_goes(side))
            def _():
                o_copy(side, n, source).start()

        o_beside(n, source).start()

    def o_arrive(n):
        @pl.when(z != e)
        def _():
            remote(o_view(n), o_view(n), sib_send.at[n], orecv.at[n], e, z, c).wait_recv()
            o_pass(n, o_view(n))

    p_begin()

    @pl.when(z == e)
    def _():
        for n in range(pieces):
            o_pass(n, o_ref.at[o_part(n), :])
        pltpu.make_async_copy(o_ref, o_out.at[c], own).start()

    s_begin()
    w_begin()
    t_begin()
    l_begin()

    wide_copy.wait()

    @pl.loop(0, wide.shape[0] // 16)
    def _(b):
        rows = pl.ds(pl.multiple_of(b * 16, 16), 16)
        pack_rows(
            gate.shape[0], F, gate.shape[2], wide.at[rows, :], gate.at[:, rows, :], up.at[:, rows, :]
        )

    packed_copies = [
        pltpu.make_async_copy(a, b, packed_sem.at[n])
        for n, (a, b) in enumerate(((gate, gate_out), (up, up_out)))
    ]
    for copy in packed_copies:
        copy.start()

    blocks = 2 * nz - 1
    for s in range(1, blocks):
        p_arrive(s)
        s_arrive(s)
        if s <= pieces:
            o_arrive(s - 1)
    for n in range(blocks - 1, pieces):
        o_arrive(n)
    for s in range(1, blocks):
        p_relay(s - 1)
        w_arrive(s)
        if s >= 2:
            p_close(s - 2)
    p_relay(blocks - 1)
    p_close(blocks - 2)
    p_close(blocks - 1)
    for s in range(blocks):
        p_end(s)
    w_end()
    s_end()
    t_end()
    l_end()
    for n in range(pieces):
        view = o_out.at[1 - c, o_part(n), :]
        remote(view, view, sib_send.at[n], sib_recv.at[n], e, z, c).wait_recv()
        o_beside(n, o_view(n)).wait_send()
        for side in range(2):

            @pl.when(o_goes(side))
            def _():
                o_copy(side, n, o_view(n)).wait_send()

    @pl.when(z == e)
    def _():
        pltpu.make_async_copy(o_ref, o_out.at[c], own).wait()

    for copy in packed_copies:
        copy.wait()


def fetch_weights(nz, columns, small, rows, tokens, lengths, block, wide, F):
    dma = pltpu.SemaphoreType.DMA
    packed = (2 * nz, wide.shape[0], -(-F // 128) * 128)
    sd = jax.ShapeDtypeStruct
    return pl.pallas_call(
        functools.partial(fetch_kernel, nz, F),
        out_shape=(
            sd((nz, 2) + columns.shape, bf16),
            sd((nz, 2) + small.shape, bf16),
            sd((2,) + rows.shape, bf16),
            sd((4,) + tokens.shape, bf16),
            sd((4,) + lengths.shape, lengths.dtype),
            sd((nz, 2, 4) + block.shape, block.dtype),
            sd(packed, wide.dtype),
            sd(packed, wide.dtype),
        ),
        in_specs=[ANY] * 7,
        out_specs=(ANY,) * 8,
        scratch_shapes=[
            pltpu.VMEM(wide.shape, wide.dtype), pltpu.VMEM(packed, wide.dtype),
            pltpu.VMEM(packed, wide.dtype), dma(()), dma((2,)),
            *line_sems(nz), *line_sems(nz), *plane_sems(), *plane_sems(), *payload_sems(nz),
            dma((6,)), dma((2, 6)), dma((6,)), dma((6,)), dma(()),
        ],
        compiler_params=pltpu.CompilerParams(
            collective_id=0, has_side_effects=True, vmem_limit_bytes=32 << 20
        ),
        cost_estimate=pl.CostEstimate(
            flops=10**11, bytes_accessed=8 * columns.size, transcendentals=0
        ),
        name="fetch_weights",
    )(columns, small, rows, tokens, lengths, block, wide)


def plane_gather_kernel(x_ref, out_ref, send, recv, own):
    e, z, c, ex, ey = place()
    greet_plane()
    begin, end = plane_stream(x_ref, lambda q: out_ref.at[q], send, recv, own)
    begin()
    end()


def greet_plane():
    e, z, c, ex, ey = place()
    barrier = pltpu.get_barrier_semaphore()
    for te in (ex, ey, (ex + 2) % 4):
        pl.semaphore_signal(
            barrier, inc=1, device_id=(te, z, c), device_id_type=pl.DeviceIdType.MESH
        )
    pl.semaphore_wait(barrier, 3)


def plane_gather(x, collective):
    return pl.pallas_call(
        plane_gather_kernel,
        out_shape=jax.ShapeDtypeStruct((4,) + x.shape, x.dtype),
        in_specs=[ANY],
        out_specs=ANY,
        scratch_shapes=plane_sems(),
        compiler_params=pltpu.CompilerParams(collective_id=collective, has_side_effects=True),
        cost_estimate=pl.CostEstimate(flops=10**6, bytes_accessed=10**6, transcendentals=0),
        name="plane_gather",
    )(x)


def plane_sum_parts(x_ref, out_ref, held, send, recv, own):
    e, z, c, ex, ey = place()
    peers = (ex, ey, (ex + 2) % 4)

    def copy(n):
        return remote(x_ref.at[peers[n]], held.at[n], send.at[n], recv.at[n], peers[n], z, c)

    kept = pltpu.make_async_copy(x_ref.at[e], held.at[3], own)

    def total():
        kept.wait()
        for n in range(3):
            copy(n).wait_recv()

        @pl.loop(0, out_ref.shape[0] // 16)
        def _(b):
            rows = pl.ds(pl.multiple_of(b * 16, 16), 16)
            acc = held[3, rows, :].astype(f32) + held[0, rows, :].astype(f32)
            acc = acc + held[1, rows, :].astype(f32)
            out_ref[rows, :] = acc + held[2, rows, :].astype(f32)

    return copy, kept, total


def plane_sum_kernel(x_ref, out_ref, held, send, recv, own):
    greet_plane()
    copy, kept, total = plane_sum_parts(x_ref, out_ref, held, send, recv, own)
    for n in (2, 0, 1):
        copy(n).start()
    kept.start()
    total()
    for n in range(3):
        copy(n).wait_send()


def plane_sum(x, collective):
    vm = pltpu.VMEM
    return pl.pallas_call(
        plane_sum_kernel,
        out_shape=jax.ShapeDtypeStruct(x.shape[1:], f32),
        in_specs=[ANY],
        out_specs=pl.BlockSpec(memory_space=vm),
        scratch_shapes=[vm(x.shape, bf16), *plane_sems()],
        compiler_params=pltpu.CompilerParams(collective_id=collective, has_side_effects=True),
        cost_estimate=pl.CostEstimate(flops=10**6, bytes_accessed=10**6, transcendentals=0),
        name="plane_sum",
    )(x)


def settle_kernel(
    nz,
    g_ref, s_ref, o_ref, x_ref, y_ref,
    g_out, s_out, o_out, x_out, y_out,
    x_held, x_send, x_recv, x_own, y_send, y_recv, y_own,
    g_mine, g_sib, g_z, s_mine, s_sib, s_z, o_mine, o_sib, o_z,
    load, sib_send, sib_recv, zsend, zrecv,
    o_load, o_sib_send, o_sib_recv, o_zsend, o_zrecv,
    o_send, o_recv, o_own,
    *sems,
):
    e, z, c, ex, ey = place()
    peers = (ex, ey, (ex + 2) % 4)
    dest = line_order(nz, z)
    greet_cross(nz)
    W = g_ref.shape[3]
    first = W // 256 * 128
    groups = (
        (g_ref, g_mine, g_sib, g_z, g_out, pl.ds(0, first)),
        (g_ref, g_mine, g_sib, g_z, g_out, pl.ds(first, W - first)),
        (s_ref, s_mine, s_sib, s_z, s_out, pl.ds(0, s_ref.shape[3])),
    )
    K = len(groups)

    def part(k, which, *index):
        return groups[k][which].at[(*index, slice(None), groups[k][5])]

    def fetch(k, i):
        return pltpu.make_async_copy(
            part(k, 0, dest[i], c), part(k, 1, i), load.at[k, i]
        )

    def hand(k, i):
        return remote(
            part(k, 0, dest[i], 1 - c), part(k, 2, i),
            sib_send.at[k, i], sib_recv.at[k, i], e, z, 1 - c,
        )

    def zcopy(k, i):
        step = jnp.where(dest[i] > z, 1, -1)
        side = jnp.where(dest[i] > z, 0, 1)
        return remote(
            part(k, 1, i), part(k, 3, side, dest[i]),
            zsend.at[k, i], zrecv.at[k, side, dest[i]], e, z + step, c,
        )

    def zwait(k, side, zz):
        slab = part(k, 3, side, zz)
        remote(slab, slab, zsend.at[k, 0], zrecv.at[k, side, zz], e, z, c).wait_recv()

    def add(target, others):
        @pl.loop(0, target.shape[0] // 16)
        def _(b):
            rows = pl.ds(pl.multiple_of(b * 16, 16), 16)
            acc = target[rows, :].astype(f32)
            for o in others:
                acc = acc + o[rows, :].astype(f32)
            target[rows, :] = acc.astype(target.dtype)

    pieces = o_load.shape[0]
    height = o_mine.shape[0] // pieces

    def o_part(n):
        return pl.ds(n * height, height)

    def o_fetch(n):
        return pltpu.make_async_copy(o_ref.at[c, o_part(n), :], o_mine.at[o_part(n), :], o_load.at[n])

    def o_hand(n):
        return remote(
            o_ref.at[1 - c, o_part(n), :], o_sib.at[o_part(n), :],
            o_sib_send.at[n], o_sib_recv.at[n], e, z, 1 - c,
        )

    def o_line(n):
        step, side = jnp.where(z < e, 1, -1), jnp.where(z < e, 0, 1)
        return remote(
            o_mine.at[o_part(n), :], o_z.at[side, o_part(n), :],
            o_zsend.at[n], o_zrecv.at[side, n], e, z + step, c,
        )

    def o_wait(side, n):
        slab = o_z.at[side, o_part(n), :]
        remote(slab, slab, o_zsend.at[n], o_zrecv.at[side, n], e, z, c).wait_recv()
        add(o_mine.at[o_part(n), :], [slab])

    def o_peer(p, n):
        view = o_out.at[o_part(n), :]
        return remote(
            o_mine.at[o_part(n), :], view, o_send.at[p, n], o_recv.at[n], peers[p], z, c
        )

    def o_kept():
        return pltpu.make_async_copy(o_mine, o_out, o_own)

    for i in range(nz):
        for k in range(K):
            hand(k, i).start()
            fetch(k, i).start()
        if i == 0:
            for n in range(pieces):
                o_fetch(n).start()
                o_hand(n).start()

    def finish(k, i):
        fetch(k, i).wait()
        hand(k, i).wait_recv()
        zz = dest[i]
        add(part(k, 1, i), [part(k, 2, i)])
        if i < nz - 1:
            for side in range(2):
                going = zz > z if side == 0 else zz < z
                behind = z > 0 if side == 0 else z < nz - 1

                @pl.when(going & behind)
                def _():
                    zwait(k, side, zz)
                    add(part(k, 1, i), [part(k, 3, side, zz)])

            zcopy(k, i).start()
            return
        for side in range(2):

            @pl.when(z > 0 if side == 0 else z < nz - 1)
            def _():
                zwait(k, side, z)
                add(part(k, 1, i), [part(k, 3, side, z)])

        streams[k][0]()

    x_copy, x_kept, x_total = plane_sum_parts(x_ref, x_out, x_held, x_send, x_recv, x_own)
    for p in (2, 0, 1):
        x_copy(p).start()
    x_kept.start()

    def y_copy(p):
        return remote(
            y_ref.at[peers[p]], y_out.at[e], y_send.at[p], y_recv.at[p], peers[p], z, c
        )

    y_kept = pltpu.make_async_copy(y_ref.at[e], y_out.at[e], y_own)
    y_kept.start()
    for p in range(3):
        y_copy(p).start()

    def o_flow(n):
        o_fetch(n).wait()
        o_hand(n).wait_recv()
        add(o_mine.at[o_part(n), :], [o_sib.at[o_part(n), :]])
        for side in range(2):
            behind = (z > 0) & (z <= e) if side == 0 else (z < nz - 1) & (z >= e)

            @pl.when(behind)
            def _():
                o_wait(side, n)

        @pl.when(z != e)
        def _():
            o_line(n).start()

        @pl.when(z == e)
        def _():
            for p in range(3):
                o_peer(p, n).start()

    streams = [
        plane_stream(
            part(k, 1, nz - 1), lambda q, k=k: part(k, 4, q), *sems[3 * k : 3 * k + 3]
        )
        for k in range(K)
    ]
    turn = K * nz // 2
    order = []
    for k in range(K):
        order += [(k, i) for i in range(1 if k else 0, nz - 1)]
        if k + 1 < K:
            order.append((k + 1, 0))
        order.append((k, nz - 1))
    for n, (k, i) in enumerate(order):
        finish(k, i)
        if n == 0:
            for m in range(pieces):
                o_flow(m)
        if n == turn:
            x_total()

    @pl.when(z == e)
    def _():
        o_kept().start()
        o_kept().wait()
        for n in range(pieces):
            for p in range(3):
                o_peer(p, n).wait_send()

    @pl.when(z != e)
    def _():
        for n in range(pieces):
            view = o_out.at[o_part(n), :]
            remote(view, view, o_send.at[0, n], o_recv.at[n], e, z, c).wait_recv()
            o_line(n).wait_send()

    y_kept.wait()
    for p in range(3):
        x_copy(p).wait_send()
        view = y_out.at[peers[p]]
        remote(view, view, y_send.at[p], y_recv.at[p], e, z, c).wait_recv()
        y_copy(p).wait_send()
    for n in range(pieces):
        o_hand(n).wait_send()
    for i in range(nz):
        for k in range(K):
            hand(k, i).wait_send()
            if i < nz - 1:
                zcopy(k, i).wait_send()
    for _, end in streams:
        end()


def settle_weights(nz, grads, small, rows, near, blocks):
    R, W = grads.shape[2:]
    D = rows.shape[2]
    dma = pltpu.SemaphoreType.DMA
    sd = jax.ShapeDtypeStruct
    vm = pltpu.VMEM
    Ws = small.shape[3]
    return pl.pallas_call(
        functools.partial(settle_kernel, nz),
        out_shape=(
            sd((4, R, W), bf16),
            sd((4, R, Ws), bf16),
            sd((R, D), bf16),
            sd(near.shape[1:], f32),
            sd(blocks.shape, bf16),
        ),
        in_specs=[ANY] * 5,
        out_specs=(ANY,) * 3 + (pl.BlockSpec(memory_space=vm), ANY),
        scratch_shapes=[
            vm(near.shape, bf16), *plane_sems(), *plane_sems(),
            vm((nz, R, W), bf16), vm((nz, R, W), bf16), vm((2, nz, R, W), bf16),
            vm((nz, R, Ws), bf16), vm((nz, R, Ws), bf16), vm((2, nz, R, Ws), bf16),
            vm((R, D), bf16), vm((R, D), bf16), vm((2, R, D), bf16),
            dma((3, nz)), dma((3, nz)), dma((3, nz)), dma((3, nz)), dma((3, 2, nz)),
            dma((6,)), dma((6,)), dma((6,)), dma((6,)), dma((2, 6)),
            dma((3, 6)), dma((6,)), dma(()),
            *plane_sems(), *plane_sems(), *plane_sems(),
        ],
        compiler_params=pltpu.CompilerParams(
            collective_id=1, has_side_effects=True, vmem_limit_bytes=56 << 20
        ),
        cost_estimate=pl.CostEstimate(flops=10**6, bytes_accessed=10**6, transcendentals=0),
        name="settle_weights",
    )(grads, small, rows, near, blocks)


def pick_kernel(width, q_ref, k_ref, v_ref, o_ref):
    e = lax.axis_index("expert")
    spare = o_ref.shape[1] - 3 * width
    if spare:
        o_ref[:, 3 * width :] = jnp.zeros((o_ref.shape[0], spare), o_ref.dtype)
    for n in range(4):

        @pl.when(e == n)
        def _():
            for i, ref in enumerate((q_ref, k_ref, v_ref)):
                o_ref[:, i * width : (i + 1) * width] = ref[:, n * width : (n + 1) * width]


def pick_columns(weights, width):
    vm = pl.BlockSpec(memory_space=pltpu.VMEM)
    return pl.pallas_call(
        functools.partial(pick_kernel, width),
        in_specs=[vm] * 3,
        out_specs=vm,
        out_shape=jax.ShapeDtypeStruct((weights[0].shape[0], -(-3 * width // 128) * 128), bf16),
        name="pick_columns",
    )(*weights)


def assemble_kernel(width, x_ref, *o_refs):
    for n in range(4):
        for i in range(3):
            cols = x_ref[n, :, i * width : (i + 1) * width]
            o_refs[i][:, n * width : (n + 1) * width] = cols.astype(f32)


def assemble_columns(x, width):
    R = x.shape[1]
    block = 32
    return pl.pallas_call(
        functools.partial(assemble_kernel, width),
        grid=(R // block,),
        in_specs=[pl.BlockSpec((4, block, x.shape[2]), lambda i: (0, i, 0))],
        out_specs=(pl.BlockSpec((block, 4 * width), lambda i: (i, 0)),) * 3,
        out_shape=(jax.ShapeDtypeStruct((R, 4 * width), f32),) * 3,
        name="assemble_columns",
    )(x)


def sum_shard(x, axis=0):
    mine = lax.psum_scatter(x, SHARD, scatter_dimension=axis, tiled=True)
    return lax.psum(mine, "expert")


def fetch(nz, fast, weights, w_output, small, tokens, lengths, block, wide, F):
    D = tokens.shape[1]
    if fast:
        width = D // 4
        columns, full_small, rows, tokens, lengths, blocks, *packed = fetch_weights(
            nz, pick_columns(weights, width), small, w_output, tokens, lengths, block, wide, F
        )
        columns, rows = columns.reshape(D, -1), rows.reshape(width, D)
        return columns, rows, full_small.reshape(D, -1), tokens, lengths, blocks, packed
    full = [lax.all_gather(w, SHARD, axis=0, tiled=True) for w in weights + (w_output, small)]
    blocks = spread_plain(nz, (block,), 0)[0]
    packed = pack_columns(wide, 2 * nz, F, -(-F // 128) * 128)
    columns = jnp.concatenate(full[:3], axis=1)
    return columns, full[3], full[4], tokens[None], lengths[None], blocks, packed


def settle(nz, fast, columns, rows, small, near, blocks):
    D, width = rows.shape[1], rows.shape[0]
    if fast:
        R = D // (2 * nz)
        parts = [x.astype(bf16).reshape(nz, 2, R, -1) for x in (columns, small)]
        near = near.astype(bf16).reshape(4, -1, D)
        blocks = blocks.reshape(4, -1, D)
        sums, small, out, near, blocks = settle_weights(
            nz, *parts, rows.astype(bf16).reshape(2, R, D), near, blocks
        )
        small, blocks = jnp.sum(small.astype(f32), axis=0), blocks.reshape(-1, D)
        return *assemble_columns(sums, width), out.astype(f32), small, near, blocks
    parts = [columns[:, i * width : (i + 1) * width] for i in range(3)] + [rows, small]
    blocks = lax.all_to_all(blocks, "expert", split_axis=0, concat_axis=0, tiled=True)
    return [sum_shard(x) for x in parts] + [near, blocks]


def spread_plain(nz, blocks, collective):
    out = []
    for block in blocks:
        for axis in ("expert", "core", "z"):
            block = lax.all_gather(block, axis, axis=0)
        out.append(block)
    return out


def spread_pair(nz, blocks, gate, up, collective):
    gate = lax.all_to_all(gate, SHARD, split_axis=0, concat_axis=0, tiled=True)
    return jnp.concatenate([gate, up], axis=2), *spread_plain(nz, blocks, collective)


def collect_plain(nz, rows, notes, dots, T):
    n_exp, cap, D = rows.shape[2:]
    places = (lax.axis_index("expert") * cap + jnp.arange(cap)).astype(f32)
    notes = notes[..., :T]
    pick = (notes[..., 2, None, :] == places[:, None]) | (notes[..., 3, None, :] == places[:, None])
    part = jnp.einsum(
        "zceps,zcepd->zcesd", pick.astype(bf16), rows, preferred_element_type=f32
    ).astype(bf16)
    part = part.transpose(2, 0, 1, 3, 4).reshape(n_exp * nz * 2 * T, D)
    part = lax.psum_scatter(part, "expert", scatter_dimension=0, tiled=True)
    part = lax.psum_scatter(part, SHARD, scatter_dimension=0, tiled=True).astype(f32)
    z, core, e = lax.axis_index("z"), lax.axis_index("core"), lax.axis_index("expert")
    return part, lax.psum(dots, ("expert",) + SHARD)[z, core, e]


def rope_tables(positions, head_width):
    half_width = head_width // 2
    exponents = jnp.arange(half_width).astype(f32) * 2.0 / head_width
    frequency = rope_base ** (-exponents)
    angles = positions.astype(f32)[..., None] * frequency
    return (jnp.cos(angles), jnp.sin(angles))


def rotate(values, cosine, sine_table):
    half_width = values.shape[-1] // 2
    leading = values[..., :half_width]
    trailing = values[..., half_width:]
    cos_rows = cosine[:, :, None, :]
    sin_rows = sine_table[:, :, None, :]
    return jnp.concatenate(
        [leading * cos_rows - trailing * sin_rows, trailing * cos_rows + leading * sin_rows],
        axis=-1,
    )


def rms_forward(values, norm_gain):
    inverse = lax.rsqrt(jnp.mean(values * values, axis=-1, keepdims=True) + eps_norm)
    return (values * inverse * norm_gain, inverse)


def rms_backward(values, inverse, norm_gain, upstream):
    weighted = upstream * norm_gain
    gain_grad = jnp.sum(upstream * values * inverse, axis=0)
    inner_mean = jnp.mean(weighted * values, axis=-1, keepdims=True)
    return (inverse * weighted - values * inverse * inverse * inverse * inner_mean, gain_grad)


def dot32(a, b):
    return jnp.dot(a, b, preferred_element_type=f32)


def dot_dims(a, b, da, db):
    return lax.dot_general(a, b, (((da,), (db,)), ((), ())), preferred_element_type=f32)


def ein32(spec, a, b):
    return jnp.einsum(spec, a, b, preferred_element_type=f32)


def on_device(
    tokens,
    seq_lengths,
    routes,
    norm_attn,
    w_query,
    w_key,
    w_value,
    w_output,
    norm_ffn,
    w_router,
    w_in,
    w_down,
    cotangent,
):
    T, D = tokens.shape
    R = w_query.shape[0]
    head_width = D // HEADS
    n_exp = lax.axis_size("expert")
    nz = lax.axis_size("z")
    n_shard = nz * lax.axis_size("core")
    experts = w_router.shape[1]
    F = w_down.shape[0]
    FF = F * n_shard
    capacity = 10 * T // (4 * experts)
    slots = experts * capacity
    highest = lax.Precision.HIGHEST
    e_index = lax.axis_index("expert")
    fast = n_exp == 4 and nz == 4

    small = jnp.concatenate([w_router, norm_attn[:, None], norm_ffn[:, None]], axis=1)
    small = jnp.pad(small, ((0, 0), (0, 128 - small.shape[1])))
    length_rows = jnp.broadcast_to(seq_lengths[:, :1], (8, 128))
    full_qkv, full_output, full_small, near_tokens, near_lengths, all_cotangent, packed = fetch(
        nz,
        fast,
        (w_query, w_key, w_value),
        w_output,
        small,
        tokens,
        length_rows,
        cotangent,
        w_in.reshape(R, 2 * FF),
        F,
    )
    full_router = full_small[:, :experts]
    gain_attn = full_small[:, experts].astype(f32)
    gain_ffn = full_small[:, experts + 1].astype(f32)

    Fp = -(-F // 128) * 128
    moved_up = lax.all_to_all(packed[1], SHARD, split_axis=0, concat_axis=0, tiled=True)
    down = jnp.pad(w_down.reshape(F, D), ((0, Fp - F), (0, 0)))

    B, H = near_tokens.shape[0], full_output.shape[0]
    heads = H // head_width
    residual_in = tokens.astype(f32)
    inverse_in = rms_forward(residual_in, gain_attn)[1]
    near_in = near_tokens.reshape(B * T, D).astype(f32)
    near_normed, near_inverse = rms_forward(near_in, gain_attn)
    normed_half = near_normed.astype(bf16)
    lengths = near_lengths[:, 0, 0]
    row_index = jnp.arange(T)
    segment = (row_index[None, :] >= lengths[:, None]).astype(jnp.int32)
    positions = row_index[None, :] - lengths[:, None] * segment
    allowed = (segment[:, :, None] == segment[:, None, :]) & (
        row_index[None, None, :] <= row_index[None, :, None]
    )
    cosine, sine_table = rope_tables(positions, head_width)
    head_shape = (B, T, heads, head_width)
    qkv = dot32(normed_half, full_qkv)
    queries = rotate(qkv[:, :H].reshape(head_shape), cosine, sine_table).astype(bf16)
    keys_rot = rotate(qkv[:, H : 2 * H].reshape(head_shape), cosine, sine_table).astype(bf16)
    values = qkv[:, 2 * H : 3 * H].astype(bf16).reshape(head_shape)
    score_scale = 1.0 / math.sqrt(head_width)
    scores = ein32("bqhd,bkhd->bhqk", queries, keys_rot) * score_scale
    scores = jnp.where(allowed[:, None], scores, masked_score)
    row_peak = jnp.max(scores, axis=-1, keepdims=True)
    log_total = row_peak + jnp.log(jnp.sum(jnp.exp(scores - row_peak), axis=-1, keepdims=True))
    attn_probs = jnp.exp(scores - log_total)
    probs_half = attn_probs.astype(bf16)
    context = ein32("bhqk,bkhd->bqhd", probs_half, values).astype(bf16)
    context_flat = context.reshape(B * T, H)

    def at_home(partial_rows, collective):
        if not fast:
            return partial_rows
        return plane_sum(partial_rows.astype(bf16).reshape(B, T, D), collective)

    residual_mid = residual_in + branch_scale * at_home(dot32(context_flat, full_output), 4)
    normed_mid, inverse_mid = rms_forward(residual_mid, gain_ffn)
    normed_mid_half = normed_mid.astype(bf16)

    logits = dot32(normed_mid_half, full_router)
    expert_ids = jnp.arange(experts)
    route_mask = (routes[:, :, None] == expert_ids[None, None, :]).astype(f32)
    chosen = jnp.sum(logits[:, None, :] * route_mask, axis=-1)
    gate_probs = jax.nn.softmax(chosen, axis=-1)
    flat_routes = routes.reshape(2 * T)
    hits = (flat_routes[:, None] == expert_ids[None, :]).astype(bf16)
    order = jnp.arange(2 * T)
    before = (order[:, None] > order[None, :]).astype(bf16)
    earlier = dot32(before, hits)
    slot_index = jnp.sum(earlier * hits.astype(f32), axis=1).astype(jnp.int32)
    target = (flat_routes * capacity + slot_index).reshape(T, 2)
    slot_ids = jnp.arange(slots)
    pick = [(target[:, k][:, None] == slot_ids[None, :]).astype(bf16) for k in range(2)]

    notes = jnp.concatenate([gate_probs, target.astype(f32), jnp.zeros((T, 4), f32)], axis=1)
    notes = jnp.pad(jnp.transpose(notes), ((0, 0), (0, -T % 128)))
    spread = spread_blocks if fast else spread_pair
    w_pair, all_normed, all_notes = spread(nz, (normed_mid_half, notes), packed[0], moved_up, 2)
    w_pair = w_pair.reshape(n_shard * R, 2 * Fp)
    devices = n_shard * n_exp
    flat_notes = all_notes.reshape(devices, 8, -1)[:, :, :T]
    wanted = (e_index * capacity + jnp.arange(capacity)).astype(f32)
    found = [flat_notes[:, 2 + k, None, :] == wanted[None, :, None] for k in range(2)]
    gate_rows = jnp.sum(
        jnp.where(found[0], flat_notes[:, 0, None, :], 0.0)
        + jnp.where(found[1], flat_notes[:, 1, None, :], 0.0),
        axis=-1,
    ).reshape(devices * capacity, 1)
    chosen_rows = (found[0] | found[1]).astype(bf16)

    def take(blocks):
        rows = ein32("spt,std->spd", chosen_rows, blocks.reshape(devices, T, D))
        return rows.astype(bf16).reshape(devices * capacity, D)

    arrived = take(all_normed)
    cotangent_rows = take(all_cotangent)
    grad_scale = gate_rows * branch_scale
    pre = dot32(arrived, w_pair)
    gate_part, up_part = pre[:, :Fp], pre[:, Fp:]
    sigmoid_gate = jax.nn.sigmoid(gate_part)
    silu_gate = gate_part * sigmoid_gate
    activated = (silu_gate * up_part).astype(bf16)
    out_sum = lax.psum_scatter(
        dot32(activated, down).astype(bf16), SHARD, scatter_dimension=0, tiled=True
    )

    raw_grad = dot_dims(cotangent_rows, down, 1, 1)
    row_dots = branch_scale * jnp.sum(raw_grad * activated.astype(f32), axis=1)
    row_dots = row_dots.reshape(devices, capacity, 1)
    token_dots = [jnp.sum(jnp.where(found[k], row_dots, 0.0), axis=1) for k in range(2)]
    token_dots = jnp.stack(token_dots, axis=1).reshape(nz, 2, n_exp, 2, T)
    token_dots = jnp.pad(token_dots, ((0, 0),) * 3 + ((0, 6), (0, -T % 128)))
    act_grad = grad_scale * raw_grad
    gate_grads = act_grad * up_part * sigmoid_gate * (1.0 + gate_part * (1.0 - sigmoid_gate))
    gate_grads, up_grads = gate_grads.astype(bf16), (act_grad * silu_gate).astype(bf16)
    pre_grad = jnp.concatenate([gate_grads, up_grads], axis=1)
    in_rows = dot_dims(pre_grad, w_pair, 1, 1).astype(bf16)
    scaled = (grad_scale * activated.astype(f32)).astype(bf16)
    grad_w_down = lined_up(dot_dims(scaled[:, :F], cotangent_rows, 0, 0))
    gate_term, up_term = [
        dot_dims(arrived, x, 0, 0).astype(bf16).reshape(n_shard, R, Fp)
        for x in (gate_grads, up_grads)
    ]
    gate_term, up_term = lax.optimization_barrier((gate_term, up_term))
    up_term = lax.all_to_all(up_term, SHARD, split_axis=0, concat_axis=0, tiled=True)
    in_rows = in_rows.reshape(nz, 2, n_exp, capacity, D)
    collect = collect_rows if fast else collect_plain
    normed_mid_grad, gate_grad = collect(nz, in_rows, all_notes, token_dots, T)
    gate_grad = jnp.transpose(gate_grad[:2, :T])
    up_term, normed_mid_grad, out_sum, gate_term = lax.optimization_barrier(
        (up_term, normed_mid_grad, out_sum, gate_term)
    )
    gate_term = lax.all_to_all(gate_term, SHARD, split_axis=0, concat_axis=0, tiled=True)

    upstream = cotangent.astype(f32)
    chosen_grad = gate_probs * (gate_grad - jnp.sum(gate_probs * gate_grad, axis=-1, keepdims=True))
    logit_grad = jnp.sum(chosen_grad[:, :, None] * route_mask, axis=1)
    normed_mid_grad = normed_mid_grad + jnp.dot(
        logit_grad, jnp.transpose(full_router.astype(f32)), precision=highest
    )
    router_grad = jnp.dot(
        jnp.transpose(normed_mid_half.astype(f32)), logit_grad, precision=highest
    )
    mid_norm_grad, gain_ffn_grad = rms_backward(
        residual_mid, inverse_mid, gain_ffn, normed_mid_grad
    )
    residual_grad = upstream + mid_norm_grad
    branch_grad = (branch_scale * residual_grad).astype(bf16)

    if fast:
        branch_grad = plane_gather(branch_grad, 5).reshape(B * T, D)
    output_grad = dot_dims(context_flat, branch_grad, 0, 0)
    context_grad = dot_dims(branch_grad, full_output, 1, 1).reshape(head_shape)
    row_delta = jnp.sum(context_grad * context.astype(f32), axis=-1)
    context_grad_half = context_grad.astype(bf16)
    probs_grad = ein32("bqhd,bkhd->bhqk", context_grad_half, values)
    scores_grad = (
        attn_probs * (probs_grad - jnp.transpose(row_delta, (0, 2, 1))[..., None]) * score_scale
    ).astype(bf16)
    queries_grad = ein32("bhqk,bkhd->bqhd", scores_grad, keys_rot)
    keys_grad = ein32("bhqk,bqhd->bkhd", scores_grad, queries)
    values_grad = ein32("bhqk,bqhd->bkhd", probs_half, context_grad_half)
    qkv_grad = jnp.concatenate(
        [
            rotate(queries_grad, cosine, -sine_table).reshape(B * T, H).astype(bf16),
            rotate(keys_grad, cosine, -sine_table).reshape(B * T, H).astype(bf16),
            values_grad.reshape(B * T, H).astype(bf16),
            jnp.zeros((B * T, full_qkv.shape[1] - 3 * H), bf16),
        ],
        axis=1,
    )
    qkv_weight_grad = dot_dims(normed_half, qkv_grad, 0, 0)
    near_grad = dot_dims(qkv_grad, full_qkv, 1, 1)
    gain_attn_grad = jnp.sum(near_grad * near_in * near_inverse, axis=0)

    small_grad = jnp.concatenate(
        [router_grad, gain_attn_grad[:, None], gain_ffn_grad[:, None]], axis=1
    )
    small_grad = jnp.pad(small_grad, ((0, 0), (0, 128 - small_grad.shape[1])))
    small_grad, gate_term = lax.optimization_barrier((small_grad, gate_term))
    sum_query, sum_key, sum_value, sum_output, small_sum, normed_in_grad, back = settle(
        nz, fast, qkv_weight_grad, output_grad, small_grad, near_grad, out_sum
    )
    grad_w_in = unpack_columns(gate_term, up_term, F)
    mixture = gate_probs[:, 0:1] * dot32(pick[0], back) + gate_probs[:, 1:2] * dot32(pick[1], back)
    activations = (residual_mid + branch_scale * mixture).astype(bf16)
    in_norm_grad = rms_backward(residual_in, inverse_in, gain_attn, normed_in_grad)[0]
    grad_tokens = residual_grad + in_norm_grad
    return (
        activations,
        grad_tokens,
        small_sum[:, experts],
        sum_query,
        sum_key,
        sum_value,
        sum_output,
        small_sum[:, experts + 1],
        small_sum[:, :experts],
        grad_w_in,
        grad_w_down,
    )


def solution(mesh):
    n_expert, n_shard = mesh.devices.shape
    chips = Mesh(mesh.devices.reshape(n_expert, n_shard // 2, 2), ("expert", "z", "core"))
    rows = P(("expert", "z", "core"), None)
    shard = P(SHARD)
    shard2 = P(SHARD, None)
    shard3 = P(SHARD, "expert", None)
    in_specs = (
        rows,
        rows,
        rows,
        shard,
        shard2,
        shard2,
        shard2,
        shard2,
        shard,
        shard2,
        shard3,
        shard3,
        rows,
    )
    out_specs = (
        rows,
        rows,
        shard,
        shard2,
        shard2,
        shard2,
        shard2,
        shard,
        shard2,
        shard3,
        shard3,
    )
    return jax.shard_map(
        on_device, mesh=chips, in_specs=in_specs, out_specs=out_specs, check_vma=False
    )
```

```python
import functools
import math

import jax
import jax.numpy as jnp
from jax import lax
from jax.experimental import pallas as pl
from jax.experimental.pallas import tpu as pltpu
from jax.sharding import Mesh, PartitionSpec as P

HEADS = 36

eps_norm = 1e-05
branch_scale = 1.4 / math.sqrt(40.0)
rope_base = 10000.0
masked_score = -1e30
bf16 = jnp.bfloat16
f32 = jnp.float32
SHARD = ("z", "core")
ANY = pl.BlockSpec(memory_space=pl.ANY)


def place():
    e, z, c = lax.axis_index("expert"), lax.axis_index("z"), lax.axis_index("core")
    across_x = e + 1 - 2 * (e % 2)
    across_y = (e + 2) % 4
    return e, z, c, across_x, across_y


def remote(src, dst, send, recv, e, z, c):
    return pltpu.make_async_remote_copy(
        src_ref=src,
        dst_ref=dst,
        send_sem=send,
        recv_sem=recv,
        device_id=(e, z, c),
        device_id_type=pl.DeviceIdType.MESH,
    )


def payload_stream(nz, ref, out, sems, split):
    zrecv, zsend, near_recv, near_send, far_recv, far_send, sib_recv, sib_send, own = sems
    e, z, c, ex, ey = place()
    diagonal = (ex + 2) % 4
    T = ref.shape[0]
    S = 2 * nz - 1

    def split_step(s):
        return (s - 1) % 2, (s - 1) // 2

    def where(s):
        if s == 0:
            return z
        side, i = split_step(s)
        return z - 1 - i if side == 0 else z + 1 + i

    def exists(s):
        if s == 0:
            return z >= 0
        zz = where(s)
        return (zz >= 0) & (zz < nz)

    def slab(s, quarter, r0=0, n=T):
        return out.at[where(s), c, quarter, pl.ds(r0, n), :]

    def first(step):
        side = 0 if step > 0 else 1
        return remote(ref, slab(0, e), zsend.at[side, nz - 1], zrecv.at[side, 0], e, z + step, c)

    def onward(s):
        side, i = split_step(s)
        step = 1 if side == 0 else -1
        return remote(
            slab(s, e), slab(s, e), zsend.at[side, i], zrecv.at[side, i + 1], e, z + step, c
        )

    def near(s, axis):
        source = ref if s == 0 else slab(s, e)
        return remote(
            source, slab(s, e), near_send.at[s, axis], near_recv.at[s, axis],
            ex if axis == 0 else ey, z, c,
        )

    def near_wait(s, axis):
        view = slab(s, ex if axis == 0 else ey)
        remote(view, view, near_send.at[s, axis], near_recv.at[s, axis], ex, z, c).wait_recv()

    axes = range(2) if split else range(1)

    def far_view(s, quarter, axis):
        if not split:
            return slab(s, quarter)
        return slab(s, quarter, 0, split) if axis == 0 else slab(s, quarter, split, T - split)

    def far(s, axis):
        view = far_view(s, ex if axis == 0 else ey, axis)
        return remote(
            view, view, far_send.at[s, axis], far_recv.at[s, axis],
            ey if axis == 0 else ex, z, c,
        )

    def far_wait(s, axis):
        view = far_view(s, diagonal, axis)
        remote(view, view, far_send.at[s, axis], far_recv.at[s, axis], ex, z, c).wait_recv()

    def beside(s, n):
        quarter = (e, ex, ey, diagonal)[n]
        source = ref if s == 0 and n == 0 else slab(s, quarter)
        return remote(
            source, slab(s, quarter), sib_send.at[s, n], sib_recv.at[s, n], e, z, 1 - c
        )

    def beside_wait(s, n):
        view = out.at[where(s), 1 - c, (e, ex, ey, diagonal)[n]]
        remote(view, view, sib_send.at[s, n], sib_recv.at[s, n], e, z, c).wait_recv()

    def inside(side):
        return z < nz - 1 if side == 0 else z > 0

    def begin():
        for step in (1, -1):

            @pl.when((z + step >= 0) & (z + step < nz))
            def _():
                first(step).start()

        near(0, 0).start()
        near(0, 1).start()
        beside(0, 0).start()
        pltpu.make_async_copy(ref, slab(0, e), own).start()

    def arrive(s):
        if s == 0:
            return

        @pl.when(exists(s))
        def _():
            side, i = split_step(s)
            remote(
                slab(s, e), slab(s, e), zsend.at[side, i], zrecv.at[side, i], e, z, c
            ).wait_recv()
            if i < nz - 2:

                @pl.when(inside(side))
                def _():
                    onward(s).start()

            near(s, 0).start()
            near(s, 1).start()
            beside(s, 0).start()

    def relay(s):
        @pl.when(exists(s))
        def _():
            near_wait(s, 0)
            far(s, 0).start()
            beside(s, 1).start()
            near_wait(s, 1)
            if split:
                far(s, 1).start()
            beside(s, 2).start()

    def close(s):
        @pl.when(exists(s))
        def _():
            for axis in axes:
                far_wait(s, axis)
            beside(s, 3).start()

    def end(s):
        @pl.when(exists(s))
        def _():
            for axis in range(2):
                near(s, axis).wait_send()
            for axis in axes:
                far(s, axis).wait_send()
            for n in range(4):
                beside(s, n).wait_send()
                beside_wait(s, n)
            if s > 0 and split_step(s)[1] < nz - 2:

                @pl.when(inside(split_step(s)[0]))
                def _():
                    onward(s).wait_send()

        if s == 0:
            for step in (1, -1):

                @pl.when((z + step >= 0) & (z + step < nz))
                def _():
                    first(step).wait_send()

            pltpu.make_async_copy(ref, slab(0, e), own).wait()

    return begin, arrive, relay, close, end


def payload_sems(nz):
    dma = pltpu.SemaphoreType.DMA
    S = 2 * nz - 1
    return [
        dma((2, nz)), dma((2, nz)), dma((S, 2)), dma((S, 2)), dma((S, 2)), dma((S, 2)),
        dma((S, 4)), dma((S, 4)), dma(()),
    ]


def spread_kernel(nz, splits, *refs):
    n = len(splits)
    (gate_ref, up_ref), refs = refs[:2], refs[2:]
    ins, refs = refs[:n], refs[n:]
    pair, outs, sems = refs[0], refs[1 : n + 1], refs[n + 1 :]
    v_sems, beside_sem, sems = sems[:3], sems[3], sems[4:]
    width = gate_ref.shape[2]
    greet_shard(nz)
    streams = [
        payload_stream(nz, ins[i], outs[i], sems[9 * i : 9 * i + 9], splits[i]) for i in range(n)
    ]
    v_begin, v_end = scatter_stream(
        nz, gate_ref, lambda i: pair.at[i, :, pl.ds(0, width)], *v_sems
    )
    beside = pltpu.make_async_copy(up_ref, pair.at[:, :, pl.ds(width, width)], beside_sem)
    for t in streams:
        t[0]()
    beside.start()
    S = 2 * nz - 1
    for s in range(1, S):
        for t in streams:
            t[1](s)
    v_begin()
    for s in range(S):
        for t in streams:
            t[2](s)
        if s >= 1:
            for t in streams:
                t[3](s - 1)
    for t in streams:
        t[3](S - 1)
    for s in range(S):
        for t in streams:
            t[4](s)
    beside.wait()
    v_end()


def spread_blocks(nz, blocks, gate, up, collective):
    sd = jax.ShapeDtypeStruct
    splits = tuple(b.shape[0] // 2 if b.shape[0] % 32 == 0 else 0 for b in blocks)
    pair = sd(gate.shape[:2] + (2 * gate.shape[2],), gate.dtype)
    return pl.pallas_call(
        functools.partial(spread_kernel, nz, splits),
        out_shape=(pair,) + tuple(sd((nz, 2, 4) + b.shape, b.dtype) for b in blocks),
        in_specs=[ANY] * (len(blocks) + 2),
        out_specs=(ANY,) * (len(blocks) + 1),
        scratch_shapes=[
            *scatter_sems(nz), pltpu.SemaphoreType.DMA(()),
            *[s for _ in blocks for s in payload_sems(nz)],
        ],
        compiler_params=pltpu.CompilerParams(collective_id=collective, has_side_effects=True),
        cost_estimate=pl.CostEstimate(flops=10**6, bytes_accessed=10**6, transcendentals=0),
        name="spread_blocks",
    )(gate, up, *blocks)


def line_order(nz, z):
    def order(i):
        code = 0
        for zz in range(nz):
            far_first = sorted(range(nz), key=lambda t: (-abs(t - zz), t))
            code += far_first[i] * nz**zz
        power = 1
        for zz in range(nz):
            power = power + (nz**zz - 1) * jnp.where(z == zz, 1, 0)
        return (code // power) % nz

    return [order(i) for i in range(nz)]


def collect_kernel(
    nz, cap,
    rows_ref, notes_ref, dots_ref,
    out_ref, dots_out,
    dots, notes, mine, theirs, block, from_x, from_y, via_x, via_y, from_z,
    note_sem, load, sib_send, sib_recv, via_send, via_recv, plain_send, plain_recv,
    sum_send, sum_recv, zsend, zrecv, dot_send, dot_recv, dot_own,
):
    e, z, c, ex, ey = place()
    diagonal = (ex + 2) % 4
    T, D = out_ref.shape
    h = T // 2
    dest = line_order(nz, z)
    who = (diagonal, ex, ey, e)

    def others():
        for d in range(1, 8 * nz):
            to = ((e * nz + z) * 2 + c + d) % (8 * nz)
            yield d, to // (2 * nz), to // 2 % nz, to % 2

    barrier = pltpu.get_barrier_semaphore()
    for _, te, tz, tc in others():
        pl.semaphore_signal(
            barrier, inc=1, device_id=(te, tz, tc), device_id_type=pl.DeviceIdType.MESH
        )
    pl.semaphore_wait(barrier, 8 * nz - 1)

    def dot(d, te, tz, tc):
        return remote(
            dots_ref.at[tz, tc, te], dots.at[d], dot_send.at[d], dot_recv.at[d], te, tz, tc
        )

    dot_kept = pltpu.make_async_copy(dots_ref.at[z, c, e], dots.at[0], dot_own)
    dot_kept.start()
    for d, te, tz, tc in others():
        dot(d, te, tz, tc).start()

    note_copy = pltpu.make_async_copy(notes_ref, notes, note_sem)
    note_copy.start()

    def fetch(i, q):
        return pltpu.make_async_copy(
            rows_ref.at[dest[i], c, who[q]], mine.at[i, q], load.at[i, q]
        )

    def hand(i, q):
        return remote(
            rows_ref.at[dest[i], 1 - c, who[q]], theirs.at[i, q],
            sib_send.at[i, q], sib_recv.at[i, q], e, z, 1 - c,
        )

    for i in range(nz):
        for q in range(4):
            hand(i, q).start()
            fetch(i, q).start()
    note_copy.wait()

    def open_out(i, q):
        fetch(i, q).wait()
        hand(i, q).wait_recv()
        places = (lax.broadcasted_iota(jnp.int32, (cap, T), 0) + e * cap).astype(f32)
        note = notes[dest[i], c, who[q]]
        pick = ((note[2:3, :] == places) | (note[3:4, :] == places)).astype(bf16)
        wide = 768 if D % 768 == 0 else 128

        @pl.loop(0, D // wide)
        def _(b):
            cols = pl.ds(pl.multiple_of(b * wide, 128), wide)
            both = mine[i, q, :, cols].astype(f32) + theirs[i, q, :, cols].astype(f32)
            block[i, q, :, cols] = lax.dot_general(
                pick, both.astype(bf16), (((0,), (0,)), ((), ())), preferred_element_type=f32
            ).astype(bf16)

    def via(i, axis):
        if axis == 0:
            return remote(
                block.at[i, 0, pl.ds(0, h), :], via_x.at[i],
                via_send.at[i, 0], via_recv.at[i, 0], ex, z, c,
            )
        return remote(
            block.at[i, 0, pl.ds(h, h), :], via_y.at[i],
            via_send.at[i, 1], via_recv.at[i, 1], ey, z, c,
        )

    def plain(i, axis):
        if axis == 0:
            return remote(
                block.at[i, 1, pl.ds(0, h), :], from_x.at[i, pl.ds(0, h), :],
                plain_send.at[i, 0], plain_recv.at[i, 0], ex, z, c,
            )
        return remote(
            block.at[i, 2, pl.ds(h, h), :], from_y.at[i, pl.ds(h, h), :],
            plain_send.at[i, 1], plain_recv.at[i, 1], ey, z, c,
        )

    def summed(i, axis):
        if axis == 0:
            return remote(
                block.at[i, 1, pl.ds(h, h), :], from_x.at[i, pl.ds(h, h), :],
                sum_send.at[i, 0], sum_recv.at[i, 0], ex, z, c,
            )
        return remote(
            block.at[i, 2, pl.ds(0, h), :], from_y.at[i, pl.ds(0, h), :],
            sum_send.at[i, 1], sum_recv.at[i, 1], ey, z, c,
        )

    def add(target, others, n):
        @pl.loop(0, n // 16)
        def _(b):
            rows = pl.ds(pl.multiple_of(b * 16, 16), 16)
            acc = target[rows, :].astype(f32)
            for o in others:
                acc = acc + o[rows, :].astype(f32)
            target[rows, :] = acc.astype(target.dtype)

    def start(i):
        open_out(i, 0)
        via(i, 0).start()
        via(i, 1).start()
        open_out(i, 1)
        plain(i, 0).start()
        open_out(i, 2)
        plain(i, 1).start()
        open_out(i, 3)

    def combine(i):
        via(i, 0).wait_recv()
        add(block.at[i, 2, pl.ds(0, h), :], [via_x.at[i]], h)
        summed(i, 1).start()
        via(i, 1).wait_recv()
        add(block.at[i, 1, pl.ds(h, h), :], [via_y.at[i]], h)
        summed(i, 0).start()

    def zcopy(i):
        step = jnp.where(dest[i] > z, 1, -1)
        side = jnp.where(dest[i] > z, 0, 1)
        return remote(
            block.at[i, 3], from_z.at[side, dest[i]],
            zsend.at[i], zrecv.at[side, dest[i]], e, z + step, c,
        )

    def zwait(side, zz):
        slab = from_z.at[side, zz]
        remote(slab, slab, zsend.at[0], zrecv.at[side, zz], e, z, c).wait_recv()

    def finish(i):
        for axis in range(2):
            plain(i, axis).wait_recv()
            summed(i, axis).wait_recv()
        zz = dest[i]
        if i < nz - 1:
            add(block.at[i, 3], [from_x.at[i], from_y.at[i]], T)
            for side in range(2):
                going = zz > z if side == 0 else zz < z
                behind = z > 0 if side == 0 else z < nz - 1

                @pl.when(going & behind)
                def _():
                    zwait(side, zz)
                    add(block.at[i, 3], [from_z.at[side, zz]], T)

            zcopy(i).start()
            return

        @pl.loop(0, T // 16)
        def _(b):
            rows = pl.ds(pl.multiple_of(b * 16, 16), 16)
            acc = block[i, 3, rows, :].astype(f32) + from_x[i, rows, :].astype(f32)
            out_ref[rows, :] = acc + from_y[i, rows, :].astype(f32)

        for side in range(2):

            @pl.when(z > 0 if side == 0 else z < nz - 1)
            def _():
                zwait(side, z)
                add(out_ref, [from_z.at[side, z]], T)

    for i in range(nz):
        start(i)
        if i >= 1:
            combine(i - 1)
        if i >= 2:
            finish(i - 2)
    combine(nz - 1)
    if nz >= 2:
        finish(nz - 2)
    finish(nz - 1)

    dot_kept.wait()
    for d, te, tz, tc in others():
        dot(d, te, tz, tc).wait_recv()
        dot(d, te, tz, tc).wait_send()
    dots_out[...] = jnp.sum(dots[...], axis=0)

    for i in range(nz):
        for q in range(4):
            hand(i, q).wait_send()
        for axis in range(2):
            via(i, axis).wait_send()
            plain(i, axis).wait_send()
            summed(i, axis).wait_send()
        if i < nz - 1:
            zcopy(i).wait_send()


def collect_rows(nz, rows, notes, dots, T):
    cap, D = rows.shape[3:]
    dma = pltpu.SemaphoreType.DMA
    vm = pltpu.VMEM
    return pl.pallas_call(
        functools.partial(collect_kernel, nz, cap),
        out_shape=(
            jax.ShapeDtypeStruct((T, D), f32),
            jax.ShapeDtypeStruct(dots.shape[3:], f32),
        ),
        in_specs=[ANY] * 3,
        out_specs=(pl.BlockSpec(memory_space=pltpu.VMEM),) * 2,
        scratch_shapes=[
            vm((8 * nz,) + dots.shape[3:], f32),
            vm(notes.shape, f32),
            vm((nz, 4, cap, D), bf16),
            vm((nz, 4, cap, D), bf16),
            vm((nz, 4, T, D), bf16),
            vm((nz, T, D), bf16),
            vm((nz, T, D), bf16),
            vm((nz, T // 2, D), bf16),
            vm((nz, T // 2, D), bf16),
            vm((2, nz, T, D), bf16),
            dma(()),
            dma((nz, 4)),
            dma((nz, 4)),
            dma((nz, 4)),
            dma((nz, 2)),
            dma((nz, 2)),
            dma((nz, 2)),
            dma((nz, 2)),
            dma((nz, 2)),
            dma((nz, 2)),
            dma((nz,)),
            dma((2, nz)),
            dma((8 * nz,)),
            dma((8 * nz,)),
            dma(()),
        ],
        compiler_params=pltpu.CompilerParams(
            collective_id=3, has_side_effects=True, vmem_limit_bytes=56 << 20
        ),
        cost_estimate=pl.CostEstimate(
            flops=10**6, bytes_accessed=10**6, transcendentals=0
        ),
        name="collect_rows",
    )(rows, notes, dots)


def pack_rows(n, F, Fp, x_ref, *o_refs):
    half = n * F
    rows = x_ref.shape[0]
    for i in range(n):
        for part in range(2):
            cols = x_ref[:, part * half + i * F : part * half + (i + 1) * F]
            if Fp > F:
                cols = jnp.concatenate([cols, jnp.zeros((rows, Fp - F), cols.dtype)], axis=1)
            o_refs[part][i] = cols


def pack_columns(w, n, F, Fp):
    rows = w.shape[0]
    block = 16
    return pl.pallas_call(
        functools.partial(pack_rows, n, F, Fp),
        grid=(rows // block,),
        in_specs=[pl.BlockSpec((block, w.shape[1]), lambda i: (i, 0))],
        out_specs=(pl.BlockSpec((n, block, Fp), lambda i: (0, i, 0)),) * 2,
        out_shape=(jax.ShapeDtypeStruct((n, rows, Fp), w.dtype),) * 2,
        name="pack_columns",
    )(w)


def unpack_kernel(n, F, gate_ref, up_ref, o_ref, line):
    half = n * F
    rows = line.shape[0]
    for i in range(n):
        for part in range(2):
            cols = (up_ref if part else gate_ref)[i, :, :F].astype(f32)
            line[:, part * half + i * F : part * half + (i + 1) * F] = cols
    tiles = 2 * half // 128
    for j in range(tiles):
        o_ref[pl.ds(j, rows, stride=tiles), :] = line[:, j * 128 : (j + 1) * 128]


def unpack_columns(gate, up, F):
    n, rows, Fp = gate.shape
    block = 96 if rows % 96 == 0 else 16
    width = 2 * n * F
    tiles = width // 128
    flat = pl.pallas_call(
        functools.partial(unpack_kernel, n, F),
        grid=(rows // block,),
        in_specs=[pl.BlockSpec((n, block, Fp), lambda i: (0, i, 0))] * 2,
        out_specs=pl.BlockSpec((block * tiles, 128), lambda i: (i, 0)),
        out_shape=jax.ShapeDtypeStruct((rows * tiles, 128), f32),
        scratch_shapes=[pltpu.VMEM((block, width), f32)],
        name="unpack_columns",
    )(gate, up)
    return flat.reshape(rows, 1, width)


def line_kernel(x_ref, o_ref):
    rows, width = x_ref.shape
    tiles = width // 128
    for j in range(tiles):
        o_ref[pl.ds(j, rows, stride=tiles), :] = x_ref[:, j * 128 : (j + 1) * 128]


def lined_up(x):
    rows, width = x.shape
    tiles = width // 128
    block = 240 if rows % 240 == 0 else 8
    flat = pl.pallas_call(
        line_kernel,
        grid=(rows // block,),
        in_specs=[pl.BlockSpec((block, width), lambda i: (i, 0))],
        out_specs=pl.BlockSpec((block * tiles, 128), lambda i: (i, 0)),
        out_shape=jax.ShapeDtypeStruct((rows * tiles, 128), x.dtype),
        name="lined_up",
    )(x)
    return flat.reshape(rows, 1, width)


def greet_cross(nz):
    e, z, c, ex, ey = place()
    barrier = pltpu.get_barrier_semaphore()

    def hail(te, tz, tc):
        pl.semaphore_signal(
            barrier, inc=1, device_id=(te, tz, tc), device_id_type=pl.DeviceIdType.MESH
        )

    hail(e, z, 1 - c)
    for te in (ex, ey, (ex + 2) % 4):
        hail(te, z, c)
    for step in (-1, 1):

        @pl.when((z + step >= 0) & (z + step < nz))
        def _():
            hail(e, z + step, c)

    pl.semaphore_wait(barrier, 4 + jnp.where(z > 0, 1, 0) + jnp.where(z < nz - 1, 1, 0))


def greet_shard(nz):
    e, z, c, ex, ey = place()
    barrier = pltpu.get_barrier_semaphore()
    n = 2 * nz
    peers = [(te, z, c) for te in (ex, ey, (ex + 2) % 4)]
    for d in range(1, n):
        to = (2 * z + c + d) % n
        peers.append((e, to // 2, to % 2))
    for peer in peers:
        pl.semaphore_signal(barrier, inc=1, device_id=peer, device_id_type=pl.DeviceIdType.MESH)
    pl.semaphore_wait(barrier, n + 2)


def scatter_stream(nz, ref, view, send, recv, own):
    e, z, c, _, _ = place()
    n = 2 * nz
    me = 2 * z + c

    def copy(d):
        to = (me + d) % n
        return remote(ref.at[to], view(me), send.at[d], recv.at[d], e, to // 2, to % 2)

    kept = pltpu.make_async_copy(ref.at[me], view(me), own)

    def begin():
        for d in range(1, n):
            copy(d).start()
        kept.start()

    def end():
        kept.wait()
        for d in range(1, n):
            land = view((me + n - d) % n)
            remote(land, land, send.at[d], recv.at[d], e, z, c).wait_recv()
            copy(d).wait_send()

    return begin, end


def scatter_sems(nz):
    dma = pltpu.SemaphoreType.DMA
    return [dma((2 * nz,)), dma((2 * nz,)), dma(())]


def line_stream(nz, ref, out, zrecv, zsend, sib_recv, sib_send, own):
    e, z, c, _, _ = place()

    def split_step(s):
        return (s - 1) % 2, (s - 1) // 2

    def where(s):
        if s == 0:
            return z
        side, i = split_step(s)
        return z - 1 - i if side == 0 else z + 1 + i

    def exists(s):
        return (where(s) >= 0) & (where(s) < nz)

    def inside(side):
        return z < nz - 1 if side == 0 else z > 0

    def slab(s):
        return out.at[where(s), c]

    def first(side):
        step = 1 if side == 0 else -1
        return remote(ref, slab(0), zsend.at[side, nz - 1], zrecv.at[side, 0], e, z + step, c)

    def onward(s):
        side, i = split_step(s)
        step = 1 if side == 0 else -1
        return remote(
            slab(s), slab(s), zsend.at[side, i], zrecv.at[side, i + 1], e, z + step, c
        )

    def beside(s):
        return remote(
            ref if s == 0 else slab(s), slab(s), sib_send.at[s], sib_recv.at[s], e, z, 1 - c
        )

    def begin():
        for side in range(2):

            @pl.when(inside(side))
            def _():
                first(side).start()

        beside(0).start()
        pltpu.make_async_copy(ref, slab(0), own).start()

    def arrive(s):
        side, i = split_step(s)

        @pl.when(exists(s))
        def _():
            remote(slab(s), slab(s), zsend.at[side, i], zrecv.at[side, i], e, z, c).wait_recv()
            if i < nz - 2:

                @pl.when(inside(side))
                def _():
                    onward(s).start()

            beside(s).start()

    def end():
        for s in range(2 * nz - 1):

            @pl.when(exists(s))
            def _():
                beside(s).wait_send()
                view = out.at[where(s), 1 - c]
                remote(view, view, sib_send.at[s], sib_recv.at[s], e, z, c).wait_recv()
                if s > 0 and split_step(s)[1] < nz - 2:

                    @pl.when(inside(split_step(s)[0]))
                    def _():
                        onward(s).wait_send()

        for side in range(2):

            @pl.when(inside(side))
            def _():
                first(side).wait_send()

        pltpu.make_async_copy(ref, slab(0), own).wait()

    return begin, arrive, end


def line_sems(nz):
    dma = pltpu.SemaphoreType.DMA
    S = 2 * nz - 1
    return [dma((2, nz)), dma((2, nz)), dma((S,)), dma((S,)), dma(())]


def plane_stream(source, views, send, recv, own):
    e, z, c, ex, ey = place()
    peers = (ex, ey, (ex + 2) % 4)

    def copy(n):
        return remote(source, views(e), send.at[n], recv.at[n], peers[n], z, c)

    def kept():
        return pltpu.make_async_copy(source, views(e), own)

    def begin():
        for n in range(3):
            copy(n).start()
        kept().start()

    def end():
        kept().wait()
        for n in range(3):
            view = views(peers[n])
            remote(view, view, send.at[n], recv.at[n], e, z, c).wait_recv()
            copy(n).wait_send()

    return begin, end


def plane_sems():
    dma = pltpu.SemaphoreType.DMA
    return [dma((3,)), dma((3,)), dma(())]


def fetch_kernel(
    nz,
    F, w_ref, s_ref, o_ref, t_ref, l_ref, p_ref, x_ref,
    w_out, s_out, o_out, t_out, l_out, p_out, gate_out, up_out,
    wide, gate, up, wide_sem, packed_sem,
    *sems,
):
    e, z, c, ex, ey = place()
    w_sems, sems = sems[:5], sems[5:]
    s_sems, sems = sems[:5], sems[5:]
    t_sems, sems = sems[:3], sems[3:]
    l_sems, sems = sems[:3], sems[3:]
    p_sems, sems = sems[:9], sems[9:]
    orecv, osend, sib_recv, sib_send, own = sems
    wide_copy = pltpu.make_async_copy(x_ref, wide, wide_sem)
    wide_copy.start()
    greet_cross(nz)
    w_begin, w_arrive, w_end = line_stream(nz, w_ref, w_out, *w_sems)
    s_begin, s_arrive, s_end = line_stream(nz, s_ref, s_out, *s_sems)
    t_begin, t_end = plane_stream(t_ref, lambda q: t_out.at[q], *t_sems)
    l_begin, l_end = plane_stream(l_ref, lambda q: l_out.at[q], *l_sems)
    p_begin, p_arrive, p_relay, p_close, p_end = payload_stream(
        nz, p_ref, p_out, p_sems, p_ref.shape[0] // 2
    )

    pieces = orecv.shape[0]
    height = o_ref.shape[0] // pieces

    def o_part(n):
        return pl.ds(n * height, height)

    def o_view(n):
        return o_out.at[c, o_part(n), :]

    def o_copy(side, n, source):
        step = 1 if side == 0 else -1
        return remote(source, o_view(n), osend.at[side, n], orecv.at[n], e, z + step, c)

    def o_beside(n, source):
        return remote(source, o_view(n), sib_send.at[n], sib_recv.at[n], e, z, 1 - c)

    def o_goes(side):
        return (z >= e) & (z < nz - 1) if side == 0 else (z <= e) & (z > 0)

    def o_pass(n, source):
        for side in range(2):

            @pl.when(o_goes(side))
            def _():
                o_copy(side, n, source).start()

        o_beside(n, source).start()

    def o_arrive(n):
        @pl.when(z != e)
        def _():
            remote(o_view(n), o_view(n), sib_send.at[n], orecv.at[n], e, z, c).wait_recv()
            o_pass(n, o_view(n))

    p_begin()

    @pl.when(z == e)
    def _():
        for n in range(pieces):
            o_pass(n, o_ref.at[o_part(n), :])
        pltpu.make_async_copy(o_ref, o_out.at[c], own).start()

    s_begin()
    w_begin()
    t_begin()
    l_begin()

    wide_copy.wait()

    @pl.loop(0, wide.shape[0] // 16)
    def _(b):
        rows = pl.ds(pl.multiple_of(b * 16, 16), 16)
        pack_rows(
            gate.shape[0], F, gate.shape[2], wide.at[rows, :], gate.at[:, rows, :], up.at[:, rows, :]
        )

    packed_copies = [
        pltpu.make_async_copy(a, b, packed_sem.at[n])
        for n, (a, b) in enumerate(((gate, gate_out), (up, up_out)))
    ]
    for copy in packed_copies:
        copy.start()

    blocks = 2 * nz - 1
    for s in range(1, blocks):
        p_arrive(s)
        s_arrive(s)
        if s <= pieces:
            o_arrive(s - 1)
    for n in range(blocks - 1, pieces):
        o_arrive(n)
    for s in range(1, blocks):
        p_relay(s - 1)
        w_arrive(s)
        if s >= 2:
            p_close(s - 2)
    p_relay(blocks - 1)
    p_close(blocks - 2)
    p_close(blocks - 1)
    for s in range(blocks):
        p_end(s)
    w_end()
    s_end()
    t_end()
    l_end()
    for n in range(pieces):
        view = o_out.at[1 - c, o_part(n), :]
        remote(view, view, sib_send.at[n], sib_recv.at[n], e, z, c).wait_recv()
        o_beside(n, o_view(n)).wait_send()
        for side in range(2):

            @pl.when(o_goes(side))
            def _():
                o_copy(side, n, o_view(n)).wait_send()

    @pl.when(z == e)
    def _():
        pltpu.make_async_copy(o_ref, o_out.at[c], own).wait()

    for copy in packed_copies:
        copy.wait()


def fetch_weights(nz, columns, small, rows, tokens, lengths, block, wide, F):
    dma = pltpu.SemaphoreType.DMA
    packed = (2 * nz, wide.shape[0], -(-F // 128) * 128)
    sd = jax.ShapeDtypeStruct
    return pl.pallas_call(
        functools.partial(fetch_kernel, nz, F),
        out_shape=(
            sd((nz, 2) + columns.shape, bf16),
            sd((nz, 2) + small.shape, bf16),
            sd((2,) + rows.shape, bf16),
            sd((4,) + tokens.shape, bf16),
            sd((4,) + lengths.shape, lengths.dtype),
            sd((nz, 2, 4) + block.shape, block.dtype),
            sd(packed, wide.dtype),
            sd(packed, wide.dtype),
        ),
        in_specs=[ANY] * 7,
        out_specs=(ANY,) * 8,
        scratch_shapes=[
            pltpu.VMEM(wide.shape, wide.dtype), pltpu.VMEM(packed, wide.dtype),
            pltpu.VMEM(packed, wide.dtype), dma(()), dma((2,)),
            *line_sems(nz), *line_sems(nz), *plane_sems(), *plane_sems(), *payload_sems(nz),
            dma((6,)), dma((2, 6)), dma((6,)), dma((6,)), dma(()),
        ],
        compiler_params=pltpu.CompilerParams(
            collective_id=0, has_side_effects=True, vmem_limit_bytes=60 << 20
        ),
        cost_estimate=pl.CostEstimate(
            flops=10**11, bytes_accessed=8 * columns.size, transcendentals=0
        ),
        name="fetch_weights",
    )(columns, small, rows, tokens, lengths, block, wide)


def plane_gather_kernel(x_ref, out_ref, send, recv, own):
    e, z, c, ex, ey = place()
    greet_plane()
    begin, end = plane_stream(x_ref, lambda q: out_ref.at[q], send, recv, own)
    begin()
    end()


def greet_plane():
    e, z, c, ex, ey = place()
    barrier = pltpu.get_barrier_semaphore()
    for te in (ex, ey, (ex + 2) % 4):
        pl.semaphore_signal(
            barrier, inc=1, device_id=(te, z, c), device_id_type=pl.DeviceIdType.MESH
        )
    pl.semaphore_wait(barrier, 3)


def plane_gather(x, collective):
    return pl.pallas_call(
        plane_gather_kernel,
        out_shape=jax.ShapeDtypeStruct((4,) + x.shape, x.dtype),
        in_specs=[ANY],
        out_specs=ANY,
        scratch_shapes=plane_sems(),
        compiler_params=pltpu.CompilerParams(collective_id=collective, has_side_effects=True),
        cost_estimate=pl.CostEstimate(flops=10**6, bytes_accessed=10**6, transcendentals=0),
        name="plane_gather",
    )(x)


def plane_sum_parts(x_ref, out_ref, held, send, recv, own):
    e, z, c, ex, ey = place()
    peers = (ex, ey, (ex + 2) % 4)

    def copy(n):
        return remote(x_ref.at[peers[n]], held.at[n], send.at[n], recv.at[n], peers[n], z, c)

    kept = pltpu.make_async_copy(x_ref.at[e], held.at[3], own)

    def total():
        kept.wait()
        for n in range(3):
            copy(n).wait_recv()

        @pl.loop(0, out_ref.shape[0] // 16)
        def _(b):
            rows = pl.ds(pl.multiple_of(b * 16, 16), 16)
            acc = held[3, rows, :].astype(f32) + held[0, rows, :].astype(f32)
            acc = acc + held[1, rows, :].astype(f32)
            out_ref[rows, :] = acc + held[2, rows, :].astype(f32)

    return copy, kept, total


def plane_sum_kernel(x_ref, out_ref, held, send, recv, own):
    greet_plane()
    copy, kept, total = plane_sum_parts(x_ref, out_ref, held, send, recv, own)
    for n in (2, 0, 1):
        copy(n).start()
    kept.start()
    total()
    for n in range(3):
        copy(n).wait_send()


def plane_sum(x, collective):
    vm = pltpu.VMEM
    return pl.pallas_call(
        plane_sum_kernel,
        out_shape=jax.ShapeDtypeStruct(x.shape[1:], f32),
        in_specs=[ANY],
        out_specs=pl.BlockSpec(memory_space=vm),
        scratch_shapes=[vm(x.shape, bf16), *plane_sems()],
        compiler_params=pltpu.CompilerParams(collective_id=collective, has_side_effects=True),
        cost_estimate=pl.CostEstimate(flops=10**6, bytes_accessed=10**6, transcendentals=0),
        name="plane_sum",
    )(x)


def settle_kernel(
    nz,
    g_ref, s_ref, o_ref, x_ref, y_ref,
    g_out, s_out, o_out, x_out, y_out,
    x_held, x_send, x_recv, x_own, y_send, y_recv, y_own,
    g_mine, g_sib, g_z, s_mine, s_sib, s_z, o_mine, o_sib, o_z,
    load, sib_send, sib_recv, zsend, zrecv,
    o_load, o_sib_send, o_sib_recv, o_zsend, o_zrecv,
    o_send, o_recv, o_own,
    *sems,
):
    e, z, c, ex, ey = place()
    peers = (ex, ey, (ex + 2) % 4)
    dest = line_order(nz, z)
    greet_cross(nz)
    W = g_ref.shape[3]
    first = W // 256 * 128
    groups = (
        (g_ref, g_mine, g_sib, g_z, g_out, pl.ds(0, first)),
        (g_ref, g_mine, g_sib, g_z, g_out, pl.ds(first, W - first)),
        (s_ref, s_mine, s_sib, s_z, s_out, pl.ds(0, s_ref.shape[3])),
    )
    K = len(groups)

    def part(k, which, *index):
        return groups[k][which].at[(*index, slice(None), groups[k][5])]

    def fetch(k, i):
        return pltpu.make_async_copy(
            part(k, 0, dest[i], c), part(k, 1, i), load.at[k, i]
        )

    def hand(k, i):
        return remote(
            part(k, 0, dest[i], 1 - c), part(k, 2, i),
            sib_send.at[k, i], sib_recv.at[k, i], e, z, 1 - c,
        )

    def zcopy(k, i):
        step = jnp.where(dest[i] > z, 1, -1)
        side = jnp.where(dest[i] > z, 0, 1)
        return remote(
            part(k, 1, i), part(k, 3, side, dest[i]),
            zsend.at[k, i], zrecv.at[k, side, dest[i]], e, z + step, c,
        )

    def zwait(k, side, zz):
        slab = part(k, 3, side, zz)
        remote(slab, slab, zsend.at[k, 0], zrecv.at[k, side, zz], e, z, c).wait_recv()

    def add(target, others):
        @pl.loop(0, target.shape[0] // 16)
        def _(b):
            rows = pl.ds(pl.multiple_of(b * 16, 16), 16)
            acc = target[rows, :].astype(f32)
            for o in others:
                acc = acc + o[rows, :].astype(f32)
            target[rows, :] = acc.astype(target.dtype)

    pieces = o_load.shape[0]
    height = o_mine.shape[0] // pieces

    def o_part(n):
        return pl.ds(n * height, height)

    def o_fetch(n):
        return pltpu.make_async_copy(o_ref.at[c, o_part(n), :], o_mine.at[o_part(n), :], o_load.at[n])

    def o_hand(n):
        return remote(
            o_ref.at[1 - c, o_part(n), :], o_sib.at[o_part(n), :],
            o_sib_send.at[n], o_sib_recv.at[n], e, z, 1 - c,
        )

    def o_line(n):
        step, side = jnp.where(z < e, 1, -1), jnp.where(z < e, 0, 1)
        return remote(
            o_mine.at[o_part(n), :], o_z.at[side, o_part(n), :],
            o_zsend.at[n], o_zrecv.at[side, n], e, z + step, c,
        )

    def o_wait(side, n):
        slab = o_z.at[side, o_part(n), :]
        remote(slab, slab, o_zsend.at[n], o_zrecv.at[side, n], e, z, c).wait_recv()
        add(o_mine.at[o_part(n), :], [slab])

    def o_peer(p, n):
        view = o_out.at[o_part(n), :]
        return remote(
            o_mine.at[o_part(n), :], view, o_send.at[p, n], o_recv.at[n], peers[p], z, c
        )

    def o_kept():
        return pltpu.make_async_copy(o_mine, o_out, o_own)

    for i in range(nz):
        for k in range(K):
            hand(k, i).start()
            fetch(k, i).start()
        if i == 0:
            for n in range(pieces):
                o_fetch(n).start()
                o_hand(n).start()

    def finish(k, i):
        fetch(k, i).wait()
        hand(k, i).wait_recv()
        zz = dest[i]
        add(part(k, 1, i), [part(k, 2, i)])
        if i < nz - 1:
            for side in range(2):
                going = zz > z if side == 0 else zz < z
                behind = z > 0 if side == 0 else z < nz - 1

                @pl.when(going & behind)
                def _():
                    zwait(k, side, zz)
                    add(part(k, 1, i), [part(k, 3, side, zz)])

            zcopy(k, i).start()
            return
        for side in range(2):

            @pl.when(z > 0 if side == 0 else z < nz - 1)
            def _():
                zwait(k, side, z)
                add(part(k, 1, i), [part(k, 3, side, z)])

        streams[k][0]()

    x_copy, x_kept, x_total = plane_sum_parts(x_ref, x_out, x_held, x_send, x_recv, x_own)
    for p in (2, 0, 1):
        x_copy(p).start()
    x_kept.start()

    def y_copy(p):
        return remote(
            y_ref.at[peers[p]], y_out.at[e], y_send.at[p], y_recv.at[p], peers[p], z, c
        )

    y_kept = pltpu.make_async_copy(y_ref.at[e], y_out.at[e], y_own)
    y_kept.start()
    for p in range(3):
        y_copy(p).start()

    def o_flow(n):
        o_fetch(n).wait()
        o_hand(n).wait_recv()
        add(o_mine.at[o_part(n), :], [o_sib.at[o_part(n), :]])
        for side in range(2):
            behind = (z > 0) & (z <= e) if side == 0 else (z < nz - 1) & (z >= e)

            @pl.when(behind)
            def _():
                o_wait(side, n)

        @pl.when(z != e)
        def _():
            o_line(n).start()

        @pl.when(z == e)
        def _():
            for p in range(3):
                o_peer(p, n).start()

    streams = [
        plane_stream(
            part(k, 1, nz - 1), lambda q, k=k: part(k, 4, q), *sems[3 * k : 3 * k + 3]
        )
        for k in range(K)
    ]
    turn = K * nz // 2
    order = []
    for k in range(K):
        order += [(k, i) for i in range(1 if k else 0, nz - 1)]
        if k + 1 < K:
            order.append((k + 1, 0))
        order.append((k, nz - 1))
    for n, (k, i) in enumerate(order):
        finish(k, i)
        if n == 0:
            for m in range(pieces):
                o_flow(m)
        if n == turn:
            x_total()

    @pl.when(z == e)
    def _():
        o_kept().start()
        o_kept().wait()
        for n in range(pieces):
            for p in range(3):
                o_peer(p, n).wait_send()

    @pl.when(z != e)
    def _():
        for n in range(pieces):
            view = o_out.at[o_part(n), :]
            remote(view, view, o_send.at[0, n], o_recv.at[n], e, z, c).wait_recv()
            o_line(n).wait_send()

    y_kept.wait()
    for p in range(3):
        x_copy(p).wait_send()
        view = y_out.at[peers[p]]
        remote(view, view, y_send.at[p], y_recv.at[p], e, z, c).wait_recv()
        y_copy(p).wait_send()
    for n in range(pieces):
        o_hand(n).wait_send()
    for i in range(nz):
        for k in range(K):
            hand(k, i).wait_send()
            if i < nz - 1:
                zcopy(k, i).wait_send()
    for _, end in streams:
        end()


def settle_weights(nz, grads, small, rows, near, blocks):
    R, W = grads.shape[2:]
    D = rows.shape[2]
    dma = pltpu.SemaphoreType.DMA
    sd = jax.ShapeDtypeStruct
    vm = pltpu.VMEM
    Ws = small.shape[3]
    return pl.pallas_call(
        functools.partial(settle_kernel, nz),
        out_shape=(
            sd((4, R, W), bf16),
            sd((4, R, Ws), bf16),
            sd((R, D), bf16),
            sd(near.shape[1:], f32),
            sd(blocks.shape, bf16),
        ),
        in_specs=[ANY] * 5,
        out_specs=(ANY,) * 3 + (pl.BlockSpec(memory_space=vm), ANY),
        scratch_shapes=[
            vm(near.shape, bf16), *plane_sems(), *plane_sems(),
            vm((nz, R, W), bf16), vm((nz, R, W), bf16), vm((2, nz, R, W), bf16),
            vm((nz, R, Ws), bf16), vm((nz, R, Ws), bf16), vm((2, nz, R, Ws), bf16),
            vm((R, D), bf16), vm((R, D), bf16), vm((2, R, D), bf16),
            dma((3, nz)), dma((3, nz)), dma((3, nz)), dma((3, nz)), dma((3, 2, nz)),
            dma((6,)), dma((6,)), dma((6,)), dma((6,)), dma((2, 6)),
            dma((3, 6)), dma((6,)), dma(()),
            *plane_sems(), *plane_sems(), *plane_sems(),
        ],
        compiler_params=pltpu.CompilerParams(
            collective_id=1, has_side_effects=True, vmem_limit_bytes=56 << 20
        ),
        cost_estimate=pl.CostEstimate(flops=10**6, bytes_accessed=10**6, transcendentals=0),
        name="settle_weights",
    )(grads, small, rows, near, blocks)


def pick_kernel(width, q_ref, k_ref, v_ref, o_ref):
    e = lax.axis_index("expert")
    spare = o_ref.shape[1] - 3 * width
    if spare:
        o_ref[:, 3 * width :] = jnp.zeros((o_ref.shape[0], spare), o_ref.dtype)
    for n in range(4):

        @pl.when(e == n)
        def _():
            for i, ref in enumerate((q_ref, k_ref, v_ref)):
                o_ref[:, i * width : (i + 1) * width] = ref[:, n * width : (n + 1) * width]


def pick_columns(weights, width):
    vm = pl.BlockSpec(memory_space=pltpu.VMEM)
    return pl.pallas_call(
        functools.partial(pick_kernel, width),
        in_specs=[vm] * 3,
        out_specs=vm,
        out_shape=jax.ShapeDtypeStruct((weights[0].shape[0], -(-3 * width // 128) * 128), bf16),
        name="pick_columns",
    )(*weights)


def assemble_kernel(width, x_ref, *o_refs):
    for n in range(4):
        for i in range(3):
            cols = x_ref[n, :, i * width : (i + 1) * width]
            o_refs[i][:, n * width : (n + 1) * width] = cols.astype(f32)


def assemble_columns(x, width):
    R = x.shape[1]
    block = 96 if R % 96 == 0 else 16
    return pl.pallas_call(
        functools.partial(assemble_kernel, width),
        grid=(R // block,),
        in_specs=[pl.BlockSpec((4, block, x.shape[2]), lambda i: (0, i, 0))],
        out_specs=(pl.BlockSpec((block, 4 * width), lambda i: (i, 0)),) * 3,
        out_shape=(jax.ShapeDtypeStruct((R, 4 * width), f32),) * 3,
        name="assemble_columns",
    )(x)


def sum_shard(x, axis=0):
    mine = lax.psum_scatter(x, SHARD, scatter_dimension=axis, tiled=True)
    return lax.psum(mine, "expert")


def fetch(nz, fast, weights, w_output, small, tokens, lengths, block, wide, F):
    D = tokens.shape[1]
    if fast:
        width = D // 4
        columns, full_small, rows, tokens, lengths, blocks, *packed = fetch_weights(
            nz, pick_columns(weights, width), small, w_output, tokens, lengths, block, wide, F
        )
        columns, rows = columns.reshape(D, -1), rows.reshape(width, D)
        return columns, rows, full_small.reshape(D, -1), tokens, lengths, blocks, packed
    full = [lax.all_gather(w, SHARD, axis=0, tiled=True) for w in weights + (w_output, small)]
    blocks = spread_plain(nz, (block,), 0)[0]
    packed = pack_columns(wide, 2 * nz, F, -(-F // 128) * 128)
    columns = jnp.concatenate(full[:3], axis=1)
    return columns, full[3], full[4], tokens[None], lengths[None], blocks, packed


def settle(nz, fast, columns, rows, small, near, blocks):
    D, width = rows.shape[1], rows.shape[0]
    if fast:
        R = D // (2 * nz)
        parts = [x.astype(bf16).reshape(nz, 2, R, -1) for x in (columns, small)]
        near = near.astype(bf16).reshape(4, -1, D)
        blocks = blocks.reshape(4, -1, D)
        sums, small, out, near, blocks = settle_weights(
            nz, *parts, rows.astype(bf16).reshape(2, R, D), near, blocks
        )
        small, blocks = jnp.sum(small.astype(f32), axis=0), blocks.reshape(-1, D)
        return *assemble_columns(sums, width), out.astype(f32), small, near, blocks
    parts = [columns[:, i * width : (i + 1) * width] for i in range(3)] + [rows, small]
    blocks = lax.all_to_all(blocks, "expert", split_axis=0, concat_axis=0, tiled=True)
    return [sum_shard(x) for x in parts] + [near, blocks]


def spread_plain(nz, blocks, collective):
    out = []
    for block in blocks:
        for axis in ("expert", "core", "z"):
            block = lax.all_gather(block, axis, axis=0)
        out.append(block)
    return out


def spread_pair(nz, blocks, gate, up, collective):
    gate = lax.all_to_all(gate, SHARD, split_axis=0, concat_axis=0, tiled=True)
    return jnp.concatenate([gate, up], axis=2), *spread_plain(nz, blocks, collective)


def collect_plain(nz, rows, notes, dots, T):
    n_exp, cap, D = rows.shape[2:]
    places = (lax.axis_index("expert") * cap + jnp.arange(cap)).astype(f32)
    notes = notes[..., :T]
    pick = (notes[..., 2, None, :] == places[:, None]) | (notes[..., 3, None, :] == places[:, None])
    part = jnp.einsum(
        "zceps,zcepd->zcesd", pick.astype(bf16), rows, preferred_element_type=f32
    ).astype(bf16)
    part = part.transpose(2, 0, 1, 3, 4).reshape(n_exp * nz * 2 * T, D)
    part = lax.psum_scatter(part, "expert", scatter_dimension=0, tiled=True)
    part = lax.psum_scatter(part, SHARD, scatter_dimension=0, tiled=True).astype(f32)
    z, core, e = lax.axis_index("z"), lax.axis_index("core"), lax.axis_index("expert")
    return part, lax.psum(dots, ("expert",) + SHARD)[z, core, e]


def rope_tables(positions, head_width):
    half_width = head_width // 2
    exponents = jnp.arange(half_width).astype(f32) * 2.0 / head_width
    frequency = rope_base ** (-exponents)
    angles = positions.astype(f32)[..., None] * frequency
    return (jnp.cos(angles), jnp.sin(angles))


def rotate(values, cosine, sine_table):
    half_width = values.shape[-1] // 2
    leading = values[..., :half_width]
    trailing = values[..., half_width:]
    cos_rows = cosine[:, :, None, :]
    sin_rows = sine_table[:, :, None, :]
    return jnp.concatenate(
        [leading * cos_rows - trailing * sin_rows, trailing * cos_rows + leading * sin_rows],
        axis=-1,
    )


def rms_forward(values, norm_gain):
    inverse = lax.rsqrt(jnp.mean(values * values, axis=-1, keepdims=True) + eps_norm)
    return (values * inverse * norm_gain, inverse)


def rms_backward(values, inverse, norm_gain, upstream):
    weighted = upstream * norm_gain
    gain_grad = jnp.sum(upstream * values * inverse, axis=0)
    inner_mean = jnp.mean(weighted * values, axis=-1, keepdims=True)
    return (inverse * weighted - values * inverse * inverse * inverse * inner_mean, gain_grad)


def dot32(a, b):
    return jnp.dot(a, b, preferred_element_type=f32)


def dot_dims(a, b, da, db):
    return lax.dot_general(a, b, (((da,), (db,)), ((), ())), preferred_element_type=f32)


def ein32(spec, a, b):
    return jnp.einsum(spec, a, b, preferred_element_type=f32)


def on_device(
    tokens,
    seq_lengths,
    routes,
    norm_attn,
    w_query,
    w_key,
    w_value,
    w_output,
    norm_ffn,
    w_router,
    w_in,
    w_down,
    cotangent,
):
    T, D = tokens.shape
    R = w_query.shape[0]
    head_width = D // HEADS
    n_exp = lax.axis_size("expert")
    nz = lax.axis_size("z")
    n_shard = nz * lax.axis_size("core")
    experts = w_router.shape[1]
    F = w_down.shape[0]
    FF = F * n_shard
    capacity = 10 * T // (4 * experts)
    slots = experts * capacity
    highest = lax.Precision.HIGHEST
    e_index = lax.axis_index("expert")
    fast = n_exp == 4 and nz == 4

    small = jnp.concatenate([w_router, norm_attn[:, None], norm_ffn[:, None]], axis=1)
    small = jnp.pad(small, ((0, 0), (0, 128 - small.shape[1])))
    length_rows = jnp.broadcast_to(seq_lengths[:, :1], (8, 128))
    full_qkv, full_output, full_small, near_tokens, near_lengths, all_cotangent, packed = fetch(
        nz,
        fast,
        (w_query, w_key, w_value),
        w_output,
        small,
        tokens,
        length_rows,
        cotangent,
        w_in.reshape(R, 2 * FF),
        F,
    )
    full_router = full_small[:, :experts]
    gain_attn = full_small[:, experts].astype(f32)
    gain_ffn = full_small[:, experts + 1].astype(f32)

    Fp = -(-F // 128) * 128
    moved_up = lax.all_to_all(packed[1], SHARD, split_axis=0, concat_axis=0, tiled=True)
    down = jnp.pad(w_down.reshape(F, D), ((0, Fp - F), (0, 0)))

    B, H = near_tokens.shape[0], full_output.shape[0]
    heads = H // head_width
    residual_in = tokens.astype(f32)
    inverse_in = rms_forward(residual_in, gain_attn)[1]
    near_in = near_tokens.reshape(B * T, D).astype(f32)
    near_normed, near_inverse = rms_forward(near_in, gain_attn)
    normed_half = near_normed.astype(bf16)
    lengths = near_lengths[:, 0, 0]
    row_index = jnp.arange(T)
    segment = (row_index[None, :] >= lengths[:, None]).astype(jnp.int32)
    positions = row_index[None, :] - lengths[:, None] * segment
    allowed = (segment[:, :, None] == segment[:, None, :]) & (
        row_index[None, None, :] <= row_index[None, :, None]
    )
    cosine, sine_table = rope_tables(positions, head_width)
    head_shape = (B, T, heads, head_width)
    qkv = dot32(normed_half, full_qkv)
    queries = rotate(qkv[:, :H].reshape(head_shape), cosine, sine_table).astype(bf16)
    keys_rot = rotate(qkv[:, H : 2 * H].reshape(head_shape), cosine, sine_table).astype(bf16)
    values = qkv[:, 2 * H : 3 * H].astype(bf16).reshape(head_shape)
    score_scale = 1.0 / math.sqrt(head_width)
    scores = ein32("bqhd,bkhd->bhqk", queries, keys_rot) * score_scale
    scores = jnp.where(allowed[:, None], scores, masked_score)
    row_peak = jnp.max(scores, axis=-1, keepdims=True)
    log_total = row_peak + jnp.log(jnp.sum(jnp.exp(scores - row_peak), axis=-1, keepdims=True))
    attn_probs = jnp.exp(scores - log_total)
    probs_half = attn_probs.astype(bf16)
    context = ein32("bhqk,bkhd->bqhd", probs_half, values).astype(bf16)
    context_flat = context.reshape(B * T, H)

    def at_home(partial_rows, collective):
        if not fast:
            return partial_rows
        return plane_sum(partial_rows.astype(bf16).reshape(B, T, D), collective)

    residual_mid = residual_in + branch_scale * at_home(dot32(context_flat, full_output), 4)
    normed_mid, inverse_mid = rms_forward(residual_mid, gain_ffn)
    normed_mid_half = normed_mid.astype(bf16)

    logits = dot32(normed_mid_half, full_router)
    expert_ids = jnp.arange(experts)
    route_mask = (routes[:, :, None] == expert_ids[None, None, :]).astype(f32)
    chosen = jnp.sum(logits[:, None, :] * route_mask, axis=-1)
    gate_probs = jax.nn.softmax(chosen, axis=-1)
    flat_routes = routes.reshape(2 * T)
    hits = (flat_routes[:, None] == expert_ids[None, :]).astype(bf16)
    order = jnp.arange(2 * T)
    before = (order[:, None] > order[None, :]).astype(bf16)
    earlier = dot32(before, hits)
    slot_index = jnp.sum(earlier * hits.astype(f32), axis=1).astype(jnp.int32)
    target = (flat_routes * capacity + slot_index).reshape(T, 2)
    slot_ids = jnp.arange(slots)
    pick = [(target[:, k][:, None] == slot_ids[None, :]).astype(bf16) for k in range(2)]

    notes = jnp.concatenate([gate_probs, target.astype(f32), jnp.zeros((T, 4), f32)], axis=1)
    notes = jnp.pad(jnp.transpose(notes), ((0, 0), (0, -T % 128)))
    spread = spread_blocks if fast else spread_pair
    w_pair, all_normed, all_notes = spread(nz, (normed_mid_half, notes), packed[0], moved_up, 2)
    w_pair = w_pair.reshape(n_shard * R, 2 * Fp)
    devices = n_shard * n_exp
    flat_notes = all_notes.reshape(devices, 8, -1)[:, :, :T]
    wanted = (e_index * capacity + jnp.arange(capacity)).astype(f32)
    found = [flat_notes[:, 2 + k, None, :] == wanted[None, :, None] for k in range(2)]
    gate_rows = jnp.sum(
        jnp.where(found[0], flat_notes[:, 0, None, :], 0.0)
        + jnp.where(found[1], flat_notes[:, 1, None, :], 0.0),
        axis=-1,
    ).reshape(devices * capacity, 1)
    chosen_rows = (found[0] | found[1]).astype(bf16)

    def take(blocks):
        rows = ein32("spt,std->spd", chosen_rows, blocks.reshape(devices, T, D))
        return rows.astype(bf16).reshape(devices * capacity, D)

    arrived = take(all_normed)
    cotangent_rows = take(all_cotangent)
    grad_scale = gate_rows * branch_scale
    pre = dot32(arrived, w_pair)
    gate_part, up_part = pre[:, :Fp], pre[:, Fp:]
    sigmoid_gate = jax.nn.sigmoid(gate_part)
    silu_gate = gate_part * sigmoid_gate
    activated = lax.optimization_barrier((silu_gate * up_part).astype(bf16))
    out_sum = lax.psum_scatter(
        dot32(activated, down).astype(bf16), SHARD, scatter_dimension=0, tiled=True
    )

    raw_grad = dot_dims(cotangent_rows, down, 1, 1)
    row_dots = branch_scale * jnp.sum(raw_grad * activated.astype(f32), axis=1)
    row_dots = row_dots.reshape(devices, capacity, 1)
    token_dots = [jnp.sum(jnp.where(found[k], row_dots, 0.0), axis=1) for k in range(2)]
    token_dots = jnp.stack(token_dots, axis=1).reshape(nz, 2, n_exp, 2, T)
    token_dots = jnp.pad(token_dots, ((0, 0),) * 3 + ((0, 6), (0, -T % 128)))
    act_grad = grad_scale * raw_grad
    gate_grads = act_grad * up_part * sigmoid_gate * (1.0 + gate_part * (1.0 - sigmoid_gate))
    gate_grads, up_grads = gate_grads.astype(bf16), (act_grad * silu_gate).astype(bf16)
    pre_grad = jnp.concatenate([gate_grads, up_grads], axis=1)
    in_rows = dot_dims(pre_grad, w_pair, 1, 1).astype(bf16)
    scaled = (grad_scale * activated.astype(f32)).astype(bf16)
    grad_w_down = lined_up(dot_dims(scaled[:, :F], cotangent_rows, 0, 0))
    gate_term, up_term = [
        dot_dims(arrived, x, 0, 0).astype(bf16).reshape(n_shard, R, Fp)
        for x in (gate_grads, up_grads)
    ]
    gate_term, up_term = lax.optimization_barrier((gate_term, up_term))
    up_term = lax.all_to_all(up_term, SHARD, split_axis=0, concat_axis=0, tiled=True)
    in_rows = in_rows.reshape(nz, 2, n_exp, capacity, D)
    collect = collect_rows if fast else collect_plain
    normed_mid_grad, gate_grad = collect(nz, in_rows, all_notes, token_dots, T)
    gate_grad = jnp.transpose(gate_grad[:2, :T])
    up_term, normed_mid_grad, out_sum, gate_term = lax.optimization_barrier(
        (up_term, normed_mid_grad, out_sum, gate_term)
    )
    gate_term = lax.all_to_all(gate_term, SHARD, split_axis=0, concat_axis=0, tiled=True)

    upstream = cotangent.astype(f32)
    chosen_grad = gate_probs * (gate_grad - jnp.sum(gate_probs * gate_grad, axis=-1, keepdims=True))
    logit_grad = jnp.sum(chosen_grad[:, :, None] * route_mask, axis=1)
    normed_mid_grad = normed_mid_grad + jnp.dot(
        logit_grad, jnp.transpose(full_router.astype(f32)), precision=highest
    )
    router_grad = jnp.dot(
        jnp.transpose(normed_mid_half.astype(f32)), logit_grad, precision=highest
    )
    mid_norm_grad, gain_ffn_grad = rms_backward(
        residual_mid, inverse_mid, gain_ffn, normed_mid_grad
    )
    residual_grad = upstream + mid_norm_grad
    branch_grad = (branch_scale * residual_grad).astype(bf16)

    if fast:
        branch_grad = plane_gather(branch_grad, 5).reshape(B * T, D)
    output_grad = dot_dims(context_flat, branch_grad, 0, 0)
    context_grad = dot_dims(branch_grad, full_output, 1, 1).reshape(head_shape)
    row_delta = jnp.sum(context_grad * context.astype(f32), axis=-1)
    context_grad_half = context_grad.astype(bf16)
    probs_grad = ein32("bqhd,bkhd->bhqk", context_grad_half, values)
    scores_grad = (
        attn_probs * (probs_grad - jnp.transpose(row_delta, (0, 2, 1))[..., None]) * score_scale
    ).astype(bf16)
    queries_grad = ein32("bhqk,bkhd->bqhd", scores_grad, keys_rot)
    keys_grad = ein32("bhqk,bqhd->bkhd", scores_grad, queries)
    values_grad = ein32("bhqk,bqhd->bkhd", probs_half, context_grad_half)
    qkv_grad = jnp.concatenate(
        [
            rotate(queries_grad, cosine, -sine_table).reshape(B * T, H).astype(bf16),
            rotate(keys_grad, cosine, -sine_table).reshape(B * T, H).astype(bf16),
            values_grad.reshape(B * T, H).astype(bf16),
            jnp.zeros((B * T, full_qkv.shape[1] - 3 * H), bf16),
        ],
        axis=1,
    )
    qkv_weight_grad = dot_dims(normed_half, qkv_grad, 0, 0)
    near_grad = dot_dims(qkv_grad, full_qkv, 1, 1)
    gain_attn_grad = jnp.sum(near_grad * near_in * near_inverse, axis=0)

    small_grad = jnp.concatenate(
        [router_grad, gain_attn_grad[:, None], gain_ffn_grad[:, None]], axis=1
    )
    small_grad = jnp.pad(small_grad, ((0, 0), (0, 128 - small_grad.shape[1])))
    small_grad, gate_term = lax.optimization_barrier((small_grad, gate_term))
    sum_query, sum_key, sum_value, sum_output, small_sum, normed_in_grad, back = settle(
        nz, fast, qkv_weight_grad, output_grad, small_grad, near_grad, out_sum
    )
    grad_w_in = unpack_columns(gate_term, up_term, F)
    mixture = gate_probs[:, 0:1] * dot32(pick[0], back) + gate_probs[:, 1:2] * dot32(pick[1], back)
    activations = (residual_mid + branch_scale * mixture).astype(bf16)
    in_norm_grad = rms_backward(residual_in, inverse_in, gain_attn, normed_in_grad)[0]
    grad_tokens = residual_grad + in_norm_grad
    return (
        activations,
        grad_tokens,
        small_sum[:, experts],
        sum_query,
        sum_key,
        sum_value,
        sum_output,
        small_sum[:, experts + 1],
        small_sum[:, :experts],
        grad_w_in,
        grad_w_down,
    )


def solution(mesh):
    n_expert, n_shard = mesh.devices.shape
    chips = Mesh(mesh.devices.reshape(n_expert, n_shard // 2, 2), ("expert", "z", "core"))
    rows = P(("expert", "z", "core"), None)
    shard = P(SHARD)
    shard2 = P(SHARD, None)
    shard3 = P(SHARD, "expert", None)
    in_specs = (
        rows,
        rows,
        rows,
        shard,
        shard2,
        shard2,
        shard2,
        shard2,
        shard,
        shard2,
        shard3,
        shard3,
        rows,
    )
    out_specs = (
        rows,
        rows,
        shard,
        shard2,
        shard2,
        shard2,
        shard2,
        shard,
        shard2,
        shard3,
        shard3,
    )
    return jax.shard_map(
        on_device, mesh=chips, in_specs=in_specs, out_specs=out_specs, check_vma=False
    )
```

```python
import functools
import math

import jax
import jax.numpy as jnp
from jax import lax
from jax.experimental import pallas as pl
from jax.experimental.pallas import tpu as pltpu
from jax.sharding import Mesh, PartitionSpec as P

HEADS = 36

eps_norm = 1e-05
branch_scale = 1.4 / math.sqrt(40.0)
rope_base = 10000.0
masked_score = -1e30
bf16 = jnp.bfloat16
f32 = jnp.float32
SHARD = ("z", "core")
ANY = pl.BlockSpec(memory_space=pl.ANY)


def place():
    e, z, c = lax.axis_index("expert"), lax.axis_index("z"), lax.axis_index("core")
    across_x = e + 1 - 2 * (e % 2)
    across_y = (e + 2) % 4
    return e, z, c, across_x, across_y


def remote(src, dst, send, recv, e, z, c):
    return pltpu.make_async_remote_copy(
        src_ref=src,
        dst_ref=dst,
        send_sem=send,
        recv_sem=recv,
        device_id=(e, z, c),
        device_id_type=pl.DeviceIdType.MESH,
    )


def payload_stream(nz, ref, out, sems, split):
    zrecv, zsend, near_recv, near_send, far_recv, far_send, sib_recv, sib_send, own = sems
    e, z, c, ex, ey = place()
    diagonal = (ex + 2) % 4
    T = ref.shape[0]
    S = 2 * nz - 1

    def split_step(s):
        return (s - 1) % 2, (s - 1) // 2

    def where(s):
        if s == 0:
            return z
        side, i = split_step(s)
        return z - 1 - i if side == 0 else z + 1 + i

    def exists(s):
        if s == 0:
            return z >= 0
        zz = where(s)
        return (zz >= 0) & (zz < nz)

    def slab(s, quarter, r0=0, n=T):
        return out.at[where(s), c, quarter, pl.ds(r0, n), :]

    def first(step):
        side = 0 if step > 0 else 1
        return remote(ref, slab(0, e), zsend.at[side, nz - 1], zrecv.at[side, 0], e, z + step, c)

    def onward(s):
        side, i = split_step(s)
        step = 1 if side == 0 else -1
        return remote(
            slab(s, e), slab(s, e), zsend.at[side, i], zrecv.at[side, i + 1], e, z + step, c
        )

    def near(s, axis):
        source = ref if s == 0 else slab(s, e)
        return remote(
            source, slab(s, e), near_send.at[s, axis], near_recv.at[s, axis],
            ex if axis == 0 else ey, z, c,
        )

    def near_wait(s, axis):
        view = slab(s, ex if axis == 0 else ey)
        remote(view, view, near_send.at[s, axis], near_recv.at[s, axis], ex, z, c).wait_recv()

    axes = range(2) if split else range(1)

    def far_view(s, quarter, axis):
        if not split:
            return slab(s, quarter)
        return slab(s, quarter, 0, split) if axis == 0 else slab(s, quarter, split, T - split)

    def far(s, axis):
        view = far_view(s, ex if axis == 0 else ey, axis)
        return remote(
            view, view, far_send.at[s, axis], far_recv.at[s, axis],
            ey if axis == 0 else ex, z, c,
        )

    def far_wait(s, axis):
        view = far_view(s, diagonal, axis)
        remote(view, view, far_send.at[s, axis], far_recv.at[s, axis], ex, z, c).wait_recv()

    def beside(s, n):
        quarter = (e, ex, ey, diagonal)[n]
        source = ref if s == 0 and n == 0 else slab(s, quarter)
        return remote(
            source, slab(s, quarter), sib_send.at[s, n], sib_recv.at[s, n], e, z, 1 - c
        )

    def beside_wait(s, n):
        view = out.at[where(s), 1 - c, (e, ex, ey, diagonal)[n]]
        remote(view, view, sib_send.at[s, n], sib_recv.at[s, n], e, z, c).wait_recv()

    def inside(side):
        return z < nz - 1 if side == 0 else z > 0

    def begin():
        for step in (1, -1):

            @pl.when((z + step >= 0) & (z + step < nz))
            def _():
                first(step).start()

        near(0, 0).start()
        near(0, 1).start()
        beside(0, 0).start()
        pltpu.make_async_copy(ref, slab(0, e), own).start()

    def arrive(s):
        if s == 0:
            return

        @pl.when(exists(s))
        def _():
            side, i = split_step(s)
            remote(
                slab(s, e), slab(s, e), zsend.at[side, i], zrecv.at[side, i], e, z, c
            ).wait_recv()
            if i < nz - 2:

                @pl.when(inside(side))
                def _():
                    onward(s).start()

            near(s, 0).start()
            near(s, 1).start()
            beside(s, 0).start()

    def relay(s):
        @pl.when(exists(s))
        def _():
            near_wait(s, 0)
            far(s, 0).start()
            beside(s, 1).start()
            near_wait(s, 1)
            if split:
                far(s, 1).start()
            beside(s, 2).start()

    def close(s):
        @pl.when(exists(s))
        def _():
            for axis in axes:
                far_wait(s, axis)
            beside(s, 3).start()

    def end(s):
        @pl.when(exists(s))
        def _():
            for axis in range(2):
                near(s, axis).wait_send()
            for axis in axes:
                far(s, axis).wait_send()
            for n in range(4):
                beside(s, n).wait_send()
                beside_wait(s, n)
            if s > 0 and split_step(s)[1] < nz - 2:

                @pl.when(inside(split_step(s)[0]))
                def _():
                    onward(s).wait_send()

        if s == 0:
            for step in (1, -1):

                @pl.when((z + step >= 0) & (z + step < nz))
                def _():
                    first(step).wait_send()

            pltpu.make_async_copy(ref, slab(0, e), own).wait()

    return begin, arrive, relay, close, end


def payload_sems(nz):
    dma = pltpu.SemaphoreType.DMA
    S = 2 * nz - 1
    return [
        dma((2, nz)), dma((2, nz)), dma((S, 2)), dma((S, 2)), dma((S, 2)), dma((S, 2)),
        dma((S, 4)), dma((S, 4)), dma(()),
    ]


def spread_kernel(nz, splits, *refs):
    n = len(splits)
    (gate_ref, up_ref), refs = refs[:2], refs[2:]
    ins, refs = refs[:n], refs[n:]
    pair, outs, sems = refs[0], refs[1 : n + 1], refs[n + 1 :]
    v_sems, beside_sem, sems = sems[:3], sems[3], sems[4:]
    width = gate_ref.shape[2]
    greet_shard(nz)
    streams = [
        payload_stream(nz, ins[i], outs[i], sems[9 * i : 9 * i + 9], splits[i]) for i in range(n)
    ]
    v_begin, v_end = scatter_stream(
        nz, gate_ref, lambda i: pair.at[i, :, pl.ds(0, width)], *v_sems
    )
    beside = pltpu.make_async_copy(up_ref, pair.at[:, :, pl.ds(width, width)], beside_sem)
    for t in streams:
        t[0]()
    beside.start()
    S = 2 * nz - 1
    for s in range(1, S):
        for t in streams:
            t[1](s)
    v_begin()
    for s in range(S):
        for t in streams:
            t[2](s)
        if s >= 1:
            for t in streams:
                t[3](s - 1)
    for t in streams:
        t[3](S - 1)
    for s in range(S):
        for t in streams:
            t[4](s)
    beside.wait()
    v_end()


def spread_blocks(nz, blocks, gate, up, collective):
    sd = jax.ShapeDtypeStruct
    splits = tuple(b.shape[0] // 2 if b.shape[0] % 32 == 0 else 0 for b in blocks)
    pair = sd(gate.shape[:2] + (2 * gate.shape[2],), gate.dtype)
    return pl.pallas_call(
        functools.partial(spread_kernel, nz, splits),
        out_shape=(pair,) + tuple(sd((nz, 2, 4) + b.shape, b.dtype) for b in blocks),
        in_specs=[ANY] * (len(blocks) + 2),
        out_specs=(ANY,) * (len(blocks) + 1),
        scratch_shapes=[
            *scatter_sems(nz), pltpu.SemaphoreType.DMA(()),
            *[s for _ in blocks for s in payload_sems(nz)],
        ],
        compiler_params=pltpu.CompilerParams(collective_id=collective, has_side_effects=True),
        cost_estimate=pl.CostEstimate(flops=10**6, bytes_accessed=10**6, transcendentals=0),
        name="spread_blocks",
    )(gate, up, *blocks)


def line_order(nz, z):
    def order(i):
        code = 0
        for zz in range(nz):
            far_first = sorted(range(nz), key=lambda t: (-abs(t - zz), t))
            code += far_first[i] * nz**zz
        power = 1
        for zz in range(nz):
            power = power + (nz**zz - 1) * jnp.where(z == zz, 1, 0)
        return (code // power) % nz

    return [order(i) for i in range(nz)]


def collect_kernel(
    nz, cap,
    rows_ref, notes_ref, dots_ref,
    out_ref, dots_out,
    dots, notes, mine, theirs, block, from_x, from_y, via_x, via_y, from_z,
    note_sem, load, sib_send, sib_recv, via_send, via_recv, plain_send, plain_recv,
    sum_send, sum_recv, zsend, zrecv, dot_send, dot_recv, dot_own,
):
    e, z, c, ex, ey = place()
    diagonal = (ex + 2) % 4
    T, D = out_ref.shape
    h = T // 2
    dest = line_order(nz, z)
    who = (diagonal, ex, ey, e)

    def others():
        for d in range(1, 8 * nz):
            to = ((e * nz + z) * 2 + c + d) % (8 * nz)
            yield d, to // (2 * nz), to // 2 % nz, to % 2

    barrier = pltpu.get_barrier_semaphore()
    for _, te, tz, tc in others():
        pl.semaphore_signal(
            barrier, inc=1, device_id=(te, tz, tc), device_id_type=pl.DeviceIdType.MESH
        )
    pl.semaphore_wait(barrier, 8 * nz - 1)

    def dot(d, te, tz, tc):
        return remote(
            dots_ref.at[tz, tc, te], dots.at[d], dot_send.at[d], dot_recv.at[d], te, tz, tc
        )

    dot_kept = pltpu.make_async_copy(dots_ref.at[z, c, e], dots.at[0], dot_own)
    dot_kept.start()
    for d, te, tz, tc in others():
        dot(d, te, tz, tc).start()

    note_copy = pltpu.make_async_copy(notes_ref, notes, note_sem)
    note_copy.start()

    def fetch(i, q):
        return pltpu.make_async_copy(
            rows_ref.at[dest[i], c, who[q]], mine.at[i, q], load.at[i, q]
        )

    def hand(i, q):
        return remote(
            rows_ref.at[dest[i], 1 - c, who[q]], theirs.at[i, q],
            sib_send.at[i, q], sib_recv.at[i, q], e, z, 1 - c,
        )

    for i in range(nz):
        for q in range(4):
            hand(i, q).start()
            fetch(i, q).start()
    note_copy.wait()

    def open_out(i, q):
        fetch(i, q).wait()
        hand(i, q).wait_recv()
        places = (lax.broadcasted_iota(jnp.int32, (cap, T), 0) + e * cap).astype(f32)
        note = notes[dest[i], c, who[q]]
        pick = ((note[2:3, :] == places) | (note[3:4, :] == places)).astype(bf16)
        wide = 768 if D % 768 == 0 else 128

        @pl.loop(0, D // wide)
        def _(b):
            cols = pl.ds(pl.multiple_of(b * wide, 128), wide)
            both = mine[i, q, :, cols].astype(f32) + theirs[i, q, :, cols].astype(f32)
            block[i, q, :, cols] = lax.dot_general(
                pick, both.astype(bf16), (((0,), (0,)), ((), ())), preferred_element_type=f32
            ).astype(bf16)

    def via(i, axis):
        if axis == 0:
            return remote(
                block.at[i, 0, pl.ds(0, h), :], via_x.at[i],
                via_send.at[i, 0], via_recv.at[i, 0], ex, z, c,
            )
        return remote(
            block.at[i, 0, pl.ds(h, h), :], via_y.at[i],
            via_send.at[i, 1], via_recv.at[i, 1], ey, z, c,
        )

    def plain(i, axis):
        if axis == 0:
            return remote(
                block.at[i, 1, pl.ds(0, h), :], from_x.at[i, pl.ds(0, h), :],
                plain_send.at[i, 0], plain_recv.at[i, 0], ex, z, c,
            )
        return remote(
            block.at[i, 2, pl.ds(h, h), :], from_y.at[i, pl.ds(h, h), :],
            plain_send.at[i, 1], plain_recv.at[i, 1], ey, z, c,
        )

    def summed(i, axis):
        if axis == 0:
            return remote(
                block.at[i, 1, pl.ds(h, h), :], from_x.at[i, pl.ds(h, h), :],
                sum_send.at[i, 0], sum_recv.at[i, 0], ex, z, c,
            )
        return remote(
            block.at[i, 2, pl.ds(0, h), :], from_y.at[i, pl.ds(0, h), :],
            sum_send.at[i, 1], sum_recv.at[i, 1], ey, z, c,
        )

    def add(target, others, n):
        @pl.loop(0, n // 16)
        def _(b):
            rows = pl.ds(pl.multiple_of(b * 16, 16), 16)
            acc = target[rows, :].astype(f32)
            for o in others:
                acc = acc + o[rows, :].astype(f32)
            target[rows, :] = acc.astype(target.dtype)

    def start(i):
        open_out(i, 0)
        via(i, 0).start()
        via(i, 1).start()
        open_out(i, 1)
        plain(i, 0).start()
        open_out(i, 2)
        plain(i, 1).start()
        open_out(i, 3)

    def combine(i):
        via(i, 0).wait_recv()
        add(block.at[i, 2, pl.ds(0, h), :], [via_x.at[i]], h)
        summed(i, 1).start()
        via(i, 1).wait_recv()
        add(block.at[i, 1, pl.ds(h, h), :], [via_y.at[i]], h)
        summed(i, 0).start()

    def zcopy(i):
        step = jnp.where(dest[i] > z, 1, -1)
        side = jnp.where(dest[i] > z, 0, 1)
        return remote(
            block.at[i, 3], from_z.at[side, dest[i]],
            zsend.at[i], zrecv.at[side, dest[i]], e, z + step, c,
        )

    def zwait(side, zz):
        slab = from_z.at[side, zz]
        remote(slab, slab, zsend.at[0], zrecv.at[side, zz], e, z, c).wait_recv()

    def finish(i):
        for axis in range(2):
            plain(i, axis).wait_recv()
            summed(i, axis).wait_recv()
        zz = dest[i]
        if i < nz - 1:
            add(block.at[i, 3], [from_x.at[i], from_y.at[i]], T)
            for side in range(2):
                going = zz > z if side == 0 else zz < z
                behind = z > 0 if side == 0 else z < nz - 1

                @pl.when(going & behind)
                def _():
                    zwait(side, zz)
                    add(block.at[i, 3], [from_z.at[side, zz]], T)

            zcopy(i).start()
            return

        @pl.loop(0, T // 16)
        def _(b):
            rows = pl.ds(pl.multiple_of(b * 16, 16), 16)
            acc = block[i, 3, rows, :].astype(f32) + from_x[i, rows, :].astype(f32)
            out_ref[rows, :] = acc + from_y[i, rows, :].astype(f32)

        for side in range(2):

            @pl.when(z > 0 if side == 0 else z < nz - 1)
            def _():
                zwait(side, z)
                add(out_ref, [from_z.at[side, z]], T)

    for i in range(nz):
        start(i)
        if i >= 1:
            combine(i - 1)
        if i >= 2:
            finish(i - 2)
    combine(nz - 1)
    if nz >= 2:
        finish(nz - 2)
    finish(nz - 1)

    dot_kept.wait()
    for d, te, tz, tc in others():
        dot(d, te, tz, tc).wait_recv()
        dot(d, te, tz, tc).wait_send()
    dots_out[...] = jnp.sum(dots[...], axis=0)

    for i in range(nz):
        for q in range(4):
            hand(i, q).wait_send()
        for axis in range(2):
            via(i, axis).wait_send()
            plain(i, axis).wait_send()
            summed(i, axis).wait_send()
        if i < nz - 1:
            zcopy(i).wait_send()


def collect_rows(nz, rows, notes, dots, T):
    cap, D = rows.shape[3:]
    dma = pltpu.SemaphoreType.DMA
    vm = pltpu.VMEM
    return pl.pallas_call(
        functools.partial(collect_kernel, nz, cap),
        out_shape=(
            jax.ShapeDtypeStruct((T, D), f32),
            jax.ShapeDtypeStruct(dots.shape[3:], f32),
        ),
        in_specs=[ANY] * 3,
        out_specs=(pl.BlockSpec(memory_space=pltpu.VMEM),) * 2,
        scratch_shapes=[
            vm((8 * nz,) + dots.shape[3:], f32),
            vm(notes.shape, f32),
            vm((nz, 4, cap, D), bf16),
            vm((nz, 4, cap, D), bf16),
            vm((nz, 4, T, D), bf16),
            vm((nz, T, D), bf16),
            vm((nz, T, D), bf16),
            vm((nz, T // 2, D), bf16),
            vm((nz, T // 2, D), bf16),
            vm((2, nz, T, D), bf16),
            dma(()),
            dma((nz, 4)),
            dma((nz, 4)),
            dma((nz, 4)),
            dma((nz, 2)),
            dma((nz, 2)),
            dma((nz, 2)),
            dma((nz, 2)),
            dma((nz, 2)),
            dma((nz, 2)),
            dma((nz,)),
            dma((2, nz)),
            dma((8 * nz,)),
            dma((8 * nz,)),
            dma(()),
        ],
        compiler_params=pltpu.CompilerParams(
            collective_id=3, has_side_effects=True, vmem_limit_bytes=56 << 20
        ),
        cost_estimate=pl.CostEstimate(
            flops=10**6, bytes_accessed=10**6, transcendentals=0
        ),
        name="collect_rows",
    )(rows, notes, dots)


def pack_rows(n, F, Fp, x_ref, *o_refs):
    half = n * F
    rows = x_ref.shape[0]
    for i in range(n):
        for part in range(2):
            cols = x_ref[:, part * half + i * F : part * half + (i + 1) * F]
            if Fp > F:
                cols = jnp.concatenate([cols, jnp.zeros((rows, Fp - F), cols.dtype)], axis=1)
            o_refs[part][i] = cols


def pack_columns(w, n, F, Fp):
    rows = w.shape[0]
    block = 16
    return pl.pallas_call(
        functools.partial(pack_rows, n, F, Fp),
        grid=(rows // block,),
        in_specs=[pl.BlockSpec((block, w.shape[1]), lambda i: (i, 0))],
        out_specs=(pl.BlockSpec((n, block, Fp), lambda i: (0, i, 0)),) * 2,
        out_shape=(jax.ShapeDtypeStruct((n, rows, Fp), w.dtype),) * 2,
        name="pack_columns",
    )(w)


def unpack_kernel(n, F, gate_ref, up_ref, o_ref, line):
    half = n * F
    rows = line.shape[0]
    for i in range(n):
        for part in range(2):
            cols = (up_ref if part else gate_ref)[i, :, :F].astype(f32)
            line[:, part * half + i * F : part * half + (i + 1) * F] = cols
    tiles = 2 * half // 128
    for j in range(tiles):
        o_ref[pl.ds(j, rows, stride=tiles), :] = line[:, j * 128 : (j + 1) * 128]


def unpack_columns(gate, up, F):
    n, rows, Fp = gate.shape
    block = 96 if rows % 96 == 0 else 16
    width = 2 * n * F
    tiles = width // 128
    flat = pl.pallas_call(
        functools.partial(unpack_kernel, n, F),
        grid=(rows // block,),
        in_specs=[pl.BlockSpec((n, block, Fp), lambda i: (0, i, 0))] * 2,
        out_specs=pl.BlockSpec((block * tiles, 128), lambda i: (i, 0)),
        out_shape=jax.ShapeDtypeStruct((rows * tiles, 128), f32),
        scratch_shapes=[pltpu.VMEM((block, width), f32)],
        name="unpack_columns",
    )(gate, up)
    return flat.reshape(rows, 1, width)


def line_kernel(x_ref, o_ref):
    rows, width = x_ref.shape
    tiles = width // 128
    for j in range(tiles):
        o_ref[pl.ds(j, rows, stride=tiles), :] = x_ref[:, j * 128 : (j + 1) * 128]


def lined_up(x, rows):
    width = x.shape[1]
    tiles = width // 128
    block = 240 if rows % 240 == 0 else 8
    flat = pl.pallas_call(
        line_kernel,
        grid=(rows // block,),
        in_specs=[pl.BlockSpec((block, width), lambda i: (i, 0))],
        out_specs=pl.BlockSpec((block * tiles, 128), lambda i: (i, 0)),
        out_shape=jax.ShapeDtypeStruct((rows * tiles, 128), x.dtype),
        name="lined_up",
    )(x)
    return flat.reshape(rows, 1, width)


def greet_cross(nz):
    e, z, c, ex, ey = place()
    barrier = pltpu.get_barrier_semaphore()

    def hail(te, tz, tc):
        pl.semaphore_signal(
            barrier, inc=1, device_id=(te, tz, tc), device_id_type=pl.DeviceIdType.MESH
        )

    hail(e, z, 1 - c)
    for te in (ex, ey, (ex + 2) % 4):
        hail(te, z, c)
    for step in (-1, 1):

        @pl.when((z + step >= 0) & (z + step < nz))
        def _():
            hail(e, z + step, c)

    pl.semaphore_wait(barrier, 4 + jnp.where(z > 0, 1, 0) + jnp.where(z < nz - 1, 1, 0))


def greet_shard(nz):
    e, z, c, ex, ey = place()
    barrier = pltpu.get_barrier_semaphore()
    n = 2 * nz
    peers = [(te, z, c) for te in (ex, ey, (ex + 2) % 4)]
    for d in range(1, n):
        to = (2 * z + c + d) % n
        peers.append((e, to // 2, to % 2))
    for peer in peers:
        pl.semaphore_signal(barrier, inc=1, device_id=peer, device_id_type=pl.DeviceIdType.MESH)
    pl.semaphore_wait(barrier, n + 2)


def scatter_stream(nz, ref, view, send, recv, own):
    e, z, c, _, _ = place()
    n = 2 * nz
    me = 2 * z + c

    def copy(d):
        to = (me + d) % n
        return remote(ref.at[to], view(me), send.at[d], recv.at[d], e, to // 2, to % 2)

    kept = pltpu.make_async_copy(ref.at[me], view(me), own)

    def begin():
        for d in range(1, n):
            copy(d).start()
        kept.start()

    def end():
        kept.wait()
        for d in range(1, n):
            land = view((me + n - d) % n)
            remote(land, land, send.at[d], recv.at[d], e, z, c).wait_recv()
            copy(d).wait_send()

    return begin, end


def scatter_sems(nz):
    dma = pltpu.SemaphoreType.DMA
    return [dma((2 * nz,)), dma((2 * nz,)), dma(())]


def line_stream(nz, ref, out, zrecv, zsend, sib_recv, sib_send, own):
    e, z, c, _, _ = place()

    def split_step(s):
        return (s - 1) % 2, (s - 1) // 2

    def where(s):
        if s == 0:
            return z
        side, i = split_step(s)
        return z - 1 - i if side == 0 else z + 1 + i

    def exists(s):
        return (where(s) >= 0) & (where(s) < nz)

    def inside(side):
        return z < nz - 1 if side == 0 else z > 0

    def slab(s):
        return out.at[where(s), c]

    def first(side):
        step = 1 if side == 0 else -1
        return remote(ref, slab(0), zsend.at[side, nz - 1], zrecv.at[side, 0], e, z + step, c)

    def onward(s):
        side, i = split_step(s)
        step = 1 if side == 0 else -1
        return remote(
            slab(s), slab(s), zsend.at[side, i], zrecv.at[side, i + 1], e, z + step, c
        )

    def beside(s):
        return remote(
            ref if s == 0 else slab(s), slab(s), sib_send.at[s], sib_recv.at[s], e, z, 1 - c
        )

    def begin():
        for side in range(2):

            @pl.when(inside(side))
            def _():
                first(side).start()

        beside(0).start()
        pltpu.make_async_copy(ref, slab(0), own).start()

    def arrive(s):
        side, i = split_step(s)

        @pl.when(exists(s))
        def _():
            remote(slab(s), slab(s), zsend.at[side, i], zrecv.at[side, i], e, z, c).wait_recv()
            if i < nz - 2:

                @pl.when(inside(side))
                def _():
                    onward(s).start()

            beside(s).start()

    def end():
        for s in range(2 * nz - 1):

            @pl.when(exists(s))
            def _():
                beside(s).wait_send()
                view = out.at[where(s), 1 - c]
                remote(view, view, sib_send.at[s], sib_recv.at[s], e, z, c).wait_recv()
                if s > 0 and split_step(s)[1] < nz - 2:

                    @pl.when(inside(split_step(s)[0]))
                    def _():
                        onward(s).wait_send()

        for side in range(2):

            @pl.when(inside(side))
            def _():
                first(side).wait_send()

        pltpu.make_async_copy(ref, slab(0), own).wait()

    return begin, arrive, end


def line_sems(nz):
    dma = pltpu.SemaphoreType.DMA
    S = 2 * nz - 1
    return [dma((2, nz)), dma((2, nz)), dma((S,)), dma((S,)), dma(())]


def plane_stream(source, views, send, recv, own):
    e, z, c, ex, ey = place()
    peers = (ex, ey, (ex + 2) % 4)

    def copy(n):
        return remote(source, views(e), send.at[n], recv.at[n], peers[n], z, c)

    def kept():
        return pltpu.make_async_copy(source, views(e), own)

    def begin():
        for n in range(3):
            copy(n).start()
        kept().start()

    def end():
        kept().wait()
        for n in range(3):
            view = views(peers[n])
            remote(view, view, send.at[n], recv.at[n], e, z, c).wait_recv()
            copy(n).wait_send()

    return begin, end


def plane_sems():
    dma = pltpu.SemaphoreType.DMA
    return [dma((3,)), dma((3,)), dma(())]


def fetch_kernel(
    nz,
    F, w_ref, s_ref, o_ref, t_ref, l_ref, p_ref, x_ref,
    w_out, s_out, o_out, t_out, l_out, p_out, gate_out, up_out,
    wide, gate, up, wide_sem, packed_sem,
    *sems,
):
    e, z, c, ex, ey = place()
    w_sems, sems = sems[:5], sems[5:]
    s_sems, sems = sems[:5], sems[5:]
    t_sems, sems = sems[:3], sems[3:]
    l_sems, sems = sems[:3], sems[3:]
    p_sems, sems = sems[:9], sems[9:]
    orecv, osend, sib_recv, sib_send, own = sems
    wide_copy = pltpu.make_async_copy(x_ref, wide, wide_sem)
    wide_copy.start()
    greet_cross(nz)
    w_begin, w_arrive, w_end = line_stream(nz, w_ref, w_out, *w_sems)
    s_begin, s_arrive, s_end = line_stream(nz, s_ref, s_out, *s_sems)
    t_begin, t_end = plane_stream(t_ref, lambda q: t_out.at[q], *t_sems)
    l_begin, l_end = plane_stream(l_ref, lambda q: l_out.at[q], *l_sems)
    p_begin, p_arrive, p_relay, p_close, p_end = payload_stream(
        nz, p_ref, p_out, p_sems, p_ref.shape[0] // 2
    )

    pieces = orecv.shape[0]
    height = o_ref.shape[0] // pieces

    def o_part(n):
        return pl.ds(n * height, height)

    def o_view(n):
        return o_out.at[c, o_part(n), :]

    def o_copy(side, n, source):
        step = 1 if side == 0 else -1
        return remote(source, o_view(n), osend.at[side, n], orecv.at[n], e, z + step, c)

    def o_beside(n, source):
        return remote(source, o_view(n), sib_send.at[n], sib_recv.at[n], e, z, 1 - c)

    def o_goes(side):
        return (z >= e) & (z < nz - 1) if side == 0 else (z <= e) & (z > 0)

    def o_pass(n, source):
        for side in range(2):

            @pl.when(o_goes(side))
            def _():
                o_copy(side, n, source).start()

        o_beside(n, source).start()

    def o_arrive(n):
        @pl.when(z != e)
        def _():
            remote(o_view(n), o_view(n), sib_send.at[n], orecv.at[n], e, z, c).wait_recv()
            o_pass(n, o_view(n))

    p_begin()

    @pl.when(z == e)
    def _():
        for n in range(pieces):
            o_pass(n, o_ref.at[o_part(n), :])
        pltpu.make_async_copy(o_ref, o_out.at[c], own).start()

    s_begin()
    w_begin()
    t_begin()
    l_begin()

    wide_copy.wait()

    @pl.loop(0, wide.shape[0] // 16)
    def _(b):
        rows = pl.ds(pl.multiple_of(b * 16, 16), 16)
        pack_rows(
            gate.shape[0], F, gate.shape[2], wide.at[rows, :], gate.at[:, rows, :], up.at[:, rows, :]
        )

    packed_copies = [
        pltpu.make_async_copy(a, b, packed_sem.at[n])
        for n, (a, b) in enumerate(((gate, gate_out), (up, up_out)))
    ]
    for copy in packed_copies:
        copy.start()

    blocks = 2 * nz - 1
    for s in range(1, blocks):
        p_arrive(s)
        s_arrive(s)
        if s <= pieces:
            o_arrive(s - 1)
    for n in range(blocks - 1, pieces):
        o_arrive(n)
    for s in range(1, blocks):
        p_relay(s - 1)
        w_arrive(s)
        if s >= 2:
            p_close(s - 2)
    p_relay(blocks - 1)
    p_close(blocks - 2)
    p_close(blocks - 1)
    for s in range(blocks):
        p_end(s)
    w_end()
    s_end()
    t_end()
    l_end()
    for n in range(pieces):
        view = o_out.at[1 - c, o_part(n), :]
        remote(view, view, sib_send.at[n], sib_recv.at[n], e, z, c).wait_recv()
        o_beside(n, o_view(n)).wait_send()
        for side in range(2):

            @pl.when(o_goes(side))
            def _():
                o_copy(side, n, o_view(n)).wait_send()

    @pl.when(z == e)
    def _():
        pltpu.make_async_copy(o_ref, o_out.at[c], own).wait()

    for copy in packed_copies:
        copy.wait()


def fetch_weights(nz, columns, small, rows, tokens, lengths, block, wide, F):
    dma = pltpu.SemaphoreType.DMA
    packed = (2 * nz, wide.shape[0], -(-F // 128) * 128)
    sd = jax.ShapeDtypeStruct
    return pl.pallas_call(
        functools.partial(fetch_kernel, nz, F),
        out_shape=(
            sd((nz, 2) + columns.shape, bf16),
            sd((nz, 2) + small.shape, bf16),
            sd((2,) + rows.shape, bf16),
            sd((4,) + tokens.shape, bf16),
            sd((4,) + lengths.shape, lengths.dtype),
            sd((nz, 2, 4) + block.shape, block.dtype),
            sd(packed, wide.dtype),
            sd(packed, wide.dtype),
        ),
        in_specs=[ANY] * 7,
        out_specs=(ANY,) * 8,
        scratch_shapes=[
            pltpu.VMEM(wide.shape, wide.dtype), pltpu.VMEM(packed, wide.dtype),
            pltpu.VMEM(packed, wide.dtype), dma(()), dma((2,)),
            *line_sems(nz), *line_sems(nz), *plane_sems(), *plane_sems(), *payload_sems(nz),
            dma((6,)), dma((2, 6)), dma((6,)), dma((6,)), dma(()),
        ],
        compiler_params=pltpu.CompilerParams(
            collective_id=0, has_side_effects=True, vmem_limit_bytes=60 << 20
        ),
        cost_estimate=pl.CostEstimate(
            flops=10**11, bytes_accessed=8 * columns.size, transcendentals=0
        ),
        name="fetch_weights",
    )(columns, small, rows, tokens, lengths, block, wide)


def plane_gather_kernel(
    x_ref, a_ref, r_ref, out_ref, d_ref, left, right, prod, load, store, send, recv, own
):
    loads = [
        pltpu.make_async_copy(a_ref, left, load.at[0]),
        pltpu.make_async_copy(r_ref, right, load.at[1]),
    ]
    for copy in loads:
        copy.start()
    greet_plane()
    begin, end = plane_stream(x_ref, lambda q: out_ref.at[q], send, recv, own)
    begin()
    for copy in loads:
        copy.wait()
    tiles, step = store.shape[0], prod.shape[1] // store.shape[0]

    def done(n):
        cols = pl.ds(n * step, step)
        return pltpu.make_async_copy(prod.at[:, cols], d_ref.at[:, cols], store.at[n])

    for n in range(tiles):

        @pl.loop(0, prod.shape[0] // 256)
        def _(m):
            rows = pl.ds(pl.multiple_of(m * 256, 256), 256)
            prod[rows, n * step : (n + 1) * step] = jnp.dot(
                left[rows, :], right[:, n * step : (n + 1) * step], preferred_element_type=f32
            )

        done(n).start()
    for n in range(tiles):
        done(n).wait()
    end()


def greet_plane():
    e, z, c, ex, ey = place()
    barrier = pltpu.get_barrier_semaphore()
    for te in (ex, ey, (ex + 2) % 4):
        pl.semaphore_signal(
            barrier, inc=1, device_id=(te, z, c), device_id_type=pl.DeviceIdType.MESH
        )
    pl.semaphore_wait(barrier, 3)


def plane_gather(x, left, right, collective):
    M, N = left.shape[0], right.shape[1]
    dma = pltpu.SemaphoreType.DMA
    vm = pltpu.VMEM
    return pl.pallas_call(
        plane_gather_kernel,
        out_shape=(
            jax.ShapeDtypeStruct((4,) + x.shape, x.dtype),
            jax.ShapeDtypeStruct((M, N), f32),
        ),
        in_specs=[ANY] * 3,
        out_specs=(ANY,) * 2,
        scratch_shapes=[
            vm(left.shape, bf16), vm(right.shape, bf16), vm((M, N), f32),
            dma((2,)), dma((N // 256,)), *plane_sems(),
        ],
        compiler_params=pltpu.CompilerParams(
            collective_id=collective, has_side_effects=True, vmem_limit_bytes=48 << 20
        ),
        cost_estimate=pl.CostEstimate(flops=10**6, bytes_accessed=10**6, transcendentals=0),
        name="plane_gather",
    )(x, left, right)


def plane_sum_parts(x_ref, out_ref, held, send, recv, own):
    e, z, c, ex, ey = place()
    peers = (ex, ey, (ex + 2) % 4)

    def copy(n):
        return remote(x_ref.at[peers[n]], held.at[n], send.at[n], recv.at[n], peers[n], z, c)

    kept = pltpu.make_async_copy(x_ref.at[e], held.at[3], own)

    def total():
        kept.wait()
        for n in range(3):
            copy(n).wait_recv()

        @pl.loop(0, out_ref.shape[0] // 16)
        def _(b):
            rows = pl.ds(pl.multiple_of(b * 16, 16), 16)
            acc = held[3, rows, :].astype(f32) + held[0, rows, :].astype(f32)
            acc = acc + held[1, rows, :].astype(f32)
            out_ref[rows, :] = acc + held[2, rows, :].astype(f32)

    return copy, kept, total


def plane_sum_kernel(x_ref, out_ref, held, send, recv, own):
    greet_plane()
    copy, kept, total = plane_sum_parts(x_ref, out_ref, held, send, recv, own)
    for n in (2, 0, 1):
        copy(n).start()
    kept.start()
    total()
    for n in range(3):
        copy(n).wait_send()


def plane_sum(x, collective):
    vm = pltpu.VMEM
    return pl.pallas_call(
        plane_sum_kernel,
        out_shape=jax.ShapeDtypeStruct(x.shape[1:], f32),
        in_specs=[ANY],
        out_specs=pl.BlockSpec(memory_space=vm),
        scratch_shapes=[vm(x.shape, bf16), *plane_sems()],
        compiler_params=pltpu.CompilerParams(collective_id=collective, has_side_effects=True),
        cost_estimate=pl.CostEstimate(flops=10**6, bytes_accessed=10**6, transcendentals=0),
        name="plane_sum",
    )(x)


def settle_kernel(
    nz,
    g_ref, s_ref, o_ref, x_ref, y_ref,
    g_out, s_out, o_out, x_out, y_out,
    x_held, x_send, x_recv, x_own, y_send, y_recv, y_own,
    g_mine, g_sib, g_z, s_mine, s_sib, s_z, o_mine, o_sib, o_z,
    load, sib_send, sib_recv, zsend, zrecv,
    o_load, o_sib_send, o_sib_recv, o_zsend, o_zrecv,
    o_send, o_recv, o_own,
    *sems,
):
    e, z, c, ex, ey = place()
    peers = (ex, ey, (ex + 2) % 4)
    dest = line_order(nz, z)
    greet_cross(nz)
    W = g_ref.shape[3]
    first = W // 256 * 128
    groups = (
        (g_ref, g_mine, g_sib, g_z, g_out, pl.ds(0, first)),
        (g_ref, g_mine, g_sib, g_z, g_out, pl.ds(first, W - first)),
        (s_ref, s_mine, s_sib, s_z, s_out, pl.ds(0, s_ref.shape[3])),
    )
    K = len(groups)

    def part(k, which, *index):
        return groups[k][which].at[(*index, slice(None), groups[k][5])]

    def fetch(k, i):
        return pltpu.make_async_copy(
            part(k, 0, dest[i], c), part(k, 1, i), load.at[k, i]
        )

    def hand(k, i):
        return remote(
            part(k, 0, dest[i], 1 - c), part(k, 2, i),
            sib_send.at[k, i], sib_recv.at[k, i], e, z, 1 - c,
        )

    def zcopy(k, i):
        step = jnp.where(dest[i] > z, 1, -1)
        side = jnp.where(dest[i] > z, 0, 1)
        return remote(
            part(k, 1, i), part(k, 3, side, dest[i]),
            zsend.at[k, i], zrecv.at[k, side, dest[i]], e, z + step, c,
        )

    def zwait(k, side, zz):
        slab = part(k, 3, side, zz)
        remote(slab, slab, zsend.at[k, 0], zrecv.at[k, side, zz], e, z, c).wait_recv()

    def add(target, others):
        @pl.loop(0, target.shape[0] // 16)
        def _(b):
            rows = pl.ds(pl.multiple_of(b * 16, 16), 16)
            acc = target[rows, :].astype(f32)
            for o in others:
                acc = acc + o[rows, :].astype(f32)
            target[rows, :] = acc.astype(target.dtype)

    pieces = o_load.shape[0]
    height = o_mine.shape[0] // pieces

    def o_part(n):
        return pl.ds(n * height, height)

    def o_fetch(n):
        return pltpu.make_async_copy(o_ref.at[c, o_part(n), :], o_mine.at[o_part(n), :], o_load.at[n])

    def o_hand(n):
        return remote(
            o_ref.at[1 - c, o_part(n), :], o_sib.at[o_part(n), :],
            o_sib_send.at[n], o_sib_recv.at[n], e, z, 1 - c,
        )

    def o_line(n):
        step, side = jnp.where(z < e, 1, -1), jnp.where(z < e, 0, 1)
        return remote(
            o_mine.at[o_part(n), :], o_z.at[side, o_part(n), :],
            o_zsend.at[n], o_zrecv.at[side, n], e, z + step, c,
        )

    def o_wait(side, n):
        slab = o_z.at[side, o_part(n), :]
        remote(slab, slab, o_zsend.at[n], o_zrecv.at[side, n], e, z, c).wait_recv()
        add(o_mine.at[o_part(n), :], [slab])

    def o_peer(p, n):
        view = o_out.at[o_part(n), :]
        return remote(
            o_mine.at[o_part(n), :], view, o_send.at[p, n], o_recv.at[n], peers[p], z, c
        )

    def o_kept():
        return pltpu.make_async_copy(o_mine, o_out, o_own)

    for i in range(nz):
        for k in range(K):
            hand(k, i).start()
            fetch(k, i).start()
        if i == 0:
            for n in range(pieces):
                o_fetch(n).start()
                o_hand(n).start()

    def finish(k, i):
        fetch(k, i).wait()
        hand(k, i).wait_recv()
        zz = dest[i]
        add(part(k, 1, i), [part(k, 2, i)])
        if i < nz - 1:
            for side in range(2):
                going = zz > z if side == 0 else zz < z
                behind = z > 0 if side == 0 else z < nz - 1

                @pl.when(going & behind)
                def _():
                    zwait(k, side, zz)
                    add(part(k, 1, i), [part(k, 3, side, zz)])

            zcopy(k, i).start()
            return
        for side in range(2):

            @pl.when(z > 0 if side == 0 else z < nz - 1)
            def _():
                zwait(k, side, z)
                add(part(k, 1, i), [part(k, 3, side, z)])

        streams[k][0]()

    x_copy, x_kept, x_total = plane_sum_parts(x_ref, x_out, x_held, x_send, x_recv, x_own)
    for p in (2, 0, 1):
        x_copy(p).start()
    x_kept.start()

    def y_copy(p):
        return remote(
            y_ref.at[peers[p]], y_out.at[e], y_send.at[p], y_recv.at[p], peers[p], z, c
        )

    y_kept = pltpu.make_async_copy(y_ref.at[e], y_out.at[e], y_own)
    y_kept.start()
    for p in range(3):
        y_copy(p).start()

    def o_flow(n):
        o_fetch(n).wait()
        o_hand(n).wait_recv()
        add(o_mine.at[o_part(n), :], [o_sib.at[o_part(n), :]])
        for side in range(2):
            behind = (z > 0) & (z <= e) if side == 0 else (z < nz - 1) & (z >= e)

            @pl.when(behind)
            def _():
                o_wait(side, n)

        @pl.when(z != e)
        def _():
            o_line(n).start()

        @pl.when(z == e)
        def _():
            for p in range(3):
                o_peer(p, n).start()

    streams = [
        plane_stream(
            part(k, 1, nz - 1), lambda q, k=k: part(k, 4, q), *sems[3 * k : 3 * k + 3]
        )
        for k in range(K)
    ]
    turn = K * nz // 2
    order = []
    for k in range(K):
        order += [(k, i) for i in range(1 if k else 0, nz - 1)]
        if k + 1 < K:
            order.append((k + 1, 0))
        order.append((k, nz - 1))
    for n, (k, i) in enumerate(order):
        finish(k, i)
        if n == 0:
            for m in range(pieces):
                o_flow(m)
        if n == turn:
            x_total()

    @pl.when(z == e)
    def _():
        o_kept().start()
        o_kept().wait()
        for n in range(pieces):
            for p in range(3):
                o_peer(p, n).wait_send()

    @pl.when(z != e)
    def _():
        for n in range(pieces):
            view = o_out.at[o_part(n), :]
            remote(view, view, o_send.at[0, n], o_recv.at[n], e, z, c).wait_recv()
            o_line(n).wait_send()

    y_kept.wait()
    for p in range(3):
        x_copy(p).wait_send()
        view = y_out.at[peers[p]]
        remote(view, view, y_send.at[p], y_recv.at[p], e, z, c).wait_recv()
        y_copy(p).wait_send()
    for n in range(pieces):
        o_hand(n).wait_send()
    for i in range(nz):
        for k in range(K):
            hand(k, i).wait_send()
            if i < nz - 1:
                zcopy(k, i).wait_send()
    for _, end in streams:
        end()


def settle_weights(nz, grads, small, rows, near, blocks):
    R, W = grads.shape[2:]
    D = rows.shape[2]
    dma = pltpu.SemaphoreType.DMA
    sd = jax.ShapeDtypeStruct
    vm = pltpu.VMEM
    Ws = small.shape[3]
    return pl.pallas_call(
        functools.partial(settle_kernel, nz),
        out_shape=(
            sd((4, R, W), bf16),
            sd((4, R, Ws), bf16),
            sd((R, D), bf16),
            sd(near.shape[1:], f32),
            sd(blocks.shape, bf16),
        ),
        in_specs=[ANY] * 5,
        out_specs=(ANY,) * 3 + (pl.BlockSpec(memory_space=vm), ANY),
        scratch_shapes=[
            vm(near.shape, bf16), *plane_sems(), *plane_sems(),
            vm((nz, R, W), bf16), vm((nz, R, W), bf16), vm((2, nz, R, W), bf16),
            vm((nz, R, Ws), bf16), vm((nz, R, Ws), bf16), vm((2, nz, R, Ws), bf16),
            vm((R, D), bf16), vm((R, D), bf16), vm((2, R, D), bf16),
            dma((3, nz)), dma((3, nz)), dma((3, nz)), dma((3, nz)), dma((3, 2, nz)),
            dma((6,)), dma((6,)), dma((6,)), dma((6,)), dma((2, 6)),
            dma((3, 6)), dma((6,)), dma(()),
            *plane_sems(), *plane_sems(), *plane_sems(),
        ],
        compiler_params=pltpu.CompilerParams(
            collective_id=1, has_side_effects=True, vmem_limit_bytes=56 << 20
        ),
        cost_estimate=pl.CostEstimate(flops=10**6, bytes_accessed=10**6, transcendentals=0),
        name="settle_weights",
    )(grads, small, rows, near, blocks)


def pick_kernel(width, q_ref, k_ref, v_ref, o_ref):
    e = lax.axis_index("expert")
    spare = o_ref.shape[1] - 3 * width
    if spare:
        o_ref[:, 3 * width :] = jnp.zeros((o_ref.shape[0], spare), o_ref.dtype)
    for n in range(4):

        @pl.when(e == n)
        def _():
            for i, ref in enumerate((q_ref, k_ref, v_ref)):
                o_ref[:, i * width : (i + 1) * width] = ref[:, n * width : (n + 1) * width]


def pick_columns(weights, width):
    vm = pl.BlockSpec(memory_space=pltpu.VMEM)
    return pl.pallas_call(
        functools.partial(pick_kernel, width),
        in_specs=[vm] * 3,
        out_specs=vm,
        out_shape=jax.ShapeDtypeStruct((weights[0].shape[0], -(-3 * width // 128) * 128), bf16),
        name="pick_columns",
    )(*weights)


def assemble_kernel(width, x_ref, *o_refs):
    for n in range(4):
        for i in range(3):
            cols = x_ref[n, :, i * width : (i + 1) * width]
            o_refs[i][:, n * width : (n + 1) * width] = cols.astype(f32)


def assemble_columns(x, width):
    R = x.shape[1]
    block = 96 if R % 96 == 0 else 16
    return pl.pallas_call(
        functools.partial(assemble_kernel, width),
        grid=(R // block,),
        in_specs=[pl.BlockSpec((4, block, x.shape[2]), lambda i: (0, i, 0))],
        out_specs=(pl.BlockSpec((block, 4 * width), lambda i: (i, 0)),) * 3,
        out_shape=(jax.ShapeDtypeStruct((R, 4 * width), f32),) * 3,
        name="assemble_columns",
    )(x)


def sum_shard(x, axis=0):
    mine = lax.psum_scatter(x, SHARD, scatter_dimension=axis, tiled=True)
    return lax.psum(mine, "expert")


def fetch(nz, fast, weights, w_output, small, tokens, lengths, block, wide, F):
    D = tokens.shape[1]
    if fast:
        width = D // 4
        columns, full_small, rows, tokens, lengths, blocks, *packed = fetch_weights(
            nz, pick_columns(weights, width), small, w_output, tokens, lengths, block, wide, F
        )
        columns, rows = columns.reshape(D, -1), rows.reshape(width, D)
        return columns, rows, full_small.reshape(D, -1), tokens, lengths, blocks, packed
    full = [lax.all_gather(w, SHARD, axis=0, tiled=True) for w in weights + (w_output, small)]
    blocks = spread_plain(nz, (block,), 0)[0]
    packed = pack_columns(wide, 2 * nz, F, -(-F // 128) * 128)
    columns = jnp.concatenate(full[:3], axis=1)
    return columns, full[3], full[4], tokens[None], lengths[None], blocks, packed


def settle(nz, fast, columns, rows, small, near, blocks):
    D, width = rows.shape[1], rows.shape[0]
    if fast:
        R = D // (2 * nz)
        parts = [x.astype(bf16).reshape(nz, 2, R, -1) for x in (columns, small)]
        near = near.astype(bf16).reshape(4, -1, D)
        blocks = blocks.reshape(4, -1, D)
        sums, small, out, near, blocks = settle_weights(
            nz, *parts, rows.astype(bf16).reshape(2, R, D), near, blocks
        )
        small, blocks = jnp.sum(small.astype(f32), axis=0), blocks.reshape(-1, D)
        return *assemble_columns(sums, width), out.astype(f32), small, near, blocks
    parts = [columns[:, i * width : (i + 1) * width] for i in range(3)] + [rows, small]
    blocks = lax.all_to_all(blocks, "expert", split_axis=0, concat_axis=0, tiled=True)
    return [sum_shard(x) for x in parts] + [near, blocks]


def spread_plain(nz, blocks, collective):
    out = []
    for block in blocks:
        for axis in ("expert", "core", "z"):
            block = lax.all_gather(block, axis, axis=0)
        out.append(block)
    return out


def spread_pair(nz, blocks, gate, up, collective):
    gate = lax.all_to_all(gate, SHARD, split_axis=0, concat_axis=0, tiled=True)
    return jnp.concatenate([gate, up], axis=2), *spread_plain(nz, blocks, collective)


def collect_plain(nz, rows, notes, dots, T):
    n_exp, cap, D = rows.shape[2:]
    places = (lax.axis_index("expert") * cap + jnp.arange(cap)).astype(f32)
    notes = notes[..., :T]
    pick = (notes[..., 2, None, :] == places[:, None]) | (notes[..., 3, None, :] == places[:, None])
    part = jnp.einsum(
        "zceps,zcepd->zcesd", pick.astype(bf16), rows, preferred_element_type=f32
    ).astype(bf16)
    part = part.transpose(2, 0, 1, 3, 4).reshape(n_exp * nz * 2 * T, D)
    part = lax.psum_scatter(part, "expert", scatter_dimension=0, tiled=True)
    part = lax.psum_scatter(part, SHARD, scatter_dimension=0, tiled=True).astype(f32)
    z, core, e = lax.axis_index("z"), lax.axis_index("core"), lax.axis_index("expert")
    return part, lax.psum(dots, ("expert",) + SHARD)[z, core, e]


def rope_tables(positions, head_width):
    half_width = head_width // 2
    exponents = jnp.arange(half_width).astype(f32) * 2.0 / head_width
    frequency = rope_base ** (-exponents)
    angles = positions.astype(f32)[..., None] * frequency
    return (jnp.cos(angles), jnp.sin(angles))


def rotate(values, cosine, sine_table):
    half_width = values.shape[-1] // 2
    leading = values[..., :half_width]
    trailing = values[..., half_width:]
    cos_rows = cosine[:, :, None, :]
    sin_rows = sine_table[:, :, None, :]
    return jnp.concatenate(
        [leading * cos_rows - trailing * sin_rows, trailing * cos_rows + leading * sin_rows],
        axis=-1,
    )


def rms_forward(values, norm_gain):
    inverse = lax.rsqrt(jnp.mean(values * values, axis=-1, keepdims=True) + eps_norm)
    return (values * inverse * norm_gain, inverse)


def rms_backward(values, inverse, norm_gain, upstream):
    weighted = upstream * norm_gain
    gain_grad = jnp.sum(upstream * values * inverse, axis=0)
    inner_mean = jnp.mean(weighted * values, axis=-1, keepdims=True)
    return (inverse * weighted - values * inverse * inverse * inverse * inner_mean, gain_grad)


def dot32(a, b):
    return jnp.dot(a, b, preferred_element_type=f32)


def dot_dims(a, b, da, db):
    return lax.dot_general(a, b, (((da,), (db,)), ((), ())), preferred_element_type=f32)


def ein32(spec, a, b):
    return jnp.einsum(spec, a, b, preferred_element_type=f32)


def on_device(
    tokens,
    seq_lengths,
    routes,
    norm_attn,
    w_query,
    w_key,
    w_value,
    w_output,
    norm_ffn,
    w_router,
    w_in,
    w_down,
    cotangent,
):
    T, D = tokens.shape
    R = w_query.shape[0]
    head_width = D // HEADS
    n_exp = lax.axis_size("expert")
    nz = lax.axis_size("z")
    n_shard = nz * lax.axis_size("core")
    experts = w_router.shape[1]
    F = w_down.shape[0]
    FF = F * n_shard
    capacity = 10 * T // (4 * experts)
    slots = experts * capacity
    highest = lax.Precision.HIGHEST
    e_index = lax.axis_index("expert")
    fast = n_exp == 4 and nz == 4

    small = jnp.concatenate([w_router, norm_attn[:, None], norm_ffn[:, None]], axis=1)
    small = jnp.pad(small, ((0, 0), (0, 128 - small.shape[1])))
    length_rows = jnp.broadcast_to(seq_lengths[:, :1], (8, 128))
    full_qkv, full_output, full_small, near_tokens, near_lengths, all_cotangent, packed = fetch(
        nz,
        fast,
        (w_query, w_key, w_value),
        w_output,
        small,
        tokens,
        length_rows,
        cotangent,
        w_in.reshape(R, 2 * FF),
        F,
    )
    full_router = full_small[:, :experts]
    gain_attn = full_small[:, experts].astype(f32)
    gain_ffn = full_small[:, experts + 1].astype(f32)

    Fp = -(-F // 128) * 128
    moved_up = lax.all_to_all(packed[1], SHARD, split_axis=0, concat_axis=0, tiled=True)
    down = jnp.pad(w_down.reshape(F, D), ((0, Fp - F), (0, 0)))

    B, H = near_tokens.shape[0], full_output.shape[0]
    heads = H // head_width
    residual_in = tokens.astype(f32)
    inverse_in = rms_forward(residual_in, gain_attn)[1]
    near_in = near_tokens.reshape(B * T, D).astype(f32)
    near_normed, near_inverse = rms_forward(near_in, gain_attn)
    normed_half = near_normed.astype(bf16)
    lengths = near_lengths[:, 0, 0]
    row_index = jnp.arange(T)
    segment = (row_index[None, :] >= lengths[:, None]).astype(jnp.int32)
    positions = row_index[None, :] - lengths[:, None] * segment
    allowed = (segment[:, :, None] == segment[:, None, :]) & (
        row_index[None, None, :] <= row_index[None, :, None]
    )
    cosine, sine_table = rope_tables(positions, head_width)
    head_shape = (B, T, heads, head_width)
    qkv = dot32(normed_half, full_qkv)
    queries = rotate(qkv[:, :H].reshape(head_shape), cosine, sine_table).astype(bf16)
    keys_rot = rotate(qkv[:, H : 2 * H].reshape(head_shape), cosine, sine_table).astype(bf16)
    values = qkv[:, 2 * H : 3 * H].astype(bf16).reshape(head_shape)
    score_scale = 1.0 / math.sqrt(head_width)
    scores = ein32("bqhd,bkhd->bhqk", queries, keys_rot) * score_scale
    scores = jnp.where(allowed[:, None], scores, masked_score)
    row_peak = jnp.max(scores, axis=-1, keepdims=True)
    log_total = row_peak + jnp.log(jnp.sum(jnp.exp(scores - row_peak), axis=-1, keepdims=True))
    attn_probs = jnp.exp(scores - log_total)
    probs_half = attn_probs.astype(bf16)
    context = ein32("bhqk,bkhd->bqhd", probs_half, values).astype(bf16)
    context_flat = context.reshape(B * T, H)

    def at_home(partial_rows, collective):
        if not fast:
            return partial_rows
        return plane_sum(partial_rows.astype(bf16).reshape(B, T, D), collective)

    residual_mid = residual_in + branch_scale * at_home(dot32(context_flat, full_output), 4)
    normed_mid, inverse_mid = rms_forward(residual_mid, gain_ffn)
    normed_mid_half = normed_mid.astype(bf16)

    logits = dot32(normed_mid_half, full_router)
    expert_ids = jnp.arange(experts)
    route_mask = (routes[:, :, None] == expert_ids[None, None, :]).astype(f32)
    chosen = jnp.sum(logits[:, None, :] * route_mask, axis=-1)
    gate_probs = jax.nn.softmax(chosen, axis=-1)
    flat_routes = routes.reshape(2 * T)
    hits = (flat_routes[:, None] == expert_ids[None, :]).astype(bf16)
    order = jnp.arange(2 * T)
    before = (order[:, None] > order[None, :]).astype(bf16)
    earlier = dot32(before, hits)
    slot_index = jnp.sum(earlier * hits.astype(f32), axis=1).astype(jnp.int32)
    target = (flat_routes * capacity + slot_index).reshape(T, 2)
    slot_ids = jnp.arange(slots)
    pick = [(target[:, k][:, None] == slot_ids[None, :]).astype(bf16) for k in range(2)]

    notes = jnp.concatenate([gate_probs, target.astype(f32), jnp.zeros((T, 4), f32)], axis=1)
    notes = jnp.pad(jnp.transpose(notes), ((0, 0), (0, -T % 128)))
    spread = spread_blocks if fast else spread_pair
    w_pair, all_normed, all_notes = spread(nz, (normed_mid_half, notes), packed[0], moved_up, 2)
    w_pair = w_pair.reshape(n_shard * R, 2 * Fp)
    devices = n_shard * n_exp
    flat_notes = all_notes.reshape(devices, 8, -1)[:, :, :T]
    wanted = (e_index * capacity + jnp.arange(capacity)).astype(f32)
    found = [flat_notes[:, 2 + k, None, :] == wanted[None, :, None] for k in range(2)]
    gate_rows = jnp.sum(
        jnp.where(found[0], flat_notes[:, 0, None, :], 0.0)
        + jnp.where(found[1], flat_notes[:, 1, None, :], 0.0),
        axis=-1,
    ).reshape(devices * capacity, 1)
    chosen_rows = (found[0] | found[1]).astype(bf16)

    def take(blocks):
        rows = ein32("spt,std->spd", chosen_rows, blocks.reshape(devices, T, D))
        return rows.astype(bf16).reshape(devices * capacity, D)

    arrived = take(all_normed)
    cotangent_rows = take(all_cotangent)
    grad_scale = gate_rows * branch_scale
    pre = dot32(arrived, w_pair)
    gate_part, up_part = pre[:, :Fp], pre[:, Fp:]
    sigmoid_gate = jax.nn.sigmoid(gate_part)
    silu_gate = gate_part * sigmoid_gate
    activated = (silu_gate * up_part).astype(bf16)
    out_sum = lax.psum_scatter(
        dot32(activated, down).astype(bf16), SHARD, scatter_dimension=0, tiled=True
    )

    raw_grad = dot_dims(cotangent_rows, down, 1, 1)
    row_dots = branch_scale * jnp.sum(raw_grad * activated.astype(f32), axis=1)
    row_dots = row_dots.reshape(devices, capacity, 1)
    token_dots = [jnp.sum(jnp.where(found[k], row_dots, 0.0), axis=1) for k in range(2)]
    token_dots = jnp.stack(token_dots, axis=1).reshape(nz, 2, n_exp, 2, T)
    token_dots = jnp.pad(token_dots, ((0, 0),) * 3 + ((0, 6), (0, -T % 128)))
    act_grad = grad_scale * raw_grad
    gate_grads = act_grad * up_part * sigmoid_gate * (1.0 + gate_part * (1.0 - sigmoid_gate))
    gate_grads, up_grads = gate_grads.astype(bf16), (act_grad * silu_gate).astype(bf16)
    pre_grad = jnp.concatenate([gate_grads, up_grads], axis=1)
    in_rows = dot_dims(pre_grad, w_pair, 1, 1).astype(bf16)
    scaled = (grad_scale * activated.astype(f32)).astype(bf16)
    gate_term, up_term = [
        dot_dims(arrived, x, 0, 0).astype(bf16).reshape(n_shard, R, Fp)
        for x in (gate_grads, up_grads)
    ]
    gate_term, up_term = lax.optimization_barrier((gate_term, up_term))
    up_term = lax.all_to_all(up_term, SHARD, split_axis=0, concat_axis=0, tiled=True)
    in_rows = in_rows.reshape(nz, 2, n_exp, capacity, D)
    collect = collect_rows if fast else collect_plain
    normed_mid_grad, gate_grad = collect(nz, in_rows, all_notes, token_dots, T)
    gate_grad = jnp.transpose(gate_grad[:2, :T])
    up_term, normed_mid_grad, out_sum, gate_term = lax.optimization_barrier(
        (up_term, normed_mid_grad, out_sum, gate_term)
    )
    gate_term = lax.all_to_all(gate_term, SHARD, split_axis=0, concat_axis=0, tiled=True)

    upstream = cotangent.astype(f32)
    chosen_grad = gate_probs * (gate_grad - jnp.sum(gate_probs * gate_grad, axis=-1, keepdims=True))
    logit_grad = jnp.sum(chosen_grad[:, :, None] * route_mask, axis=1)
    normed_mid_grad = normed_mid_grad + jnp.dot(
        logit_grad, jnp.transpose(full_router.astype(f32)), precision=highest
    )
    router_grad = jnp.dot(
        jnp.transpose(normed_mid_half.astype(f32)), logit_grad, precision=highest
    )
    mid_norm_grad, gain_ffn_grad = rms_backward(
        residual_mid, inverse_mid, gain_ffn, normed_mid_grad
    )
    residual_grad = upstream + mid_norm_grad
    branch_grad = (branch_scale * residual_grad).astype(bf16)

    if fast:
        branch_grad, down_term = plane_gather(
            branch_grad, jnp.transpose(scaled), cotangent_rows, 5
        )
        branch_grad = branch_grad.reshape(B * T, D)
    else:
        down_term = dot_dims(scaled, cotangent_rows, 0, 0)
    grad_w_down = lined_up(down_term, F)
    output_grad = dot_dims(context_flat, branch_grad, 0, 0)
    context_grad = dot_dims(branch_grad, full_output, 1, 1).reshape(head_shape)
    row_delta = jnp.sum(context_grad * context.astype(f32), axis=-1)
    context_grad_half = context_grad.astype(bf16)
    probs_grad = ein32("bqhd,bkhd->bhqk", context_grad_half, values)
    scores_grad = (
        attn_probs * (probs_grad - jnp.transpose(row_delta, (0, 2, 1))[..., None]) * score_scale
    ).astype(bf16)
    queries_grad = ein32("bhqk,bkhd->bqhd", scores_grad, keys_rot)
    keys_grad = ein32("bhqk,bqhd->bkhd", scores_grad, queries)
    values_grad = ein32("bhqk,bqhd->bkhd", probs_half, context_grad_half)
    qkv_grad = jnp.concatenate(
        [
            rotate(queries_grad, cosine, -sine_table).reshape(B * T, H).astype(bf16),
            rotate(keys_grad, cosine, -sine_table).reshape(B * T, H).astype(bf16),
            values_grad.reshape(B * T, H).astype(bf16),
            jnp.zeros((B * T, full_qkv.shape[1] - 3 * H), bf16),
        ],
        axis=1,
    )
    qkv_weight_grad = dot_dims(normed_half, qkv_grad, 0, 0)
    near_grad = dot_dims(qkv_grad, full_qkv, 1, 1)
    gain_attn_grad = jnp.sum(near_grad * near_in * near_inverse, axis=0)

    small_grad = jnp.concatenate(
        [router_grad, gain_attn_grad[:, None], gain_ffn_grad[:, None]], axis=1
    )
    small_grad = jnp.pad(small_grad, ((0, 0), (0, 128 - small_grad.shape[1])))
    small_grad, gate_term = lax.optimization_barrier((small_grad, gate_term))
    sum_query, sum_key, sum_value, sum_output, small_sum, normed_in_grad, back = settle(
        nz, fast, qkv_weight_grad, output_grad, small_grad, near_grad, out_sum
    )
    grad_w_in = unpack_columns(gate_term, up_term, F)
    mixture = gate_probs[:, 0:1] * dot32(pick[0], back) + gate_probs[:, 1:2] * dot32(pick[1], back)
    activations = (residual_mid + branch_scale * mixture).astype(bf16)
    in_norm_grad = rms_backward(residual_in, inverse_in, gain_attn, normed_in_grad)[0]
    grad_tokens = residual_grad + in_norm_grad
    return (
        activations,
        grad_tokens,
        small_sum[:, experts],
        sum_query,
        sum_key,
        sum_value,
        sum_output,
        small_sum[:, experts + 1],
        small_sum[:, :experts],
        grad_w_in,
        grad_w_down,
    )


def solution(mesh):
    n_expert, n_shard = mesh.devices.shape
    chips = Mesh(mesh.devices.reshape(n_expert, n_shard // 2, 2), ("expert", "z", "core"))
    rows = P(("expert", "z", "core"), None)
    shard = P(SHARD)
    shard2 = P(SHARD, None)
    shard3 = P(SHARD, "expert", None)
    in_specs = (
        rows,
        rows,
        rows,
        shard,
        shard2,
        shard2,
        shard2,
        shard2,
        shard,
        shard2,
        shard3,
        shard3,
        rows,
    )
    out_specs = (
        rows,
        rows,
        shard,
        shard2,
        shard2,
        shard2,
        shard2,
        shard,
        shard2,
        shard3,
        shard3,
    )
    return jax.shard_map(
        on_device, mesh=chips, in_specs=in_specs, out_specs=out_specs, check_vma=False
    )
```

```python
import functools
import math

import jax
import jax.numpy as jnp
from jax import lax
from jax.experimental import pallas as pl
from jax.experimental.pallas import tpu as pltpu
from jax.sharding import Mesh, PartitionSpec as P

HEADS = 36

eps_norm = 1e-05
branch_scale = 1.4 / math.sqrt(40.0)
rope_base = 10000.0
masked_score = -1e30
bf16 = jnp.bfloat16
f32 = jnp.float32
SHARD = ("z", "core")
ANY = pl.BlockSpec(memory_space=pl.ANY)


def place():
    e, z, c = lax.axis_index("expert"), lax.axis_index("z"), lax.axis_index("core")
    across_x = e + 1 - 2 * (e % 2)
    across_y = (e + 2) % 4
    return e, z, c, across_x, across_y


def remote(src, dst, send, recv, e, z, c):
    return pltpu.make_async_remote_copy(
        src_ref=src,
        dst_ref=dst,
        send_sem=send,
        recv_sem=recv,
        device_id=(e, z, c),
        device_id_type=pl.DeviceIdType.MESH,
    )


def payload_stream(nz, ref, out, sems, split):
    zrecv, zsend, near_recv, near_send, far_recv, far_send, sib_recv, sib_send, own = sems
    e, z, c, ex, ey = place()
    diagonal = (ex + 2) % 4
    T = ref.shape[0]
    S = 2 * nz - 1

    def split_step(s):
        return (s - 1) % 2, (s - 1) // 2

    def where(s):
        if s == 0:
            return z
        side, i = split_step(s)
        return z - 1 - i if side == 0 else z + 1 + i

    def exists(s):
        if s == 0:
            return z >= 0
        zz = where(s)
        return (zz >= 0) & (zz < nz)

    def slab(s, quarter, r0=0, n=T):
        return out.at[where(s), c, quarter, pl.ds(r0, n), :]

    def first(step):
        side = 0 if step > 0 else 1
        return remote(ref, slab(0, e), zsend.at[side, nz - 1], zrecv.at[side, 0], e, z + step, c)

    def onward(s):
        side, i = split_step(s)
        step = 1 if side == 0 else -1
        return remote(
            slab(s, e), slab(s, e), zsend.at[side, i], zrecv.at[side, i + 1], e, z + step, c
        )

    def near(s, axis):
        source = ref if s == 0 else slab(s, e)
        return remote(
            source, slab(s, e), near_send.at[s, axis], near_recv.at[s, axis],
            ex if axis == 0 else ey, z, c,
        )

    def near_wait(s, axis):
        view = slab(s, ex if axis == 0 else ey)
        remote(view, view, near_send.at[s, axis], near_recv.at[s, axis], ex, z, c).wait_recv()

    axes = range(2) if split else range(1)

    def far_view(s, quarter, axis):
        if not split:
            return slab(s, quarter)
        return slab(s, quarter, 0, split) if axis == 0 else slab(s, quarter, split, T - split)

    def far(s, axis):
        view = far_view(s, ex if axis == 0 else ey, axis)
        return remote(
            view, view, far_send.at[s, axis], far_recv.at[s, axis],
            ey if axis == 0 else ex, z, c,
        )

    def far_wait(s, axis):
        view = far_view(s, diagonal, axis)
        remote(view, view, far_send.at[s, axis], far_recv.at[s, axis], ex, z, c).wait_recv()

    def beside(s, n):
        quarter = (e, ex, ey, diagonal)[n]
        source = ref if s == 0 and n == 0 else slab(s, quarter)
        return remote(
            source, slab(s, quarter), sib_send.at[s, n], sib_recv.at[s, n], e, z, 1 - c
        )

    def beside_wait(s, n):
        view = out.at[where(s), 1 - c, (e, ex, ey, diagonal)[n]]
        remote(view, view, sib_send.at[s, n], sib_recv.at[s, n], e, z, c).wait_recv()

    def inside(side):
        return z < nz - 1 if side == 0 else z > 0

    def begin():
        for step in (1, -1):

            @pl.when((z + step >= 0) & (z + step < nz))
            def _():
                first(step).start()

        near(0, 0).start()
        near(0, 1).start()
        beside(0, 0).start()
        pltpu.make_async_copy(ref, slab(0, e), own).start()

    def arrive(s):
        if s == 0:
            return

        @pl.when(exists(s))
        def _():
            side, i = split_step(s)
            remote(
                slab(s, e), slab(s, e), zsend.at[side, i], zrecv.at[side, i], e, z, c
            ).wait_recv()
            if i < nz - 2:

                @pl.when(inside(side))
                def _():
                    onward(s).start()

            near(s, 0).start()
            near(s, 1).start()
            beside(s, 0).start()

    def relay(s):
        @pl.when(exists(s))
        def _():
            near_wait(s, 0)
            far(s, 0).start()
            beside(s, 1).start()
            near_wait(s, 1)
            if split:
                far(s, 1).start()
            beside(s, 2).start()

    def close(s):
        @pl.when(exists(s))
        def _():
            for axis in axes:
                far_wait(s, axis)
            beside(s, 3).start()

    def end(s):
        @pl.when(exists(s))
        def _():
            for axis in range(2):
                near(s, axis).wait_send()
            for axis in axes:
                far(s, axis).wait_send()
            for n in range(4):
                beside(s, n).wait_send()
                beside_wait(s, n)
            if s > 0 and split_step(s)[1] < nz - 2:

                @pl.when(inside(split_step(s)[0]))
                def _():
                    onward(s).wait_send()

        if s == 0:
            for step in (1, -1):

                @pl.when((z + step >= 0) & (z + step < nz))
                def _():
                    first(step).wait_send()

            pltpu.make_async_copy(ref, slab(0, e), own).wait()

    return begin, arrive, relay, close, end


def payload_sems(nz):
    dma = pltpu.SemaphoreType.DMA
    S = 2 * nz - 1
    return [
        dma((2, nz)), dma((2, nz)), dma((S, 2)), dma((S, 2)), dma((S, 2)), dma((S, 2)),
        dma((S, 4)), dma((S, 4)), dma(()),
    ]


def spread_kernel(nz, splits, *refs):
    n = len(splits)
    (gate_ref, up_ref), refs = refs[:2], refs[2:]
    ins, refs = refs[:n], refs[n:]
    pair, outs, sems = refs[0], refs[1 : n + 1], refs[n + 1 :]
    v_sems, beside_sem, sems = sems[:3], sems[3], sems[4:]
    width = gate_ref.shape[2]
    greet_shard(nz)
    streams = [
        payload_stream(nz, ins[i], outs[i], sems[9 * i : 9 * i + 9], splits[i]) for i in range(n)
    ]
    v_begin, v_end = scatter_stream(
        nz, gate_ref, lambda i: pair.at[i, :, pl.ds(0, width)], *v_sems
    )
    beside = pltpu.make_async_copy(up_ref, pair.at[:, :, pl.ds(width, width)], beside_sem)
    for t in streams:
        t[0]()
    beside.start()
    S = 2 * nz - 1
    for s in range(1, S):
        for t in streams:
            t[1](s)
    v_begin()
    for s in range(S):
        for t in streams:
            t[2](s)
        if s >= 1:
            for t in streams:
                t[3](s - 1)
    for t in streams:
        t[3](S - 1)
    for s in range(S):
        for t in streams:
            t[4](s)
    beside.wait()
    v_end()


def spread_blocks(nz, blocks, gate, up, collective):
    sd = jax.ShapeDtypeStruct
    splits = tuple(b.shape[0] // 2 if b.shape[0] % 32 == 0 else 0 for b in blocks)
    pair = sd(gate.shape[:2] + (2 * gate.shape[2],), gate.dtype)
    return pl.pallas_call(
        functools.partial(spread_kernel, nz, splits),
        out_shape=(pair,) + tuple(sd((nz, 2, 4) + b.shape, b.dtype) for b in blocks),
        in_specs=[ANY] * (len(blocks) + 2),
        out_specs=(ANY,) * (len(blocks) + 1),
        scratch_shapes=[
            *scatter_sems(nz), pltpu.SemaphoreType.DMA(()),
            *[s for _ in blocks for s in payload_sems(nz)],
        ],
        compiler_params=pltpu.CompilerParams(collective_id=collective, has_side_effects=True),
        cost_estimate=pl.CostEstimate(flops=10**6, bytes_accessed=10**6, transcendentals=0),
        name="spread_blocks",
    )(gate, up, *blocks)


def line_order(nz, z):
    def order(i):
        code = 0
        for zz in range(nz):
            far_first = sorted(range(nz), key=lambda t: (-abs(t - zz), t))
            code += far_first[i] * nz**zz
        power = 1
        for zz in range(nz):
            power = power + (nz**zz - 1) * jnp.where(z == zz, 1, 0)
        return (code // power) % nz

    return [order(i) for i in range(nz)]


def collect_kernel(
    nz, cap,
    rows_ref, notes_ref, dots_ref,
    out_ref, dots_out,
    dots, notes, mine, theirs, block, from_x, from_y, via_x, via_y, from_z,
    note_sem, load, sib_send, sib_recv, via_send, via_recv, plain_send, plain_recv,
    sum_send, sum_recv, zsend, zrecv, dot_send, dot_recv, dot_own,
):
    e, z, c, ex, ey = place()
    diagonal = (ex + 2) % 4
    T, D = out_ref.shape
    h = T // 2
    dest = line_order(nz, z)
    who = (diagonal, ex, ey, e)

    def others():
        for d in range(1, 8 * nz):
            to = ((e * nz + z) * 2 + c + d) % (8 * nz)
            yield d, to // (2 * nz), to // 2 % nz, to % 2

    barrier = pltpu.get_barrier_semaphore()
    for _, te, tz, tc in others():
        pl.semaphore_signal(
            barrier, inc=1, device_id=(te, tz, tc), device_id_type=pl.DeviceIdType.MESH
        )
    pl.semaphore_wait(barrier, 8 * nz - 1)

    def dot(d, te, tz, tc):
        return remote(
            dots_ref.at[tz, tc, te], dots.at[d], dot_send.at[d], dot_recv.at[d], te, tz, tc
        )

    dot_kept = pltpu.make_async_copy(dots_ref.at[z, c, e], dots.at[0], dot_own)
    dot_kept.start()
    for d, te, tz, tc in others():
        dot(d, te, tz, tc).start()

    note_copy = pltpu.make_async_copy(notes_ref, notes, note_sem)
    note_copy.start()

    def fetch(i, q):
        return pltpu.make_async_copy(
            rows_ref.at[dest[i], c, who[q]], mine.at[i, q], load.at[i, q]
        )

    def hand(i, q):
        return remote(
            rows_ref.at[dest[i], 1 - c, who[q]], theirs.at[i, q],
            sib_send.at[i, q], sib_recv.at[i, q], e, z, 1 - c,
        )

    for i in range(nz):
        for q in range(4):
            hand(i, q).start()
            fetch(i, q).start()
    note_copy.wait()

    def open_out(i, q):
        fetch(i, q).wait()
        hand(i, q).wait_recv()
        places = (lax.broadcasted_iota(jnp.int32, (cap, T), 0) + e * cap).astype(f32)
        note = notes[dest[i], c, who[q]]
        pick = ((note[2:3, :] == places) | (note[3:4, :] == places)).astype(bf16)
        wide = 768 if D % 768 == 0 else 128

        @pl.loop(0, D // wide)
        def _(b):
            cols = pl.ds(pl.multiple_of(b * wide, 128), wide)
            both = mine[i, q, :, cols].astype(f32) + theirs[i, q, :, cols].astype(f32)
            block[i, q, :, cols] = lax.dot_general(
                pick, both.astype(bf16), (((0,), (0,)), ((), ())), preferred_element_type=f32
            ).astype(bf16)

    def via(i, axis):
        if axis == 0:
            return remote(
                block.at[i, 0, pl.ds(0, h), :], via_x.at[i],
                via_send.at[i, 0], via_recv.at[i, 0], ex, z, c,
            )
        return remote(
            block.at[i, 0, pl.ds(h, h), :], via_y.at[i],
            via_send.at[i, 1], via_recv.at[i, 1], ey, z, c,
        )

    def plain(i, axis):
        if axis == 0:
            return remote(
                block.at[i, 1, pl.ds(0, h), :], from_x.at[i, pl.ds(0, h), :],
                plain_send.at[i, 0], plain_recv.at[i, 0], ex, z, c,
            )
        return remote(
            block.at[i, 2, pl.ds(h, h), :], from_y.at[i, pl.ds(h, h), :],
            plain_send.at[i, 1], plain_recv.at[i, 1], ey, z, c,
        )

    def summed(i, axis):
        if axis == 0:
            return remote(
                block.at[i, 1, pl.ds(h, h), :], from_x.at[i, pl.ds(h, h), :],
                sum_send.at[i, 0], sum_recv.at[i, 0], ex, z, c,
            )
        return remote(
            block.at[i, 2, pl.ds(0, h), :], from_y.at[i, pl.ds(0, h), :],
            sum_send.at[i, 1], sum_recv.at[i, 1], ey, z, c,
        )

    def add(target, others, n):
        @pl.loop(0, n // 16)
        def _(b):
            rows = pl.ds(pl.multiple_of(b * 16, 16), 16)
            acc = target[rows, :].astype(f32)
            for o in others:
                acc = acc + o[rows, :].astype(f32)
            target[rows, :] = acc.astype(target.dtype)

    def start(i):
        open_out(i, 0)
        via(i, 0).start()
        via(i, 1).start()
        open_out(i, 1)
        plain(i, 0).start()
        open_out(i, 2)
        plain(i, 1).start()
        open_out(i, 3)

    def combine(i):
        via(i, 0).wait_recv()
        add(block.at[i, 2, pl.ds(0, h), :], [via_x.at[i]], h)
        summed(i, 1).start()
        via(i, 1).wait_recv()
        add(block.at[i, 1, pl.ds(h, h), :], [via_y.at[i]], h)
        summed(i, 0).start()

    def zcopy(i):
        step = jnp.where(dest[i] > z, 1, -1)
        side = jnp.where(dest[i] > z, 0, 1)
        return remote(
            block.at[i, 3], from_z.at[side, dest[i]],
            zsend.at[i], zrecv.at[side, dest[i]], e, z + step, c,
        )

    def zwait(side, zz):
        slab = from_z.at[side, zz]
        remote(slab, slab, zsend.at[0], zrecv.at[side, zz], e, z, c).wait_recv()

    def finish(i):
        for axis in range(2):
            plain(i, axis).wait_recv()
            summed(i, axis).wait_recv()
        zz = dest[i]
        if i < nz - 1:
            add(block.at[i, 3], [from_x.at[i], from_y.at[i]], T)
            for side in range(2):
                going = zz > z if side == 0 else zz < z
                behind = z > 0 if side == 0 else z < nz - 1

                @pl.when(going & behind)
                def _():
                    zwait(side, zz)
                    add(block.at[i, 3], [from_z.at[side, zz]], T)

            zcopy(i).start()
            return

        @pl.loop(0, T // 16)
        def _(b):
            rows = pl.ds(pl.multiple_of(b * 16, 16), 16)
            acc = block[i, 3, rows, :].astype(f32) + from_x[i, rows, :].astype(f32)
            out_ref[rows, :] = acc + from_y[i, rows, :].astype(f32)

        for side in range(2):

            @pl.when(z > 0 if side == 0 else z < nz - 1)
            def _():
                zwait(side, z)
                add(out_ref, [from_z.at[side, z]], T)

    for i in range(nz):
        start(i)
        if i >= 1:
            combine(i - 1)
        if i >= 2:
            finish(i - 2)
    combine(nz - 1)
    if nz >= 2:
        finish(nz - 2)
    finish(nz - 1)

    dot_kept.wait()
    for d, te, tz, tc in others():
        dot(d, te, tz, tc).wait_recv()
        dot(d, te, tz, tc).wait_send()
    dots_out[...] = jnp.sum(dots[...], axis=0)

    for i in range(nz):
        for q in range(4):
            hand(i, q).wait_send()
        for axis in range(2):
            via(i, axis).wait_send()
            plain(i, axis).wait_send()
            summed(i, axis).wait_send()
        if i < nz - 1:
            zcopy(i).wait_send()


def collect_rows(nz, rows, notes, dots, T):
    cap, D = rows.shape[3:]
    dma = pltpu.SemaphoreType.DMA
    vm = pltpu.VMEM
    return pl.pallas_call(
        functools.partial(collect_kernel, nz, cap),
        out_shape=(
            jax.ShapeDtypeStruct((T, D), f32),
            jax.ShapeDtypeStruct(dots.shape[3:], f32),
        ),
        in_specs=[ANY] * 3,
        out_specs=(pl.BlockSpec(memory_space=pltpu.VMEM),) * 2,
        scratch_shapes=[
            vm((8 * nz,) + dots.shape[3:], f32),
            vm(notes.shape, f32),
            vm((nz, 4, cap, D), bf16),
            vm((nz, 4, cap, D), bf16),
            vm((nz, 4, T, D), bf16),
            vm((nz, T, D), bf16),
            vm((nz, T, D), bf16),
            vm((nz, T // 2, D), bf16),
            vm((nz, T // 2, D), bf16),
            vm((2, nz, T, D), bf16),
            dma(()),
            dma((nz, 4)),
            dma((nz, 4)),
            dma((nz, 4)),
            dma((nz, 2)),
            dma((nz, 2)),
            dma((nz, 2)),
            dma((nz, 2)),
            dma((nz, 2)),
            dma((nz, 2)),
            dma((nz,)),
            dma((2, nz)),
            dma((8 * nz,)),
            dma((8 * nz,)),
            dma(()),
        ],
        compiler_params=pltpu.CompilerParams(
            collective_id=3, has_side_effects=True, vmem_limit_bytes=56 << 20
        ),
        cost_estimate=pl.CostEstimate(
            flops=10**6, bytes_accessed=10**6, transcendentals=0
        ),
        name="collect_rows",
    )(rows, notes, dots)


def pack_rows(n, F, Fp, x_ref, *o_refs):
    half = n * F
    rows = x_ref.shape[0]
    for i in range(n):
        for part in range(2):
            cols = x_ref[:, part * half + i * F : part * half + (i + 1) * F]
            if Fp > F:
                cols = jnp.concatenate([cols, jnp.zeros((rows, Fp - F), cols.dtype)], axis=1)
            o_refs[part][i] = cols


def pack_columns(w, n, F, Fp):
    rows = w.shape[0]
    block = 16
    return pl.pallas_call(
        functools.partial(pack_rows, n, F, Fp),
        grid=(rows // block,),
        in_specs=[pl.BlockSpec((block, w.shape[1]), lambda i: (i, 0))],
        out_specs=(pl.BlockSpec((n, block, Fp), lambda i: (0, i, 0)),) * 2,
        out_shape=(jax.ShapeDtypeStruct((n, rows, Fp), w.dtype),) * 2,
        name="pack_columns",
    )(w)


def unpack_kernel(n, F, gate_ref, up_ref, o_ref, line):
    half = n * F
    rows = line.shape[0]
    for i in range(n):
        for part in range(2):
            cols = (up_ref if part else gate_ref)[i, :, :F].astype(f32)
            line[:, part * half + i * F : part * half + (i + 1) * F] = cols
    tiles = 2 * half // 128
    for j in range(tiles):
        o_ref[pl.ds(j, rows, stride=tiles), :] = line[:, j * 128 : (j + 1) * 128]


def unpack_columns(gate, up, F):
    n, rows, Fp = gate.shape
    block = 96 if rows % 96 == 0 else 16
    width = 2 * n * F
    tiles = width // 128
    flat = pl.pallas_call(
        functools.partial(unpack_kernel, n, F),
        grid=(rows // block,),
        in_specs=[pl.BlockSpec((n, block, Fp), lambda i: (0, i, 0))] * 2,
        out_specs=pl.BlockSpec((block * tiles, 128), lambda i: (i, 0)),
        out_shape=jax.ShapeDtypeStruct((rows * tiles, 128), f32),
        scratch_shapes=[pltpu.VMEM((block, width), f32)],
        name="unpack_columns",
    )(gate, up)
    return flat.reshape(rows, 1, width)


def line_kernel(x_ref, o_ref):
    rows, width = x_ref.shape
    tiles = width // 128
    for j in range(tiles):
        o_ref[pl.ds(j, rows, stride=tiles), :] = x_ref[:, j * 128 : (j + 1) * 128]


def lined_up(x, rows):
    width = x.shape[1]
    tiles = width // 128
    block = 240 if rows % 240 == 0 else 8
    flat = pl.pallas_call(
        line_kernel,
        grid=(rows // block,),
        in_specs=[pl.BlockSpec((block, width), lambda i: (i, 0))],
        out_specs=pl.BlockSpec((block * tiles, 128), lambda i: (i, 0)),
        out_shape=jax.ShapeDtypeStruct((rows * tiles, 128), x.dtype),
        name="lined_up",
    )(x)
    return flat.reshape(rows, 1, width)


def greet_cross(nz):
    e, z, c, ex, ey = place()
    barrier = pltpu.get_barrier_semaphore()

    def hail(te, tz, tc):
        pl.semaphore_signal(
            barrier, inc=1, device_id=(te, tz, tc), device_id_type=pl.DeviceIdType.MESH
        )

    hail(e, z, 1 - c)
    for te in (ex, ey, (ex + 2) % 4):
        hail(te, z, c)
    for step in (-1, 1):

        @pl.when((z + step >= 0) & (z + step < nz))
        def _():
            hail(e, z + step, c)

    pl.semaphore_wait(barrier, 4 + jnp.where(z > 0, 1, 0) + jnp.where(z < nz - 1, 1, 0))


def greet_shard(nz):
    e, z, c, ex, ey = place()
    barrier = pltpu.get_barrier_semaphore()
    n = 2 * nz
    peers = [(te, z, c) for te in (ex, ey, (ex + 2) % 4)]
    for d in range(1, n):
        to = (2 * z + c + d) % n
        peers.append((e, to // 2, to % 2))
    for peer in peers:
        pl.semaphore_signal(barrier, inc=1, device_id=peer, device_id_type=pl.DeviceIdType.MESH)
    pl.semaphore_wait(barrier, n + 2)


def scatter_stream(nz, ref, view, send, recv, own):
    e, z, c, _, _ = place()
    n = 2 * nz
    me = 2 * z + c

    def copy(d):
        to = (me + d) % n
        return remote(ref.at[to], view(me), send.at[d], recv.at[d], e, to // 2, to % 2)

    kept = pltpu.make_async_copy(ref.at[me], view(me), own)

    def begin():
        for d in range(1, n):
            copy(d).start()
        kept.start()

    def end():
        kept.wait()
        for d in range(1, n):
            land = view((me + n - d) % n)
            remote(land, land, send.at[d], recv.at[d], e, z, c).wait_recv()
            copy(d).wait_send()

    return begin, end


def scatter_sems(nz):
    dma = pltpu.SemaphoreType.DMA
    return [dma((2 * nz,)), dma((2 * nz,)), dma(())]


def line_stream(nz, ref, out, zrecv, zsend, sib_recv, sib_send, own):
    e, z, c, _, _ = place()

    def split_step(s):
        return (s - 1) % 2, (s - 1) // 2

    def where(s):
        if s == 0:
            return z
        side, i = split_step(s)
        return z - 1 - i if side == 0 else z + 1 + i

    def exists(s):
        return (where(s) >= 0) & (where(s) < nz)

    def inside(side):
        return z < nz - 1 if side == 0 else z > 0

    def slab(s):
        return out.at[where(s), c]

    def first(side):
        step = 1 if side == 0 else -1
        return remote(ref, slab(0), zsend.at[side, nz - 1], zrecv.at[side, 0], e, z + step, c)

    def onward(s):
        side, i = split_step(s)
        step = 1 if side == 0 else -1
        return remote(
            slab(s), slab(s), zsend.at[side, i], zrecv.at[side, i + 1], e, z + step, c
        )

    def beside(s):
        return remote(
            ref if s == 0 else slab(s), slab(s), sib_send.at[s], sib_recv.at[s], e, z, 1 - c
        )

    def begin():
        for side in range(2):

            @pl.when(inside(side))
            def _():
                first(side).start()

        beside(0).start()
        pltpu.make_async_copy(ref, slab(0), own).start()

    def arrive(s):
        side, i = split_step(s)

        @pl.when(exists(s))
        def _():
            remote(slab(s), slab(s), zsend.at[side, i], zrecv.at[side, i], e, z, c).wait_recv()
            if i < nz - 2:

                @pl.when(inside(side))
                def _():
                    onward(s).start()

            beside(s).start()

    def end():
        for s in range(2 * nz - 1):

            @pl.when(exists(s))
            def _():
                beside(s).wait_send()
                view = out.at[where(s), 1 - c]
                remote(view, view, sib_send.at[s], sib_recv.at[s], e, z, c).wait_recv()
                if s > 0 and split_step(s)[1] < nz - 2:

                    @pl.when(inside(split_step(s)[0]))
                    def _():
                        onward(s).wait_send()

        for side in range(2):

            @pl.when(inside(side))
            def _():
                first(side).wait_send()

        pltpu.make_async_copy(ref, slab(0), own).wait()

    return begin, arrive, end


def line_sems(nz):
    dma = pltpu.SemaphoreType.DMA
    S = 2 * nz - 1
    return [dma((2, nz)), dma((2, nz)), dma((S,)), dma((S,)), dma(())]


def plane_stream(source, views, send, recv, own):
    e, z, c, ex, ey = place()
    peers = (ex, ey, (ex + 2) % 4)

    def copy(n):
        return remote(source, views(e), send.at[n], recv.at[n], peers[n], z, c)

    def kept():
        return pltpu.make_async_copy(source, views(e), own)

    def begin():
        for n in range(3):
            copy(n).start()
        kept().start()

    def end():
        kept().wait()
        for n in range(3):
            view = views(peers[n])
            remote(view, view, send.at[n], recv.at[n], e, z, c).wait_recv()
            copy(n).wait_send()

    return begin, end


def plane_sems():
    dma = pltpu.SemaphoreType.DMA
    return [dma((3,)), dma((3,)), dma(())]


def fetch_kernel(
    nz,
    F, w_ref, s_ref, o_ref, t_ref, l_ref, p_ref, x_ref,
    w_out, s_out, o_out, t_out, l_out, p_out, gate_out, up_out,
    wide, gate, up, wide_sem, packed_sem,
    *sems,
):
    e, z, c, ex, ey = place()
    w_sems, sems = sems[:5], sems[5:]
    s_sems, sems = sems[:5], sems[5:]
    t_sems, sems = sems[:3], sems[3:]
    l_sems, sems = sems[:3], sems[3:]
    p_sems, sems = sems[:9], sems[9:]
    orecv, osend, sib_recv, sib_send, own = sems
    wide_copy = pltpu.make_async_copy(x_ref, wide, wide_sem)
    wide_copy.start()
    greet_cross(nz)
    w_begin, w_arrive, w_end = line_stream(nz, w_ref, w_out, *w_sems)
    s_begin, s_arrive, s_end = line_stream(nz, s_ref, s_out, *s_sems)
    t_begin, t_end = plane_stream(t_ref, lambda q: t_out.at[q], *t_sems)
    l_begin, l_end = plane_stream(l_ref, lambda q: l_out.at[q], *l_sems)
    p_begin, p_arrive, p_relay, p_close, p_end = payload_stream(
        nz, p_ref, p_out, p_sems, p_ref.shape[0] // 2
    )

    pieces = orecv.shape[0]
    height = o_ref.shape[0] // pieces

    def o_part(n):
        return pl.ds(n * height, height)

    def o_view(n):
        return o_out.at[c, o_part(n), :]

    def o_copy(side, n, source):
        step = 1 if side == 0 else -1
        return remote(source, o_view(n), osend.at[side, n], orecv.at[n], e, z + step, c)

    def o_beside(n, source):
        return remote(source, o_view(n), sib_send.at[n], sib_recv.at[n], e, z, 1 - c)

    def o_goes(side):
        return (z >= e) & (z < nz - 1) if side == 0 else (z <= e) & (z > 0)

    def o_pass(n, source):
        for side in range(2):

            @pl.when(o_goes(side))
            def _():
                o_copy(side, n, source).start()

        o_beside(n, source).start()

    def o_arrive(n):
        @pl.when(z != e)
        def _():
            remote(o_view(n), o_view(n), sib_send.at[n], orecv.at[n], e, z, c).wait_recv()
            o_pass(n, o_view(n))

    p_begin()

    @pl.when(z == e)
    def _():
        for n in range(pieces):
            o_pass(n, o_ref.at[o_part(n), :])
        pltpu.make_async_copy(o_ref, o_out.at[c], own).start()

    s_begin()
    w_begin()
    t_begin()
    l_begin()

    wide_copy.wait()

    @pl.loop(0, wide.shape[0] // 16)
    def _(b):
        rows = pl.ds(pl.multiple_of(b * 16, 16), 16)
        pack_rows(
            gate.shape[0], F, gate.shape[2], wide.at[rows, :], gate.at[:, rows, :], up.at[:, rows, :]
        )

    packed_copies = [
        pltpu.make_async_copy(a, b, packed_sem.at[n])
        for n, (a, b) in enumerate(((gate, gate_out), (up, up_out)))
    ]
    for copy in packed_copies:
        copy.start()

    blocks = 2 * nz - 1
    for s in range(1, blocks):
        p_arrive(s)
        s_arrive(s)
        if s <= pieces:
            o_arrive(s - 1)
    for n in range(blocks - 1, pieces):
        o_arrive(n)
    for s in range(1, blocks):
        p_relay(s - 1)
        w_arrive(s)
        if s >= 2:
            p_close(s - 2)
    p_relay(blocks - 1)
    p_close(blocks - 2)
    p_close(blocks - 1)
    for s in range(blocks):
        p_end(s)
    w_end()
    s_end()
    t_end()
    l_end()
    for n in range(pieces):
        view = o_out.at[1 - c, o_part(n), :]
        remote(view, view, sib_send.at[n], sib_recv.at[n], e, z, c).wait_recv()
        o_beside(n, o_view(n)).wait_send()
        for side in range(2):

            @pl.when(o_goes(side))
            def _():
                o_copy(side, n, o_view(n)).wait_send()

    @pl.when(z == e)
    def _():
        pltpu.make_async_copy(o_ref, o_out.at[c], own).wait()

    for copy in packed_copies:
        copy.wait()


def fetch_weights(nz, columns, small, rows, tokens, lengths, block, wide, F):
    dma = pltpu.SemaphoreType.DMA
    packed = (2 * nz, wide.shape[0], -(-F // 128) * 128)
    sd = jax.ShapeDtypeStruct
    return pl.pallas_call(
        functools.partial(fetch_kernel, nz, F),
        out_shape=(
            sd((nz, 2) + columns.shape, bf16),
            sd((nz, 2) + small.shape, bf16),
            sd((2,) + rows.shape, bf16),
            sd((4,) + tokens.shape, bf16),
            sd((4,) + lengths.shape, lengths.dtype),
            sd((nz, 2, 4) + block.shape, block.dtype),
            sd(packed, wide.dtype),
            sd(packed, wide.dtype),
        ),
        in_specs=[ANY] * 7,
        out_specs=(ANY,) * 8,
        scratch_shapes=[
            pltpu.VMEM(wide.shape, wide.dtype), pltpu.VMEM(packed, wide.dtype),
            pltpu.VMEM(packed, wide.dtype), dma(()), dma((2,)),
            *line_sems(nz), *line_sems(nz), *plane_sems(), *plane_sems(), *payload_sems(nz),
            dma((6,)), dma((2, 6)), dma((6,)), dma((6,)), dma(()),
        ],
        compiler_params=pltpu.CompilerParams(
            collective_id=0, has_side_effects=True, vmem_limit_bytes=60 << 20
        ),
        cost_estimate=pl.CostEstimate(
            flops=10**11, bytes_accessed=8 * columns.size, transcendentals=0
        ),
        name="fetch_weights",
    )(columns, small, rows, tokens, lengths, block, wide)


def plane_gather_kernel(
    x_ref, a_ref, r_ref, out_ref, d_ref, left, right, prod, load, store, send, recv, own
):
    loads = [
        pltpu.make_async_copy(a_ref, left, load.at[0]),
        pltpu.make_async_copy(r_ref, right, load.at[1]),
    ]
    for copy in loads:
        copy.start()
    greet_plane()
    begin, end = plane_stream(x_ref, lambda q: out_ref.at[q], send, recv, own)
    begin()
    for copy in loads:
        copy.wait()
    tiles, step = store.shape[0], prod.shape[1] // store.shape[0]

    def done(n):
        cols = pl.ds(n * step, step)
        return pltpu.make_async_copy(prod.at[:, cols], d_ref.at[:, cols], store.at[n])

    for n in range(tiles):

        @pl.loop(0, prod.shape[0] // 256)
        def _(m):
            rows = pl.ds(pl.multiple_of(m * 256, 256), 256)
            prod[rows, n * step : (n + 1) * step] = jnp.dot(
                left[rows, :], right[:, n * step : (n + 1) * step], preferred_element_type=f32
            )

        done(n).start()
    for n in range(tiles):
        done(n).wait()
    end()


def greet_plane():
    e, z, c, ex, ey = place()
    barrier = pltpu.get_barrier_semaphore()
    for te in (ex, ey, (ex + 2) % 4):
        pl.semaphore_signal(
            barrier, inc=1, device_id=(te, z, c), device_id_type=pl.DeviceIdType.MESH
        )
    pl.semaphore_wait(barrier, 3)


def plane_gather(x, left, right, collective):
    M, N = left.shape[0], right.shape[1]
    dma = pltpu.SemaphoreType.DMA
    vm = pltpu.VMEM
    return pl.pallas_call(
        plane_gather_kernel,
        out_shape=(
            jax.ShapeDtypeStruct((4,) + x.shape, x.dtype),
            jax.ShapeDtypeStruct((M, N), f32),
        ),
        in_specs=[ANY] * 3,
        out_specs=(ANY,) * 2,
        scratch_shapes=[
            vm(left.shape, bf16), vm(right.shape, bf16), vm((M, N), f32),
            dma((2,)), dma((N // 256,)), *plane_sems(),
        ],
        compiler_params=pltpu.CompilerParams(
            collective_id=collective, has_side_effects=True, vmem_limit_bytes=48 << 20
        ),
        cost_estimate=pl.CostEstimate(flops=10**6, bytes_accessed=10**6, transcendentals=0),
        name="plane_gather",
    )(x, left, right)


def plane_sum_parts(x_ref, out_ref, held, send, recv, own):
    e, z, c, ex, ey = place()
    peers = (ex, ey, (ex + 2) % 4)

    def copy(n):
        return remote(x_ref.at[peers[n]], held.at[n], send.at[n], recv.at[n], peers[n], z, c)

    kept = pltpu.make_async_copy(x_ref.at[e], held.at[3], own)

    def total():
        kept.wait()
        for n in range(3):
            copy(n).wait_recv()

        @pl.loop(0, out_ref.shape[0] // 16)
        def _(b):
            rows = pl.ds(pl.multiple_of(b * 16, 16), 16)
            acc = held[3, rows, :].astype(f32) + held[0, rows, :].astype(f32)
            acc = acc + held[1, rows, :].astype(f32)
            out_ref[rows, :] = acc + held[2, rows, :].astype(f32)

    return copy, kept, total


def plane_sum_kernel(x_ref, out_ref, held, send, recv, own):
    greet_plane()
    copy, kept, total = plane_sum_parts(x_ref, out_ref, held, send, recv, own)
    for n in (2, 0, 1):
        copy(n).start()
    kept.start()
    total()
    for n in range(3):
        copy(n).wait_send()


def plane_sum(x, collective):
    vm = pltpu.VMEM
    return pl.pallas_call(
        plane_sum_kernel,
        out_shape=jax.ShapeDtypeStruct(x.shape[1:], f32),
        in_specs=[ANY],
        out_specs=pl.BlockSpec(memory_space=vm),
        scratch_shapes=[vm(x.shape, bf16), *plane_sems()],
        compiler_params=pltpu.CompilerParams(collective_id=collective, has_side_effects=True),
        cost_estimate=pl.CostEstimate(flops=10**6, bytes_accessed=10**6, transcendentals=0),
        name="plane_sum",
    )(x)


def settle_kernel(
    nz,
    g_ref, s_ref, o_ref, x_ref, y_ref,
    g_out, s_out, o_out, x_out, y_out,
    x_held, x_send, x_recv, x_own, y_send, y_recv, y_own,
    g_mine, g_sib, g_z, s_mine, s_sib, s_z, o_mine, o_sib, o_z,
    load, sib_send, sib_recv, zsend, zrecv,
    o_load, o_sib_send, o_sib_recv, o_zsend, o_zrecv,
    o_send, o_recv, o_own,
    *sems,
):
    e, z, c, ex, ey = place()
    peers = (ex, ey, (ex + 2) % 4)
    dest = line_order(nz, z)
    greet_cross(nz)
    W = g_ref.shape[3]
    first = W // 256 * 128
    groups = (
        (g_ref, g_mine, g_sib, g_z, g_out, pl.ds(0, first)),
        (g_ref, g_mine, g_sib, g_z, g_out, pl.ds(first, W - first)),
        (s_ref, s_mine, s_sib, s_z, s_out, pl.ds(0, s_ref.shape[3])),
    )
    K = len(groups)

    def part(k, which, *index):
        return groups[k][which].at[(*index, slice(None), groups[k][5])]

    def fetch(k, i):
        return pltpu.make_async_copy(
            part(k, 0, dest[i], c), part(k, 1, i), load.at[k, i]
        )

    def hand(k, i):
        return remote(
            part(k, 0, dest[i], 1 - c), part(k, 2, i),
            sib_send.at[k, i], sib_recv.at[k, i], e, z, 1 - c,
        )

    def zcopy(k, i):
        step = jnp.where(dest[i] > z, 1, -1)
        side = jnp.where(dest[i] > z, 0, 1)
        return remote(
            part(k, 1, i), part(k, 3, side, dest[i]),
            zsend.at[k, i], zrecv.at[k, side, dest[i]], e, z + step, c,
        )

    def zwait(k, side, zz):
        slab = part(k, 3, side, zz)
        remote(slab, slab, zsend.at[k, 0], zrecv.at[k, side, zz], e, z, c).wait_recv()

    def add(target, others):
        @pl.loop(0, target.shape[0] // 16)
        def _(b):
            rows = pl.ds(pl.multiple_of(b * 16, 16), 16)
            acc = target[rows, :].astype(f32)
            for o in others:
                acc = acc + o[rows, :].astype(f32)
            target[rows, :] = acc.astype(target.dtype)

    pieces = o_load.shape[0]
    height = o_mine.shape[0] // pieces

    def o_part(n):
        return pl.ds(n * height, height)

    def o_fetch(n):
        return pltpu.make_async_copy(o_ref.at[c, o_part(n), :], o_mine.at[o_part(n), :], o_load.at[n])

    def o_hand(n):
        return remote(
            o_ref.at[1 - c, o_part(n), :], o_sib.at[o_part(n), :],
            o_sib_send.at[n], o_sib_recv.at[n], e, z, 1 - c,
        )

    def o_line(n):
        step, side = jnp.where(z < e, 1, -1), jnp.where(z < e, 0, 1)
        return remote(
            o_mine.at[o_part(n), :], o_z.at[side, o_part(n), :],
            o_zsend.at[n], o_zrecv.at[side, n], e, z + step, c,
        )

    def o_wait(side, n):
        slab = o_z.at[side, o_part(n), :]
        remote(slab, slab, o_zsend.at[n], o_zrecv.at[side, n], e, z, c).wait_recv()
        add(o_mine.at[o_part(n), :], [slab])

    def o_peer(p, n):
        view = o_out.at[o_part(n), :]
        return remote(
            o_mine.at[o_part(n), :], view, o_send.at[p, n], o_recv.at[n], peers[p], z, c
        )

    def o_kept():
        return pltpu.make_async_copy(o_mine, o_out, o_own)

    for i in range(nz):
        for k in range(K):
            hand(k, i).start()
            fetch(k, i).start()
        if i == 0:
            for n in range(pieces):
                o_fetch(n).start()
                o_hand(n).start()

    def finish(k, i):
        fetch(k, i).wait()
        hand(k, i).wait_recv()
        zz = dest[i]
        add(part(k, 1, i), [part(k, 2, i)])
        if i < nz - 1:
            for side in range(2):
                going = zz > z if side == 0 else zz < z
                behind = z > 0 if side == 0 else z < nz - 1

                @pl.when(going & behind)
                def _():
                    zwait(k, side, zz)
                    add(part(k, 1, i), [part(k, 3, side, zz)])

            zcopy(k, i).start()
            return
        for side in range(2):

            @pl.when(z > 0 if side == 0 else z < nz - 1)
            def _():
                zwait(k, side, z)
                add(part(k, 1, i), [part(k, 3, side, z)])

        streams[k][0]()

    x_copy, x_kept, x_total = plane_sum_parts(x_ref, x_out, x_held, x_send, x_recv, x_own)
    for p in (2, 0, 1):
        x_copy(p).start()
    x_kept.start()

    def y_copy(p):
        return remote(
            y_ref.at[peers[p]], y_out.at[e], y_send.at[p], y_recv.at[p], peers[p], z, c
        )

    y_kept = pltpu.make_async_copy(y_ref.at[e], y_out.at[e], y_own)
    y_kept.start()
    for p in range(3):
        y_copy(p).start()

    def o_flow(n):
        o_fetch(n).wait()
        o_hand(n).wait_recv()
        add(o_mine.at[o_part(n), :], [o_sib.at[o_part(n), :]])
        for side in range(2):
            behind = (z > 0) & (z <= e) if side == 0 else (z < nz - 1) & (z >= e)

            @pl.when(behind)
            def _():
                o_wait(side, n)

        @pl.when(z != e)
        def _():
            o_line(n).start()

        @pl.when(z == e)
        def _():
            for p in range(3):
                o_peer(p, n).start()

    streams = [
        plane_stream(
            part(k, 1, nz - 1), lambda q, k=k: part(k, 4, q), *sems[3 * k : 3 * k + 3]
        )
        for k in range(K)
    ]
    turn = K * nz // 2
    order = []
    for k in range(K):
        order += [(k, i) for i in range(1 if k else 0, nz - 1)]
        if k + 1 < K:
            order.append((k + 1, 0))
        order.append((k, nz - 1))
    for n, (k, i) in enumerate(order):
        finish(k, i)
        if n == 0:
            for m in range(pieces):
                o_flow(m)
        if n == turn:
            x_total()

    @pl.when(z == e)
    def _():
        o_kept().start()
        o_kept().wait()
        for n in range(pieces):
            for p in range(3):
                o_peer(p, n).wait_send()

    @pl.when(z != e)
    def _():
        for n in range(pieces):
            view = o_out.at[o_part(n), :]
            remote(view, view, o_send.at[0, n], o_recv.at[n], e, z, c).wait_recv()
            o_line(n).wait_send()

    y_kept.wait()
    for p in range(3):
        x_copy(p).wait_send()
        view = y_out.at[peers[p]]
        remote(view, view, y_send.at[p], y_recv.at[p], e, z, c).wait_recv()
        y_copy(p).wait_send()
    for n in range(pieces):
        o_hand(n).wait_send()
    for i in range(nz):
        for k in range(K):
            hand(k, i).wait_send()
            if i < nz - 1:
                zcopy(k, i).wait_send()
    for _, end in streams:
        end()


def settle_weights(nz, grads, small, rows, near, blocks):
    R, W = grads.shape[2:]
    D = rows.shape[2]
    dma = pltpu.SemaphoreType.DMA
    sd = jax.ShapeDtypeStruct
    vm = pltpu.VMEM
    Ws = small.shape[3]
    return pl.pallas_call(
        functools.partial(settle_kernel, nz),
        out_shape=(
            sd((4, R, W), bf16),
            sd((4, R, Ws), bf16),
            sd((R, D), bf16),
            sd(near.shape[1:], f32),
            sd(blocks.shape, bf16),
        ),
        in_specs=[ANY] * 5,
        out_specs=(ANY,) * 3 + (pl.BlockSpec(memory_space=vm), ANY),
        scratch_shapes=[
            vm(near.shape, bf16), *plane_sems(), *plane_sems(),
            vm((nz, R, W), bf16), vm((nz, R, W), bf16), vm((2, nz, R, W), bf16),
            vm((nz, R, Ws), bf16), vm((nz, R, Ws), bf16), vm((2, nz, R, Ws), bf16),
            vm((R, D), bf16), vm((R, D), bf16), vm((2, R, D), bf16),
            dma((3, nz)), dma((3, nz)), dma((3, nz)), dma((3, nz)), dma((3, 2, nz)),
            dma((6,)), dma((6,)), dma((6,)), dma((6,)), dma((2, 6)),
            dma((3, 6)), dma((6,)), dma(()),
            *plane_sems(), *plane_sems(), *plane_sems(),
        ],
        compiler_params=pltpu.CompilerParams(
            collective_id=1, has_side_effects=True, vmem_limit_bytes=56 << 20
        ),
        cost_estimate=pl.CostEstimate(flops=10**6, bytes_accessed=10**6, transcendentals=0),
        name="settle_weights",
    )(grads, small, rows, near, blocks)


def pick_kernel(width, q_ref, k_ref, v_ref, o_ref):
    e = lax.axis_index("expert")
    spare = o_ref.shape[1] - 3 * width
    if spare:
        o_ref[:, 3 * width :] = jnp.zeros((o_ref.shape[0], spare), o_ref.dtype)
    for n in range(4):

        @pl.when(e == n)
        def _():
            for i, ref in enumerate((q_ref, k_ref, v_ref)):
                o_ref[:, i * width : (i + 1) * width] = ref[:, n * width : (n + 1) * width]


def pick_columns(weights, width):
    vm = pl.BlockSpec(memory_space=pltpu.VMEM)
    return pl.pallas_call(
        functools.partial(pick_kernel, width),
        in_specs=[vm] * 3,
        out_specs=vm,
        out_shape=jax.ShapeDtypeStruct((weights[0].shape[0], -(-3 * width // 128) * 128), bf16),
        name="pick_columns",
    )(*weights)


def assemble_kernel(width, x_ref, *o_refs):
    for n in range(4):
        for i in range(3):
            cols = x_ref[n, :, i * width : (i + 1) * width]
            o_refs[i][:, n * width : (n + 1) * width] = cols.astype(f32)


def assemble_columns(x, width):
    R = x.shape[1]
    block = 96 if R % 96 == 0 else 16
    return pl.pallas_call(
        functools.partial(assemble_kernel, width),
        grid=(R // block,),
        in_specs=[pl.BlockSpec((4, block, x.shape[2]), lambda i: (0, i, 0))],
        out_specs=(pl.BlockSpec((block, 4 * width), lambda i: (i, 0)),) * 3,
        out_shape=(jax.ShapeDtypeStruct((R, 4 * width), f32),) * 3,
        name="assemble_columns",
    )(x)


def sum_shard(x, axis=0):
    mine = lax.psum_scatter(x, SHARD, scatter_dimension=axis, tiled=True)
    return lax.psum(mine, "expert")


def fetch(nz, fast, weights, w_output, small, tokens, lengths, block, wide, F):
    D = tokens.shape[1]
    if fast:
        width = D // 4
        columns, full_small, rows, tokens, lengths, blocks, *packed = fetch_weights(
            nz, pick_columns(weights, width), small, w_output, tokens, lengths, block, wide, F
        )
        columns, rows = columns.reshape(D, -1), rows.reshape(width, D)
        return columns, rows, full_small.reshape(D, -1), tokens, lengths, blocks, packed
    full = [lax.all_gather(w, SHARD, axis=0, tiled=True) for w in weights + (w_output, small)]
    blocks = spread_plain(nz, (block,), 0)[0]
    packed = pack_columns(wide, 2 * nz, F, -(-F // 128) * 128)
    columns = jnp.concatenate(full[:3], axis=1)
    return columns, full[3], full[4], tokens[None], lengths[None], blocks, packed


def settle(nz, fast, columns, rows, small, near, blocks):
    D, width = rows.shape[1], rows.shape[0]
    if fast:
        R = D // (2 * nz)
        parts = [x.astype(bf16).reshape(nz, 2, R, -1) for x in (columns, small)]
        near = near.astype(bf16).reshape(4, -1, D)
        blocks = blocks.reshape(4, -1, D)
        sums, small, out, near, blocks = settle_weights(
            nz, *parts, rows.astype(bf16).reshape(2, R, D), near, blocks
        )
        small, blocks = jnp.sum(small.astype(f32), axis=0), blocks.reshape(-1, D)
        return *assemble_columns(sums, width), out.astype(f32), small, near, blocks
    parts = [columns[:, i * width : (i + 1) * width] for i in range(3)] + [rows, small]
    blocks = lax.all_to_all(blocks, "expert", split_axis=0, concat_axis=0, tiled=True)
    return [sum_shard(x) for x in parts] + [near, blocks]


def spread_plain(nz, blocks, collective):
    out = []
    for block in blocks:
        for axis in ("expert", "core", "z"):
            block = lax.all_gather(block, axis, axis=0)
        out.append(block)
    return out


def spread_pair(nz, blocks, gate, up, collective):
    gate = lax.all_to_all(gate, SHARD, split_axis=0, concat_axis=0, tiled=True)
    return jnp.concatenate([gate, up], axis=2), *spread_plain(nz, blocks, collective)


def collect_plain(nz, rows, notes, dots, T):
    n_exp, cap, D = rows.shape[2:]
    places = (lax.axis_index("expert") * cap + jnp.arange(cap)).astype(f32)
    notes = notes[..., :T]
    pick = (notes[..., 2, None, :] == places[:, None]) | (notes[..., 3, None, :] == places[:, None])
    part = jnp.einsum(
        "zceps,zcepd->zcesd", pick.astype(bf16), rows, preferred_element_type=f32
    ).astype(bf16)
    part = part.transpose(2, 0, 1, 3, 4).reshape(n_exp * nz * 2 * T, D)
    part = lax.psum_scatter(part, "expert", scatter_dimension=0, tiled=True)
    part = lax.psum_scatter(part, SHARD, scatter_dimension=0, tiled=True).astype(f32)
    z, core, e = lax.axis_index("z"), lax.axis_index("core"), lax.axis_index("expert")
    return part, lax.psum(dots, ("expert",) + SHARD)[z, core, e]


def rope_tables(positions, head_width):
    half_width = head_width // 2
    exponents = jnp.arange(half_width).astype(f32) * 2.0 / head_width
    frequency = rope_base ** (-exponents)
    angles = positions.astype(f32)[..., None] * frequency
    return (jnp.cos(angles), jnp.sin(angles))


def rotate(values, cosine, sine_table):
    half_width = values.shape[-1] // 2
    leading = values[..., :half_width]
    trailing = values[..., half_width:]
    cos_rows = cosine[:, :, None, :]
    sin_rows = sine_table[:, :, None, :]
    return jnp.concatenate(
        [leading * cos_rows - trailing * sin_rows, trailing * cos_rows + leading * sin_rows],
        axis=-1,
    )


def rms_forward(values, norm_gain):
    inverse = lax.rsqrt(jnp.mean(values * values, axis=-1, keepdims=True) + eps_norm)
    return (values * inverse * norm_gain, inverse)


def rms_backward(values, inverse, norm_gain, upstream):
    weighted = upstream * norm_gain
    gain_grad = jnp.sum(upstream * values * inverse, axis=0)
    inner_mean = jnp.mean(weighted * values, axis=-1, keepdims=True)
    return (inverse * weighted - values * inverse * inverse * inverse * inner_mean, gain_grad)


def dot32(a, b):
    return jnp.dot(a, b, preferred_element_type=f32)


def dot_dims(a, b, da, db):
    return lax.dot_general(a, b, (((da,), (db,)), ((), ())), preferred_element_type=f32)


def ein32(spec, a, b):
    return jnp.einsum(spec, a, b, preferred_element_type=f32)


def on_device(
    tokens,
    seq_lengths,
    routes,
    norm_attn,
    w_query,
    w_key,
    w_value,
    w_output,
    norm_ffn,
    w_router,
    w_in,
    w_down,
    cotangent,
):
    T, D = tokens.shape
    R = w_query.shape[0]
    head_width = D // HEADS
    n_exp = lax.axis_size("expert")
    nz = lax.axis_size("z")
    n_shard = nz * lax.axis_size("core")
    experts = w_router.shape[1]
    F = w_down.shape[0]
    FF = F * n_shard
    capacity = 10 * T // (4 * experts)
    slots = experts * capacity
    highest = lax.Precision.HIGHEST
    e_index = lax.axis_index("expert")
    fast = n_exp == 4 and nz == 4

    small = jnp.concatenate([w_router, norm_attn[:, None], norm_ffn[:, None]], axis=1)
    small = jnp.pad(small, ((0, 0), (0, 128 - small.shape[1])))
    length_rows = jnp.broadcast_to(seq_lengths[:, :1], (8, 128))
    full_qkv, full_output, full_small, near_tokens, near_lengths, all_cotangent, packed = fetch(
        nz,
        fast,
        (w_query, w_key, w_value),
        w_output,
        small,
        tokens,
        length_rows,
        cotangent,
        w_in.reshape(R, 2 * FF),
        F,
    )
    full_router = full_small[:, :experts]
    gain_attn = full_small[:, experts].astype(f32)
    gain_ffn = full_small[:, experts + 1].astype(f32)

    Fp = -(-F // 128) * 128
    moved_up = lax.all_to_all(packed[1], SHARD, split_axis=0, concat_axis=0, tiled=True)
    down = jnp.pad(w_down.reshape(F, D), ((0, Fp - F), (0, 0)))

    B, H = near_tokens.shape[0], full_output.shape[0]
    heads = H // head_width
    residual_in = tokens.astype(f32)
    inverse_in = rms_forward(residual_in, gain_attn)[1]
    near_in = near_tokens.reshape(B * T, D).astype(f32)
    near_normed, near_inverse = rms_forward(near_in, gain_attn)
    normed_half = near_normed.astype(bf16)
    lengths = near_lengths[:, 0, 0]
    row_index = jnp.arange(T)
    segment = (row_index[None, :] >= lengths[:, None]).astype(jnp.int32)
    positions = row_index[None, :] - lengths[:, None] * segment
    allowed = (segment[:, :, None] == segment[:, None, :]) & (
        row_index[None, None, :] <= row_index[None, :, None]
    )
    cosine, sine_table = rope_tables(positions, head_width)
    head_shape = (B, T, heads, head_width)
    qkv = dot32(normed_half, full_qkv)
    queries = rotate(qkv[:, :H].reshape(head_shape), cosine, sine_table).astype(bf16)
    keys_rot = rotate(qkv[:, H : 2 * H].reshape(head_shape), cosine, sine_table).astype(bf16)
    values = qkv[:, 2 * H : 3 * H].astype(bf16).reshape(head_shape)
    score_scale = 1.0 / math.sqrt(head_width)
    scores = ein32("bqhd,bkhd->bhqk", queries, keys_rot) * score_scale
    scores = jnp.where(allowed[:, None], scores, masked_score)
    row_peak = jnp.max(scores, axis=-1, keepdims=True)
    log_total = row_peak + jnp.log(jnp.sum(jnp.exp(scores - row_peak), axis=-1, keepdims=True))
    attn_probs = jnp.exp(scores - log_total)
    probs_half = attn_probs.astype(bf16)
    context = ein32("bhqk,bkhd->bqhd", probs_half, values).astype(bf16)
    context_flat = context.reshape(B * T, H)

    def at_home(partial_rows, collective):
        if not fast:
            return partial_rows
        return plane_sum(partial_rows.astype(bf16).reshape(B, T, D), collective)

    residual_mid = residual_in + branch_scale * at_home(dot32(context_flat, full_output), 4)
    normed_mid, inverse_mid = rms_forward(residual_mid, gain_ffn)
    normed_mid_half = normed_mid.astype(bf16)

    logits = dot32(normed_mid_half, full_router)
    expert_ids = jnp.arange(experts)
    route_mask = (routes[:, :, None] == expert_ids[None, None, :]).astype(f32)
    chosen = jnp.sum(logits[:, None, :] * route_mask, axis=-1)
    gate_probs = jax.nn.softmax(chosen, axis=-1)
    flat_routes = routes.reshape(2 * T)
    hits = (flat_routes[:, None] == expert_ids[None, :]).astype(bf16)
    order = jnp.arange(2 * T)
    before = (order[:, None] > order[None, :]).astype(bf16)
    earlier = dot32(before, hits)
    slot_index = jnp.sum(earlier * hits.astype(f32), axis=1).astype(jnp.int32)
    target = (flat_routes * capacity + slot_index).reshape(T, 2)
    slot_ids = jnp.arange(slots)
    pick = [(target[:, k][:, None] == slot_ids[None, :]).astype(bf16) for k in range(2)]

    notes = jnp.concatenate([gate_probs, target.astype(f32), jnp.zeros((T, 4), f32)], axis=1)
    notes = jnp.pad(jnp.transpose(notes), ((0, 0), (0, -T % 128)))
    spread = spread_blocks if fast else spread_pair
    w_pair, all_normed, all_notes = spread(nz, (normed_mid_half, notes), packed[0], moved_up, 2)
    w_pair = w_pair.reshape(n_shard * R, 2 * Fp)
    devices = n_shard * n_exp
    flat_notes = all_notes.reshape(devices, 8, -1)[:, :, :T]
    wanted = (e_index * capacity + jnp.arange(capacity)).astype(f32)
    found = [flat_notes[:, 2 + k, None, :] == wanted[None, :, None] for k in range(2)]
    gate_rows = jnp.sum(
        jnp.where(found[0], flat_notes[:, 0, None, :], 0.0)
        + jnp.where(found[1], flat_notes[:, 1, None, :], 0.0),
        axis=-1,
    ).reshape(devices * capacity, 1)
    chosen_rows = (found[0] | found[1]).astype(bf16)

    def take(blocks):
        rows = ein32("spt,std->spd", chosen_rows, blocks.reshape(devices, T, D))
        return rows.astype(bf16).reshape(devices * capacity, D)

    arrived = take(all_normed)
    grad_scale = gate_rows * branch_scale
    pre = dot32(arrived, w_pair)
    gate_part, up_part = pre[:, :Fp], pre[:, Fp:]
    sigmoid_gate = jax.nn.sigmoid(gate_part)
    silu_gate = gate_part * sigmoid_gate
    activated = (silu_gate * up_part).astype(bf16)
    out_rows, all_cotangent = lax.optimization_barrier(
        (dot32(activated, down).astype(bf16), all_cotangent)
    )
    out_sum = lax.psum_scatter(out_rows, SHARD, scatter_dimension=0, tiled=True)
    cotangent_rows = take(all_cotangent)

    raw_grad = dot_dims(cotangent_rows, down, 1, 1)
    row_dots = branch_scale * jnp.sum(raw_grad * activated.astype(f32), axis=1)
    row_dots = row_dots.reshape(devices, capacity, 1)
    token_dots = [jnp.sum(jnp.where(found[k], row_dots, 0.0), axis=1) for k in range(2)]
    token_dots = jnp.stack(token_dots, axis=1).reshape(nz, 2, n_exp, 2, T)
    token_dots = jnp.pad(token_dots, ((0, 0),) * 3 + ((0, 6), (0, -T % 128)))
    act_grad = grad_scale * raw_grad
    gate_grads = act_grad * up_part * sigmoid_gate * (1.0 + gate_part * (1.0 - sigmoid_gate))
    gate_grads, up_grads = gate_grads.astype(bf16), (act_grad * silu_gate).astype(bf16)
    pre_grad = jnp.concatenate([gate_grads, up_grads], axis=1)
    in_rows = dot_dims(pre_grad, w_pair, 1, 1).astype(bf16)
    scaled = (grad_scale * activated.astype(f32)).astype(bf16)
    gate_term, up_term = [
        dot_dims(arrived, x, 0, 0).astype(bf16).reshape(n_shard, R, Fp)
        for x in (gate_grads, up_grads)
    ]
    gate_term, up_term = lax.optimization_barrier((gate_term, up_term))
    up_term = lax.all_to_all(up_term, SHARD, split_axis=0, concat_axis=0, tiled=True)
    in_rows = in_rows.reshape(nz, 2, n_exp, capacity, D)
    collect = collect_rows if fast else collect_plain
    normed_mid_grad, gate_grad = collect(nz, in_rows, all_notes, token_dots, T)
    gate_grad = jnp.transpose(gate_grad[:2, :T])
    up_term, normed_mid_grad, out_sum, gate_term = lax.optimization_barrier(
        (up_term, normed_mid_grad, out_sum, gate_term)
    )
    gate_term = lax.all_to_all(gate_term, SHARD, split_axis=0, concat_axis=0, tiled=True)

    upstream = cotangent.astype(f32)
    chosen_grad = gate_probs * (gate_grad - jnp.sum(gate_probs * gate_grad, axis=-1, keepdims=True))
    logit_grad = jnp.sum(chosen_grad[:, :, None] * route_mask, axis=1)
    normed_mid_grad = normed_mid_grad + jnp.dot(
        logit_grad, jnp.transpose(full_router.astype(f32)), precision=highest
    )
    router_grad = jnp.dot(
        jnp.transpose(normed_mid_half.astype(f32)), logit_grad, precision=highest
    )
    mid_norm_grad, gain_ffn_grad = rms_backward(
        residual_mid, inverse_mid, gain_ffn, normed_mid_grad
    )
    residual_grad = upstream + mid_norm_grad
    branch_grad = (branch_scale * residual_grad).astype(bf16)

    if fast:
        branch_grad, down_term = plane_gather(
            branch_grad, jnp.transpose(scaled), cotangent_rows, 5
        )
        branch_grad = branch_grad.reshape(B * T, D)
    else:
        down_term = dot_dims(scaled, cotangent_rows, 0, 0)
    grad_w_down = lined_up(down_term, F)
    output_grad = dot_dims(context_flat, branch_grad, 0, 0)
    context_grad = dot_dims(branch_grad, full_output, 1, 1).reshape(head_shape)
    row_delta = jnp.sum(context_grad * context.astype(f32), axis=-1)
    context_grad_half = context_grad.astype(bf16)
    probs_grad = ein32("bqhd,bkhd->bhqk", context_grad_half, values)
    scores_grad = (
        attn_probs * (probs_grad - jnp.transpose(row_delta, (0, 2, 1))[..., None]) * score_scale
    ).astype(bf16)
    queries_grad = ein32("bhqk,bkhd->bqhd", scores_grad, keys_rot)
    keys_grad = ein32("bhqk,bqhd->bkhd", scores_grad, queries)
    values_grad = ein32("bhqk,bqhd->bkhd", probs_half, context_grad_half)
    qkv_grad = jnp.concatenate(
        [
            rotate(queries_grad, cosine, -sine_table).reshape(B * T, H).astype(bf16),
            rotate(keys_grad, cosine, -sine_table).reshape(B * T, H).astype(bf16),
            values_grad.reshape(B * T, H).astype(bf16),
            jnp.zeros((B * T, full_qkv.shape[1] - 3 * H), bf16),
        ],
        axis=1,
    )
    qkv_weight_grad = dot_dims(normed_half, qkv_grad, 0, 0)
    near_grad = dot_dims(qkv_grad, full_qkv, 1, 1)
    gain_attn_grad = jnp.sum(near_grad * near_in * near_inverse, axis=0)

    small_grad = jnp.concatenate(
        [router_grad, gain_attn_grad[:, None], gain_ffn_grad[:, None]], axis=1
    )
    small_grad = jnp.pad(small_grad, ((0, 0), (0, 128 - small_grad.shape[1])))
    small_grad, gate_term = lax.optimization_barrier((small_grad, gate_term))
    sum_query, sum_key, sum_value, sum_output, small_sum, normed_in_grad, back = settle(
        nz, fast, qkv_weight_grad, output_grad, small_grad, near_grad, out_sum
    )
    grad_w_in = unpack_columns(gate_term, up_term, F)
    mixture = gate_probs[:, 0:1] * dot32(pick[0], back) + gate_probs[:, 1:2] * dot32(pick[1], back)
    activations = (residual_mid + branch_scale * mixture).astype(bf16)
    in_norm_grad = rms_backward(residual_in, inverse_in, gain_attn, normed_in_grad)[0]
    grad_tokens = residual_grad + in_norm_grad
    return (
        activations,
        grad_tokens,
        small_sum[:, experts],
        sum_query,
        sum_key,
        sum_value,
        sum_output,
        small_sum[:, experts + 1],
        small_sum[:, :experts],
        grad_w_in,
        grad_w_down,
    )


def solution(mesh):
    n_expert, n_shard = mesh.devices.shape
    chips = Mesh(mesh.devices.reshape(n_expert, n_shard // 2, 2), ("expert", "z", "core"))
    rows = P(("expert", "z", "core"), None)
    shard = P(SHARD)
    shard2 = P(SHARD, None)
    shard3 = P(SHARD, "expert", None)
    in_specs = (
        rows,
        rows,
        rows,
        shard,
        shard2,
        shard2,
        shard2,
        shard2,
        shard,
        shard2,
        shard3,
        shard3,
        rows,
    )
    out_specs = (
        rows,
        rows,
        shard,
        shard2,
        shard2,
        shard2,
        shard2,
        shard,
        shard2,
        shard3,
        shard3,
    )
    return jax.shard_map(
        on_device, mesh=chips, in_specs=in_specs, out_specs=out_specs, check_vma=False
    )
```

```python
import functools
import math

import jax
import jax.numpy as jnp
from jax import lax
from jax.experimental import pallas as pl
from jax.experimental.pallas import tpu as pltpu
from jax.sharding import Mesh, PartitionSpec as P

HEADS = 36

eps_norm = 1e-05
branch_scale = 1.4 / math.sqrt(40.0)
rope_base = 10000.0
masked_score = -1e30
bf16 = jnp.bfloat16
f32 = jnp.float32
SHARD = ("z", "core")
ANY = pl.BlockSpec(memory_space=pl.ANY)


def place():
    e, z, c = lax.axis_index("expert"), lax.axis_index("z"), lax.axis_index("core")
    across_x = e + 1 - 2 * (e % 2)
    across_y = (e + 2) % 4
    return e, z, c, across_x, across_y


def remote(src, dst, send, recv, e, z, c):
    return pltpu.make_async_remote_copy(
        src_ref=src,
        dst_ref=dst,
        send_sem=send,
        recv_sem=recv,
        device_id=(e, z, c),
        device_id_type=pl.DeviceIdType.MESH,
    )


def payload_stream(nz, ref, out, sems, split):
    zrecv, zsend, near_recv, near_send, far_recv, far_send, sib_recv, sib_send, own = sems
    e, z, c, ex, ey = place()
    diagonal = (ex + 2) % 4
    T = ref.shape[0]
    S = 2 * nz - 1

    def split_step(s):
        return (s - 1) % 2, (s - 1) // 2

    def where(s):
        if s == 0:
            return z
        side, i = split_step(s)
        return z - 1 - i if side == 0 else z + 1 + i

    def exists(s):
        if s == 0:
            return z >= 0
        zz = where(s)
        return (zz >= 0) & (zz < nz)

    def slab(s, quarter, r0=0, n=T):
        return out.at[where(s), c, quarter, pl.ds(r0, n), :]

    def first(step):
        side = 0 if step > 0 else 1
        return remote(ref, slab(0, e), zsend.at[side, nz - 1], zrecv.at[side, 0], e, z + step, c)

    def onward(s):
        side, i = split_step(s)
        step = 1 if side == 0 else -1
        return remote(
            slab(s, e), slab(s, e), zsend.at[side, i], zrecv.at[side, i + 1], e, z + step, c
        )

    def near(s, axis):
        source = ref if s == 0 else slab(s, e)
        return remote(
            source, slab(s, e), near_send.at[s, axis], near_recv.at[s, axis],
            ex if axis == 0 else ey, z, c,
        )

    def near_wait(s, axis):
        view = slab(s, ex if axis == 0 else ey)
        remote(view, view, near_send.at[s, axis], near_recv.at[s, axis], ex, z, c).wait_recv()

    axes = range(2) if split else range(1)

    def far_view(s, quarter, axis):
        if not split:
            return slab(s, quarter)
        return slab(s, quarter, 0, split) if axis == 0 else slab(s, quarter, split, T - split)

    def far(s, axis):
        view = far_view(s, ex if axis == 0 else ey, axis)
        return remote(
            view, view, far_send.at[s, axis], far_recv.at[s, axis],
            ey if axis == 0 else ex, z, c,
        )

    def far_wait(s, axis):
        view = far_view(s, diagonal, axis)
        remote(view, view, far_send.at[s, axis], far_recv.at[s, axis], ex, z, c).wait_recv()

    def beside(s, n):
        quarter = (e, ex, ey, diagonal)[n]
        source = ref if s == 0 and n == 0 else slab(s, quarter)
        return remote(
            source, slab(s, quarter), sib_send.at[s, n], sib_recv.at[s, n], e, z, 1 - c
        )

    def beside_wait(s, n):
        view = out.at[where(s), 1 - c, (e, ex, ey, diagonal)[n]]
        remote(view, view, sib_send.at[s, n], sib_recv.at[s, n], e, z, c).wait_recv()

    def inside(side):
        return z < nz - 1 if side == 0 else z > 0

    def begin():
        for step in (1, -1):

            @pl.when((z + step >= 0) & (z + step < nz))
            def _():
                first(step).start()

        near(0, 0).start()
        near(0, 1).start()
        beside(0, 0).start()
        pltpu.make_async_copy(ref, slab(0, e), own).start()

    def arrive(s):
        if s == 0:
            return

        @pl.when(exists(s))
        def _():
            side, i = split_step(s)
            remote(
                slab(s, e), slab(s, e), zsend.at[side, i], zrecv.at[side, i], e, z, c
            ).wait_recv()
            if i < nz - 2:

                @pl.when(inside(side))
                def _():
                    onward(s).start()

            near(s, 0).start()
            near(s, 1).start()
            beside(s, 0).start()

    def relay(s):
        @pl.when(exists(s))
        def _():
            near_wait(s, 0)
            far(s, 0).start()
            beside(s, 1).start()
            near_wait(s, 1)
            if split:
                far(s, 1).start()
            beside(s, 2).start()

    def close(s):
        @pl.when(exists(s))
        def _():
            for axis in axes:
                far_wait(s, axis)
            beside(s, 3).start()

    def end(s):
        @pl.when(exists(s))
        def _():
            for axis in range(2):
                near(s, axis).wait_send()
            for axis in axes:
                far(s, axis).wait_send()
            for n in range(4):
                beside(s, n).wait_send()
                beside_wait(s, n)
            if s > 0 and split_step(s)[1] < nz - 2:

                @pl.when(inside(split_step(s)[0]))
                def _():
                    onward(s).wait_send()

        if s == 0:
            for step in (1, -1):

                @pl.when((z + step >= 0) & (z + step < nz))
                def _():
                    first(step).wait_send()

            pltpu.make_async_copy(ref, slab(0, e), own).wait()

    return begin, arrive, relay, close, end


def payload_sems(nz):
    dma = pltpu.SemaphoreType.DMA
    S = 2 * nz - 1
    return [
        dma((2, nz)), dma((2, nz)), dma((S, 2)), dma((S, 2)), dma((S, 2)), dma((S, 2)),
        dma((S, 4)), dma((S, 4)), dma(()),
    ]


def spread_kernel(nz, splits, *refs):
    n = len(splits)
    (gate_ref, up_ref), refs = refs[:2], refs[2:]
    ins, refs = refs[:n], refs[n:]
    pair, outs, sems = refs[0], refs[1 : n + 1], refs[n + 1 :]
    v_sems, beside_sem, sems = sems[:3], sems[3], sems[4:]
    width = gate_ref.shape[2]
    greet_shard(nz)
    streams = [
        payload_stream(nz, ins[i], outs[i], sems[9 * i : 9 * i + 9], splits[i]) for i in range(n)
    ]
    v_begin, v_end = scatter_stream(
        nz, gate_ref, lambda i: pair.at[i, :, pl.ds(0, width)], *v_sems
    )
    beside = pltpu.make_async_copy(up_ref, pair.at[:, :, pl.ds(width, width)], beside_sem)
    for t in streams:
        t[0]()
    beside.start()
    S = 2 * nz - 1
    for s in range(1, S):
        for t in streams:
            t[1](s)
    v_begin()
    for s in range(S):
        for t in streams:
            t[2](s)
        if s >= 1:
            for t in streams:
                t[3](s - 1)
    for t in streams:
        t[3](S - 1)
    for s in range(S):
        for t in streams:
            t[4](s)
    beside.wait()
    v_end()


def spread_blocks(nz, blocks, gate, up, collective):
    sd = jax.ShapeDtypeStruct
    splits = tuple(b.shape[0] // 2 if b.shape[0] % 32 == 0 else 0 for b in blocks)
    pair = sd(gate.shape[:2] + (2 * gate.shape[2],), gate.dtype)
    return pl.pallas_call(
        functools.partial(spread_kernel, nz, splits),
        out_shape=(pair,) + tuple(sd((nz, 2, 4) + b.shape, b.dtype) for b in blocks),
        in_specs=[ANY] * (len(blocks) + 2),
        out_specs=(ANY,) * (len(blocks) + 1),
        scratch_shapes=[
            *scatter_sems(nz), pltpu.SemaphoreType.DMA(()),
            *[s for _ in blocks for s in payload_sems(nz)],
        ],
        compiler_params=pltpu.CompilerParams(collective_id=collective, has_side_effects=True),
        cost_estimate=pl.CostEstimate(flops=10**6, bytes_accessed=10**6, transcendentals=0),
        name="spread_blocks",
    )(gate, up, *blocks)


def line_order(nz, z):
    def order(i):
        code = 0
        for zz in range(nz):
            far_first = sorted(range(nz), key=lambda t: (-abs(t - zz), t))
            code += far_first[i] * nz**zz
        power = 1
        for zz in range(nz):
            power = power + (nz**zz - 1) * jnp.where(z == zz, 1, 0)
        return (code // power) % nz

    return [order(i) for i in range(nz)]


def collect_kernel(
    nz, cap,
    rows_ref, notes_ref, dots_ref,
    out_ref, dots_out,
    dots, notes, mine, theirs, block, from_x, from_y, via_x, via_y, from_z,
    note_sem, load, sib_send, sib_recv, via_send, via_recv, plain_send, plain_recv,
    sum_send, sum_recv, zsend, zrecv, dot_send, dot_recv, dot_own,
):
    e, z, c, ex, ey = place()
    diagonal = (ex + 2) % 4
    T, D = out_ref.shape
    h = T // 2
    dest = line_order(nz, z)
    who = (diagonal, ex, ey, e)

    def others():
        for d in range(1, 8 * nz):
            to = ((e * nz + z) * 2 + c + d) % (8 * nz)
            yield d, to // (2 * nz), to // 2 % nz, to % 2

    barrier = pltpu.get_barrier_semaphore()
    for _, te, tz, tc in others():
        pl.semaphore_signal(
            barrier, inc=1, device_id=(te, tz, tc), device_id_type=pl.DeviceIdType.MESH
        )
    pl.semaphore_wait(barrier, 8 * nz - 1)

    def dot(d, te, tz, tc):
        return remote(
            dots_ref.at[tz, tc, te], dots.at[d], dot_send.at[d], dot_recv.at[d], te, tz, tc
        )

    dot_kept = pltpu.make_async_copy(dots_ref.at[z, c, e], dots.at[0], dot_own)

    note_copy = pltpu.make_async_copy(notes_ref, notes, note_sem)
    note_copy.start()

    def fetch(i, q):
        return pltpu.make_async_copy(
            rows_ref.at[dest[i], c, who[q]], mine.at[i, q], load.at[i, q]
        )

    def hand(i, q):
        return remote(
            rows_ref.at[dest[i], 1 - c, who[q]], theirs.at[i, q],
            sib_send.at[i, q], sib_recv.at[i, q], e, z, 1 - c,
        )

    for i in range(nz):
        for q in range(4):
            hand(i, q).start()
            fetch(i, q).start()
    dot_kept.start()
    for d, te, tz, tc in others():
        dot(d, te, tz, tc).start()
    note_copy.wait()

    def open_out(i, q):
        fetch(i, q).wait()
        hand(i, q).wait_recv()
        places = (lax.broadcasted_iota(jnp.int32, (cap, T), 0) + e * cap).astype(f32)
        note = notes[dest[i], c, who[q]]
        pick = ((note[2:3, :] == places) | (note[3:4, :] == places)).astype(bf16)
        wide = 768 if D % 768 == 0 else 128

        @pl.loop(0, D // wide)
        def _(b):
            cols = pl.ds(pl.multiple_of(b * wide, 128), wide)
            both = mine[i, q, :, cols].astype(f32) + theirs[i, q, :, cols].astype(f32)
            block[i, q, :, cols] = lax.dot_general(
                pick, both.astype(bf16), (((0,), (0,)), ((), ())), preferred_element_type=f32
            ).astype(bf16)

    def via(i, axis):
        if axis == 0:
            return remote(
                block.at[i, 0, pl.ds(0, h), :], via_x.at[i],
                via_send.at[i, 0], via_recv.at[i, 0], ex, z, c,
            )
        return remote(
            block.at[i, 0, pl.ds(h, h), :], via_y.at[i],
            via_send.at[i, 1], via_recv.at[i, 1], ey, z, c,
        )

    def plain(i, axis):
        if axis == 0:
            return remote(
                block.at[i, 1, pl.ds(0, h), :], from_x.at[i, pl.ds(0, h), :],
                plain_send.at[i, 0], plain_recv.at[i, 0], ex, z, c,
            )
        return remote(
            block.at[i, 2, pl.ds(h, h), :], from_y.at[i, pl.ds(h, h), :],
            plain_send.at[i, 1], plain_recv.at[i, 1], ey, z, c,
        )

    def summed(i, axis):
        if axis == 0:
            return remote(
                block.at[i, 1, pl.ds(h, h), :], from_x.at[i, pl.ds(h, h), :],
                sum_send.at[i, 0], sum_recv.at[i, 0], ex, z, c,
            )
        return remote(
            block.at[i, 2, pl.ds(0, h), :], from_y.at[i, pl.ds(0, h), :],
            sum_send.at[i, 1], sum_recv.at[i, 1], ey, z, c,
        )

    def add(target, others, n):
        @pl.loop(0, n // 16)
        def _(b):
            rows = pl.ds(pl.multiple_of(b * 16, 16), 16)
            acc = target[rows, :].astype(f32)
            for o in others:
                acc = acc + o[rows, :].astype(f32)
            target[rows, :] = acc.astype(target.dtype)

    def start(i):
        open_out(i, 0)
        via(i, 0).start()
        via(i, 1).start()
        open_out(i, 1)
        plain(i, 0).start()
        open_out(i, 2)
        plain(i, 1).start()
        open_out(i, 3)

    def combine(i):
        via(i, 0).wait_recv()
        add(block.at[i, 2, pl.ds(0, h), :], [via_x.at[i]], h)
        summed(i, 1).start()
        via(i, 1).wait_recv()
        add(block.at[i, 1, pl.ds(h, h), :], [via_y.at[i]], h)
        summed(i, 0).start()

    def zcopy(i):
        step = jnp.where(dest[i] > z, 1, -1)
        side = jnp.where(dest[i] > z, 0, 1)
        return remote(
            block.at[i, 3], from_z.at[side, dest[i]],
            zsend.at[i], zrecv.at[side, dest[i]], e, z + step, c,
        )

    def zwait(side, zz):
        slab = from_z.at[side, zz]
        remote(slab, slab, zsend.at[0], zrecv.at[side, zz], e, z, c).wait_recv()

    def finish(i):
        for axis in range(2):
            plain(i, axis).wait_recv()
            summed(i, axis).wait_recv()
        zz = dest[i]
        if i < nz - 1:
            add(block.at[i, 3], [from_x.at[i], from_y.at[i]], T)
            for side in range(2):
                going = zz > z if side == 0 else zz < z
                behind = z > 0 if side == 0 else z < nz - 1

                @pl.when(going & behind)
                def _():
                    zwait(side, zz)
                    add(block.at[i, 3], [from_z.at[side, zz]], T)

            zcopy(i).start()
            return

        @pl.loop(0, T // 16)
        def _(b):
            rows = pl.ds(pl.multiple_of(b * 16, 16), 16)
            acc = block[i, 3, rows, :].astype(f32) + from_x[i, rows, :].astype(f32)
            out_ref[rows, :] = acc + from_y[i, rows, :].astype(f32)

        for side in range(2):

            @pl.when(z > 0 if side == 0 else z < nz - 1)
            def _():
                zwait(side, z)
                add(out_ref, [from_z.at[side, z]], T)

    for i in range(nz):
        start(i)
        if i >= 1:
            combine(i - 1)
        if i >= 2:
            finish(i - 2)
    combine(nz - 1)
    if nz >= 2:
        finish(nz - 2)
    finish(nz - 1)

    dot_kept.wait()
    for d, te, tz, tc in others():
        dot(d, te, tz, tc).wait_recv()
        dot(d, te, tz, tc).wait_send()
    dots_out[...] = jnp.sum(dots[...], axis=0)

    for i in range(nz):
        for q in range(4):
            hand(i, q).wait_send()
        for axis in range(2):
            via(i, axis).wait_send()
            plain(i, axis).wait_send()
            summed(i, axis).wait_send()
        if i < nz - 1:
            zcopy(i).wait_send()


def collect_rows(nz, rows, notes, dots, T):
    cap, D = rows.shape[3:]
    dma = pltpu.SemaphoreType.DMA
    vm = pltpu.VMEM
    return pl.pallas_call(
        functools.partial(collect_kernel, nz, cap),
        out_shape=(
            jax.ShapeDtypeStruct((T, D), f32),
            jax.ShapeDtypeStruct(dots.shape[3:], f32),
        ),
        in_specs=[ANY] * 3,
        out_specs=(pl.BlockSpec(memory_space=pltpu.VMEM),) * 2,
        scratch_shapes=[
            vm((8 * nz,) + dots.shape[3:], f32),
            vm(notes.shape, f32),
            vm((nz, 4, cap, D), bf16),
            vm((nz, 4, cap, D), bf16),
            vm((nz, 4, T, D), bf16),
            vm((nz, T, D), bf16),
            vm((nz, T, D), bf16),
            vm((nz, T // 2, D), bf16),
            vm((nz, T // 2, D), bf16),
            vm((2, nz, T, D), bf16),
            dma(()),
            dma((nz, 4)),
            dma((nz, 4)),
            dma((nz, 4)),
            dma((nz, 2)),
            dma((nz, 2)),
            dma((nz, 2)),
            dma((nz, 2)),
            dma((nz, 2)),
            dma((nz, 2)),
            dma((nz,)),
            dma((2, nz)),
            dma((8 * nz,)),
            dma((8 * nz,)),
            dma(()),
        ],
        compiler_params=pltpu.CompilerParams(
            collective_id=3, has_side_effects=True, vmem_limit_bytes=56 << 20
        ),
        cost_estimate=pl.CostEstimate(
            flops=10**6, bytes_accessed=10**6, transcendentals=0
        ),
        name="collect_rows",
    )(rows, notes, dots)


def pack_rows(n, F, Fp, x_ref, *o_refs):
    half = n * F
    rows = x_ref.shape[0]
    for i in range(n):
        for part in range(2):
            cols = x_ref[:, part * half + i * F : part * half + (i + 1) * F]
            if Fp > F:
                cols = jnp.concatenate([cols, jnp.zeros((rows, Fp - F), cols.dtype)], axis=1)
            o_refs[part][i] = cols


def pack_columns(w, n, F, Fp):
    rows = w.shape[0]
    block = 16
    return pl.pallas_call(
        functools.partial(pack_rows, n, F, Fp),
        grid=(rows // block,),
        in_specs=[pl.BlockSpec((block, w.shape[1]), lambda i: (i, 0))],
        out_specs=(pl.BlockSpec((n, block, Fp), lambda i: (0, i, 0)),) * 2,
        out_shape=(jax.ShapeDtypeStruct((n, rows, Fp), w.dtype),) * 2,
        name="pack_columns",
    )(w)


def unpack_kernel(n, F, gate_ref, up_ref, o_ref, line):
    half = n * F
    rows = line.shape[0]
    for i in range(n):
        for part in range(2):
            cols = (up_ref if part else gate_ref)[i, :, :F].astype(f32)
            line[:, part * half + i * F : part * half + (i + 1) * F] = cols
    tiles = 2 * half // 128
    for j in range(tiles):
        o_ref[pl.ds(j, rows, stride=tiles), :] = line[:, j * 128 : (j + 1) * 128]


def unpack_columns(gate, up, F):
    n, rows, Fp = gate.shape
    block = 96 if rows % 96 == 0 else 16
    width = 2 * n * F
    tiles = width // 128
    flat = pl.pallas_call(
        functools.partial(unpack_kernel, n, F),
        grid=(rows // block,),
        in_specs=[pl.BlockSpec((n, block, Fp), lambda i: (0, i, 0))] * 2,
        out_specs=pl.BlockSpec((block * tiles, 128), lambda i: (i, 0)),
        out_shape=jax.ShapeDtypeStruct((rows * tiles, 128), f32),
        scratch_shapes=[pltpu.VMEM((block, width), f32)],
        name="unpack_columns",
    )(gate, up)
    return flat.reshape(rows, 1, width)


def line_kernel(x_ref, o_ref):
    rows, width = x_ref.shape
    tiles = width // 128
    for j in range(tiles):
        o_ref[pl.ds(j, rows, stride=tiles), :] = x_ref[:, j * 128 : (j + 1) * 128]


def lined_up(x, rows):
    width = x.shape[1]
    tiles = width // 128
    block = 240 if rows % 240 == 0 else 8
    flat = pl.pallas_call(
        line_kernel,
        grid=(rows // block,),
        in_specs=[pl.BlockSpec((block, width), lambda i: (i, 0))],
        out_specs=pl.BlockSpec((block * tiles, 128), lambda i: (i, 0)),
        out_shape=jax.ShapeDtypeStruct((rows * tiles, 128), x.dtype),
        name="lined_up",
    )(x)
    return flat.reshape(rows, 1, width)


def greet_cross(nz):
    e, z, c, ex, ey = place()
    barrier = pltpu.get_barrier_semaphore()

    def hail(te, tz, tc):
        pl.semaphore_signal(
            barrier, inc=1, device_id=(te, tz, tc), device_id_type=pl.DeviceIdType.MESH
        )

    hail(e, z, 1 - c)
    for te in (ex, ey, (ex + 2) % 4):
        hail(te, z, c)
    for step in (-1, 1):

        @pl.when((z + step >= 0) & (z + step < nz))
        def _():
            hail(e, z + step, c)

    pl.semaphore_wait(barrier, 4 + jnp.where(z > 0, 1, 0) + jnp.where(z < nz - 1, 1, 0))


def greet_shard(nz):
    e, z, c, ex, ey = place()
    barrier = pltpu.get_barrier_semaphore()
    n = 2 * nz
    peers = [(te, z, c) for te in (ex, ey, (ex + 2) % 4)]
    for d in range(1, n):
        to = (2 * z + c + d) % n
        peers.append((e, to // 2, to % 2))
    for peer in peers:
        pl.semaphore_signal(barrier, inc=1, device_id=peer, device_id_type=pl.DeviceIdType.MESH)
    pl.semaphore_wait(barrier, n + 2)


def scatter_stream(nz, ref, view, send, recv, own):
    e, z, c, _, _ = place()
    n = 2 * nz
    me = 2 * z + c

    def copy(d):
        to = (me + d) % n
        return remote(ref.at[to], view(me), send.at[d], recv.at[d], e, to // 2, to % 2)

    kept = pltpu.make_async_copy(ref.at[me], view(me), own)

    def begin():
        for d in range(1, n):
            copy(d).start()
        kept.start()

    def end():
        kept.wait()
        for d in range(1, n):
            land = view((me + n - d) % n)
            remote(land, land, send.at[d], recv.at[d], e, z, c).wait_recv()
            copy(d).wait_send()

    return begin, end


def scatter_sems(nz):
    dma = pltpu.SemaphoreType.DMA
    return [dma((2 * nz,)), dma((2 * nz,)), dma(())]


def line_stream(nz, ref, out, zrecv, zsend, sib_recv, sib_send, own):
    e, z, c, _, _ = place()

    def split_step(s):
        return (s - 1) % 2, (s - 1) // 2

    def where(s):
        if s == 0:
            return z
        side, i = split_step(s)
        return z - 1 - i if side == 0 else z + 1 + i

    def exists(s):
        return (where(s) >= 0) & (where(s) < nz)

    def inside(side):
        return z < nz - 1 if side == 0 else z > 0

    def slab(s):
        return out.at[where(s), c]

    def first(side):
        step = 1 if side == 0 else -1
        return remote(ref, slab(0), zsend.at[side, nz - 1], zrecv.at[side, 0], e, z + step, c)

    def onward(s):
        side, i = split_step(s)
        step = 1 if side == 0 else -1
        return remote(
            slab(s), slab(s), zsend.at[side, i], zrecv.at[side, i + 1], e, z + step, c
        )

    def beside(s):
        return remote(
            ref if s == 0 else slab(s), slab(s), sib_send.at[s], sib_recv.at[s], e, z, 1 - c
        )

    def begin():
        for side in range(2):

            @pl.when(inside(side))
            def _():
                first(side).start()

        beside(0).start()
        pltpu.make_async_copy(ref, slab(0), own).start()

    def arrive(s):
        side, i = split_step(s)

        @pl.when(exists(s))
        def _():
            remote(slab(s), slab(s), zsend.at[side, i], zrecv.at[side, i], e, z, c).wait_recv()
            if i < nz - 2:

                @pl.when(inside(side))
                def _():
                    onward(s).start()

            beside(s).start()

    def end():
        for s in range(2 * nz - 1):

            @pl.when(exists(s))
            def _():
                beside(s).wait_send()
                view = out.at[where(s), 1 - c]
                remote(view, view, sib_send.at[s], sib_recv.at[s], e, z, c).wait_recv()
                if s > 0 and split_step(s)[1] < nz - 2:

                    @pl.when(inside(split_step(s)[0]))
                    def _():
                        onward(s).wait_send()

        for side in range(2):

            @pl.when(inside(side))
            def _():
                first(side).wait_send()

        pltpu.make_async_copy(ref, slab(0), own).wait()

    return begin, arrive, end


def line_sems(nz):
    dma = pltpu.SemaphoreType.DMA
    S = 2 * nz - 1
    return [dma((2, nz)), dma((2, nz)), dma((S,)), dma((S,)), dma(())]


def plane_stream(source, views, send, recv, own):
    e, z, c, ex, ey = place()
    peers = (ex, ey, (ex + 2) % 4)

    def copy(n):
        return remote(source, views(e), send.at[n], recv.at[n], peers[n], z, c)

    def kept():
        return pltpu.make_async_copy(source, views(e), own)

    def begin():
        for n in range(3):
            copy(n).start()
        kept().start()

    def end():
        kept().wait()
        for n in range(3):
            view = views(peers[n])
            remote(view, view, send.at[n], recv.at[n], e, z, c).wait_recv()
            copy(n).wait_send()

    return begin, end


def plane_sems():
    dma = pltpu.SemaphoreType.DMA
    return [dma((3,)), dma((3,)), dma(())]


def fetch_kernel(
    nz,
    F, w_ref, s_ref, o_ref, t_ref, l_ref, p_ref, x_ref,
    w_out, s_out, o_out, t_out, l_out, p_out, gate_out, up_out,
    wide, gate, up, wide_sem, packed_sem,
    *sems,
):
    e, z, c, ex, ey = place()
    w_sems, sems = sems[:5], sems[5:]
    s_sems, sems = sems[:5], sems[5:]
    t_sems, sems = sems[:3], sems[3:]
    l_sems, sems = sems[:3], sems[3:]
    p_sems, sems = sems[:9], sems[9:]
    orecv, osend, sib_recv, sib_send, own = sems
    wide_copy = pltpu.make_async_copy(x_ref, wide, wide_sem)
    wide_copy.start()
    greet_cross(nz)
    w_begin, w_arrive, w_end = line_stream(nz, w_ref, w_out, *w_sems)
    s_begin, s_arrive, s_end = line_stream(nz, s_ref, s_out, *s_sems)
    t_begin, t_end = plane_stream(t_ref, lambda q: t_out.at[q], *t_sems)
    l_begin, l_end = plane_stream(l_ref, lambda q: l_out.at[q], *l_sems)
    p_begin, p_arrive, p_relay, p_close, p_end = payload_stream(
        nz, p_ref, p_out, p_sems, p_ref.shape[0] // 2
    )

    pieces = orecv.shape[0]
    height = o_ref.shape[0] // pieces

    def o_part(n):
        return pl.ds(n * height, height)

    def o_view(n):
        return o_out.at[c, o_part(n), :]

    def o_copy(side, n, source):
        step = 1 if side == 0 else -1
        return remote(source, o_view(n), osend.at[side, n], orecv.at[n], e, z + step, c)

    def o_beside(n, source):
        return remote(source, o_view(n), sib_send.at[n], sib_recv.at[n], e, z, 1 - c)

    def o_goes(side):
        return (z >= e) & (z < nz - 1) if side == 0 else (z <= e) & (z > 0)

    def o_pass(n, source):
        for side in range(2):

            @pl.when(o_goes(side))
            def _():
                o_copy(side, n, source).start()

        o_beside(n, source).start()

    def o_arrive(n):
        @pl.when(z != e)
        def _():
            remote(o_view(n), o_view(n), sib_send.at[n], orecv.at[n], e, z, c).wait_recv()
            o_pass(n, o_view(n))

    p_begin()

    @pl.when(z == e)
    def _():
        for n in range(pieces):
            o_pass(n, o_ref.at[o_part(n), :])
        pltpu.make_async_copy(o_ref, o_out.at[c], own).start()

    s_begin()
    w_begin()
    t_begin()
    l_begin()

    wide_copy.wait()

    @pl.loop(0, wide.shape[0] // 16)
    def _(b):
        rows = pl.ds(pl.multiple_of(b * 16, 16), 16)
        pack_rows(
            gate.shape[0], F, gate.shape[2], wide.at[rows, :], gate.at[:, rows, :], up.at[:, rows, :]
        )

    packed_copies = [
        pltpu.make_async_copy(a, b, packed_sem.at[n])
        for n, (a, b) in enumerate(((gate, gate_out), (up, up_out)))
    ]
    for copy in packed_copies:
        copy.start()

    blocks = 2 * nz - 1
    for s in range(1, blocks):
        p_arrive(s)
        s_arrive(s)
        if s <= pieces:
            o_arrive(s - 1)
    for n in range(blocks - 1, pieces):
        o_arrive(n)
    for s in range(1, blocks):
        p_relay(s - 1)
        w_arrive(s)
        if s >= 2:
            p_close(s - 2)
    p_relay(blocks - 1)
    p_close(blocks - 2)
    p_close(blocks - 1)
    for s in range(blocks):
        p_end(s)
    w_end()
    s_end()
    t_end()
    l_end()
    for n in range(pieces):
        view = o_out.at[1 - c, o_part(n), :]
        remote(view, view, sib_send.at[n], sib_recv.at[n], e, z, c).wait_recv()
        o_beside(n, o_view(n)).wait_send()
        for side in range(2):

            @pl.when(o_goes(side))
            def _():
                o_copy(side, n, o_view(n)).wait_send()

    @pl.when(z == e)
    def _():
        pltpu.make_async_copy(o_ref, o_out.at[c], own).wait()

    for copy in packed_copies:
        copy.wait()


def fetch_weights(nz, columns, small, rows, tokens, lengths, block, wide, F):
    dma = pltpu.SemaphoreType.DMA
    packed = (2 * nz, wide.shape[0], -(-F // 128) * 128)
    sd = jax.ShapeDtypeStruct
    return pl.pallas_call(
        functools.partial(fetch_kernel, nz, F),
        out_shape=(
            sd((nz, 2) + columns.shape, bf16),
            sd((nz, 2) + small.shape, bf16),
            sd((2,) + rows.shape, bf16),
            sd((4,) + tokens.shape, bf16),
            sd((4,) + lengths.shape, lengths.dtype),
            sd((nz, 2, 4) + block.shape, block.dtype),
            sd(packed, wide.dtype),
            sd(packed, wide.dtype),
        ),
        in_specs=[ANY] * 7,
        out_specs=(ANY,) * 8,
        scratch_shapes=[
            pltpu.VMEM(wide.shape, wide.dtype), pltpu.VMEM(packed, wide.dtype),
            pltpu.VMEM(packed, wide.dtype), dma(()), dma((2,)),
            *line_sems(nz), *line_sems(nz), *plane_sems(), *plane_sems(), *payload_sems(nz),
            dma((6,)), dma((2, 6)), dma((6,)), dma((6,)), dma(()),
        ],
        compiler_params=pltpu.CompilerParams(
            collective_id=0, has_side_effects=True, vmem_limit_bytes=60 << 20
        ),
        cost_estimate=pl.CostEstimate(
            flops=10**11, bytes_accessed=8 * columns.size, transcendentals=0
        ),
        name="fetch_weights",
    )(columns, small, rows, tokens, lengths, block, wide)


def plane_gather_kernel(
    x_ref, a_ref, r_ref, out_ref, d_ref, left, right, prod, load, store, send, recv, own
):
    loads = [
        pltpu.make_async_copy(a_ref, left, load.at[0]),
        pltpu.make_async_copy(r_ref, right, load.at[1]),
    ]
    for copy in loads:
        copy.start()
    greet_plane()
    begin, end = plane_stream(x_ref, lambda q: out_ref.at[q], send, recv, own)
    begin()
    for copy in loads:
        copy.wait()
    tiles, step = store.shape[0], prod.shape[1] // store.shape[0]

    def done(n):
        cols = pl.ds(n * step, step)
        return pltpu.make_async_copy(prod.at[:, cols], d_ref.at[:, cols], store.at[n])

    for n in range(tiles):

        @pl.loop(0, prod.shape[0] // 256)
        def _(m):
            rows = pl.ds(pl.multiple_of(m * 256, 256), 256)
            prod[rows, n * step : (n + 1) * step] = jnp.dot(
                left[rows, :], right[:, n * step : (n + 1) * step], preferred_element_type=f32
            )

        done(n).start()
    for n in range(tiles):
        done(n).wait()
    end()


def greet_plane():
    e, z, c, ex, ey = place()
    barrier = pltpu.get_barrier_semaphore()
    for te in (ex, ey, (ex + 2) % 4):
        pl.semaphore_signal(
            barrier, inc=1, device_id=(te, z, c), device_id_type=pl.DeviceIdType.MESH
        )
    pl.semaphore_wait(barrier, 3)


def plane_gather(x, left, right, collective):
    M, N = left.shape[0], right.shape[1]
    dma = pltpu.SemaphoreType.DMA
    vm = pltpu.VMEM
    return pl.pallas_call(
        plane_gather_kernel,
        out_shape=(
            jax.ShapeDtypeStruct((4,) + x.shape, x.dtype),
            jax.ShapeDtypeStruct((M, N), f32),
        ),
        in_specs=[ANY] * 3,
        out_specs=(ANY,) * 2,
        scratch_shapes=[
            vm(left.shape, bf16), vm(right.shape, bf16), vm((M, N), f32),
            dma((2,)), dma((N // 256,)), *plane_sems(),
        ],
        compiler_params=pltpu.CompilerParams(
            collective_id=collective, has_side_effects=True, vmem_limit_bytes=48 << 20
        ),
        cost_estimate=pl.CostEstimate(flops=10**6, bytes_accessed=10**6, transcendentals=0),
        name="plane_gather",
    )(x, left, right)


def plane_sum_parts(x_ref, out_ref, held, send, recv, own):
    e, z, c, ex, ey = place()
    peers = (ex, ey, (ex + 2) % 4)

    def copy(n):
        return remote(x_ref.at[peers[n]], held.at[n], send.at[n], recv.at[n], peers[n], z, c)

    kept = pltpu.make_async_copy(x_ref.at[e], held.at[3], own)

    def total():
        kept.wait()
        for n in range(3):
            copy(n).wait_recv()

        @pl.loop(0, out_ref.shape[0] // 16)
        def _(b):
            rows = pl.ds(pl.multiple_of(b * 16, 16), 16)
            acc = held[3, rows, :].astype(f32) + held[0, rows, :].astype(f32)
            acc = acc + held[1, rows, :].astype(f32)
            out_ref[rows, :] = acc + held[2, rows, :].astype(f32)

    return copy, kept, total


def plane_sum_kernel(x_ref, out_ref, held, send, recv, own):
    greet_plane()
    copy, kept, total = plane_sum_parts(x_ref, out_ref, held, send, recv, own)
    for n in (2, 0, 1):
        copy(n).start()
    kept.start()
    total()
    for n in range(3):
        copy(n).wait_send()


def plane_sum(x, collective):
    vm = pltpu.VMEM
    return pl.pallas_call(
        plane_sum_kernel,
        out_shape=jax.ShapeDtypeStruct(x.shape[1:], f32),
        in_specs=[ANY],
        out_specs=pl.BlockSpec(memory_space=vm),
        scratch_shapes=[vm(x.shape, bf16), *plane_sems()],
        compiler_params=pltpu.CompilerParams(collective_id=collective, has_side_effects=True),
        cost_estimate=pl.CostEstimate(flops=10**6, bytes_accessed=10**6, transcendentals=0),
        name="plane_sum",
    )(x)


def settle_kernel(
    nz,
    g_ref, s_ref, o_ref, x_ref, y_ref,
    g_out, s_out, o_out, x_out, y_out,
    x_held, x_send, x_recv, x_own, y_send, y_recv, y_own,
    g_mine, g_sib, g_z, s_mine, s_sib, s_z, o_mine, o_sib, o_z,
    load, sib_send, sib_recv, zsend, zrecv,
    o_load, o_sib_send, o_sib_recv, o_zsend, o_zrecv,
    o_send, o_recv, o_own,
    *sems,
):
    e, z, c, ex, ey = place()
    peers = (ex, ey, (ex + 2) % 4)
    dest = line_order(nz, z)
    greet_cross(nz)
    W = g_ref.shape[3]
    first = W // 384 * 128
    groups = (
        (g_ref, g_mine, g_sib, g_z, g_out, pl.ds(0, first)),
        (g_ref, g_mine, g_sib, g_z, g_out, pl.ds(first, first)),
        (g_ref, g_mine, g_sib, g_z, g_out, pl.ds(2 * first, W - 2 * first)),
        (s_ref, s_mine, s_sib, s_z, s_out, pl.ds(0, s_ref.shape[3])),
    )
    K = len(groups)

    def part(k, which, *index):
        return groups[k][which].at[(*index, slice(None), groups[k][5])]

    def fetch(k, i):
        return pltpu.make_async_copy(
            part(k, 0, dest[i], c), part(k, 1, i), load.at[k, i]
        )

    def hand(k, i):
        return remote(
            part(k, 0, dest[i], 1 - c), part(k, 2, i),
            sib_send.at[k, i], sib_recv.at[k, i], e, z, 1 - c,
        )

    def zcopy(k, i):
        step = jnp.where(dest[i] > z, 1, -1)
        side = jnp.where(dest[i] > z, 0, 1)
        return remote(
            part(k, 1, i), part(k, 3, side, dest[i]),
            zsend.at[k, i], zrecv.at[k, side, dest[i]], e, z + step, c,
        )

    def zwait(k, side, zz):
        slab = part(k, 3, side, zz)
        remote(slab, slab, zsend.at[k, 0], zrecv.at[k, side, zz], e, z, c).wait_recv()

    def add(target, others):
        @pl.loop(0, target.shape[0] // 16)
        def _(b):
            rows = pl.ds(pl.multiple_of(b * 16, 16), 16)
            acc = target[rows, :].astype(f32)
            for o in others:
                acc = acc + o[rows, :].astype(f32)
            target[rows, :] = acc.astype(target.dtype)

    pieces = o_load.shape[0]
    height = o_mine.shape[0] // pieces

    def o_part(n):
        return pl.ds(n * height, height)

    def o_fetch(n):
        return pltpu.make_async_copy(o_ref.at[c, o_part(n), :], o_mine.at[o_part(n), :], o_load.at[n])

    def o_hand(n):
        return remote(
            o_ref.at[1 - c, o_part(n), :], o_sib.at[o_part(n), :],
            o_sib_send.at[n], o_sib_recv.at[n], e, z, 1 - c,
        )

    def o_line(n):
        step, side = jnp.where(z < e, 1, -1), jnp.where(z < e, 0, 1)
        return remote(
            o_mine.at[o_part(n), :], o_z.at[side, o_part(n), :],
            o_zsend.at[n], o_zrecv.at[side, n], e, z + step, c,
        )

    def o_wait(side, n):
        slab = o_z.at[side, o_part(n), :]
        remote(slab, slab, o_zsend.at[n], o_zrecv.at[side, n], e, z, c).wait_recv()
        add(o_mine.at[o_part(n), :], [slab])

    def o_peer(p, n):
        view = o_out.at[o_part(n), :]
        return remote(
            o_mine.at[o_part(n), :], view, o_send.at[p, n], o_recv.at[n], peers[p], z, c
        )

    def o_kept():
        return pltpu.make_async_copy(o_mine, o_out, o_own)

    for i in range(nz):
        for k in range(K):
            hand(k, i).start()
            fetch(k, i).start()
        if i == 0:
            for n in range(pieces):
                o_fetch(n).start()
                o_hand(n).start()

    def finish(k, i):
        fetch(k, i).wait()
        hand(k, i).wait_recv()
        zz = dest[i]
        add(part(k, 1, i), [part(k, 2, i)])
        if i < nz - 1:
            for side in range(2):
                going = zz > z if side == 0 else zz < z
                behind = z > 0 if side == 0 else z < nz - 1

                @pl.when(going & behind)
                def _():
                    zwait(k, side, zz)
                    add(part(k, 1, i), [part(k, 3, side, zz)])

            zcopy(k, i).start()
            return
        for side in range(2):

            @pl.when(z > 0 if side == 0 else z < nz - 1)
            def _():
                zwait(k, side, z)
                add(part(k, 1, i), [part(k, 3, side, z)])

        streams[k][0]()

    x_copy, x_kept, x_total = plane_sum_parts(x_ref, x_out, x_held, x_send, x_recv, x_own)
    for p in (2, 0, 1):
        x_copy(p).start()
    x_kept.start()

    def y_copy(p):
        return remote(
            y_ref.at[peers[p]], y_out.at[e], y_send.at[p], y_recv.at[p], peers[p], z, c
        )

    y_kept = pltpu.make_async_copy(y_ref.at[e], y_out.at[e], y_own)
    y_kept.start()
    for p in range(3):
        y_copy(p).start()

    def o_flow(n):
        o_fetch(n).wait()
        o_hand(n).wait_recv()
        add(o_mine.at[o_part(n), :], [o_sib.at[o_part(n), :]])
        for side in range(2):
            behind = (z > 0) & (z <= e) if side == 0 else (z < nz - 1) & (z >= e)

            @pl.when(behind)
            def _():
                o_wait(side, n)

        @pl.when(z != e)
        def _():
            o_line(n).start()

        @pl.when(z == e)
        def _():
            for p in range(3):
                o_peer(p, n).start()

    streams = [
        plane_stream(
            part(k, 1, nz - 1), lambda q, k=k: part(k, 4, q), *sems[3 * k : 3 * k + 3]
        )
        for k in range(K)
    ]
    turn = K * nz // 2
    order = []
    for k in range(K):
        order += [(k, i) for i in range(1 if k else 0, nz - 1)]
        if k + 1 < K:
            order.append((k + 1, 0))
        order.append((k, nz - 1))
    for n, (k, i) in enumerate(order):
        finish(k, i)
        if n == 0:
            for m in range(pieces):
                o_flow(m)
        if n == turn:
            x_total()

    @pl.when(z == e)
    def _():
        o_kept().start()
        o_kept().wait()
        for n in range(pieces):
            for p in range(3):
                o_peer(p, n).wait_send()

    @pl.when(z != e)
    def _():
        for n in range(pieces):
            view = o_out.at[o_part(n), :]
            remote(view, view, o_send.at[0, n], o_recv.at[n], e, z, c).wait_recv()
            o_line(n).wait_send()

    y_kept.wait()
    for p in range(3):
        x_copy(p).wait_send()
        view = y_out.at[peers[p]]
        remote(view, view, y_send.at[p], y_recv.at[p], e, z, c).wait_recv()
        y_copy(p).wait_send()
    for n in range(pieces):
        o_hand(n).wait_send()
    for i in range(nz):
        for k in range(K):
            hand(k, i).wait_send()
            if i < nz - 1:
                zcopy(k, i).wait_send()
    for _, end in streams:
        end()


def settle_weights(nz, grads, small, rows, near, blocks):
    R, W = grads.shape[2:]
    D = rows.shape[2]
    dma = pltpu.SemaphoreType.DMA
    sd = jax.ShapeDtypeStruct
    vm = pltpu.VMEM
    Ws = small.shape[3]
    return pl.pallas_call(
        functools.partial(settle_kernel, nz),
        out_shape=(
            sd((4, R, W), bf16),
            sd((4, R, Ws), bf16),
            sd((R, D), bf16),
            sd(near.shape[1:], f32),
            sd(blocks.shape, bf16),
        ),
        in_specs=[ANY] * 5,
        out_specs=(ANY,) * 3 + (pl.BlockSpec(memory_space=vm), ANY),
        scratch_shapes=[
            vm(near.shape, bf16), *plane_sems(), *plane_sems(),
            vm((nz, R, W), bf16), vm((nz, R, W), bf16), vm((2, nz, R, W), bf16),
            vm((nz, R, Ws), bf16), vm((nz, R, Ws), bf16), vm((2, nz, R, Ws), bf16),
            vm((R, D), bf16), vm((R, D), bf16), vm((2, R, D), bf16),
            dma((4, nz)), dma((4, nz)), dma((4, nz)), dma((4, nz)), dma((4, 2, nz)),
            dma((6,)), dma((6,)), dma((6,)), dma((6,)), dma((2, 6)),
            dma((3, 6)), dma((6,)), dma(()),
            *plane_sems(), *plane_sems(), *plane_sems(), *plane_sems(),
        ],
        compiler_params=pltpu.CompilerParams(
            collective_id=1, has_side_effects=True, vmem_limit_bytes=56 << 20
        ),
        cost_estimate=pl.CostEstimate(flops=10**6, bytes_accessed=10**6, transcendentals=0),
        name="settle_weights",
    )(grads, small, rows, near, blocks)


def pick_kernel(width, q_ref, k_ref, v_ref, o_ref):
    e = lax.axis_index("expert")
    spare = o_ref.shape[1] - 3 * width
    if spare:
        o_ref[:, 3 * width :] = jnp.zeros((o_ref.shape[0], spare), o_ref.dtype)
    for n in range(4):

        @pl.when(e == n)
        def _():
            for i, ref in enumerate((q_ref, k_ref, v_ref)):
                o_ref[:, i * width : (i + 1) * width] = ref[:, n * width : (n + 1) * width]


def pick_columns(weights, width):
    vm = pl.BlockSpec(memory_space=pltpu.VMEM)
    return pl.pallas_call(
        functools.partial(pick_kernel, width),
        in_specs=[vm] * 3,
        out_specs=vm,
        out_shape=jax.ShapeDtypeStruct((weights[0].shape[0], -(-3 * width // 128) * 128), bf16),
        name="pick_columns",
    )(*weights)


def assemble_kernel(width, x_ref, *o_refs):
    for n in range(4):
        for i in range(3):
            cols = x_ref[n, :, i * width : (i + 1) * width]
            o_refs[i][:, n * width : (n + 1) * width] = cols.astype(f32)


def assemble_columns(x, width):
    R = x.shape[1]
    block = 96 if R % 96 == 0 else 16
    return pl.pallas_call(
        functools.partial(assemble_kernel, width),
        grid=(R // block,),
        in_specs=[pl.BlockSpec((4, block, x.shape[2]), lambda i: (0, i, 0))],
        out_specs=(pl.BlockSpec((block, 4 * width), lambda i: (i, 0)),) * 3,
        out_shape=(jax.ShapeDtypeStruct((R, 4 * width), f32),) * 3,
        name="assemble_columns",
    )(x)


def sum_shard(x, axis=0):
    mine = lax.psum_scatter(x, SHARD, scatter_dimension=axis, tiled=True)
    return lax.psum(mine, "expert")


def fetch(nz, fast, weights, w_output, small, tokens, lengths, block, wide, F):
    D = tokens.shape[1]
    if fast:
        width = D // 4
        columns, full_small, rows, tokens, lengths, blocks, *packed = fetch_weights(
            nz, pick_columns(weights, width), small, w_output, tokens, lengths, block, wide, F
        )
        columns, rows = columns.reshape(D, -1), rows.reshape(width, D)
        return columns, rows, full_small.reshape(D, -1), tokens, lengths, blocks, packed
    full = [lax.all_gather(w, SHARD, axis=0, tiled=True) for w in weights + (w_output, small)]
    blocks = spread_plain(nz, (block,), 0)[0]
    packed = pack_columns(wide, 2 * nz, F, -(-F // 128) * 128)
    columns = jnp.concatenate(full[:3], axis=1)
    return columns, full[3], full[4], tokens[None], lengths[None], blocks, packed


def settle(nz, fast, columns, rows, small, near, blocks):
    D, width = rows.shape[1], rows.shape[0]
    if fast:
        R = D // (2 * nz)
        parts = [x.astype(bf16).reshape(nz, 2, R, -1) for x in (columns, small)]
        near = near.astype(bf16).reshape(4, -1, D)
        blocks = blocks.reshape(4, -1, D)
        sums, small, out, near, blocks = settle_weights(
            nz, *parts, rows.astype(bf16).reshape(2, R, D), near, blocks
        )
        small, blocks = jnp.sum(small.astype(f32), axis=0), blocks.reshape(-1, D)
        return *assemble_columns(sums, width), out.astype(f32), small, near, blocks
    parts = [columns[:, i * width : (i + 1) * width] for i in range(3)] + [rows, small]
    blocks = lax.all_to_all(blocks, "expert", split_axis=0, concat_axis=0, tiled=True)
    return [sum_shard(x) for x in parts] + [near, blocks]


def spread_plain(nz, blocks, collective):
    out = []
    for block in blocks:
        for axis in ("expert", "core", "z"):
            block = lax.all_gather(block, axis, axis=0)
        out.append(block)
    return out


def spread_pair(nz, blocks, gate, up, collective):
    gate = lax.all_to_all(gate, SHARD, split_axis=0, concat_axis=0, tiled=True)
    return jnp.concatenate([gate, up], axis=2), *spread_plain(nz, blocks, collective)


def collect_plain(nz, rows, notes, dots, T):
    n_exp, cap, D = rows.shape[2:]
    places = (lax.axis_index("expert") * cap + jnp.arange(cap)).astype(f32)
    notes = notes[..., :T]
    pick = (notes[..., 2, None, :] == places[:, None]) | (notes[..., 3, None, :] == places[:, None])
    part = jnp.einsum(
        "zceps,zcepd->zcesd", pick.astype(bf16), rows, preferred_element_type=f32
    ).astype(bf16)
    part = part.transpose(2, 0, 1, 3, 4).reshape(n_exp * nz * 2 * T, D)
    part = lax.psum_scatter(part, "expert", scatter_dimension=0, tiled=True)
    part = lax.psum_scatter(part, SHARD, scatter_dimension=0, tiled=True).astype(f32)
    z, core, e = lax.axis_index("z"), lax.axis_index("core"), lax.axis_index("expert")
    return part, lax.psum(dots, ("expert",) + SHARD)[z, core, e]


def rope_tables(positions, head_width):
    half_width = head_width // 2
    exponents = jnp.arange(half_width).astype(f32) * 2.0 / head_width
    frequency = rope_base ** (-exponents)
    angles = positions.astype(f32)[..., None] * frequency
    return (jnp.cos(angles), jnp.sin(angles))


def rotate(values, cosine, sine_table):
    half_width = values.shape[-1] // 2
    leading = values[..., :half_width]
    trailing = values[..., half_width:]
    cos_rows = cosine[:, :, None, :]
    sin_rows = sine_table[:, :, None, :]
    return jnp.concatenate(
        [leading * cos_rows - trailing * sin_rows, trailing * cos_rows + leading * sin_rows],
        axis=-1,
    )


def rms_forward(values, norm_gain):
    inverse = lax.rsqrt(jnp.mean(values * values, axis=-1, keepdims=True) + eps_norm)
    return (values * inverse * norm_gain, inverse)


def rms_backward(values, inverse, norm_gain, upstream):
    weighted = upstream * norm_gain
    gain_grad = jnp.sum(upstream * values * inverse, axis=0)
    inner_mean = jnp.mean(weighted * values, axis=-1, keepdims=True)
    return (inverse * weighted - values * inverse * inverse * inverse * inner_mean, gain_grad)


def dot32(a, b):
    return jnp.dot(a, b, preferred_element_type=f32)


def dot_dims(a, b, da, db):
    return lax.dot_general(a, b, (((da,), (db,)), ((), ())), preferred_element_type=f32)


def ein32(spec, a, b):
    return jnp.einsum(spec, a, b, preferred_element_type=f32)


def on_device(
    tokens,
    seq_lengths,
    routes,
    norm_attn,
    w_query,
    w_key,
    w_value,
    w_output,
    norm_ffn,
    w_router,
    w_in,
    w_down,
    cotangent,
):
    T, D = tokens.shape
    R = w_query.shape[0]
    head_width = D // HEADS
    n_exp = lax.axis_size("expert")
    nz = lax.axis_size("z")
    n_shard = nz * lax.axis_size("core")
    experts = w_router.shape[1]
    F = w_down.shape[0]
    FF = F * n_shard
    capacity = 10 * T // (4 * experts)
    slots = experts * capacity
    highest = lax.Precision.HIGHEST
    e_index = lax.axis_index("expert")
    fast = n_exp == 4 and nz == 4

    small = jnp.concatenate([w_router, norm_attn[:, None], norm_ffn[:, None]], axis=1)
    small = jnp.pad(small, ((0, 0), (0, 128 - small.shape[1])))
    length_rows = jnp.broadcast_to(seq_lengths[:, :1], (8, 128))
    full_qkv, full_output, full_small, near_tokens, near_lengths, all_cotangent, packed = fetch(
        nz,
        fast,
        (w_query, w_key, w_value),
        w_output,
        small,
        tokens,
        length_rows,
        cotangent,
        w_in.reshape(R, 2 * FF),
        F,
    )
    full_router = full_small[:, :experts]
    gain_attn = full_small[:, experts].astype(f32)
    gain_ffn = full_small[:, experts + 1].astype(f32)

    Fp = -(-F // 128) * 128
    moved_up = lax.all_to_all(packed[1], SHARD, split_axis=0, concat_axis=0, tiled=True)
    down = jnp.pad(w_down.reshape(F, D), ((0, Fp - F), (0, 0)))

    B, H = near_tokens.shape[0], full_output.shape[0]
    heads = H // head_width
    residual_in = tokens.astype(f32)
    inverse_in = rms_forward(residual_in, gain_attn)[1]
    near_in = near_tokens.reshape(B * T, D).astype(f32)
    near_normed, near_inverse = rms_forward(near_in, gain_attn)
    normed_half = near_normed.astype(bf16)
    lengths = near_lengths[:, 0, 0]
    row_index = jnp.arange(T)
    segment = (row_index[None, :] >= lengths[:, None]).astype(jnp.int32)
    positions = row_index[None, :] - lengths[:, None] * segment
    allowed = (segment[:, :, None] == segment[:, None, :]) & (
        row_index[None, None, :] <= row_index[None, :, None]
    )
    cosine, sine_table = rope_tables(positions, head_width)
    head_shape = (B, T, heads, head_width)
    qkv = dot32(normed_half, full_qkv)
    queries = rotate(qkv[:, :H].reshape(head_shape), cosine, sine_table).astype(bf16)
    keys_rot = rotate(qkv[:, H : 2 * H].reshape(head_shape), cosine, sine_table).astype(bf16)
    values = qkv[:, 2 * H : 3 * H].astype(bf16).reshape(head_shape)
    score_scale = 1.0 / math.sqrt(head_width)
    scores = ein32("bqhd,bkhd->bhqk", queries, keys_rot) * score_scale
    scores = jnp.where(allowed[:, None], scores, masked_score)
    row_peak = jnp.max(scores, axis=-1, keepdims=True)
    log_total = row_peak + jnp.log(jnp.sum(jnp.exp(scores - row_peak), axis=-1, keepdims=True))
    attn_probs = jnp.exp(scores - log_total)
    probs_half = attn_probs.astype(bf16)
    context = ein32("bhqk,bkhd->bqhd", probs_half, values).astype(bf16)
    context_flat = context.reshape(B * T, H)

    def at_home(partial_rows, collective):
        if not fast:
            return partial_rows
        return plane_sum(partial_rows.astype(bf16).reshape(B, T, D), collective)

    residual_mid = residual_in + branch_scale * at_home(dot32(context_flat, full_output), 4)
    normed_mid, inverse_mid = rms_forward(residual_mid, gain_ffn)
    normed_mid_half = normed_mid.astype(bf16)

    logits = dot32(normed_mid_half, full_router)
    expert_ids = jnp.arange(experts)
    route_mask = (routes[:, :, None] == expert_ids[None, None, :]).astype(f32)
    chosen = jnp.sum(logits[:, None, :] * route_mask, axis=-1)
    gate_probs = jax.nn.softmax(chosen, axis=-1)
    flat_routes = routes.reshape(2 * T)
    hits = (flat_routes[:, None] == expert_ids[None, :]).astype(bf16)
    order = jnp.arange(2 * T)
    before = (order[:, None] > order[None, :]).astype(bf16)
    earlier = dot32(before, hits)
    slot_index = jnp.sum(earlier * hits.astype(f32), axis=1).astype(jnp.int32)
    target = (flat_routes * capacity + slot_index).reshape(T, 2)
    slot_ids = jnp.arange(slots)
    pick = [(target[:, k][:, None] == slot_ids[None, :]).astype(bf16) for k in range(2)]

    notes = jnp.concatenate([gate_probs, target.astype(f32), jnp.zeros((T, 4), f32)], axis=1)
    notes = jnp.pad(jnp.transpose(notes), ((0, 0), (0, -T % 128)))
    spread = spread_blocks if fast else spread_pair
    w_pair, all_normed, all_notes = spread(nz, (normed_mid_half, notes), packed[0], moved_up, 2)
    w_pair = w_pair.reshape(n_shard * R, 2 * Fp)
    devices = n_shard * n_exp
    flat_notes = all_notes.reshape(devices, 8, -1)[:, :, :T]
    wanted = (e_index * capacity + jnp.arange(capacity)).astype(f32)
    found = [flat_notes[:, 2 + k, None, :] == wanted[None, :, None] for k in range(2)]
    gate_rows = jnp.sum(
        jnp.where(found[0], flat_notes[:, 0, None, :], 0.0)
        + jnp.where(found[1], flat_notes[:, 1, None, :], 0.0),
        axis=-1,
    ).reshape(devices * capacity, 1)
    chosen_rows = (found[0] | found[1]).astype(bf16)

    def take(blocks):
        rows = ein32("spt,std->spd", chosen_rows, blocks.reshape(devices, T, D))
        return rows.astype(bf16).reshape(devices * capacity, D)

    arrived = take(all_normed)
    grad_scale = gate_rows * branch_scale
    pre = dot32(arrived, w_pair)
    gate_part, up_part = pre[:, :Fp], pre[:, Fp:]
    sigmoid_gate = jax.nn.sigmoid(gate_part)
    silu_gate = gate_part * sigmoid_gate
    activated = (silu_gate * up_part).astype(bf16)
    out_rows, all_cotangent = lax.optimization_barrier(
        (dot32(activated, down).astype(bf16), all_cotangent)
    )
    out_sum = lax.psum_scatter(out_rows, SHARD, scatter_dimension=0, tiled=True)
    cotangent_rows = take(all_cotangent)

    raw_grad = dot_dims(cotangent_rows, down, 1, 1)
    row_dots = branch_scale * jnp.sum(raw_grad * activated.astype(f32), axis=1)
    row_dots = row_dots.reshape(devices, capacity, 1)
    token_dots = [jnp.sum(jnp.where(found[k], row_dots, 0.0), axis=1) for k in range(2)]
    token_dots = jnp.stack(token_dots, axis=1).reshape(nz, 2, n_exp, 2, T)
    token_dots = jnp.pad(token_dots, ((0, 0),) * 3 + ((0, 6), (0, -T % 128)))
    act_grad = grad_scale * raw_grad
    gate_grads = act_grad * up_part * sigmoid_gate * (1.0 + gate_part * (1.0 - sigmoid_gate))
    gate_grads, up_grads = gate_grads.astype(bf16), (act_grad * silu_gate).astype(bf16)
    pre_grad = jnp.concatenate([gate_grads, up_grads], axis=1)
    in_rows = dot_dims(pre_grad, w_pair, 1, 1).astype(bf16)
    scaled = (grad_scale * activated.astype(f32)).astype(bf16)
    gate_term, up_term = [
        dot_dims(arrived, x, 0, 0).astype(bf16).reshape(n_shard, R, Fp)
        for x in (gate_grads, up_grads)
    ]
    gate_term, up_term = lax.optimization_barrier((gate_term, up_term))
    up_term = lax.all_to_all(up_term, SHARD, split_axis=0, concat_axis=0, tiled=True)
    in_rows = in_rows.reshape(nz, 2, n_exp, capacity, D)
    collect = collect_rows if fast else collect_plain
    normed_mid_grad, gate_grad = collect(nz, in_rows, all_notes, token_dots, T)
    gate_grad = jnp.transpose(gate_grad[:2, :T])
    up_term, normed_mid_grad, out_sum, gate_term = lax.optimization_barrier(
        (up_term, normed_mid_grad, out_sum, gate_term)
    )
    gate_term = lax.all_to_all(gate_term, SHARD, split_axis=0, concat_axis=0, tiled=True)

    upstream = cotangent.astype(f32)
    chosen_grad = gate_probs * (gate_grad - jnp.sum(gate_probs * gate_grad, axis=-1, keepdims=True))
    logit_grad = jnp.sum(chosen_grad[:, :, None] * route_mask, axis=1)
    normed_mid_grad = normed_mid_grad + jnp.dot(
        logit_grad, jnp.transpose(full_router.astype(f32)), precision=highest
    )
    router_grad = jnp.dot(
        jnp.transpose(normed_mid_half.astype(f32)), logit_grad, precision=highest
    )
    mid_norm_grad, gain_ffn_grad = rms_backward(
        residual_mid, inverse_mid, gain_ffn, normed_mid_grad
    )
    residual_grad = upstream + mid_norm_grad
    branch_grad = (branch_scale * residual_grad).astype(bf16)

    if fast:
        branch_grad, down_term = plane_gather(
            branch_grad, jnp.transpose(scaled), cotangent_rows, 5
        )
        branch_grad = branch_grad.reshape(B * T, D)
    else:
        down_term = dot_dims(scaled, cotangent_rows, 0, 0)
    grad_w_down = lined_up(down_term, F)
    output_grad = dot_dims(context_flat, branch_grad, 0, 0)
    context_grad = dot_dims(branch_grad, full_output, 1, 1).reshape(head_shape)
    row_delta = jnp.sum(context_grad * context.astype(f32), axis=-1)
    context_grad_half = context_grad.astype(bf16)
    probs_grad = ein32("bqhd,bkhd->bhqk", context_grad_half, values)
    scores_grad = (
        attn_probs * (probs_grad - jnp.transpose(row_delta, (0, 2, 1))[..., None]) * score_scale
    ).astype(bf16)
    queries_grad = ein32("bhqk,bkhd->bqhd", scores_grad, keys_rot)
    keys_grad = ein32("bhqk,bqhd->bkhd", scores_grad, queries)
    values_grad = ein32("bhqk,bqhd->bkhd", probs_half, context_grad_half)
    qkv_grad = jnp.concatenate(
        [
            rotate(queries_grad, cosine, -sine_table).reshape(B * T, H).astype(bf16),
            rotate(keys_grad, cosine, -sine_table).reshape(B * T, H).astype(bf16),
            values_grad.reshape(B * T, H).astype(bf16),
            jnp.zeros((B * T, full_qkv.shape[1] - 3 * H), bf16),
        ],
        axis=1,
    )
    qkv_weight_grad = dot_dims(normed_half, qkv_grad, 0, 0)
    near_grad = dot_dims(qkv_grad, full_qkv, 1, 1)
    gain_attn_grad = jnp.sum(near_grad * near_in * near_inverse, axis=0)

    small_grad = jnp.concatenate(
        [router_grad, gain_attn_grad[:, None], gain_ffn_grad[:, None]], axis=1
    )
    small_grad = jnp.pad(small_grad, ((0, 0), (0, 128 - small_grad.shape[1])))
    small_grad, gate_term = lax.optimization_barrier((small_grad, gate_term))
    sum_query, sum_key, sum_value, sum_output, small_sum, normed_in_grad, back = settle(
        nz, fast, qkv_weight_grad, output_grad, small_grad, near_grad, out_sum
    )
    grad_w_in = unpack_columns(gate_term, up_term, F)
    mixture = gate_probs[:, 0:1] * dot32(pick[0], back) + gate_probs[:, 1:2] * dot32(pick[1], back)
    activations = (residual_mid + branch_scale * mixture).astype(bf16)
    in_norm_grad = rms_backward(residual_in, inverse_in, gain_attn, normed_in_grad)[0]
    grad_tokens = residual_grad + in_norm_grad
    return (
        activations,
        grad_tokens,
        small_sum[:, experts],
        sum_query,
        sum_key,
        sum_value,
        sum_output,
        small_sum[:, experts + 1],
        small_sum[:, :experts],
        grad_w_in,
        grad_w_down,
    )


def solution(mesh):
    n_expert, n_shard = mesh.devices.shape
    chips = Mesh(mesh.devices.reshape(n_expert, n_shard // 2, 2), ("expert", "z", "core"))
    rows = P(("expert", "z", "core"), None)
    shard = P(SHARD)
    shard2 = P(SHARD, None)
    shard3 = P(SHARD, "expert", None)
    in_specs = (
        rows,
        rows,
        rows,
        shard,
        shard2,
        shard2,
        shard2,
        shard2,
        shard,
        shard2,
        shard3,
        shard3,
        rows,
    )
    out_specs = (
        rows,
        rows,
        shard,
        shard2,
        shard2,
        shard2,
        shard2,
        shard,
        shard2,
        shard3,
        shard3,
    )
    return jax.shard_map(
        on_device, mesh=chips, in_specs=in_specs, out_specs=out_specs, check_vma=False
    )
```
